32 devices in a mesh: seq: 4 (over y, x), ctx: 8 (over z, core).
Axes of the slice: x: 2, y: 2, z: 4, core: 2. Of those that a mesh axis runs over, the one named last changes fastest.
Arguments:
- tokens: bfloat16 [4, 1024, 1088], P('seq', 'ctx'), may hold values from -6 to 6
- lengths: int32 [4], P('seq'), may hold values from 1 to 1024, 3072 in all
- block_order: int32 [16], replicated, may hold values from 0 to 15, each once
- attention_weights: bfloat16 [4352, 1088], P(('seq', 'ctx'))
- up_weights: bfloat16 [1088, 4352], P(None, ('seq', 'ctx')), may hold values from -0.1875 to 0.1875
- down_weights: bfloat16 [4352, 1088], P(('seq', 'ctx')), may hold values from -0.09375 to 0.09375
- norm_gains: bfloat16 [2176], P(('seq', 'ctx')), may hold values from 0.25 to 1.75
- biases: bfloat16 [10880], P(('seq', 'ctx')), may hold values from -1.796875 to 1.796875
- cotangent: bfloat16 [4, 1024, 1088], P('seq', 'ctx'), may hold values from -6 to 6
Outputs:
- output: bfloat16 [4, 1024, 1088], P('seq', 'ctx')
- grad_tokens: float32 [4, 1024, 1088], P('seq', 'ctx')
- grad_attention: float32 [4352, 1088], P(('seq', 'ctx'))
- grad_up: float32 [1088, 4352], P(None, ('seq', 'ctx'))
- grad_down: float32 [4352, 1088], P(('seq', 'ctx'))
- grad_gains: float32 [2176], P(('seq', 'ctx'))
- grad_biases: float32 [10880], P(('seq', 'ctx'))
The draws below stay inside these ranges and needn't reach their ends.
Inputs may be any that keep to these rules, and one draw needn't show every extreme that they name: The 4 lengths add up to 3072; the longest is exactly 1024. `block_order`: each of the 16 blocks of positions is named exactly once.
All inputs are finite; a program needn't handle non-finite values. No bound on the sum of `lengths` on one device may be relied on, other than what follows from the above.
Results may differ from the reference program's by a relative error of at most 0.011.
Values may be sent and summed in bfloat16 or wider, within the bound.
A program may use at most 256 MiB of HBM per device.

```python
import math
import jax
import jax.numpy as jnp
import numpy as np
from jax import lax

D = 1088
HEADS = 17
HDIM = 64
FF = 4352
SLOT = 1024
SEQS = 4
BLOCK_LEN = 64
BLOCKS = 16


def draw_attention_weights(key, part):
    row_index = jnp.arange(4 * D)[:, None]
    scales = jnp.where(row_index < 3 * D, D ** (-0.5), (SLOT / D) ** 0.5 / 4.0).astype(jnp.float32)
    base = jax.random.normal(key, (4 * D, D), jnp.float32)
    return (base * scales).astype(jnp.bfloat16)


def steps_of(own_key, dims, pieces, low, top_value):
    def one(axis_at, parts):
        heights = jax.random.uniform(jax.random.fold_in(jax.random.fold_in(own_key, 6), axis_at), (parts,), jnp.float32, low / len(pieces), top_value / len(pieces))
        return jnp.repeat(jnp.exp(heights), dims[axis_at] // parts).reshape((-1,) + (1,) * (len(dims) - axis_at - 1))

    factor_of = one(*pieces[0])
    for cut in pieces[1:]:
        factor_of = factor_of * one(*cut)
    return factor_of


def split_up(amount, total, limit, lean):
    weights = [(1 << 20) // math.isqrt(standing ** lean) + 1 for standing in range(2, amount + 1)]
    rest, counts = total - limit - (amount - 1), [1] * (amount - 1)
    while rest > 0:
        candidates = [i for i in range(amount - 1) if counts[i] < limit]
        whole, remaining = sum([weights[i] for i in candidates]), rest
        for i in candidates:
            extra = min(limit - counts[i], max(1, remaining * weights[i] // whole), rest)
            counts[i] = counts[i] + extra
            rest = rest - extra
    return np.array([limit] + counts)


def ragged_sizes(key, number_of, total, bound, slope):
    if number_of == 2:
        one = jax.random.randint(key, (), max(1, total - bound), min(bound, total - 1) + 1)
        return jnp.stack([one, total - one])
    tallies = jnp.asarray(split_up(number_of, total, bound, slope), jnp.int32)
    twos = (number_of - 1) // 2
    source_of, sink = tallies[1:1 + 2 * twos:2], tallies[2:2 + 2 * twos:2]
    margin = jnp.minimum(source_of - 1, bound - sink)
    shifted = jax.random.randint(jax.random.fold_in(key, 1), (twos,), 0, 1 << 20) % (margin + 1)
    tallies = tallies.at[1:1 + 2 * twos:2].set(source_of - shifted).at[2:2 + 2 * twos:2].set(sink + shifted)
    return tallies[jax.random.permutation(jax.random.fold_in(key, 2), number_of)]


def noise(stream_key, dims, width, reach, split=(), held_as=jnp.bfloat16):
    loudness = steps_of(stream_key, dims, split, -0.22, 0.18) if split else 1.0
    array = jax.random.normal(stream_key, dims, jnp.float32) * width * loudness
    return jnp.minimum(jnp.maximum(array, -reach), reach).astype(held_as)


def setup_inputs(seed: int = 0) -> dict:
    arg_keys = jax.random.split(jax.random.key(seed), 10)
    tokens = noise(arg_keys[0], (SEQS, SLOT, D), 1.0, 6.0, ((0, 4), (1, 8)))
    lengths = ragged_sizes(arg_keys[1], SEQS, 3 * SLOT, SLOT, 1).astype(jnp.int32)
    block_order = jax.random.permutation(arg_keys[2], BLOCKS).astype(jnp.int32)
    attention_weights = draw_attention_weights(jax.random.fold_in(arg_keys[9], 71), 0)
    up_weights = noise(arg_keys[4], (D, FF), D ** -0.5, 0.1875, ((1, 32),))
    down_weights = noise(arg_keys[5], (FF, D), FF ** -0.5, 0.09375, ((0, 32),))
    norm_gains = jnp.clip(1.0 + 0.15 * jax.random.normal(arg_keys[6], (2 * D,), jnp.float32), 0.25, 1.75).astype(jnp.bfloat16)
    biases = noise(arg_keys[7], (6 * D + FF,), 0.3, 1.796875, ((0, 32),))
    cotangent = noise(arg_keys[8], (SEQS, SLOT, D), 1.0, 6.0, ((0, 4), (1, 8)))
    return dict(tokens=tokens, lengths=lengths, block_order=block_order, attention_weights=attention_weights, up_weights=up_weights, down_weights=down_weights, norm_gains=norm_gains, biases=biases, cotangent=cotangent)


@jax.custom_vjp
def low(v):
    return lax.optimization_barrier(v.astype(jnp.bfloat16)).astype(jnp.float32)

@jax.custom_vjp
def low_back(v):
    return v

def low_keep(v):
    return (low(v), None)

def low_pass(kept, grad):
    return (grad,)

def back_keep(v):
    return (v, None)

def back_low(kept, grad):
    return (low(grad),)
low.defvjp(low_keep, low_pass)
low_back.defvjp(back_keep, back_low)
epsilon = 1e-05

def matmul(left, right):
    return jnp.dot(left, right, precision=lax.Precision.HIGHEST, preferred_element_type=jnp.float32)

def layer_norm(values, gain, shift):
    centre = values - lax.optimization_barrier(jnp.mean(values, axis=-1, keepdims=True))
    spread = lax.optimization_barrier(jnp.mean(centre * centre, axis=-1, keepdims=True))
    return centre * lax.rsqrt(spread + epsilon) * gain + shift

def slot_positions(block_order):
    within = jnp.arange(BLOCK_LEN, dtype=jnp.int32)
    return (block_order[:, None] * BLOCK_LEN + within[None, :]).reshape(SLOT).astype(jnp.int32)

def attend(queries, keys, values, position, live):
    block_rows = math.gcd(512, SLOT)
    key_heads = keys.reshape(SLOT, HEADS, HDIM)
    value_heads = values.reshape(SLOT, HEADS, HDIM)
    key_live = live > 0
    scale_factor = HDIM ** (-0.5)

    def score_block(block_inputs):
        query_rows, query_where = block_inputs
        query_heads = query_rows.reshape(block_rows, HEADS, HDIM)
        scores = jnp.einsum('qhd,khd->hqk', query_heads, key_heads, precision=lax.Precision.HIGHEST) * scale_factor
        scores = low_back(scores)
        visible = (position[None, :] <= query_where[:, None]) & key_live[None, :]
        scores = jnp.where(visible[None], scores, -1e+30)
        attn_probs = low(jax.nn.softmax(scores, axis=-1))
        mixed = jnp.einsum('hqk,khd->qhd', attn_probs, value_heads, precision=lax.Precision.HIGHEST)
        return mixed.reshape(block_rows, D)
    block_count = SLOT // block_rows
    mixed_all = lax.map(jax.checkpoint(score_block), (queries.reshape(block_count, block_rows, D), position.reshape(block_count, block_rows)))
    return mixed_all.reshape(SLOT, D)

def forward_single(inputs, position, live, attention, weight_up, weight_down, gain_vector, bias_vector):
    gain_first = gain_vector[:D]
    gain_second = gain_vector[D:]
    shift_first = bias_vector[0:D]
    bias_query = bias_vector[D:2 * D]
    bias_value = bias_vector[2 * D:3 * D]
    bias_output = bias_vector[3 * D:4 * D]
    shift_second = bias_vector[4 * D:5 * D]
    bias_down = bias_vector[5 * D:6 * D]
    bias_up = bias_vector[6 * D:]
    normed_first = low(layer_norm(inputs, gain_first, shift_first))
    queries = low(low_back(matmul(normed_first, attention[:D]) + bias_query))
    keys = low(low_back(matmul(normed_first, attention[D:2 * D])))
    values = low(low_back(matmul(normed_first, attention[2 * D:3 * D]) + bias_value))
    attended = low(low_back(attend(queries, keys, values, position, live)))
    branch = low_back(matmul(attended, attention[3 * D:]) + bias_output)
    hidden = inputs + branch
    normed_second = low(layer_norm(hidden, gain_second, shift_second))
    preact = low_back(matmul(normed_second, weight_up) + bias_up)
    activated = low(jax.nn.gelu(preact, approximate=False))
    live_rows = live.astype(inputs.dtype)[:, None]
    return live_rows * (hidden + matmul(activated, weight_down) + bias_down)

def reference(tokens, lengths, block_order, attention_weights, up_weights, down_weights, norm_gains, biases, cotangent):
    position = slot_positions(block_order)
    inputs = tokens.astype(jnp.float32)
    params = (attention_weights.astype(jnp.float32), up_weights.astype(jnp.float32), down_weights.astype(jnp.float32), norm_gains.astype(jnp.float32), biases.astype(jnp.float32))

    def whole(all_inputs, attention, weight_up, weight_down, gain_vector, bias_vector):

        def single_sequence(sequence_inputs):
            rows_in, seq_length = sequence_inputs
            live = (position < seq_length).astype(jnp.int32)
            return forward_single(rows_in, position, live, attention, weight_up, weight_down, gain_vector, bias_vector)
        return lax.map(single_sequence, (all_inputs, lengths))
    output, pullback = jax.vjp(whole, inputs, *params)
    grads = pullback(cotangent.astype(jnp.float32))
    return (output.astype(jnp.bfloat16), grads[0], grads[1], grads[2], grads[3], grads[4], grads[5])
```

```python
import math

import jax
import jax.numpy as jnp
from jax import lax
from jax.sharding import PartitionSpec as P

HEADS = 17
EPS = 1e-05
F32 = jnp.float32
BF16 = jnp.bfloat16


def norm_stats(values):
    centre = values - jnp.mean(values, axis=-1, keepdims=True)
    rstd = lax.rsqrt(jnp.mean(centre * centre, axis=-1, keepdims=True) + EPS)
    return centre * rstd, rstd


def norm_back(grad, xhat, rstd, gain):
    e = grad * gain
    mean_e = jnp.mean(e, axis=-1, keepdims=True)
    mean_ex = jnp.mean(e * xhat, axis=-1, keepdims=True)
    return (e - mean_e - xhat * mean_ex) * rstd


def dot(a, b, ca, cb):
    return lax.dot_general(a, b, (((ca,), (cb,)), ((), ())), preferred_element_type=F32)


def rows_sum(v):
    return jnp.sum(v.astype(F32), axis=0, keepdims=True)


class Sizes:
    def __init__(self, rows, width, block_count):
        self.rows, self.width = rows, width
        self.ctx, self.seq = lax.axis_size("ctx"), lax.axis_size("seq")
        self.slot = rows * self.ctx
        self.block_len = self.slot // block_count
        self.head = width // HEADS
        self.full = HEADS // self.ctx
        self.full_width = self.full * self.head
        self.main = self.full_width * self.ctx
        self.rest = HEADS - self.full * self.ctx
        self.rest_width = self.rest * self.head
        self.shard = width // self.ctx


def stage_a(z, x, w):
    k = lax.axis_index("ctx")
    x_all = lax.all_gather(x, "ctx", axis=0, tiled=True)
    w_all = lax.all_gather(w, "seq", axis=0)
    wm = w_all[:3, :, : z.main].reshape(3, z.shard, z.ctx, z.full_width)
    wf = lax.all_to_all(wm, "ctx", split_axis=2, concat_axis=1, tiled=True).reshape(
        3, z.width, z.full_width
    )
    wr = lax.all_gather(w_all[:3, :, z.main :], "ctx", axis=1, tiled=True)
    wo = lax.all_gather(w_all[3], "ctx", axis=0, tiled=True)
    wo_f = lax.dynamic_slice_in_dim(wo, k * z.full_width, z.full_width)
    wo_r = wo[z.main :]
    return x_all, wf, wr, wo_f, wo_r


def heads_of(v, h):
    return v.reshape(v.shape[0], -1, h).transpose(1, 0, 2)


def attend(z, q, k, v, qpos, kpos, length):
    s = jnp.einsum("hqd,hkd->hkq", heads_of(q, z.head), heads_of(k, z.head), preferred_element_type=F32)
    s = s * (z.head ** -0.5)
    seen = (kpos[:, None] <= qpos[None, :]) & (kpos[:, None] < length)
    s = jnp.where(seen[None], s, -1e30)
    e = jnp.exp(s - jnp.max(s, axis=1, keepdims=True))
    p = (e / jnp.sum(e, axis=1, keepdims=True)).astype(BF16)
    o = jnp.einsum("hkq,hkd->qhd", p, heads_of(v, z.head), preferred_element_type=F32)
    return p, o.reshape(q.shape).astype(BF16)


def stage_b(z, x_all, wf, wr, gain, shift, bq_f, bq_r, bv_f, bv_r, pos, length):
    i = lax.axis_index("ctx")
    n1 = (norm_stats(x_all.astype(F32))[0] * gain + shift).astype(BF16)
    mine = lax.dynamic_slice_in_dim(n1, i * z.rows, z.rows)
    qpos = lax.dynamic_slice_in_dim(pos, i * z.rows, z.rows)
    out = dict(n1=n1)
    if z.full:
        q = (dot(n1, wf[0], 1, 0) + bq_f).astype(BF16)
        k = dot(n1, wf[1], 1, 0).astype(BF16)
        v = (dot(n1, wf[2], 1, 0) + bv_f).astype(BF16)
        p, o = attend(z, q, k, v, pos, pos, length)
        out.update(q_f=q, k_f=k, v_f=v, p_f=p, o_f=o)
    if z.rest:
        q = (dot(mine, wr[0], 1, 0) + bq_r).astype(BF16)
        k = dot(n1, wr[1], 1, 0).astype(BF16)
        v = (dot(n1, wr[2], 1, 0) + bv_r).astype(BF16)
        p, o = attend(z, q, k, v, qpos, pos, length)
        out.update(q_r=q, k_r=k, v_r=v, p_r=p, o_r=o)
    return out


def stage_c(z, b, wo_f, wo_r, x, cot, live, up_t, down, prm):
    branch = prm["b_o"]
    if z.full:
        part = dot(b["o_f"], wo_f, 1, 0).astype(BF16)
        branch = branch + lax.psum_scatter(part.astype(F32), "ctx", scatter_dimension=0, tiled=True)
    if z.rest:
        branch = branch + dot(b["o_r"], wo_r, 1, 0)
    hidden = x.astype(F32) + branch
    xhat, rstd = norm_stats(hidden)
    n2 = (xhat * prm["gain2"] + prm["shift2"]).astype(BF16)
    upstream = (live * cot.astype(F32)).astype(BF16)
    n2a = lax.all_gather(n2, "seq", axis=0, tiled=True)
    ua = lax.all_gather(upstream, "seq", axis=0, tiled=True)
    pre = dot(n2a, up_t, 1, 1) + prm["b_up"]
    cdf = 0.5 * (1.0 + lax.erf(pre * (0.5 ** 0.5)))
    act = (pre * cdf).astype(BF16)
    dgelu = cdf + pre * jnp.exp(-0.5 * pre * pre) * (1.0 / math.sqrt(2.0 * math.pi))
    gact = dot(ua, down, 1, 1)
    gpre = (gact * dgelu).astype(BF16)
    gn2p = dot(gpre, up_t, 1, 0).astype(BF16)
    gn2 = lax.psum_scatter(gn2p.astype(F32), "seq", scatter_dimension=0, tiled=True)
    ffp = dot(act, down, 1, 0).astype(BF16)
    ff = lax.psum_scatter(ffp.astype(F32), "seq", scatter_dimension=0, tiled=True)
    output = (live * (hidden + ff + prm["b_down"])).astype(BF16)
    g_up_t = dot(gpre, n2a, 0, 0).astype(BF16)
    g_down = dot(act, ua, 0, 0).astype(BF16)
    gh = upstream.astype(F32) + norm_back(gn2, xhat, rstd, prm["gain2"])
    gb = gh.astype(BF16)
    small = dict(gain2=rows_sum(gn2 * xhat), shift2=rows_sum(gn2), b_o=rows_sum(gb),
                 b_down=rows_sum(upstream), b_up=rows_sum(gpre))
    return output, gh, gb, g_up_t, g_down, small


def attend_back(z, q, k, v, p, go):
    gp = jnp.einsum("hqd,hkd->hkq", heads_of(go, z.head), heads_of(v, z.head), preferred_element_type=F32)
    pf = p.astype(F32)
    delta = jnp.sum(gp * pf, axis=1, keepdims=True)
    gs = (pf * (gp - delta)).astype(BF16)
    sc = z.head ** -0.5
    gq = jnp.einsum("hkq,hkd->qhd", gs, heads_of(k, z.head), preferred_element_type=F32) * sc
    gk = jnp.einsum("hkq,hqd->khd", gs, heads_of(q, z.head), preferred_element_type=F32) * sc
    gv = jnp.einsum("hkq,hqd->khd", p, heads_of(go, z.head), preferred_element_type=F32)
    return gq.reshape(q.shape).astype(BF16), gk.reshape(k.shape).astype(BF16), gv.reshape(v.shape).astype(BF16)


def stage_d(z, b, gb, gba, wo_f, wo_r):
    i = lax.axis_index("ctx")
    n1 = b["n1"]
    mine = lax.dynamic_slice_in_dim(n1, i * z.rows, z.rows)
    out = {}
    if z.full:
        go = dot(gba, wo_f, 1, 1).astype(BF16)
        gq, gk, gv = attend_back(z, b["q_f"], b["k_f"], b["v_f"], b["p_f"], go)
        out.update(gq_f=gq, gk_f=gk, gv_f=gv, gwo_f=dot(b["o_f"], gba, 0, 0))
        out["gw_f"] = jnp.stack([dot(n1, g, 0, 0) for g in (gq, gk, gv)])
    if z.rest:
        go = dot(gb, wo_r, 1, 1).astype(BF16)
        gq, gk, gv = attend_back(z, b["q_r"], b["k_r"], b["v_r"], b["p_r"], go)
        out.update(gq_r=gq, gk_r=gk, gv_r=gv, gwo_r=dot(b["o_r"], gb, 0, 0))
        out["gw_r"] = jnp.stack([dot(mine, gq, 0, 0), dot(n1, gk, 0, 0), dot(n1, gv, 0, 0)])
    return out


def stage_e(z, d, wf, wr, x, gh, gain1, small):
    i, s = lax.axis_index("ctx"), lax.axis_index("seq")
    part = 0.0
    own = 0.0
    if z.full:
        part = part + dot(d["gq_f"], wf[0], 1, 1) + dot(d["gk_f"], wf[1], 1, 1) + dot(d["gv_f"], wf[2], 1, 1)
    if z.rest:
        part = part + dot(d["gk_r"], wr[1], 1, 1) + dot(d["gv_r"], wr[2], 1, 1)
        own = own + dot(d["gq_r"], wr[0], 1, 1)
    gn1 = own + lax.psum_scatter(part.astype(BF16).astype(F32), "ctx", scatter_dimension=0, tiled=True)
    xhat, rstd = norm_stats(x.astype(F32))
    gtok = gh + norm_back(gn1, xhat, rstd, gain1)
    small = dict(small, gain1=rows_sum(gn1 * xhat), shift1=rows_sum(gn1))
    row = jnp.zeros((1, z.width), F32)
    for name, key in (("b_q", "gq"), ("b_v", "gv")):
        r = row
        if z.full:
            r = lax.dynamic_update_slice(r, rows_sum(d[key + "_f"]), (0, i * z.full_width))
        if z.rest:
            r = r.at[:, z.main :].add(rows_sum(d[key + "_r"]))
        small[name] = r
    full = jnp.zeros((4, z.width, z.width), F32)
    if z.full:
        full = lax.dynamic_update_slice(full, d["gw_f"], (0, 0, i * z.full_width))
        full = lax.dynamic_update_slice(full, d["gwo_f"][None], (3, i * z.full_width, 0))
    if z.rest:
        full = full.at[:3, :, z.main :].add(d["gw_r"])
        full = full.at[3, z.main :, :].add(d["gwo_r"])
    gw = lax.psum_scatter(full.reshape(4 * z.width, z.width).astype(BF16), ("seq", "ctx"), scatter_dimension=0, tiled=True)
    return gtok, gw.astype(F32), small


def shards(tokens, lengths, block_order, attention_weights, up_weights, down_weights, norm_gains, biases, cotangent):
    z = Sizes(tokens.shape[1], tokens.shape[2], block_order.shape[0])
    i, s = lax.axis_index("ctx"), lax.axis_index("seq")
    D = z.width
    x, cot = tokens[0], cotangent[0]
    length = lengths[0]
    pos = (block_order[:, None] * z.block_len + jnp.arange(z.block_len, dtype=jnp.int32)[None, :]).reshape(z.slot)
    my_pos = lax.dynamic_slice_in_dim(pos, i * z.rows, z.rows)
    live = (my_pos < length).astype(F32)[:, None]
    both = lax.all_gather(jnp.concatenate([norm_gains, biases]), ("seq", "ctx"), axis=0)
    gains = both[:, : norm_gains.shape[0]].reshape(-1).astype(F32)
    bias = both[:, norm_gains.shape[0] :].reshape(-1).astype(F32)
    row = lambda v: v[None, :]
    piece = [row(bias[j * D : (j + 1) * D]) for j in range(6)]
    gain1, gain2 = row(gains[:D]), row(gains[D:])
    b_up = row(lax.dynamic_slice_in_dim(bias[6 * D :], s * (z.ctx * up_weights.shape[1]), z.ctx * up_weights.shape[1]))
    prm = dict(gain2=gain2, shift2=piece[4], b_o=piece[3], b_down=piece[5], b_up=b_up)
    fslice = lambda v: lax.dynamic_slice(v, (0, i * z.full_width), (1, z.full_width))
    up_t = lax.all_gather(up_weights.T, "ctx", axis=0, tiled=True)
    down = lax.all_gather(down_weights, "ctx", axis=0, tiled=True)

    x_all, wf, wr, wo_f, wo_r = stage_a(z, x, attention_weights)
    b = stage_b(z, x_all, wf, wr, gain1, piece[0], fslice(piece[1]), piece[1][:, z.main :],
                fslice(piece[2]), piece[2][:, z.main :], pos, length)
    output, gh, gb, g_up_t, g_down, small = stage_c(z, b, wo_f, wo_r, x, cot, live, up_t, down, prm)
    g_up_own = lax.psum_scatter(g_up_t, "ctx", scatter_dimension=0, tiled=True).astype(F32).T
    g_down_own = lax.psum_scatter(g_down, "ctx", scatter_dimension=0, tiled=True).astype(F32)
    gba = lax.all_gather(gb, "ctx", axis=0, tiled=True) if z.full else None
    d = stage_d(z, b, gb, gba, wo_f, wo_r)
    gtok, gw, small = stage_e(z, d, wf, wr, x, gh, gain1, small)
    b_up_g = lax.psum(small.pop("b_up"), "ctx")
    b_up_all = lax.all_gather(b_up_g[0], "seq", axis=0, tiled=True)
    tot = lax.psum(jnp.concatenate([small[n] for n in ("gain1", "gain2", "shift1", "b_q", "b_v", "b_o", "shift2", "b_down")]), ("seq", "ctx"))
    me = s * z.ctx + i
    n_g, n_b = norm_gains.shape[0], biases.shape[0]
    g_gain = lax.dynamic_slice_in_dim(tot[:2].reshape(-1), me * n_g, n_g)
    g_bias = lax.dynamic_slice_in_dim(jnp.concatenate([tot[2:].reshape(-1), b_up_all]), me * n_b, n_b)
    return output[None], gtok[None], gw, g_up_own, g_down_own, g_gain, g_bias


def solution(mesh):
    in_specs = (
        P("seq", "ctx", None), P("seq"), P(), P(("seq", "ctx"), None), P(None, ("seq", "ctx")),
        P(("seq", "ctx"), None), P(("seq", "ctx")), P(("seq", "ctx")), P("seq", "ctx", None),
    )
    out_specs = (
        P("seq", "ctx", None), P("seq", "ctx", None), P(("seq", "ctx"), None), P(None, ("seq", "ctx")),
        P(("seq", "ctx"), None), P(("seq", "ctx")), P(("seq", "ctx")),
    )
    return jax.shard_map(shards, mesh=mesh, in_specs=in_specs, out_specs=out_specs, check_vma=False)
```

```python
import math
from functools import partial

import jax
import jax.numpy as jnp
from jax import lax
from jax.experimental import pallas as pl
from jax.experimental.pallas import tpu as pltpu
from jax.sharding import PartitionSpec as P

HEADS = 17
EPS = 1e-05
F32 = jnp.float32
BF16 = jnp.bfloat16


def norm_stats(values):
    centre = values - jnp.mean(values, axis=-1, keepdims=True)
    rstd = lax.rsqrt(jnp.mean(centre * centre, axis=-1, keepdims=True) + EPS)
    return centre * rstd, rstd


def norm_back(grad, xhat, rstd, gain):
    e = grad * gain
    mean_e = jnp.mean(e, axis=-1, keepdims=True)
    mean_ex = jnp.mean(e * xhat, axis=-1, keepdims=True)
    return (e - mean_e - xhat * mean_ex) * rstd


def dot(a, b, ca, cb):
    return lax.dot_general(a, b, (((ca,), (cb,)), ((), ())), preferred_element_type=F32)


def rows_sum(v):
    return jnp.sum(v.astype(F32), axis=0, keepdims=True)


class Sizes:
    def __init__(self, rows, width, block_count):
        self.rows, self.width = rows, width
        self.ctx, self.seq = lax.axis_size("ctx"), lax.axis_size("seq")
        self.slot = rows * self.ctx
        self.block_len = self.slot // block_count
        self.head = width // HEADS
        self.full = HEADS // self.ctx
        self.full_width = self.full * self.head
        self.main = self.full_width * self.ctx
        self.rest = HEADS - self.full * self.ctx
        self.rest_width = self.rest * self.head
        self.shard = width // self.ctx


def stage_a(z, x, w):
    k = lax.axis_index("ctx")
    x_all = lax.all_gather(x, "ctx", axis=0, tiled=True)
    w_all = lax.all_gather(w, "seq", axis=0)
    wm = w_all[:3, :, : z.main].reshape(3, z.shard, z.ctx, z.full_width)
    wf = lax.all_to_all(wm, "ctx", split_axis=2, concat_axis=1, tiled=True).reshape(
        3, z.width, z.full_width
    )
    wr = lax.all_gather(w_all[:3, :, z.main :], "ctx", axis=1, tiled=True)
    wo = lax.all_gather(w_all[3], "ctx", axis=0, tiled=True)
    wo_f = lax.dynamic_slice_in_dim(wo, k * z.full_width, z.full_width)
    wo_r = wo[z.main :]
    return x_all, wf, wr, wo_f, wo_r


def heads_of(v, h):
    return v.reshape(v.shape[0], -1, h).transpose(1, 0, 2)


def attend(z, q, k, v, qpos, kpos, length):
    s = jnp.einsum("hqd,hkd->hkq", heads_of(q, z.head), heads_of(k, z.head), preferred_element_type=F32)
    s = s * (z.head ** -0.5)
    seen = (kpos[:, None] <= qpos[None, :]) & (kpos[:, None] < length)
    s = jnp.where(seen[None], s, -1e30)
    e = jnp.exp(s - jnp.max(s, axis=1, keepdims=True))
    p = (e / jnp.sum(e, axis=1, keepdims=True)).astype(BF16)
    o = jnp.einsum("hkq,hkd->qhd", p, heads_of(v, z.head), preferred_element_type=F32)
    return p, o.reshape(q.shape).astype(BF16)


def stage_b(z, x_all, wf, wr, gain, shift, bq_f, bq_r, bv_f, bv_r, pos, length):
    i = lax.axis_index("ctx")
    n1 = (norm_stats(x_all.astype(F32))[0] * gain + shift).astype(BF16)
    mine = lax.dynamic_slice_in_dim(n1, i * z.rows, z.rows)
    qpos = lax.dynamic_slice_in_dim(pos, i * z.rows, z.rows)
    out = dict(n1=n1)
    if z.full:
        q = (dot(n1, wf[0], 1, 0) + bq_f).astype(BF16)
        k = dot(n1, wf[1], 1, 0).astype(BF16)
        v = (dot(n1, wf[2], 1, 0) + bv_f).astype(BF16)
        p, o = attend(z, q, k, v, pos, pos, length)
        out.update(q_f=q, k_f=k, v_f=v, p_f=p, o_f=o)
    if z.rest:
        q = (dot(mine, wr[0], 1, 0) + bq_r).astype(BF16)
        k = dot(n1, wr[1], 1, 0).astype(BF16)
        v = (dot(n1, wr[2], 1, 0) + bv_r).astype(BF16)
        p, o = attend(z, q, k, v, qpos, pos, length)
        out.update(q_r=q, k_r=k, v_r=v, p_r=p, o_r=o)
    return out


def stage_c(z, b, wo_f, wo_r, x, upstream, ua, live, up_t, down, prm):
    branch = prm["b_o"]
    if z.full:
        part = dot(b["o_f"], wo_f, 1, 0).astype(BF16)
        branch = branch + lax.psum_scatter(part.astype(F32), "ctx", scatter_dimension=0, tiled=True)
    if z.rest:
        branch = branch + dot(b["o_r"], wo_r, 1, 0)
    hidden = x.astype(F32) + branch
    xhat, rstd = norm_stats(hidden)
    n2 = (xhat * prm["gain2"] + prm["shift2"]).astype(BF16)
    n2a = lax.all_gather(n2, "seq", axis=0, tiled=True)
    pre = dot(n2a, up_t, 1, 1) + prm["b_up"]
    cdf = 0.5 * (1.0 + lax.erf(pre * (0.5 ** 0.5)))
    act = (pre * cdf).astype(BF16)
    dgelu = cdf + pre * jnp.exp(-0.5 * pre * pre) * (1.0 / math.sqrt(2.0 * math.pi))
    gact = dot(ua, down, 1, 1)
    gpre = (gact * dgelu).astype(BF16)
    gn2p = dot(gpre, up_t, 1, 0).astype(BF16)
    gn2 = lax.psum_scatter(gn2p.astype(F32), "seq", scatter_dimension=0, tiled=True)
    ffp = dot(act, down, 1, 0).astype(BF16)
    ff = lax.psum_scatter(ffp.astype(F32), "seq", scatter_dimension=0, tiled=True)
    output = (live * (hidden + ff + prm["b_down"])).astype(BF16)
    g_up_t = dot(gpre, n2a, 0, 0).astype(BF16)
    g_down = dot(act, ua, 0, 0).astype(BF16)
    gh = upstream.astype(F32) + norm_back(gn2, xhat, rstd, prm["gain2"])
    gb = gh.astype(BF16)
    small = dict(gain2=rows_sum(gn2 * xhat), shift2=rows_sum(gn2), b_o=rows_sum(gb),
                 b_down=rows_sum(upstream), b_up=rows_sum(gpre))
    return output, gh, gb, g_up_t, g_down, small


def attend_back(z, q, k, v, p, go):
    gp = jnp.einsum("hqd,hkd->hkq", heads_of(go, z.head), heads_of(v, z.head), preferred_element_type=F32)
    pf = p.astype(F32)
    delta = jnp.sum(gp * pf, axis=1, keepdims=True)
    gs = (pf * (gp - delta)).astype(BF16)
    sc = z.head ** -0.5
    gq = jnp.einsum("hkq,hkd->qhd", gs, heads_of(k, z.head), preferred_element_type=F32) * sc
    gk = jnp.einsum("hkq,hqd->khd", gs, heads_of(q, z.head), preferred_element_type=F32) * sc
    gv = jnp.einsum("hkq,hqd->khd", p, heads_of(go, z.head), preferred_element_type=F32)
    return gq.reshape(q.shape).astype(BF16), gk.reshape(k.shape).astype(BF16), gv.reshape(v.shape).astype(BF16)


def stage_d(z, b, gb, gba, wo_f, wo_r):
    i = lax.axis_index("ctx")
    n1 = b["n1"]
    mine = lax.dynamic_slice_in_dim(n1, i * z.rows, z.rows)
    out = {}
    if z.full:
        go = dot(gba, wo_f, 1, 1).astype(BF16)
        gq, gk, gv = attend_back(z, b["q_f"], b["k_f"], b["v_f"], b["p_f"], go)
        out.update(gq_f=gq, gk_f=gk, gv_f=gv, gwo_f=dot(b["o_f"], gba, 0, 0))
        out["gw_f"] = jnp.stack([dot(n1, g, 0, 0) for g in (gq, gk, gv)])
    if z.rest:
        go = dot(gb, wo_r, 1, 1).astype(BF16)
        gq, gk, gv = attend_back(z, b["q_r"], b["k_r"], b["v_r"], b["p_r"], go)
        out.update(gq_r=gq, gk_r=gk, gv_r=gv, gwo_r=dot(b["o_r"], gb, 0, 0))
        out["gw_r"] = jnp.stack([dot(mine, gq, 0, 0), dot(n1, gk, 0, 0), dot(n1, gv, 0, 0)])
    return out


def stage_e(z, d, wf, wr, x, gh, gain1, small):
    i, s = lax.axis_index("ctx"), lax.axis_index("seq")
    part = 0.0
    own = 0.0
    if z.full:
        part = part + dot(d["gq_f"], wf[0], 1, 1) + dot(d["gk_f"], wf[1], 1, 1) + dot(d["gv_f"], wf[2], 1, 1)
    if z.rest:
        part = part + dot(d["gk_r"], wr[1], 1, 1) + dot(d["gv_r"], wr[2], 1, 1)
        own = own + dot(d["gq_r"], wr[0], 1, 1)
    gn1 = own + lax.psum_scatter(part.astype(BF16).astype(F32), "ctx", scatter_dimension=0, tiled=True)
    xhat, rstd = norm_stats(x.astype(F32))
    gtok = gh + norm_back(gn1, xhat, rstd, gain1)
    small = dict(small, gain1=rows_sum(gn1 * xhat), shift1=rows_sum(gn1))
    row = jnp.zeros((1, z.width), F32)
    for name, key in (("b_q", "gq"), ("b_v", "gv")):
        r = row
        if z.full:
            r = lax.dynamic_update_slice(r, rows_sum(d[key + "_f"]), (0, i * z.full_width))
        if z.rest:
            r = r.at[:, z.main :].add(rows_sum(d[key + "_r"]))
        small[name] = r
    full = jnp.zeros((4, z.width, z.width), F32)
    if z.full:
        full = lax.dynamic_update_slice(full, d["gw_f"], (0, 0, i * z.full_width))
        full = lax.dynamic_update_slice(full, d["gwo_f"][None], (3, i * z.full_width, 0))
    if z.rest:
        full = full.at[:3, :, z.main :].add(d["gw_r"])
        full = full.at[3, z.main :, :].add(d["gwo_r"])
    gw = lax.psum_scatter(full.reshape(4 * z.width, z.width).astype(BF16), ("seq", "ctx"), scatter_dimension=0, tiled=True)
    b_up_all = lax.all_gather(lax.psum(small.pop("b_up"), "ctx")[0], "seq", axis=0, tiled=True)
    names = list(small)
    tot = lax.psum(jnp.concatenate([small[n] for n in names]), ("seq", "ctx"))
    return gtok, gw.astype(F32), {n: tot[j : j + 1] for j, n in enumerate(names)}, b_up_all


MESH = pl.DeviceIdType.MESH
DMA = pltpu.SemaphoreType.DMA
VMEM_LIMIT = 56 << 20


def rcopy(src, dst, ssem, rsem, **dev):
    return pltpu.make_async_remote_copy(
        src_ref=src, dst_ref=dst, send_sem=ssem, recv_sem=rsem, device_id=dev, device_id_type=MESH
    )


def greet(ctx_peers, seq_peers):
    sem = pltpu.get_barrier_semaphore()
    for p in ctx_peers:
        pl.semaphore_signal(sem, inc=1, device_id={"ctx": p}, device_id_type=MESH)
    for p in seq_peers:
        pl.semaphore_signal(sem, inc=1, device_id={"seq": p}, device_id_type=MESH)
    pl.semaphore_wait(sem, len(ctx_peers) + len(seq_peers))


class Place:
    def __init__(self, z):
        self.k, self.s = lax.axis_index("ctx"), lax.axis_index("seq")
        self.chips = z.ctx // 2
        self.core = lax.rem(self.k, 2)
        self.chip = self.k // 2
        self.sib = self.k + 1 - 2 * self.core
        self.ring = [lax.rem(self.chip + i, self.chips) for i in range(self.chips)]
        self.same = [2 * q + self.core for q in self.ring]
        self.back = [2 * lax.rem(self.chip + self.chips - i, self.chips) + self.core for i in range(self.chips)]
        self.seqs = [lax.rem(self.s + i, z.seq) for i in range(z.seq)]
        self.seqs_back = [lax.rem(self.s + z.seq - i, z.seq) for i in range(z.seq)]


def call(body, name, outs, ins, scratch, cid, in_spaces, out_spaces, cost=None):
    spaces = {"v": pltpu.VMEM, "a": pl.ANY}
    return pl.pallas_call(
        body,
        name=name,
        out_shape=outs,
        in_specs=[pl.BlockSpec(memory_space=spaces[c]) for c in in_spaces],
        out_specs=[pl.BlockSpec(memory_space=spaces[c]) for c in out_spaces],
        scratch_shapes=scratch,
        compiler_params=pltpu.CompilerParams(
            collective_id=cid, has_side_effects=True, vmem_limit_bytes=VMEM_LIMIT
        ),
        cost_estimate=cost,
    )(*ins)


def sds(shape, dtype=BF16):
    return jax.ShapeDtypeStruct(shape, dtype)


class CtxGather:
    def __init__(self, at, own, dst, sems):
        self.at, self.own, self.dst, self.sems = at, own, dst, sems

    def send(self):
        at, ss, rs = self.at, self.sems[0], self.sems[1]
        for i in range(1, at.chips):
            rcopy(self.own, self.dst.at[at.k], ss.at[i], rs.at[i], ctx=at.same[i]).start()
        rcopy(self.own, self.dst.at[at.k], ss.at[0], rs.at[0], ctx=at.sib).start()
        pltpu.make_async_copy(self.own, self.dst.at[at.k], self.sems[4]).start()

    def forward(self, i):
        at, ss, rs, fs, fr = self.at, *self.sems[:4]
        src = at.back[i]
        rcopy(self.own, self.dst.at[src], ss.at[i], rs.at[i], ctx=at.same[i]).wait_recv()
        rcopy(self.dst.at[src], self.dst.at[src], fs.at[i], fr.at[i], ctx=at.sib).start()

    def finish(self):
        at, ss, rs, fs, fr = self.at, *self.sems[:4]
        pltpu.make_async_copy(self.own, self.dst.at[at.k], self.sems[4]).wait()
        rcopy(self.own, self.dst.at[at.k], ss.at[0], rs.at[0], ctx=at.sib).wait()
        for i in range(1, at.chips):
            rcopy(self.own, self.dst.at[at.k], ss.at[i], rs.at[i], ctx=at.same[i]).wait_send()
            rcopy(self.own, self.dst.at[at.k], fs.at[i], fr.at[i], ctx=at.sib).wait()

    @staticmethod
    def scratch(z):
        n = z.ctx // 2
        return [DMA((n,)), DMA((n,)), DMA((n,)), DMA((n,)), DMA]


def kernel_a(z, x, up, w, wm, wr, pk, xa, ua, wf, wra, wo2, wol, pa, *sems):
    at = Place(z)
    k, s, C = at.k, at.s, z.ctx
    g = CtxGather(at, x, xa, sems[:5])
    mz_s, mz_r, rz_s, rz_r, mx_s, mx_r, rx_s, rx_r, us, ur, oz_s, oz_r, ox_s, ox_r, loc, pz_s, pz_r, px_s, px_r = sems[5:]
    others = [lax.rem(k + i, C) for i in range(1, C)]
    greet(others, at.seqs[1:])
    last0 = z.main - (C - 1) * z.shard
    lastrows = w.at[pl.ds(last0, z.rest_width)]

    def cols(j):
        return wm.at[:, pl.ds(pl.multiple_of(j * z.full_width, z.full_width), z.full_width)]

    for i in range(1, C):
        rcopy(pk, pa.at[s, k], pz_s.at[i], pz_r.at[i], ctx=others[i - 1]).start()
    pltpu.make_async_copy(pk, pa.at[s, k], loc.at[3]).start()

    @pl.when(s < 3)
    def _():
        for i in range(1, C):
            j = lax.rem(k + i, C)
            rcopy(cols(j), wf.at[s, k], mz_s.at[i], mz_r.at[k], ctx=j).start()
            rcopy(wr, wra.at[s, k], rz_s.at[i], rz_r.at[k], ctx=j).start()
        pltpu.make_async_copy(cols(k), wf.at[s, k], loc.at[0]).start()
        pltpu.make_async_copy(wr, wra.at[s, k], loc.at[1]).start()

    @pl.when(s == 3)
    def _():
        @pl.when(k < C - 1)
        def _():
            rcopy(w, wo2.at[0], oz_s.at[0], oz_r.at[0], ctx=lax.rem(k + 1, C)).start()

        @pl.when(k == C - 1)
        def _():
            for i in range(1, C):
                rcopy(lastrows, wol, oz_s.at[i], oz_r.at[1], ctx=lax.rem(k + i, C)).start()
            pltpu.make_async_copy(lastrows, wol, loc.at[1]).start()

        pltpu.make_async_copy(w, wo2.at[1], loc.at[0]).start()
        for i in range(1, 4):
            rcopy(w, wo2.at[1], ox_s.at[0, i], ox_r.at[0], seq=at.seqs[i]).start()

    g.send()
    for i in range(1, z.seq):
        rcopy(up, ua.at[s], us.at[i], ur.at[i], seq=at.seqs[i]).start()
    pltpu.make_async_copy(up, ua.at[s], loc.at[2]).start()

    for i in range(1, C):
        rcopy(pk, pa.at[s, lax.rem(k + C - i, C)], pz_s.at[i], pz_r.at[i], ctx=k).wait_recv()
    pltpu.make_async_copy(pk, pa.at[s, k], loc.at[3]).wait()
    for i in range(1, z.seq):
        rcopy(pa.at[s], pa.at[s], px_s.at[i], px_r.at[i], seq=at.seqs[i]).start()

    @pl.when(s < 3)
    def _():
        for n in range(C):
            src = lax.rem(k + C - n, C)
            if n == 0:
                pltpu.make_async_copy(cols(k), wf.at[s, k], loc.at[0]).wait()
                pltpu.make_async_copy(wr, wra.at[s, k], loc.at[1]).wait()
            else:
                rcopy(cols(k), wf.at[s, src], mz_s.at[0], mz_r.at[src], ctx=k).wait_recv()
                rcopy(wr, wra.at[s, src], rz_s.at[0], rz_r.at[src], ctx=k).wait_recv()
            for i in range(1, 4):
                to = at.seqs[i]
                rcopy(wf.at[s, src], wf.at[s, src], mx_s.at[n, i], mx_r.at[s, src], seq=to).start()
                rcopy(wra.at[s, src], wra.at[s, src], rx_s.at[n, i], rx_r.at[s, src], seq=to).start()

    @pl.when(s == 3)
    def _():
        pltpu.make_async_copy(w, wo2.at[1], loc.at[0]).wait()

        @pl.when(k > 0)
        def _():
            rcopy(w, wo2.at[0], oz_s.at[0], oz_r.at[0], ctx=k).wait_recv()
            for i in range(1, 4):
                rcopy(wo2.at[0], wo2.at[0], ox_s.at[1, i], ox_r.at[1], seq=at.seqs[i]).start()

        @pl.when(k < C - 1)
        def _():
            rcopy(lastrows, wol, oz_s.at[1], oz_r.at[1], ctx=k).wait_recv()

        @pl.when(k == C - 1)
        def _():
            pltpu.make_async_copy(lastrows, wol, loc.at[1]).wait()

        for i in range(1, 4):
            rcopy(wol, wol, ox_s.at[2, i], ox_r.at[2], seq=at.seqs[i]).start()

    for i in range(1, at.chips):
        g.forward(i)
    g.finish()
    pltpu.make_async_copy(up, ua.at[s], loc.at[2]).wait()
    for i in range(1, z.seq):
        rcopy(up, ua.at[s], us.at[i], ur.at[i], seq=at.seqs[i]).wait()

    for i in range(1, C):
        rcopy(pk, pa.at[s, k], pz_s.at[i], pz_r.at[i], ctx=k).wait_send()
    for i in range(1, z.seq):
        rcopy(pa.at[s], pa.at[at.seqs_back[i]], px_s.at[i], px_r.at[i], seq=s).wait()

    for m in range(3):
        @pl.when(s != m)
        def _():
            for src in range(C):
                rcopy(wf.at[m, src], wf.at[m, src], mx_s.at[0, 0], mx_r.at[m, src], seq=s).wait_recv()
                rcopy(wra.at[m, src], wra.at[m, src], rx_s.at[0, 0], rx_r.at[m, src], seq=s).wait_recv()

    @pl.when(s != 3)
    def _():
        rcopy(w, wo2.at[1], ox_s.at[0, 0], ox_r.at[0], seq=s).wait_recv()

        @pl.when(k > 0)
        def _():
            rcopy(w, wo2.at[0], ox_s.at[1, 0], ox_r.at[1], seq=s).wait_recv()

        rcopy(wol, wol, ox_s.at[2, 0], ox_r.at[2], seq=s).wait_recv()

    @pl.when(s < 3)
    def _():
        for i in range(1, C):
            rcopy(cols(k), wf.at[s, k], mz_s.at[i], mz_r.at[k], ctx=k).wait_send()
            rcopy(wr, wra.at[s, k], rz_s.at[i], rz_r.at[k], ctx=k).wait_send()
        for n in range(C):
            for i in range(1, 4):
                rcopy(wf.at[s, k], wf.at[s, k], mx_s.at[n, i], mx_r.at[s, k], seq=s).wait_send()
                rcopy(wra.at[s, k], wra.at[s, k], rx_s.at[n, i], rx_r.at[s, k], seq=s).wait_send()

    @pl.when(s == 3)
    def _():
        @pl.when(k < C - 1)
        def _():
            rcopy(w, wo2.at[0], oz_s.at[0], oz_r.at[0], ctx=k).wait_send()

        @pl.when(k == C - 1)
        def _():
            for i in range(1, C):
                rcopy(lastrows, wol, oz_s.at[i], oz_r.at[1], ctx=k).wait_send()

        for i in range(1, 4):
            rcopy(w, wo2.at[1], ox_s.at[0, i], ox_r.at[0], seq=s).wait_send()

            @pl.when(k > 0)
            def _():
                rcopy(wo2.at[0], wo2.at[0], ox_s.at[1, i], ox_r.at[1], seq=s).wait_send()

            rcopy(wol, wol, ox_s.at[2, i], ox_r.at[2], seq=s).wait_send()


def stage_a_kernel(z, x, up, w, pk):
    C, k = z.ctx, lax.axis_index("ctx")
    outs = [
        sds((C, z.rows, z.width)), sds((z.seq, z.rows, z.width)), sds((3, C, z.shard, z.full_width)),
        sds((3, C, z.shard, z.rest_width)), sds((2, z.shard, z.width)), sds((z.rest_width, z.width)),
        sds((z.seq, C) + pk.shape),
    ]
    scratch = CtxGather.scratch(z) + [
        DMA((C,)), DMA((C,)), DMA((C,)), DMA((C,)), DMA((C, 4)), DMA((3, C)), DMA((C, 4)), DMA((3, C)),
        DMA((4,)), DMA((4,)), DMA((C,)), DMA((2,)), DMA((3, 4)), DMA((3,)), DMA((4,)),
        DMA((C,)), DMA((C,)), DMA((z.seq,)), DMA((z.seq,)),
    ]
    xa, ua, wf, wra, wo2, wol, pa = call(
        partial(kernel_a, z), "gather_in", outs, (x, up, w, w[:, : z.main], w[:, z.main :], pk), scratch, 0, "a" * 6, "a" * 7
    )
    wo_f = lax.dynamic_slice_in_dim(
        wo2.reshape(2 * z.shard, z.width), z.shard - (z.shard - z.full_width) * k, z.full_width
    )
    return (
        xa.reshape(z.slot, z.width), ua.reshape(z.seq * z.rows, z.width), wf.reshape(3, z.width, z.full_width),
        wra.reshape(3, z.width, z.rest_width), wo_f, wol, pa,
    )


def matmul(a, b, ca=1, cb=0):
    return lax.dot_general(a, b, (((ca,), (cb,)), ((), ())), preferred_element_type=F32)


def block(z, d):
    return pl.ds(pl.multiple_of(d * z.rows, z.rows), z.rows)


class CtxReduce:
    def __init__(self, at, part, bufs):
        self.at, self.part = at, part
        self.sb, self.sr, self.zb, self.zr, self.ss, self.sn, self.zs, self.zn = bufs

    def sib(self, t):
        return rcopy(self.sb.at[t], self.sr.at[t], self.ss.at[t], self.sn.at[t], ctx=self.at.sib)

    def far(self, t):
        return rcopy(self.zb.at[t], self.zr.at[t], self.zs.at[t], self.zn.at[t], ctx=self.at.same[t])

    def start(self):
        at = self.at
        order = list(range(1, at.chips)) + [0]
        for t in order:
            self.sb[t] = self.part(2 * at.ring[t] + 1 - at.core).astype(BF16)
            self.sib(t).start()
        for t in order[:-1]:
            mine = self.part(at.same[t])
            self.sib(t).wait_recv()
            self.zb[t] = (mine + self.sr[t].astype(F32)).astype(BF16)
            self.far(t).start()

    def finish(self):
        at = self.at
        total = self.part(at.k)
        self.sib(0).wait_recv()
        total = total + self.sr[0].astype(F32)
        for t in range(1, at.chips):
            self.far(t).wait_recv()
            total = total + self.zr[t].astype(F32)
        return total

    def close(self):
        for t in range(self.at.chips):
            self.sib(t).wait_send()
            if t:
                self.far(t).wait_send()

    @staticmethod
    def scratch(z):
        n = z.ctx // 2
        return [pltpu.VMEM((n, z.rows, z.width), BF16)] * 4 + [DMA((n,))] * 4


def kernel_c(z, o_f, wo_f, o_r, wo_r, x, b_o, gain2, shift2, hid, xh, rs_o, n2a, n2, ns, nr, *bufs):
    at = Place(z)
    greet([at.sib] + at.same[1:], at.seqs[1:])
    red = CtxReduce(at, lambda d: matmul(o_f[block(z, d)], wo_f[...]), bufs)
    red.start()
    own = matmul(o_r[...], wo_r[...]) + b_o[...] + x[...].astype(F32)
    hidden = red.finish() + own
    xhat, rstd = norm_stats(hidden)
    n2[...] = (xhat * gain2[...] + shift2[...]).astype(BF16)
    copies = [rcopy(n2, n2a.at[at.s], ns.at[i], nr.at[i], seq=at.seqs[i]) for i in range(1, z.seq)]
    for c in copies:
        c.start()
    n2a[at.s] = n2[...]
    hid[...] = hidden
    xh[...] = xhat
    rs_o[...] = jnp.broadcast_to(rstd, rs_o.shape)
    red.close()
    for c in copies:
        c.wait()


def stage_c_kernel(z, b, wo_f, wo_r, x, prm):
    outs = [sds((z.rows, z.width), F32), sds((z.rows, z.width), F32), sds((z.rows, 128), F32), sds((z.seq, z.rows, z.width))]
    scratch = [pltpu.VMEM((z.rows, z.width), BF16), DMA((z.seq,)), DMA((z.seq,))] + CtxReduce.scratch(z)
    return call(
        partial(kernel_c, z), "project_out", outs,
        (b["o_f"], wo_f, b["o_r"], wo_r, x, prm["b_o"], prm["gain2"], prm["shift2"]), scratch, 1, "v" * 8, "v" * 4,
    )


def kernel_f(z, n2a, ua, up_t, down, b_up, hid, xh, rs_i, gain2, b_down, live, out, gh_o, gb_o, gup, gdown, sm, bu,
             act, gpre, gsend, grecv, fsend, frecv, gs, gr, fs, fr):
    at = Place(z)
    greet([], at.seqs[1:])
    S, R, D = z.seq, z.rows, z.width
    units = up_t.shape[0]
    n2 = n2a[...]
    u = ua[...]
    step = 256
    for c0 in range(0, units, step):
        c = slice(c0, min(c0 + step, units))
        pre = matmul(n2, up_t[c], 1, 1) + b_up[:, c]
        gact = matmul(u, down[c], 1, 1)
        cdf = 0.5 * (1.0 + lax.erf(pre * (0.5 ** 0.5)))
        act[:, c] = (pre * cdf).astype(BF16)
        dgelu = cdf + pre * jnp.exp(-0.5 * pre * pre) * (1.0 / math.sqrt(2.0 * math.pi))
        g = (gact * dgelu).astype(BF16)
        gpre[:, c] = g
        bu[:, c] = jnp.sum(g.astype(F32), axis=0, keepdims=True)

    def gcopy(i):
        return rcopy(gsend.at[i], grecv.at[i], gs.at[i], gr.at[i], seq=at.seqs[i])

    def fcopy(i):
        return rcopy(fsend.at[i], frecv.at[i], fs.at[i], fr.at[i], seq=at.seqs[i])

    for i in range(1, S):
        gsend[i] = matmul(gpre[block(z, at.seqs[i])], up_t[...]).astype(BF16)
        gcopy(i).start()
    mine = block(z, at.s)
    gn2 = matmul(gpre[mine], up_t[...])
    for i in range(1, S):
        fsend[i] = matmul(act[block(z, at.seqs[i])], down[...]).astype(BF16)
        fcopy(i).start()
    ff = matmul(act[mine], down[...])
    for i in range(1, S):
        gcopy(i).wait_recv()
        gn2 = gn2 + grecv[i].astype(F32)
    xhat = xh[...]
    up_own = ua[mine].astype(F32)
    gh = up_own + norm_back(gn2, xhat, rs_i[:, :1], gain2[...])
    gb = gh.astype(BF16)
    gh_o[...] = gh
    gb_o[...] = gb
    sm[0:1] = jnp.sum(gn2 * xhat, axis=0, keepdims=True)
    sm[1:2] = jnp.sum(gn2, axis=0, keepdims=True)
    sm[2:3] = jnp.sum(gb.astype(F32), axis=0, keepdims=True)
    sm[3:4] = jnp.sum(up_own, axis=0, keepdims=True)
    for c0 in range(0, units, step):
        c = slice(c0, min(c0 + step, units))
        gup[c] = matmul(gpre[:, c], n2, 0, 0).astype(BF16)
        gdown[c] = matmul(act[:, c], u, 0, 0).astype(BF16)
    for i in range(1, S):
        fcopy(i).wait_recv()
        ff = ff + frecv[i].astype(F32)
    out[...] = (live[:, :1] * (hid[...] + ff + b_down[...])).astype(BF16)
    for i in range(1, S):
        gcopy(i).wait_send()
        fcopy(i).wait_send()


def stage_f_kernel(z, n2a, ua, up_t, down, prm, hid, xh, rs, live):
    R, D, S, U = z.rows, z.width, z.seq, up_t.shape[0]
    outs = [sds((R, D)), sds((R, D), F32), sds((R, D)), sds((U, D)), sds((U, D)), sds((4, D), F32), sds((1, U), F32)]
    scratch = [pltpu.VMEM((S * R, U), BF16)] * 2 + [pltpu.VMEM((S, R, D), BF16)] * 4 + [DMA((S,))] * 4
    return call(
        partial(kernel_f, z), "feed_forward", outs,
        (n2a.reshape(S * R, D), ua, up_t, down, prm["b_up"], hid, xh, rs, prm["gain2"], prm["b_down"],
         jnp.broadcast_to(live, (R, 128))), scratch, 2, "v" * 11, "v" * 7,
    )


def kernel_g(z, own, dst, *sems):
    at = Place(z)
    g = CtxGather(at, own, dst, sems)
    greet([at.sib] + at.same[1:], [])
    g.send()
    for i in range(1, at.chips):
        g.forward(i)
    g.finish()


def gather_ctx_kernel(z, own):
    return call(partial(kernel_g, z), "gather_back", [sds((z.ctx, z.rows, z.width))], (own,), CtxGather.scratch(z), 3, "a", "a")[0]


class SmallSum:
    def __init__(self, at, buf, rsib, rchip, rseq, sems):
        self.at, self.buf, self.rsib, self.rchip, self.rseq = at, buf, rsib, rchip, rseq
        self.s0, self.r0, self.s1, self.r1, self.s2, self.r2 = sems

    def sib(self):
        return rcopy(self.buf.at[0], self.rsib, self.s0, self.r0, ctx=self.at.sib)

    def chip(self, i):
        return rcopy(self.buf.at[1], self.rchip.at[i], self.s1.at[i], self.r1.at[i], ctx=self.at.same[i])

    def line(self, i):
        return rcopy(self.buf.at[2], self.rseq.at[i], self.s2.at[i], self.r2.at[i], seq=self.at.seqs[i])

    def first(self, value):
        self.buf[0] = value
        self.sib().start()

    def second(self):
        self.sib().wait_recv()
        self.buf[1] = self.buf[0] + self.rsib[...]
        for i in range(1, self.at.chips):
            self.chip(i).start()

    def third(self):
        total = self.buf[1]
        for i in range(1, self.at.chips):
            self.chip(i).wait_recv()
            total = total + self.rchip[i]
        self.buf[2] = total
        for i in range(1, len(self.at.seqs)):
            self.line(i).start()

    def last(self):
        total = self.buf[2]
        for i in range(1, len(self.at.seqs)):
            self.line(i).wait_recv()
            total = total + self.rseq[i]
        return total

    def close(self):
        self.sib().wait_send()
        for i in range(1, self.at.chips):
            self.chip(i).wait_send()
        for i in range(1, len(self.at.seqs)):
            self.line(i).wait_send()

    @staticmethod
    def scratch(z, rows):
        n, shape = z.ctx // 2, (rows, z.width)
        return [
            pltpu.VMEM((3,) + shape, F32), pltpu.VMEM(shape, F32), pltpu.VMEM((n,) + shape, F32),
            pltpu.VMEM((z.seq,) + shape, F32), DMA, DMA, DMA((n,)), DMA((n,)), DMA((z.seq,)), DMA((z.seq,)),
        ]


def kernel_e(z, gq, gk, gv, gkr, gvr, gqr, wf, wr, x, gh, gain1, gwf, gwr, gwo, gwor, sme,
             gtok, ga, tot, bup,
             rf, rr, ro, ror, sf_s, sf_r, sr_s, sr_r, so_s, so_r, sor_s, sor_r,
             zs, zr, land, landr, zs_s, zs_r, zr_s, zr_r,
             buf32, obs, obn, orrs, orr, ob_s, ob_r, orr_s, orr_r, *rest):
    at = Place(z)
    s, k, C, S, FW = at.s, at.k, z.ctx, z.seq, z.full_width
    bufs, small_e, small_l = rest[:8], rest[8:18], rest[18:]
    greet([lax.rem(k + i, C) for i in range(1, C)], at.seqs[1:])

    def up(ref, dst, ssem, rsem, i, m=None):
        return rcopy(ref if m is None else ref.at[m], dst.at[i], ssem.at[i], rsem.at[i], seq=at.seqs[i])

    for i in range(1, S):
        m = at.seqs[i]

        @pl.when(m < 3)
        def _():
            up(gwf, rf, sf_s, sf_r, i, m).start()
            up(gwr, rr, sr_s, sr_r, i, m).start()

        @pl.when(m == 3)
        def _():
            up(gwo, ro, so_s, so_r, i).start()
            up(gwor, ror, sor_s, sor_r, i).start()

    se = SmallSum(at, *small_e[:4], small_e[4:])
    se.first(sme[...])

    def part(d):
        r = block(z, d)
        return (
            matmul(gq[r], wf[0], 1, 1) + matmul(gk[r], wf[1], 1, 1) + matmul(gv[r], wf[2], 1, 1)
            + matmul(gkr[r], wr[1], 1, 1) + matmul(gvr[r], wr[2], 1, 1)
        )

    red = CtxReduce(at, part, bufs)
    red.start()
    se.second()

    def zf(i):
        return rcopy(zs.at[lax.rem(k + i, C)], land.at[i], zs_s.at[i], zs_r.at[i], ctx=lax.rem(k + i, C))

    def zrr(i):
        return rcopy(zr.at[lax.rem(k + i, C)], landr.at[i], zr_s.at[i], zr_r.at[i], ctx=lax.rem(k + i, C))

    def shift():
        return rcopy(obs, obn, ob_s, ob_r, ctx=lax.rem(k + C - 1, C))

    def tail(i):
        return rcopy(orrs, orr.at[i], orr_s, orr_r.at[i], ctx=C - 1)

    @pl.when(s < 3)
    def _():
        for i in range(1, S):
            up(gwf, rf, sf_s, sf_r, i, 0).wait_recv()
            up(gwr, rr, sr_s, sr_r, i, 0).wait_recv()

        def add(j, _):
            t, u = gwf[s, j].astype(F32), gwr[s, j].astype(F32)
            for i in range(1, S):
                t = t + rf[i, j].astype(F32)
                u = u + rr[i, j].astype(F32)
            zs[j] = t.astype(BF16)
            zr[j] = u.astype(BF16)
            return 0

        lax.fori_loop(0, C, add, 0)
        for i in range(1, C):
            zf(i).start()
            zrr(i).start()

    @pl.when(s == 3)
    def _():
        for i in range(1, S):
            up(gwo, ro, so_s, so_r, i).wait_recv()
            up(gwor, ror, sor_s, sor_r, i).wait_recv()
        t, u = gwo[...].astype(F32), gwor[...].astype(F32)
        for i in range(1, S):
            t = t + ro[i].astype(F32)
            u = u + ror[i].astype(F32)
        buf32[pl.ds(0, FW)] = t
        obs[...] = t.astype(BF16)
        orrs[...] = u.astype(BF16)

        @pl.when(k > 0)
        def _():
            shift().start()

        for i in range(C - 1):
            @pl.when(k == i)
            def _():
                tail(i).start()

    se.third()
    gn1 = red.finish() + matmul(gqr[...], wr[0], 1, 1)
    xhat, rstd = norm_stats(x[...].astype(F32))
    sl = SmallSum(at, *small_l[:4], small_l[4:])
    sl.first(jnp.concatenate([jnp.sum(gn1 * xhat, axis=0, keepdims=True), jnp.sum(gn1, axis=0, keepdims=True)], axis=0))
    gtok[...] = gh[...] + norm_back(gn1, xhat, rstd, gain1[...])
    sl.second()
    early = se.last()
    tot[...] = early
    bup[s] = se.buf[2, 6:7]
    for i in range(1, S):
        bup[at.seqs_back[i]] = se.rseq[i, 6:7]

    @pl.when(s < 3)
    def _():
        ga[:, pl.ds(pl.multiple_of(k * FW, FW), FW)] = zs[k].astype(F32)
        remain = zr[k].astype(F32)
        for i in range(1, C):
            zf(i).wait_recv()
            zrr(i).wait_recv()
            j = lax.rem(k + C - i, C)
            ga[:, pl.ds(pl.multiple_of(j * FW, FW), FW)] = land[i].astype(F32)
            remain = remain + landr[i].astype(F32)
        ga[:, z.main :] = remain
        for i in range(1, C):
            zf(i).wait_send()
            zrr(i).wait_send()

    sl.third()

    @pl.when(s == 3)
    def _():
        @pl.when(k < C - 1)
        def _():
            shift().wait_recv()
            buf32[pl.ds(FW, FW)] = obn[...].astype(F32)

        @pl.when(k == C - 1)
        def _():
            u = orrs[...].astype(F32)
            for i in range(C - 1):
                tail(i).wait_recv()
                u = u + orr[i].astype(F32)
            buf32[pl.ds(FW, z.rest_width)] = u

        ga[...] = buf32[pl.ds(pl.multiple_of((z.shard - FW) * k, 8), z.shard)]

        @pl.when(k > 0)
        def _():
            shift().wait_send()

        @pl.when(k < C - 1)
        def _():
            tail(0).wait_send()

    late = sl.last()
    tot[6:8] = late
    red.close()
    se.close()
    sl.close()
    for i in range(1, S):
        m = at.seqs[i]

        @pl.when(m < 3)
        def _():
            up(gwf, rf, sf_s, sf_r, i, m).wait_send()
            up(gwr, rr, sr_s, sr_r, i, m).wait_send()

        @pl.when(m == 3)
        def _():
            up(gwo, ro, so_s, so_r, i).wait_send()
            up(gwor, ror, sor_s, sor_r, i).wait_send()


def stage_e_kernel(z, d, wf, wr, x, gh, gain1, small):
    C, S, D, FW, RW, SH = z.ctx, z.seq, z.width, z.full_width, z.rest_width, z.shard
    i = lax.axis_index("ctx")
    rows = []
    for key in ("gq", "gv"):
        row = lax.dynamic_update_slice(jnp.zeros((1, D), F32), rows_sum(d[key + "_f"]), (0, i * FW))
        rows.append(row + jnp.pad(rows_sum(d[key + "_r"]), ((0, 0), (z.main, 0))))
    sme = jnp.concatenate([small["gain2"], small["shift2"], small["b_o"], small["b_down"], *rows, small["b_up"],
                           jnp.zeros((1, D), F32)], axis=0)
    outs = [sds((z.rows, D), F32), sds((SH, D), F32), sds((8, D), F32), sds((S, 1, D), F32)]
    V = pltpu.VMEM
    scratch = [
        V((S, C, SH, FW), BF16), V((S, C, SH, RW), BF16), V((S, FW, D), BF16), V((S, RW, D), BF16),
        *[DMA((S,)) for _ in range(8)],
        V((C, SH, FW), BF16), V((C, SH, RW), BF16), V((C, SH, FW), BF16), V((C, SH, RW), BF16),
        *[DMA((C,)) for _ in range(4)],
        V((2 * FW, D), F32), V((FW, D), BF16), V((FW, D), BF16), V((RW, D), BF16), V((C, RW, D), BF16),
        DMA, DMA, DMA, DMA((C,)),
        *CtxReduce.scratch(z), *SmallSum.scratch(z, 8), *SmallSum.scratch(z, 2),
    ]
    low = lambda v: v.astype(BF16)
    gtok, ga, tot, bup = call(
        partial(kernel_e, z), "gradients_out", outs,
        (d["gq_f"], d["gk_f"], d["gv_f"], d["gk_r"], d["gv_r"], d["gq_r"], wf, wr, x, gh, gain1,
         low(d["gw_f"]).reshape(3, C, SH, FW), low(d["gw_r"]).reshape(3, C, SH, RW), low(d["gwo_f"]), low(d["gwo_r"]), sme),
        scratch, 4, "v" * 16, "v" * 4,
    )
    names = ("gain2", "shift2", "b_o", "b_down", "b_q", "b_v", "gain1", "shift1")
    return gtok, ga, {n: tot[j : j + 1] for j, n in enumerate(names)}, bup.reshape(-1)


def shards(tokens, lengths, block_order, attention_weights, up_weights, down_weights, norm_gains, biases, cotangent):
    z = Sizes(tokens.shape[1], tokens.shape[2], block_order.shape[0])
    i, s = lax.axis_index("ctx"), lax.axis_index("seq")
    D = z.width
    x, cot = tokens[0], cotangent[0]
    length = lengths[0]
    pos = (block_order[:, None] * z.block_len + jnp.arange(z.block_len, dtype=jnp.int32)[None, :]).reshape(z.slot)
    my_pos = lax.dynamic_slice_in_dim(pos, i * z.rows, z.rows)
    live = (my_pos < length).astype(F32)[:, None]
    n_g, n_b = norm_gains.shape[0], biases.shape[0]
    lanes = -(-(n_g + n_b) // 1024) * 8
    packed = jnp.pad(jnp.concatenate([norm_gains, biases]), (0, lanes * 128 - n_g - n_b)).reshape(lanes, 128)
    upstream = (live * cot.astype(F32)).astype(BF16)
    fast = z.full > 0 and z.seq == 4 and 0 < z.width - z.main <= z.shard and z.ctx * up_weights.shape[1] == z.width and z.slot * D * 2 <= (4 << 20)
    if fast:
        x_all, ua, wf, wr, wo_f, wo_r, both = stage_a_kernel(z, x, upstream, attention_weights, packed)
    else:
        x_all, wf, wr, wo_f, wo_r = stage_a(z, x, attention_weights)
        ua = lax.all_gather(upstream, "seq", axis=0, tiled=True)
        both = lax.all_gather(packed, ("seq", "ctx"), axis=0)
    both = both.reshape(z.seq * z.ctx, lanes * 128)
    gains = both[:, :n_g].reshape(-1).astype(F32)
    bias = both[:, n_g : n_g + n_b].reshape(-1).astype(F32)
    row = lambda v: v[None, :]
    piece = [row(bias[j * D : (j + 1) * D]) for j in range(6)]
    gain1, gain2 = row(gains[:D]), row(gains[D:])
    b_up = row(lax.dynamic_slice_in_dim(bias[6 * D :], s * (z.ctx * up_weights.shape[1]), z.ctx * up_weights.shape[1]))
    prm = dict(gain2=gain2, shift2=piece[4], b_o=piece[3], b_down=piece[5], b_up=b_up)
    fslice = lambda v: lax.dynamic_slice(v, (0, i * z.full_width), (1, z.full_width))
    up_t = lax.all_gather(up_weights.T, "ctx", axis=0, tiled=True)
    down = lax.all_gather(down_weights, "ctx", axis=0, tiled=True)

    b = stage_b(z, x_all, wf, wr, gain1, piece[0], fslice(piece[1]), piece[1][:, z.main :],
                fslice(piece[2]), piece[2][:, z.main :], pos, length)
    if fast:
        hid, xh, rs, n2a = stage_c_kernel(z, b, wo_f, wo_r, x, prm)
        output, gh, gb, g_up_t, g_down, sm, bu = stage_f_kernel(z, n2a, ua, up_t, down, prm, hid, xh, rs, live)
        small = dict(gain2=sm[0:1], shift2=sm[1:2], b_o=sm[2:3], b_down=sm[3:4], b_up=bu)
    else:
        output, gh, gb, g_up_t, g_down, small = stage_c(z, b, wo_f, wo_r, x, upstream, ua, live, up_t, down, prm)
    g_up_own = lax.psum_scatter(g_up_t, "ctx", scatter_dimension=0, tiled=True).astype(F32).T
    g_down_own = lax.psum_scatter(g_down, "ctx", scatter_dimension=0, tiled=True).astype(F32)
    if fast:
        gba = gather_ctx_kernel(z, gb).reshape(z.slot, D)
    else:
        gba = lax.all_gather(gb, "ctx", axis=0, tiled=True) if z.full else None
    d = stage_d(z, b, gb, gba, wo_f, wo_r)
    if fast:
        gtok, gw, tot, b_up_all = stage_e_kernel(z, d, wf, wr, x, gh, gain1, small)
    else:
        gtok, gw, tot, b_up_all = stage_e(z, d, wf, wr, x, gh, gain1, small)
    me = s * z.ctx + i
    g_gain = lax.dynamic_slice_in_dim(jnp.concatenate([tot["gain1"][0], tot["gain2"][0]]), me * n_g, n_g)
    g_bias = lax.dynamic_slice_in_dim(jnp.concatenate([tot[n][0] for n in ("shift1", "b_q", "b_v", "b_o", "shift2", "b_down")] + [b_up_all]), me * n_b, n_b)
    return output[None], gtok[None], gw, g_up_own, g_down_own, g_gain, g_bias


def solution(mesh):
    in_specs = (
        P("seq", "ctx", None), P("seq"), P(), P(("seq", "ctx"), None), P(None, ("seq", "ctx")),
        P(("seq", "ctx"), None), P(("seq", "ctx")), P(("seq", "ctx")), P("seq", "ctx", None),
    )
    out_specs = (
        P("seq", "ctx", None), P("seq", "ctx", None), P(("seq", "ctx"), None), P(None, ("seq", "ctx")),
        P(("seq", "ctx"), None), P(("seq", "ctx")), P(("seq", "ctx")),
    )
    return jax.shard_map(shards, mesh=mesh, in_specs=in_specs, out_specs=out_specs, check_vma=False)
```

```python
import math
from functools import partial

import jax
import jax.numpy as jnp
from jax import lax
from jax.experimental import pallas as pl
from jax.experimental.pallas import tpu as pltpu
from jax.sharding import PartitionSpec as P

HEADS = 17
EPS = 1e-05
F32 = jnp.float32
BF16 = jnp.bfloat16


def norm_stats(values):
    centre = values - jnp.mean(values, axis=-1, keepdims=True)
    rstd = lax.rsqrt(jnp.mean(centre * centre, axis=-1, keepdims=True) + EPS)
    return centre * rstd, rstd


def norm_back(grad, xhat, rstd, gain):
    e = grad * gain
    mean_e = jnp.mean(e, axis=-1, keepdims=True)
    mean_ex = jnp.mean(e * xhat, axis=-1, keepdims=True)
    return (e - mean_e - xhat * mean_ex) * rstd


def dot(a, b, ca, cb):
    return lax.dot_general(a, b, (((ca,), (cb,)), ((), ())), preferred_element_type=F32)


def rows_sum(v):
    return jnp.sum(v.astype(F32), axis=0, keepdims=True)


class Sizes:
    def __init__(self, rows, width, block_count):
        self.rows, self.width = rows, width
        self.ctx, self.seq = lax.axis_size("ctx"), lax.axis_size("seq")
        self.slot = rows * self.ctx
        self.block_len = self.slot // block_count
        self.head = width // HEADS
        self.full = HEADS // self.ctx
        self.full_width = self.full * self.head
        self.main = self.full_width * self.ctx
        self.rest = HEADS - self.full * self.ctx
        self.rest_width = self.rest * self.head
        self.shard = width // self.ctx


def stage_a(z, x, w):
    k = lax.axis_index("ctx")
    x_all = lax.all_gather(x, "ctx", axis=0, tiled=True)
    w_all = lax.all_gather(w, "seq", axis=0)
    wm = w_all[:3, :, : z.main].reshape(3, z.shard, z.ctx, z.full_width)
    wf = lax.all_to_all(wm, "ctx", split_axis=2, concat_axis=1, tiled=True).reshape(
        3, z.width, z.full_width
    )
    wr = lax.all_gather(w_all[:3, :, z.main :], "ctx", axis=1, tiled=True)
    wo = lax.all_gather(w_all[3], "ctx", axis=0, tiled=True)
    wo_f = lax.dynamic_slice_in_dim(wo, k * z.full_width, z.full_width)
    wo_r = wo[z.main :]
    return x_all, wf, wr, wo_f, wo_r


def heads_of(v, h):
    return v.reshape(v.shape[0], -1, h).transpose(1, 0, 2)


def attend(z, q, k, v, qpos, kpos, length):
    s = jnp.einsum("hqd,hkd->hkq", heads_of(q, z.head), heads_of(k, z.head), preferred_element_type=F32)
    s = s * (z.head ** -0.5)
    seen = (kpos[:, None] <= qpos[None, :]) & (kpos[:, None] < length)
    s = jnp.where(seen[None], s, -1e30)
    e = jnp.exp(s - jnp.max(s, axis=1, keepdims=True))
    p = (e / jnp.sum(e, axis=1, keepdims=True)).astype(BF16)
    o = jnp.einsum("hkq,hkd->qhd", p, heads_of(v, z.head), preferred_element_type=F32)
    return p, o.reshape(q.shape).astype(BF16)


def stage_b(z, x_all, wf, wr, gain, shift, bq_f, bq_r, bv_f, bv_r, pos, length):
    i = lax.axis_index("ctx")
    n1 = (norm_stats(x_all.astype(F32))[0] * gain + shift).astype(BF16)
    mine = lax.dynamic_slice_in_dim(n1, i * z.rows, z.rows)
    qpos = lax.dynamic_slice_in_dim(pos, i * z.rows, z.rows)
    out = dict(n1=n1)
    if z.full:
        q = (dot(n1, wf[0], 1, 0) + bq_f).astype(BF16)
        k = dot(n1, wf[1], 1, 0).astype(BF16)
        v = (dot(n1, wf[2], 1, 0) + bv_f).astype(BF16)
        p, o = attend(z, q, k, v, pos, pos, length)
        out.update(q_f=q, k_f=k, v_f=v, p_f=p, o_f=o)
    if z.rest:
        q = (dot(mine, wr[0], 1, 0) + bq_r).astype(BF16)
        k = dot(n1, wr[1], 1, 0).astype(BF16)
        v = (dot(n1, wr[2], 1, 0) + bv_r).astype(BF16)
        p, o = attend(z, q, k, v, qpos, pos, length)
        out.update(q_r=q, k_r=k, v_r=v, p_r=p, o_r=o)
    return out


def stage_c(z, b, wo_f, wo_r, x, upstream, ua, live, up_t, down, prm):
    branch = prm["b_o"]
    if z.full:
        part = dot(b["o_f"], wo_f, 1, 0).astype(BF16)
        branch = branch + lax.psum_scatter(part.astype(F32), "ctx", scatter_dimension=0, tiled=True)
    if z.rest:
        branch = branch + dot(b["o_r"], wo_r, 1, 0)
    hidden = x.astype(F32) + branch
    xhat, rstd = norm_stats(hidden)
    n2 = (xhat * prm["gain2"] + prm["shift2"]).astype(BF16)
    n2a = lax.all_gather(n2, "seq", axis=0, tiled=True)
    pre = dot(n2a, up_t, 1, 1) + prm["b_up"]
    cdf = 0.5 * (1.0 + lax.erf(pre * (0.5 ** 0.5)))
    act = (pre * cdf).astype(BF16)
    dgelu = cdf + pre * jnp.exp(-0.5 * pre * pre) * (1.0 / math.sqrt(2.0 * math.pi))
    gact = dot(ua, down, 1, 1)
    gpre = (gact * dgelu).astype(BF16)
    gn2p = dot(gpre, up_t, 1, 0).astype(BF16)
    gn2 = lax.psum_scatter(gn2p.astype(F32), "seq", scatter_dimension=0, tiled=True)
    ffp = dot(act, down, 1, 0).astype(BF16)
    ff = lax.psum_scatter(ffp.astype(F32), "seq", scatter_dimension=0, tiled=True)
    output = (live * (hidden + ff + prm["b_down"])).astype(BF16)
    g_up_t = dot(gpre, n2a, 0, 0).astype(BF16)
    g_down = dot(act, ua, 0, 0).astype(BF16)
    gh = upstream.astype(F32) + norm_back(gn2, xhat, rstd, prm["gain2"])
    gb = gh.astype(BF16)
    small = dict(gain2=rows_sum(gn2 * xhat), shift2=rows_sum(gn2), b_o=rows_sum(gb),
                 b_down=rows_sum(upstream), b_up=rows_sum(gpre))
    return output, gh, gb, g_up_t, g_down, small


def attend_back(z, q, k, v, p, go):
    gp = jnp.einsum("hqd,hkd->hkq", heads_of(go, z.head), heads_of(v, z.head), preferred_element_type=F32)
    pf = p.astype(F32)
    delta = jnp.sum(gp * pf, axis=1, keepdims=True)
    gs = (pf * (gp - delta)).astype(BF16)
    sc = z.head ** -0.5
    gq = jnp.einsum("hkq,hkd->qhd", gs, heads_of(k, z.head), preferred_element_type=F32) * sc
    gk = jnp.einsum("hkq,hqd->khd", gs, heads_of(q, z.head), preferred_element_type=F32) * sc
    gv = jnp.einsum("hkq,hqd->khd", p, heads_of(go, z.head), preferred_element_type=F32)
    return gq.reshape(q.shape).astype(BF16), gk.reshape(k.shape).astype(BF16), gv.reshape(v.shape).astype(BF16)


def stage_d(z, b, gb, gba, wo_f, wo_r):
    i = lax.axis_index("ctx")
    n1 = b["n1"]
    mine = lax.dynamic_slice_in_dim(n1, i * z.rows, z.rows)
    out = {}
    if z.full:
        go = dot(gba, wo_f, 1, 1).astype(BF16)
        gq, gk, gv = attend_back(z, b["q_f"], b["k_f"], b["v_f"], b["p_f"], go)
        out.update(gq_f=gq, gk_f=gk, gv_f=gv, gwo_f=dot(b["o_f"], gba, 0, 0))
        out["gw_f"] = jnp.stack([dot(n1, g, 0, 0) for g in (gq, gk, gv)])
    if z.rest:
        go = dot(gb, wo_r, 1, 1).astype(BF16)
        gq, gk, gv = attend_back(z, b["q_r"], b["k_r"], b["v_r"], b["p_r"], go)
        out.update(gq_r=gq, gk_r=gk, gv_r=gv, gwo_r=dot(b["o_r"], gb, 0, 0))
        out["gw_r"] = jnp.stack([dot(mine, gq, 0, 0), dot(n1, gk, 0, 0), dot(n1, gv, 0, 0)])
    return out


def stage_e(z, d, wf, wr, x, gh, gain1, small):
    i, s = lax.axis_index("ctx"), lax.axis_index("seq")
    part = 0.0
    own = 0.0
    if z.full:
        part = part + dot(d["gq_f"], wf[0], 1, 1) + dot(d["gk_f"], wf[1], 1, 1) + dot(d["gv_f"], wf[2], 1, 1)
    if z.rest:
        part = part + dot(d["gk_r"], wr[1], 1, 1) + dot(d["gv_r"], wr[2], 1, 1)
        own = own + dot(d["gq_r"], wr[0], 1, 1)
    gn1 = own + lax.psum_scatter(part.astype(BF16).astype(F32), "ctx", scatter_dimension=0, tiled=True)
    xhat, rstd = norm_stats(x.astype(F32))
    gtok = gh + norm_back(gn1, xhat, rstd, gain1)
    small = dict(small, gain1=rows_sum(gn1 * xhat), shift1=rows_sum(gn1))
    row = jnp.zeros((1, z.width), F32)
    for name, key in (("b_q", "gq"), ("b_v", "gv")):
        r = row
        if z.full:
            r = lax.dynamic_update_slice(r, rows_sum(d[key + "_f"]), (0, i * z.full_width))
        if z.rest:
            r = r.at[:, z.main :].add(rows_sum(d[key + "_r"]))
        small[name] = r
    full = jnp.zeros((4, z.width, z.width), F32)
    if z.full:
        full = lax.dynamic_update_slice(full, d["gw_f"], (0, 0, i * z.full_width))
        full = lax.dynamic_update_slice(full, d["gwo_f"][None], (3, i * z.full_width, 0))
    if z.rest:
        full = full.at[:3, :, z.main :].add(d["gw_r"])
        full = full.at[3, z.main :, :].add(d["gwo_r"])
    gw = lax.psum_scatter(full.reshape(4 * z.width, z.width).astype(BF16), ("seq", "ctx"), scatter_dimension=0, tiled=True)
    b_up_all = lax.all_gather(lax.psum(small.pop("b_up"), "ctx")[0], "seq", axis=0, tiled=True)
    names = list(small)
    tot = lax.psum(jnp.concatenate([small[n] for n in names]), ("seq", "ctx"))
    return gtok, gw.astype(F32), {n: tot[j : j + 1] for j, n in enumerate(names)}, b_up_all


MESH = pl.DeviceIdType.MESH
DMA = pltpu.SemaphoreType.DMA
VMEM_LIMIT = 56 << 20


def rcopy(src, dst, ssem, rsem, **dev):
    return pltpu.make_async_remote_copy(
        src_ref=src, dst_ref=dst, send_sem=ssem, recv_sem=rsem, device_id=dev, device_id_type=MESH
    )


def greet(ctx_peers, seq_peers):
    sem = pltpu.get_barrier_semaphore()
    for p in ctx_peers:
        pl.semaphore_signal(sem, inc=1, device_id={"ctx": p}, device_id_type=MESH)
    for p in seq_peers:
        pl.semaphore_signal(sem, inc=1, device_id={"seq": p}, device_id_type=MESH)
    pl.semaphore_wait(sem, len(ctx_peers) + len(seq_peers))


class Place:
    def __init__(self, z):
        self.k, self.s = lax.axis_index("ctx"), lax.axis_index("seq")
        self.chips = z.ctx // 2
        self.core = lax.rem(self.k, 2)
        self.chip = self.k // 2
        self.sib = self.k + 1 - 2 * self.core
        self.ring = [lax.rem(self.chip + i, self.chips) for i in range(self.chips)]
        self.same = [2 * q + self.core for q in self.ring]
        self.back = [2 * lax.rem(self.chip + self.chips - i, self.chips) + self.core for i in range(self.chips)]
        self.seqs = [lax.rem(self.s + i, z.seq) for i in range(z.seq)]
        self.seqs_back = [lax.rem(self.s + z.seq - i, z.seq) for i in range(z.seq)]


def call(body, name, outs, ins, scratch, cid, in_spaces, out_spaces, cost=None):
    spaces = {"v": pltpu.VMEM, "a": pl.ANY}
    return pl.pallas_call(
        body,
        name=name,
        out_shape=outs,
        in_specs=[pl.BlockSpec(memory_space=spaces[c]) for c in in_spaces],
        out_specs=[pl.BlockSpec(memory_space=spaces[c]) for c in out_spaces],
        scratch_shapes=scratch,
        compiler_params=pltpu.CompilerParams(
            collective_id=cid, has_side_effects=True, vmem_limit_bytes=VMEM_LIMIT
        ),
        cost_estimate=cost,
    )(*ins)


def sds(shape, dtype=BF16):
    return jax.ShapeDtypeStruct(shape, dtype)


class CtxGather:
    def __init__(self, at, own, dst, sems):
        self.at, self.own, self.dst, self.sems = at, own, dst, sems

    def send(self):
        at, ss, rs = self.at, self.sems[0], self.sems[1]
        for i in range(1, at.chips):
            rcopy(self.own, self.dst.at[at.k], ss.at[i], rs.at[i], ctx=at.same[i]).start()
        rcopy(self.own, self.dst.at[at.k], ss.at[0], rs.at[0], ctx=at.sib).start()
        pltpu.make_async_copy(self.own, self.dst.at[at.k], self.sems[4]).start()

    def forward(self, i):
        at, ss, rs, fs, fr = self.at, *self.sems[:4]
        src = at.back[i]
        rcopy(self.own, self.dst.at[src], ss.at[i], rs.at[i], ctx=at.same[i]).wait_recv()
        rcopy(self.dst.at[src], self.dst.at[src], fs.at[i], fr.at[i], ctx=at.sib).start()

    def finish(self):
        at, ss, rs, fs, fr = self.at, *self.sems[:4]
        pltpu.make_async_copy(self.own, self.dst.at[at.k], self.sems[4]).wait()
        rcopy(self.own, self.dst.at[at.k], ss.at[0], rs.at[0], ctx=at.sib).wait()
        for i in range(1, at.chips):
            rcopy(self.own, self.dst.at[at.k], ss.at[i], rs.at[i], ctx=at.same[i]).wait_send()
            rcopy(self.own, self.dst.at[at.k], fs.at[i], fr.at[i], ctx=at.sib).wait()

    @staticmethod
    def scratch(z):
        n = z.ctx // 2
        return [DMA((n,)), DMA((n,)), DMA((n,)), DMA((n,)), DMA]


def kernel_a(z, x, up, w, wm, wr, pk, xa, ua, wf, wra, wo2, wol, pa, *sems):
    at = Place(z)
    k, s, C = at.k, at.s, z.ctx
    g = CtxGather(at, x, xa, sems[:5])
    mz_s, mz_r, rz_s, rz_r, mx_s, mx_r, rx_s, rx_r, us, ur, oz_s, oz_r, ox_s, ox_r, loc, pz_s, pz_r, px_s, px_r = sems[5:]
    others = [lax.rem(k + i, C) for i in range(1, C)]
    greet(others, at.seqs[1:])
    last0 = z.main - (C - 1) * z.shard
    lastrows = w.at[pl.ds(last0, z.rest_width)]

    def cols(j):
        return wm.at[:, pl.ds(pl.multiple_of(j * z.full_width, z.full_width), z.full_width)]

    for i in range(1, C):
        rcopy(pk, pa.at[s, k], pz_s.at[i], pz_r.at[i], ctx=others[i - 1]).start()
    pltpu.make_async_copy(pk, pa.at[s, k], loc.at[3]).start()

    @pl.when(s < 3)
    def _():
        for i in range(1, C):
            j = lax.rem(k + i, C)
            rcopy(cols(j), wf.at[s, k], mz_s.at[i], mz_r.at[k], ctx=j).start()
            rcopy(wr, wra.at[s, k], rz_s.at[i], rz_r.at[k], ctx=j).start()
        pltpu.make_async_copy(cols(k), wf.at[s, k], loc.at[0]).start()
        pltpu.make_async_copy(wr, wra.at[s, k], loc.at[1]).start()

    @pl.when(s == 3)
    def _():
        @pl.when(k < C - 1)
        def _():
            rcopy(w, wo2.at[0], oz_s.at[0], oz_r.at[0], ctx=lax.rem(k + 1, C)).start()

        @pl.when(k == C - 1)
        def _():
            for i in range(1, C):
                rcopy(lastrows, wol, oz_s.at[i], oz_r.at[1], ctx=lax.rem(k + i, C)).start()
            pltpu.make_async_copy(lastrows, wol, loc.at[1]).start()

        pltpu.make_async_copy(w, wo2.at[1], loc.at[0]).start()
        for i in range(1, 4):
            rcopy(w, wo2.at[1], ox_s.at[0, i], ox_r.at[0], seq=at.seqs[i]).start()

    g.send()
    for i in range(1, z.seq):
        rcopy(up, ua.at[s], us.at[i], ur.at[i], seq=at.seqs[i]).start()
    pltpu.make_async_copy(up, ua.at[s], loc.at[2]).start()

    for i in range(1, C):
        rcopy(pk, pa.at[s, lax.rem(k + C - i, C)], pz_s.at[i], pz_r.at[i], ctx=k).wait_recv()
    pltpu.make_async_copy(pk, pa.at[s, k], loc.at[3]).wait()
    for i in range(1, z.seq):
        rcopy(pa.at[s], pa.at[s], px_s.at[i], px_r.at[i], seq=at.seqs[i]).start()

    @pl.when(s < 3)
    def _():
        for n in range(C):
            src = lax.rem(k + C - n, C)
            if n == 0:
                pltpu.make_async_copy(cols(k), wf.at[s, k], loc.at[0]).wait()
                pltpu.make_async_copy(wr, wra.at[s, k], loc.at[1]).wait()
            else:
                rcopy(cols(k), wf.at[s, src], mz_s.at[0], mz_r.at[src], ctx=k).wait_recv()
                rcopy(wr, wra.at[s, src], rz_s.at[0], rz_r.at[src], ctx=k).wait_recv()
            for i in range(1, 4):
                to = at.seqs[i]
                rcopy(wf.at[s, src], wf.at[s, src], mx_s.at[n, i], mx_r.at[s, src], seq=to).start()
                rcopy(wra.at[s, src], wra.at[s, src], rx_s.at[n, i], rx_r.at[s, src], seq=to).start()

    @pl.when(s == 3)
    def _():
        pltpu.make_async_copy(w, wo2.at[1], loc.at[0]).wait()

        @pl.when(k > 0)
        def _():
            rcopy(w, wo2.at[0], oz_s.at[0], oz_r.at[0], ctx=k).wait_recv()
            for i in range(1, 4):
                rcopy(wo2.at[0], wo2.at[0], ox_s.at[1, i], ox_r.at[1], seq=at.seqs[i]).start()

        @pl.when(k < C - 1)
        def _():
            rcopy(lastrows, wol, oz_s.at[1], oz_r.at[1], ctx=k).wait_recv()

        @pl.when(k == C - 1)
        def _():
            pltpu.make_async_copy(lastrows, wol, loc.at[1]).wait()

        for i in range(1, 4):
            rcopy(wol, wol, ox_s.at[2, i], ox_r.at[2], seq=at.seqs[i]).start()

    for i in range(1, at.chips):
        g.forward(i)
    g.finish()
    pltpu.make_async_copy(up, ua.at[s], loc.at[2]).wait()
    for i in range(1, z.seq):
        rcopy(up, ua.at[s], us.at[i], ur.at[i], seq=at.seqs[i]).wait()

    for i in range(1, C):
        rcopy(pk, pa.at[s, k], pz_s.at[i], pz_r.at[i], ctx=k).wait_send()
    for i in range(1, z.seq):
        rcopy(pa.at[s], pa.at[at.seqs_back[i]], px_s.at[i], px_r.at[i], seq=s).wait()

    for m in range(3):
        @pl.when(s != m)
        def _():
            for src in range(C):
                rcopy(wf.at[m, src], wf.at[m, src], mx_s.at[0, 0], mx_r.at[m, src], seq=s).wait_recv()
                rcopy(wra.at[m, src], wra.at[m, src], rx_s.at[0, 0], rx_r.at[m, src], seq=s).wait_recv()

    @pl.when(s != 3)
    def _():
        rcopy(w, wo2.at[1], ox_s.at[0, 0], ox_r.at[0], seq=s).wait_recv()

        @pl.when(k > 0)
        def _():
            rcopy(w, wo2.at[0], ox_s.at[1, 0], ox_r.at[1], seq=s).wait_recv()

        rcopy(wol, wol, ox_s.at[2, 0], ox_r.at[2], seq=s).wait_recv()

    @pl.when(s < 3)
    def _():
        for i in range(1, C):
            rcopy(cols(k), wf.at[s, k], mz_s.at[i], mz_r.at[k], ctx=k).wait_send()
            rcopy(wr, wra.at[s, k], rz_s.at[i], rz_r.at[k], ctx=k).wait_send()
        for n in range(C):
            for i in range(1, 4):
                rcopy(wf.at[s, k], wf.at[s, k], mx_s.at[n, i], mx_r.at[s, k], seq=s).wait_send()
                rcopy(wra.at[s, k], wra.at[s, k], rx_s.at[n, i], rx_r.at[s, k], seq=s).wait_send()

    @pl.when(s == 3)
    def _():
        @pl.when(k < C - 1)
        def _():
            rcopy(w, wo2.at[0], oz_s.at[0], oz_r.at[0], ctx=k).wait_send()

        @pl.when(k == C - 1)
        def _():
            for i in range(1, C):
                rcopy(lastrows, wol, oz_s.at[i], oz_r.at[1], ctx=k).wait_send()

        for i in range(1, 4):
            rcopy(w, wo2.at[1], ox_s.at[0, i], ox_r.at[0], seq=s).wait_send()

            @pl.when(k > 0)
            def _():
                rcopy(wo2.at[0], wo2.at[0], ox_s.at[1, i], ox_r.at[1], seq=s).wait_send()

            rcopy(wol, wol, ox_s.at[2, i], ox_r.at[2], seq=s).wait_send()


def stage_a_kernel(z, x, up, w, pk):
    C, k = z.ctx, lax.axis_index("ctx")
    outs = [
        sds((C, z.rows, z.width)), sds((z.seq, z.rows, z.width)), sds((3, C, z.shard, z.full_width)),
        sds((3, C, z.shard, z.rest_width)), sds((2, z.shard, z.width)), sds((z.rest_width, z.width)),
        sds((z.seq, C) + pk.shape),
    ]
    scratch = CtxGather.scratch(z) + [
        DMA((C,)), DMA((C,)), DMA((C,)), DMA((C,)), DMA((C, 4)), DMA((3, C)), DMA((C, 4)), DMA((3, C)),
        DMA((4,)), DMA((4,)), DMA((C,)), DMA((2,)), DMA((3, 4)), DMA((3,)), DMA((4,)),
        DMA((C,)), DMA((C,)), DMA((z.seq,)), DMA((z.seq,)),
    ]
    xa, ua, wf, wra, wo2, wol, pa = call(
        partial(kernel_a, z), "gather_in", outs, (x, up, w, w[:, : z.main], w[:, z.main :], pk), scratch, 0, "a" * 6, "a" * 7
    )
    wo_f = lax.dynamic_slice_in_dim(
        wo2.reshape(2 * z.shard, z.width), z.shard - (z.shard - z.full_width) * k, z.full_width
    )
    return (
        xa.reshape(z.slot, z.width), ua.reshape(z.seq * z.rows, z.width), wf.reshape(3, z.width, z.full_width),
        wra.reshape(3, z.width, z.rest_width), wo_f, wol, pa,
    )


def matmul(a, b, ca=1, cb=0):
    return lax.dot_general(a, b, (((ca,), (cb,)), ((), ())), preferred_element_type=F32)


def block(z, d):
    return pl.ds(pl.multiple_of(d * z.rows, z.rows), z.rows)


class CtxReduce:
    def __init__(self, at, part, bufs):
        self.at, self.part = at, part
        self.sb, self.sr, self.zb, self.zr, self.ss, self.sn, self.zs, self.zn = bufs

    def sib(self, t):
        return rcopy(self.sb.at[t], self.sr.at[t], self.ss.at[t], self.sn.at[t], ctx=self.at.sib)

    def far(self, t):
        return rcopy(self.zb.at[t], self.zr.at[t], self.zs.at[t], self.zn.at[t], ctx=self.at.same[t])

    def start(self):
        at = self.at
        order = list(range(1, at.chips)) + [0]
        for t in order:
            self.sb[t] = self.part(2 * at.ring[t] + 1 - at.core).astype(BF16)
            self.sib(t).start()
        for t in order[:-1]:
            mine = self.part(at.same[t])
            self.sib(t).wait_recv()
            self.zb[t] = (mine + self.sr[t].astype(F32)).astype(BF16)
            self.far(t).start()

    def finish(self):
        at = self.at
        total = self.part(at.k)
        self.sib(0).wait_recv()
        total = total + self.sr[0].astype(F32)
        for t in range(1, at.chips):
            self.far(t).wait_recv()
            total = total + self.zr[t].astype(F32)
        return total

    def close(self):
        for t in range(self.at.chips):
            self.sib(t).wait_send()
            if t:
                self.far(t).wait_send()

    @staticmethod
    def scratch(z):
        n = z.ctx // 2
        return [pltpu.VMEM((n, z.rows, z.width), BF16)] * 4 + [DMA((n,))] * 4


def kernel_c(z, o_f, wo_f, o_r, wo_r, x, b_o, gain2, shift2, hid, xh, rs_o, n2a, n2, ns, nr, *bufs):
    at = Place(z)
    greet([at.sib] + at.same[1:], at.seqs[1:])
    red = CtxReduce(at, lambda d: matmul(o_f[block(z, d)], wo_f[...]), bufs)
    red.start()
    own = matmul(o_r[...], wo_r[...]) + b_o[...] + x[...].astype(F32)
    hidden = red.finish() + own
    xhat, rstd = norm_stats(hidden)
    n2[...] = (xhat * gain2[...] + shift2[...]).astype(BF16)
    copies = [rcopy(n2, n2a.at[at.s], ns.at[i], nr.at[i], seq=at.seqs[i]) for i in range(1, z.seq)]
    for c in copies:
        c.start()
    n2a[at.s] = n2[...]
    hid[...] = hidden
    xh[...] = xhat
    rs_o[...] = jnp.broadcast_to(rstd, rs_o.shape)
    red.close()
    for c in copies:
        c.wait()


def stage_c_kernel(z, b, wo_f, wo_r, x, prm):
    outs = [sds((z.rows, z.width), F32), sds((z.rows, z.width), F32), sds((z.rows, 128), F32), sds((z.seq, z.rows, z.width))]
    scratch = [pltpu.VMEM((z.rows, z.width), BF16), DMA((z.seq,)), DMA((z.seq,))] + CtxReduce.scratch(z)
    return call(
        partial(kernel_c, z), "project_out", outs,
        (b["o_f"], wo_f, b["o_r"], wo_r, x, prm["b_o"], prm["gain2"], prm["shift2"]), scratch, 1, "v" * 8, "v" * 4,
    )


def kernel_f(z, n2a, ua, up_t, down, b_up, hid, xh, rs_i, gain2, b_down, live, out, gh_o, gb_o, gup, gdown, sm, bu,
             act, gpre, gsend, grecv, fsend, frecv, gs, gr, fs, fr):
    at = Place(z)
    greet([], at.seqs[1:])
    S, R, D = z.seq, z.rows, z.width
    units = up_t.shape[0]
    n2 = n2a[...]
    u = ua[...]
    step = 256
    for c0 in range(0, units, step):
        c = slice(c0, min(c0 + step, units))
        pre = matmul(n2, up_t[c], 1, 1) + b_up[:, c]
        gact = matmul(u, down[c], 1, 1)
        cdf = 0.5 * (1.0 + lax.erf(pre * (0.5 ** 0.5)))
        act[:, c] = (pre * cdf).astype(BF16)
        dgelu = cdf + pre * jnp.exp(-0.5 * pre * pre) * (1.0 / math.sqrt(2.0 * math.pi))
        g = (gact * dgelu).astype(BF16)
        gpre[:, c] = g
        bu[:, c] = jnp.sum(g.astype(F32), axis=0, keepdims=True)

    def gcopy(i):
        return rcopy(gsend.at[i], grecv.at[i], gs.at[i], gr.at[i], seq=at.seqs[i])

    def fcopy(i):
        return rcopy(fsend.at[i], frecv.at[i], fs.at[i], fr.at[i], seq=at.seqs[i])

    for i in range(1, S):
        gsend[i] = matmul(gpre[block(z, at.seqs[i])], up_t[...]).astype(BF16)
        gcopy(i).start()
    mine = block(z, at.s)
    gn2 = matmul(gpre[mine], up_t[...])
    for i in range(1, S):
        fsend[i] = matmul(act[block(z, at.seqs[i])], down[...]).astype(BF16)
        fcopy(i).start()
    ff = matmul(act[mine], down[...])
    for i in range(1, S):
        gcopy(i).wait_recv()
        gn2 = gn2 + grecv[i].astype(F32)
    xhat = xh[...]
    up_own = ua[mine].astype(F32)
    gh = up_own + norm_back(gn2, xhat, rs_i[:, :1], gain2[...])
    gb = gh.astype(BF16)
    gh_o[...] = gh
    gb_o[...] = gb
    sm[0:1] = jnp.sum(gn2 * xhat, axis=0, keepdims=True)
    sm[1:2] = jnp.sum(gn2, axis=0, keepdims=True)
    sm[2:3] = jnp.sum(gb.astype(F32), axis=0, keepdims=True)
    sm[3:4] = jnp.sum(up_own, axis=0, keepdims=True)
    for c0 in range(0, units, step):
        c = slice(c0, min(c0 + step, units))
        gup[c] = matmul(gpre[:, c], n2, 0, 0).astype(BF16)
        gdown[c] = matmul(act[:, c], u, 0, 0).astype(BF16)
    for i in range(1, S):
        fcopy(i).wait_recv()
        ff = ff + frecv[i].astype(F32)
    out[...] = (live[:, :1] * (hid[...] + ff + b_down[...])).astype(BF16)
    for i in range(1, S):
        gcopy(i).wait_send()
        fcopy(i).wait_send()


def stage_f_kernel(z, n2a, ua, up_t, down, prm, hid, xh, rs, live):
    R, D, S, U = z.rows, z.width, z.seq, up_t.shape[0]
    outs = [sds((R, D)), sds((R, D), F32), sds((R, D)), sds((U, D)), sds((U, D)), sds((4, D), F32), sds((1, U), F32)]
    scratch = [pltpu.VMEM((S * R, U), BF16)] * 2 + [pltpu.VMEM((S, R, D), BF16)] * 4 + [DMA((S,))] * 4
    return call(
        partial(kernel_f, z), "feed_forward", outs,
        (n2a.reshape(S * R, D), ua, up_t, down, prm["b_up"], hid, xh, rs, prm["gain2"], prm["b_down"],
         jnp.broadcast_to(live, (R, 128))), scratch, 2, "v" * 11, "v" * 7,
    )


def kernel_g(z, own, dst, *sems):
    at = Place(z)
    g = CtxGather(at, own, dst, sems)
    greet([at.sib] + at.same[1:], [])
    g.send()
    for i in range(1, at.chips):
        g.forward(i)
    g.finish()


def gather_ctx_kernel(z, own):
    return call(partial(kernel_g, z), "gather_back", [sds((z.ctx, z.rows, z.width))], (own,), CtxGather.scratch(z), 3, "a", "a")[0]


class SmallSum:
    def __init__(self, at, buf, rsib, rchip, rseq, sems):
        self.at, self.buf, self.rsib, self.rchip, self.rseq = at, buf, rsib, rchip, rseq
        self.s0, self.r0, self.s1, self.r1, self.s2, self.r2 = sems

    def sib(self):
        return rcopy(self.buf.at[0], self.rsib, self.s0, self.r0, ctx=self.at.sib)

    def chip(self, i):
        return rcopy(self.buf.at[1], self.rchip.at[i], self.s1.at[i], self.r1.at[i], ctx=self.at.same[i])

    def line(self, i):
        return rcopy(self.buf.at[2], self.rseq.at[i], self.s2.at[i], self.r2.at[i], seq=self.at.seqs[i])

    def first(self, value):
        self.buf[0] = value
        self.sib().start()

    def second(self):
        self.sib().wait_recv()
        self.buf[1] = self.buf[0] + self.rsib[...]
        for i in range(1, self.at.chips):
            self.chip(i).start()

    def third(self):
        total = self.buf[1]
        for i in range(1, self.at.chips):
            self.chip(i).wait_recv()
            total = total + self.rchip[i]
        self.buf[2] = total
        for i in range(1, len(self.at.seqs)):
            self.line(i).start()

    def last(self):
        total = self.buf[2]
        for i in range(1, len(self.at.seqs)):
            self.line(i).wait_recv()
            total = total + self.rseq[i]
        return total

    def close(self):
        self.sib().wait_send()
        for i in range(1, self.at.chips):
            self.chip(i).wait_send()
        for i in range(1, len(self.at.seqs)):
            self.line(i).wait_send()

    @staticmethod
    def scratch(z, rows):
        n, shape = z.ctx // 2, (rows, z.width)
        return [
            pltpu.VMEM((3,) + shape, F32), pltpu.VMEM(shape, F32), pltpu.VMEM((n,) + shape, F32),
            pltpu.VMEM((z.seq,) + shape, F32), DMA, DMA, DMA((n,)), DMA((n,)), DMA((z.seq,)), DMA((z.seq,)),
        ]


def kernel_e(z, gq, gk, gv, gkr, gvr, gqr, wf, wr, x, gh, gain1, gwf, gwr, gwo, gwor, sme,
             gtok, ga, tot, bup,
             rf, rr, ro, ror, sf_s, sf_r, sr_s, sr_r, so_s, so_r, sor_s, sor_r,
             zs, zr, land, landr, zs_s, zs_r, zr_s, zr_r,
             buf32, obs, obn, orrs, orr, ob_s, ob_r, orr_s, orr_r, *rest):
    at = Place(z)
    s, k, C, S, FW = at.s, at.k, z.ctx, z.seq, z.full_width
    bufs, small_e, small_l = rest[:8], rest[8:18], rest[18:]
    greet([lax.rem(k + i, C) for i in range(1, C)], at.seqs[1:])

    def up(ref, dst, ssem, rsem, i, m=None):
        return rcopy(ref if m is None else ref.at[m], dst.at[i], ssem.at[i], rsem.at[i], seq=at.seqs[i])

    for i in range(1, S):
        m = at.seqs[i]

        @pl.when(m < 3)
        def _():
            up(gwf, rf, sf_s, sf_r, i, m).start()
            up(gwr, rr, sr_s, sr_r, i, m).start()

        @pl.when(m == 3)
        def _():
            up(gwo, ro, so_s, so_r, i).start()
            up(gwor, ror, sor_s, sor_r, i).start()

    se = SmallSum(at, *small_e[:4], small_e[4:])
    se.first(sme[...])

    def part(d):
        r = block(z, d)
        return (
            matmul(gq[r], wf[0], 1, 1) + matmul(gk[r], wf[1], 1, 1) + matmul(gv[r], wf[2], 1, 1)
            + matmul(gkr[r], wr[1], 1, 1) + matmul(gvr[r], wr[2], 1, 1)
        )

    red = CtxReduce(at, part, bufs)
    red.start()
    se.second()

    def zf(i):
        return rcopy(zs.at[lax.rem(k + i, C)], land.at[i], zs_s.at[i], zs_r.at[i], ctx=lax.rem(k + i, C))

    def zrr(i):
        return rcopy(zr.at[lax.rem(k + i, C)], landr.at[i], zr_s.at[i], zr_r.at[i], ctx=lax.rem(k + i, C))

    def shift():
        return rcopy(obs, obn, ob_s, ob_r, ctx=lax.rem(k + C - 1, C))

    def tail(i):
        return rcopy(orrs, orr.at[i], orr_s, orr_r.at[i], ctx=C - 1)

    @pl.when(s < 3)
    def _():
        for i in range(1, S):
            up(gwf, rf, sf_s, sf_r, i, 0).wait_recv()
            up(gwr, rr, sr_s, sr_r, i, 0).wait_recv()

        def add(j, _):
            t, u = gwf[s, j].astype(F32), gwr[s, j].astype(F32)
            for i in range(1, S):
                t = t + rf[i, j].astype(F32)
                u = u + rr[i, j].astype(F32)
            zs[j] = t.astype(BF16)
            zr[j] = u.astype(BF16)
            return 0

        lax.fori_loop(0, C, add, 0)
        for i in range(1, C):
            zf(i).start()
            zrr(i).start()

    @pl.when(s == 3)
    def _():
        for i in range(1, S):
            up(gwo, ro, so_s, so_r, i).wait_recv()
            up(gwor, ror, sor_s, sor_r, i).wait_recv()
        t, u = gwo[...].astype(F32), gwor[...].astype(F32)
        for i in range(1, S):
            t = t + ro[i].astype(F32)
            u = u + ror[i].astype(F32)
        buf32[pl.ds(0, FW)] = t
        obs[...] = t.astype(BF16)
        orrs[...] = u.astype(BF16)

        @pl.when(k > 0)
        def _():
            shift().start()

        for i in range(C - 1):
            @pl.when(k == i)
            def _():
                tail(i).start()

    se.third()
    gn1 = red.finish() + matmul(gqr[...], wr[0], 1, 1)
    xhat, rstd = norm_stats(x[...].astype(F32))
    sl = SmallSum(at, *small_l[:4], small_l[4:])
    sl.first(jnp.concatenate([jnp.sum(gn1 * xhat, axis=0, keepdims=True), jnp.sum(gn1, axis=0, keepdims=True)], axis=0))
    gtok[...] = gh[...] + norm_back(gn1, xhat, rstd, gain1[...])
    sl.second()
    early = se.last()
    tot[...] = early
    bup[s] = se.buf[2, 6:7]
    for i in range(1, S):
        bup[at.seqs_back[i]] = se.rseq[i, 6:7]

    @pl.when(s < 3)
    def _():
        ga[:, pl.ds(pl.multiple_of(k * FW, FW), FW)] = zs[k].astype(F32)
        remain = zr[k].astype(F32)
        for i in range(1, C):
            zf(i).wait_recv()
            zrr(i).wait_recv()
            j = lax.rem(k + C - i, C)
            ga[:, pl.ds(pl.multiple_of(j * FW, FW), FW)] = land[i].astype(F32)
            remain = remain + landr[i].astype(F32)
        ga[:, z.main :] = remain
        for i in range(1, C):
            zf(i).wait_send()
            zrr(i).wait_send()

    sl.third()

    @pl.when(s == 3)
    def _():
        @pl.when(k < C - 1)
        def _():
            shift().wait_recv()
            buf32[pl.ds(FW, FW)] = obn[...].astype(F32)

        @pl.when(k == C - 1)
        def _():
            u = orrs[...].astype(F32)
            for i in range(C - 1):
                tail(i).wait_recv()
                u = u + orr[i].astype(F32)
            buf32[pl.ds(FW, z.rest_width)] = u

        ga[...] = buf32[pl.ds(pl.multiple_of((z.shard - FW) * k, 8), z.shard)]

        @pl.when(k > 0)
        def _():
            shift().wait_send()

        @pl.when(k < C - 1)
        def _():
            tail(0).wait_send()

    late = sl.last()
    tot[6:8] = late
    red.close()
    se.close()
    sl.close()
    for i in range(1, S):
        m = at.seqs[i]

        @pl.when(m < 3)
        def _():
            up(gwf, rf, sf_s, sf_r, i, m).wait_send()
            up(gwr, rr, sr_s, sr_r, i, m).wait_send()

        @pl.when(m == 3)
        def _():
            up(gwo, ro, so_s, so_r, i).wait_send()
            up(gwor, ror, sor_s, sor_r, i).wait_send()


def stage_e_kernel(z, d, wf, wr, x, gh, gain1, small):
    C, S, D, FW, RW, SH = z.ctx, z.seq, z.width, z.full_width, z.rest_width, z.shard
    sme = jnp.concatenate([small["gain2"], small["shift2"], small["b_o"], small["b_down"], d["sums"], small["b_up"],
                           jnp.zeros((1, D), F32)], axis=0)
    outs = [sds((z.rows, D), F32), sds((SH, D), F32), sds((8, D), F32), sds((S, 1, D), F32)]
    V = pltpu.VMEM
    scratch = [
        V((S, C, SH, FW), BF16), V((S, C, SH, RW), BF16), V((S, FW, D), BF16), V((S, RW, D), BF16),
        *[DMA((S,)) for _ in range(8)],
        V((C, SH, FW), BF16), V((C, SH, RW), BF16), V((C, SH, FW), BF16), V((C, SH, RW), BF16),
        *[DMA((C,)) for _ in range(4)],
        V((2 * FW, D), F32), V((FW, D), BF16), V((FW, D), BF16), V((RW, D), BF16), V((C, RW, D), BF16),
        DMA, DMA, DMA, DMA((C,)),
        *CtxReduce.scratch(z), *SmallSum.scratch(z, 8), *SmallSum.scratch(z, 2),
    ]
    low = lambda v: v.astype(BF16)
    gtok, ga, tot, bup = call(
        partial(kernel_e, z), "gradients_out", outs,
        (d["gq_f"], d["gk_f"], d["gv_f"], d["gk_r"], d["gv_r"], d["gq_r"], wf, wr, x, gh, gain1,
         low(d["gw_f"]).reshape(3, C, SH, FW), low(d["gw_r"]).reshape(3, C, SH, RW), low(d["gwo_f"]), low(d["gwo_r"]), sme),
        scratch, 4, "v" * 16, "v" * 4,
    )
    names = ("gain2", "shift2", "b_o", "b_down", "b_q", "b_v", "gain1", "shift1")
    return gtok, ga, {n: tot[j : j + 1] for j, n in enumerate(names)}, bup.reshape(-1)


NEG = -1e30


def turn(v):
    return jnp.transpose(v.astype(F32)).astype(BF16)


def of_head(v, h, head):
    lane = lax.broadcasted_iota(jnp.int32, v.shape, 1) // head
    return jnp.where(lane == h, v.astype(F32), 0.0)


def attend_block(k, v_t, q, mask, head, p_ref):
    parts = []
    for h in range(k.shape[1] // head):
        qh = (of_head(q, h, head) * head ** -0.5).astype(BF16)
        s = matmul(k, qh, 1, 1) + mask
        e = jnp.exp(s - jnp.max(s, axis=0, keepdims=True))
        p = (e * (1.0 / jnp.sum(e, axis=0, keepdims=True))).astype(BF16)
        p_ref[h] = p
        parts.append(matmul(v_t[h * head : (h + 1) * head], p))
    o_t = parts[0] if len(parts) == 1 else jnp.concatenate(parts, axis=0)
    return jnp.transpose(o_t).astype(BF16)


def kernel_b(z, qb, xa, gain, shift, wf, wr, bqf, bqr, bvf, bvr, kpos, qpos,
             n1, q_f, k_f, v_f, p_f, o_f, q_r, k_r, v_r, p_r, o_r, vt):
    step = pl.program_id(0)

    @pl.when(step == 0)
    def _():
        def rows(j, _):
            r = block(z, j)
            n1[r] = (norm_stats(xa[r].astype(F32))[0] * gain[...] + shift[...]).astype(BF16)
            return 0

        lax.fori_loop(0, z.ctx, rows, 0)
        n = n1[...]
        q_f[...] = (matmul(n, wf[0]) + bqf[...]).astype(BF16)
        k_f[...] = matmul(n, wf[1]).astype(BF16)
        v = (matmul(n, wf[2]) + bvf[...]).astype(BF16)
        v_f[...] = v
        vt[...] = turn(v)
        mine = block(z, lax.axis_index("ctx"))
        qr = (matmul(n1[mine], wr[0]) + bqr[...]).astype(BF16)
        kr = matmul(n, wr[1]).astype(BF16)
        vr = (matmul(n, wr[2]) + bvr[...]).astype(BF16)
        q_r[...] = qr
        k_r[...] = kr
        v_r[...] = vr
        mask = jnp.where(kpos[...] <= qpos[:, mine], 0.0, NEG)
        o_r[...] = attend_block(kr, turn(vr), qr, mask, z.head, p_r)

    r = pl.ds(pl.multiple_of(step * qb, qb), qb)
    mask = jnp.where(kpos[...] <= qpos[:, r], 0.0, NEG)
    o_f[...] = attend_block(k_f[...], vt[...], q_f[r], mask, z.head, p_f.at[0])


def whole(shape):
    n = len(shape)
    return pl.BlockSpec(shape, lambda i: (0,) * n)


def stage_b_kernel(z, x_all, wf, wr, gain, shift, bq_f, bq_r, bv_f, bv_r, pos, length):
    N, D, FW, RW, R, qb = z.slot, z.width, z.full_width, z.rest_width, z.rows, 256
    kpos = jnp.where(pos < length, pos, 1 << 30)[:, None]
    ins = (x_all, gain, shift, wf, wr, bq_f, bq_r, bv_f, bv_r, kpos, pos[None, :])
    names = ("n1", "q_f", "k_f", "v_f", "p_f", "o_f", "q_r", "k_r", "v_r", "p_r", "o_r")
    shapes = [(N, D), (N, FW), (N, FW), (N, FW), (N // qb, z.full, N, qb), (N, FW), (R, RW), (N, RW), (N, RW), (z.rest, N, R), (R, RW)]
    specs = [whole(s) for s in shapes]
    specs[4] = pl.BlockSpec((1, z.full, N, qb), lambda i: (i, 0, 0, 0))
    specs[5] = pl.BlockSpec((qb, FW), lambda i: (i, 0))
    out = pl.pallas_call(
        partial(kernel_b, z, qb), name="attention",
        grid=(N // qb,), out_shape=[sds(s) for s in shapes], in_specs=[whole(a.shape) for a in ins], out_specs=specs,
        scratch_shapes=[pltpu.VMEM((FW, N), BF16)],
        compiler_params=pltpu.CompilerParams(vmem_limit_bytes=VMEM_LIMIT),
        cost_estimate=pl.CostEstimate(flops=4 * 10**9, bytes_accessed=20 << 20, transcendentals=3 * 10**6),
    )(*ins)
    return dict(zip(names, out))


def attend_block_back(k_t, v, q, go, p_ref, head, gk, gv):
    parts = []
    for h in range(v.shape[1] // head):
        goh = of_head(go, h, head).astype(BF16)
        p = p_ref[h]
        pf = p.astype(F32)
        gp = matmul(v, goh, 1, 1)
        delta = jnp.sum(gp * pf, axis=0, keepdims=True)
        gs = (pf * (gp - delta)).astype(BF16)
        gk[...] += matmul(gs, of_head(q, h, head).astype(BF16))
        gv[...] += matmul(p, goh)
        parts.append(matmul(k_t[h * head : (h + 1) * head], gs))
    g_t = parts[0] if len(parts) == 1 else jnp.concatenate(parts, axis=0)
    return (jnp.transpose(g_t) * head ** -0.5).astype(BF16)


def kernel_d(z, qb, gba, wo_f, wo_r, n1, q_f, k_f, v_f, p_f, o_f, q_r, k_r, v_r, p_r, o_r,
             gq_f, gk_f, gv_f, gq_r, gk_r, gv_r, gw_f, gw_r, gwo_f, gwo_r, sums, go, kt, gk, gv, gkr, gvr):
    step, last = pl.program_id(0), pl.num_programs(0) - 1
    scale = z.head ** -0.5
    mine = block(z, lax.axis_index("ctx"))

    @pl.when(step == 0)
    def _():
        go[...] = matmul(gba[...], wo_f[...], 1, 1).astype(BF16)
        kt[...] = turn(k_f[...])
        gk[...] = jnp.zeros_like(gk)
        gv[...] = jnp.zeros_like(gv)
        gkr[...] = jnp.zeros_like(gkr)
        gvr[...] = jnp.zeros_like(gvr)
        gwo_f[...] = matmul(o_f[...], gba[...], 0, 0).astype(BF16)
        gb = gba[mine]
        gwo_r[...] = matmul(o_r[...], gb, 0, 0).astype(BF16)
        gor = matmul(gb, wo_r[...], 1, 1).astype(BF16)
        gq_r[...] = attend_block_back(turn(k_r[...]), v_r[...], q_r[...], gor, p_r, z.head, gkr, gvr)

    r = pl.ds(pl.multiple_of(step * qb, qb), qb)
    gq_f[r] = attend_block_back(kt[...], v_f[...], q_f[r], go[r], p_f.at[0], z.head, gk, gv)

    @pl.when(step == last)
    def _():
        gk_f[...] = (gk[...] * scale).astype(BF16)
        gv_f[...] = gv[...].astype(BF16)
        gk_r[...] = (gkr[...] * scale).astype(BF16)
        gv_r[...] = gvr[...].astype(BF16)
        n = n1[...]
        for m, g in enumerate((gq_f, gk_f, gv_f)):
            gw_f[m] = matmul(n, g[...], 0, 0).astype(BF16)
        gw_r[0] = matmul(n1[mine], gq_r[...], 0, 0).astype(BF16)
        gw_r[1] = matmul(n, gk_r[...], 0, 0).astype(BF16)
        gw_r[2] = matmul(n, gv_r[...], 0, 0).astype(BF16)
        at = lax.axis_index("ctx")
        for j, (a, b) in enumerate(((gq_f, gq_r), (gv_f, gv_r))):
            s = jnp.sum(a[...].astype(F32), axis=0, keepdims=True)
            for c in range(z.ctx):
                sums[j : j + 1, c * z.full_width : (c + 1) * z.full_width] = jnp.where(at == c, s, 0.0)
            sums[j : j + 1, z.main :] = jnp.sum(b[...].astype(F32), axis=0, keepdims=True)


def stage_d_kernel(z, b, gba, wo_f, wo_r):
    N, D, FW, RW, R, qb = z.slot, z.width, z.full_width, z.rest_width, z.rows, 256
    names = ("q_f", "k_f", "v_f", "p_f", "o_f", "q_r", "k_r", "v_r", "p_r", "o_r")
    ins = (gba, wo_f, wo_r, b["n1"]) + tuple(b[n] for n in names)
    in_specs = [whole(a.shape) for a in ins]
    in_specs[7] = pl.BlockSpec((1, z.full, N, qb), lambda i: (i, 0, 0, 0))
    outs = ("gq_f", "gk_f", "gv_f", "gq_r", "gk_r", "gv_r", "gw_f", "gw_r", "gwo_f", "gwo_r", "sums")
    shapes = [(N, FW)] * 3 + [(R, RW), (N, RW), (N, RW), (3, D, FW), (3, D, RW), (FW, D), (RW, D), (2, D)]
    out = pl.pallas_call(
        partial(kernel_d, z, qb), name="attention_back",
        grid=(N // qb,), out_shape=[sds(s) for s in shapes[:-1]] + [sds(shapes[-1], F32)],
        in_specs=in_specs, out_specs=[whole(s) for s in shapes],
        scratch_shapes=[pltpu.VMEM((N, FW), BF16), pltpu.VMEM((FW, N), BF16), pltpu.VMEM((N, FW), F32), pltpu.VMEM((N, FW), F32),
                        pltpu.VMEM((N, RW), F32), pltpu.VMEM((N, RW), F32)],
        compiler_params=pltpu.CompilerParams(vmem_limit_bytes=VMEM_LIMIT),
        cost_estimate=pl.CostEstimate(flops=8 * 10**9, bytes_accessed=30 << 20, transcendentals=0),
    )(*ins)
    return dict(zip(outs, out))


def shards(tokens, lengths, block_order, attention_weights, up_weights, down_weights, norm_gains, biases, cotangent):
    z = Sizes(tokens.shape[1], tokens.shape[2], block_order.shape[0])
    i, s = lax.axis_index("ctx"), lax.axis_index("seq")
    D = z.width
    x, cot = tokens[0], cotangent[0]
    length = lengths[0]
    pos = (block_order[:, None] * z.block_len + jnp.arange(z.block_len, dtype=jnp.int32)[None, :]).reshape(z.slot)
    my_pos = lax.dynamic_slice_in_dim(pos, i * z.rows, z.rows)
    live = (my_pos < length).astype(F32)[:, None]
    n_g, n_b = norm_gains.shape[0], biases.shape[0]
    lanes = -(-(n_g + n_b) // 1024) * 8
    packed = jnp.pad(jnp.concatenate([norm_gains, biases]), (0, lanes * 128 - n_g - n_b)).reshape(lanes, 128)
    upstream = (live * cot.astype(F32)).astype(BF16)
    fast = z.full > 0 and z.seq == 4 and 0 < z.width - z.main <= z.shard and z.ctx * up_weights.shape[1] == z.width and z.slot * D * 2 <= (4 << 20)
    if fast:
        x_all, ua, wf, wr, wo_f, wo_r, both = stage_a_kernel(z, x, upstream, attention_weights, packed)
    else:
        x_all, wf, wr, wo_f, wo_r = stage_a(z, x, attention_weights)
        ua = lax.all_gather(upstream, "seq", axis=0, tiled=True)
        both = lax.all_gather(packed, ("seq", "ctx"), axis=0)
    both = both.reshape(z.seq * z.ctx, lanes * 128)
    gains = both[:, :n_g].reshape(-1).astype(F32)
    bias = both[:, n_g : n_g + n_b].reshape(-1).astype(F32)
    row = lambda v: v[None, :]
    piece = [row(bias[j * D : (j + 1) * D]) for j in range(6)]
    gain1, gain2 = row(gains[:D]), row(gains[D:])
    b_up = row(lax.dynamic_slice_in_dim(bias[6 * D :], s * (z.ctx * up_weights.shape[1]), z.ctx * up_weights.shape[1]))
    prm = dict(gain2=gain2, shift2=piece[4], b_o=piece[3], b_down=piece[5], b_up=b_up)
    fslice = lambda v: lax.dynamic_slice(v, (0, i * z.full_width), (1, z.full_width))
    up_t = lax.all_gather(up_weights.T, "ctx", axis=0, tiled=True)
    down = lax.all_gather(down_weights, "ctx", axis=0, tiled=True)

    b = (stage_b_kernel if fast else stage_b)(z, x_all, wf, wr, gain1, piece[0], fslice(piece[1]), piece[1][:, z.main :],
                fslice(piece[2]), piece[2][:, z.main :], pos, length)
    if fast:
        hid, xh, rs, n2a = stage_c_kernel(z, b, wo_f, wo_r, x, prm)
        output, gh, gb, g_up_t, g_down, sm, bu = stage_f_kernel(z, n2a, ua, up_t, down, prm, hid, xh, rs, live)
        small = dict(gain2=sm[0:1], shift2=sm[1:2], b_o=sm[2:3], b_down=sm[3:4], b_up=bu)
    else:
        output, gh, gb, g_up_t, g_down, small = stage_c(z, b, wo_f, wo_r, x, upstream, ua, live, up_t, down, prm)
    g_up_own = lax.psum_scatter(g_up_t, "ctx", scatter_dimension=0, tiled=True).astype(F32).T
    g_down_own = lax.psum_scatter(g_down, "ctx", scatter_dimension=0, tiled=True).astype(F32)
    if fast:
        gba = gather_ctx_kernel(z, gb).reshape(z.slot, D)
    else:
        gba = lax.all_gather(gb, "ctx", axis=0, tiled=True) if z.full else None
    if fast:
        d = stage_d_kernel(z, b, gba, wo_f, wo_r)
        gtok, gw, tot, b_up_all = stage_e_kernel(z, d, wf, wr, x, gh, gain1, small)
    else:
        d = stage_d(z, b, gb, gba, wo_f, wo_r)
        gtok, gw, tot, b_up_all = stage_e(z, d, wf, wr, x, gh, gain1, small)
    me = s * z.ctx + i
    g_gain = lax.dynamic_slice_in_dim(jnp.concatenate([tot["gain1"][0], tot["gain2"][0]]), me * n_g, n_g)
    g_bias = lax.dynamic_slice_in_dim(jnp.concatenate([tot[n][0] for n in ("shift1", "b_q", "b_v", "b_o", "shift2", "b_down")] + [b_up_all]), me * n_b, n_b)
    return output[None], gtok[None], gw, g_up_own, g_down_own, g_gain, g_bias


def solution(mesh):
    in_specs = (
        P("seq", "ctx", None), P("seq"), P(), P(("seq", "ctx"), None), P(None, ("seq", "ctx")),
        P(("seq", "ctx"), None), P(("seq", "ctx")), P(("seq", "ctx")), P("seq", "ctx", None),
    )
    out_specs = (
        P("seq", "ctx", None), P("seq", "ctx", None), P(("seq", "ctx"), None), P(None, ("seq", "ctx")),
        P(("seq", "ctx"), None), P(("seq", "ctx")), P(("seq", "ctx")),
    )
    return jax.shard_map(shards, mesh=mesh, in_specs=in_specs, out_specs=out_specs, check_vma=False)
```

```python
import math
from functools import partial

import jax
import jax.numpy as jnp
from jax import lax
from jax.experimental import pallas as pl
from jax.experimental.pallas import tpu as pltpu
from jax.sharding import PartitionSpec as P

HEADS = 17
EPS = 1e-05
F32 = jnp.float32
BF16 = jnp.bfloat16


def norm_stats(values):
    centre = values - jnp.mean(values, axis=-1, keepdims=True)
    rstd = lax.rsqrt(jnp.mean(centre * centre, axis=-1, keepdims=True) + EPS)
    return centre * rstd, rstd


def norm_back(grad, xhat, rstd, gain):
    e = grad * gain
    mean_e = jnp.mean(e, axis=-1, keepdims=True)
    mean_ex = jnp.mean(e * xhat, axis=-1, keepdims=True)
    return (e - mean_e - xhat * mean_ex) * rstd


def dot(a, b, ca, cb):
    return lax.dot_general(a, b, (((ca,), (cb,)), ((), ())), preferred_element_type=F32)


def rows_sum(v):
    return jnp.sum(v.astype(F32), axis=0, keepdims=True)


class Sizes:
    def __init__(self, rows, width, block_count):
        self.rows, self.width = rows, width
        self.ctx, self.seq = lax.axis_size("ctx"), lax.axis_size("seq")
        self.slot = rows * self.ctx
        self.block_len = self.slot // block_count
        self.head = width // HEADS
        self.full = HEADS // self.ctx
        self.full_width = self.full * self.head
        self.main = self.full_width * self.ctx
        self.rest = HEADS - self.full * self.ctx
        self.rest_width = self.rest * self.head
        self.shard = width // self.ctx


def stage_a(z, x, w):
    k = lax.axis_index("ctx")
    x_all = lax.all_gather(x, "ctx", axis=0, tiled=True)
    w_all = lax.all_gather(w, "seq", axis=0)
    wm = w_all[:3, :, : z.main].reshape(3, z.shard, z.ctx, z.full_width)
    wf = lax.all_to_all(wm, "ctx", split_axis=2, concat_axis=1, tiled=True).reshape(
        3, z.width, z.full_width
    )
    wr = lax.all_gather(w_all[:3, :, z.main :], "ctx", axis=1, tiled=True)
    wo = lax.all_gather(w_all[3], "ctx", axis=0, tiled=True)
    wo_f = lax.dynamic_slice_in_dim(wo, k * z.full_width, z.full_width)
    wo_r = wo[z.main :]
    return x_all, wf, wr, wo_f, wo_r


def heads_of(v, h):
    return v.reshape(v.shape[0], -1, h).transpose(1, 0, 2)


def attend(z, q, k, v, qpos, kpos, length):
    s = jnp.einsum("hqd,hkd->hkq", heads_of(q, z.head), heads_of(k, z.head), preferred_element_type=F32)
    s = s * (z.head ** -0.5)
    seen = (kpos[:, None] <= qpos[None, :]) & (kpos[:, None] < length)
    s = jnp.where(seen[None], s, -1e30)
    e = jnp.exp(s - jnp.max(s, axis=1, keepdims=True))
    p = (e / jnp.sum(e, axis=1, keepdims=True)).astype(BF16)
    o = jnp.einsum("hkq,hkd->qhd", p, heads_of(v, z.head), preferred_element_type=F32)
    return p, o.reshape(q.shape).astype(BF16)


def stage_b(z, x_all, wf, wr, gain, shift, bq_f, bq_r, bv_f, bv_r, pos, length):
    i = lax.axis_index("ctx")
    n1 = (norm_stats(x_all.astype(F32))[0] * gain + shift).astype(BF16)
    mine = lax.dynamic_slice_in_dim(n1, i * z.rows, z.rows)
    qpos = lax.dynamic_slice_in_dim(pos, i * z.rows, z.rows)
    out = dict(n1=n1)
    if z.full:
        q = (dot(n1, wf[0], 1, 0) + bq_f).astype(BF16)
        k = dot(n1, wf[1], 1, 0).astype(BF16)
        v = (dot(n1, wf[2], 1, 0) + bv_f).astype(BF16)
        p, o = attend(z, q, k, v, pos, pos, length)
        out.update(q_f=q, k_f=k, v_f=v, p_f=p, o_f=o)
    if z.rest:
        q = (dot(mine, wr[0], 1, 0) + bq_r).astype(BF16)
        k = dot(n1, wr[1], 1, 0).astype(BF16)
        v = (dot(n1, wr[2], 1, 0) + bv_r).astype(BF16)
        p, o = attend(z, q, k, v, qpos, pos, length)
        out.update(q_r=q, k_r=k, v_r=v, p_r=p, o_r=o)
    return out


def stage_c(z, b, wo_f, wo_r, x, upstream, ua, live, up_t, down, prm):
    branch = prm["b_o"]
    if z.full:
        part = dot(b["o_f"], wo_f, 1, 0).astype(BF16)
        branch = branch + lax.psum_scatter(part.astype(F32), "ctx", scatter_dimension=0, tiled=True)
    if z.rest:
        branch = branch + dot(b["o_r"], wo_r, 1, 0)
    hidden = x.astype(F32) + branch
    xhat, rstd = norm_stats(hidden)
    n2 = (xhat * prm["gain2"] + prm["shift2"]).astype(BF16)
    n2a = lax.all_gather(n2, "seq", axis=0, tiled=True)
    pre = dot(n2a, up_t, 1, 1) + prm["b_up"]
    cdf = 0.5 * (1.0 + lax.erf(pre * (0.5 ** 0.5)))
    act = (pre * cdf).astype(BF16)
    dgelu = cdf + pre * jnp.exp(-0.5 * pre * pre) * (1.0 / math.sqrt(2.0 * math.pi))
    gact = dot(ua, down, 1, 1)
    gpre = (gact * dgelu).astype(BF16)
    gn2p = dot(gpre, up_t, 1, 0).astype(BF16)
    gn2 = lax.psum_scatter(gn2p.astype(F32), "seq", scatter_dimension=0, tiled=True)
    ffp = dot(act, down, 1, 0).astype(BF16)
    ff = lax.psum_scatter(ffp.astype(F32), "seq", scatter_dimension=0, tiled=True)
    output = (live * (hidden + ff + prm["b_down"])).astype(BF16)
    g_up_t = dot(gpre, n2a, 0, 0).astype(BF16)
    g_down = dot(act, ua, 0, 0).astype(BF16)
    gh = upstream.astype(F32) + norm_back(gn2, xhat, rstd, prm["gain2"])
    gb = gh.astype(BF16)
    small = dict(gain2=rows_sum(gn2 * xhat), shift2=rows_sum(gn2), b_o=rows_sum(gb),
                 b_down=rows_sum(upstream), b_up=rows_sum(gpre))
    return output, gh, gb, g_up_t, g_down, small


def attend_back(z, q, k, v, p, go):
    gp = jnp.einsum("hqd,hkd->hkq", heads_of(go, z.head), heads_of(v, z.head), preferred_element_type=F32)
    pf = p.astype(F32)
    delta = jnp.sum(gp * pf, axis=1, keepdims=True)
    gs = (pf * (gp - delta)).astype(BF16)
    sc = z.head ** -0.5
    gq = jnp.einsum("hkq,hkd->qhd", gs, heads_of(k, z.head), preferred_element_type=F32) * sc
    gk = jnp.einsum("hkq,hqd->khd", gs, heads_of(q, z.head), preferred_element_type=F32) * sc
    gv = jnp.einsum("hkq,hqd->khd", p, heads_of(go, z.head), preferred_element_type=F32)
    return gq.reshape(q.shape).astype(BF16), gk.reshape(k.shape).astype(BF16), gv.reshape(v.shape).astype(BF16)


def stage_d(z, b, gb, gba, wo_f, wo_r):
    i = lax.axis_index("ctx")
    n1 = b["n1"]
    mine = lax.dynamic_slice_in_dim(n1, i * z.rows, z.rows)
    out = {}
    if z.full:
        go = dot(gba, wo_f, 1, 1).astype(BF16)
        gq, gk, gv = attend_back(z, b["q_f"], b["k_f"], b["v_f"], b["p_f"], go)
        out.update(gq_f=gq, gk_f=gk, gv_f=gv, gwo_f=dot(b["o_f"], gba, 0, 0))
        out["gw_f"] = jnp.stack([dot(n1, g, 0, 0) for g in (gq, gk, gv)])
    if z.rest:
        go = dot(gb, wo_r, 1, 1).astype(BF16)
        gq, gk, gv = attend_back(z, b["q_r"], b["k_r"], b["v_r"], b["p_r"], go)
        out.update(gq_r=gq, gk_r=gk, gv_r=gv, gwo_r=dot(b["o_r"], gb, 0, 0))
        out["gw_r"] = jnp.stack([dot(mine, gq, 0, 0), dot(n1, gk, 0, 0), dot(n1, gv, 0, 0)])
    return out


def stage_e(z, d, wf, wr, x, gh, gain1, small):
    i, s = lax.axis_index("ctx"), lax.axis_index("seq")
    part = 0.0
    own = 0.0
    if z.full:
        part = part + dot(d["gq_f"], wf[0], 1, 1) + dot(d["gk_f"], wf[1], 1, 1) + dot(d["gv_f"], wf[2], 1, 1)
    if z.rest:
        part = part + dot(d["gk_r"], wr[1], 1, 1) + dot(d["gv_r"], wr[2], 1, 1)
        own = own + dot(d["gq_r"], wr[0], 1, 1)
    gn1 = own + lax.psum_scatter(part.astype(BF16).astype(F32), "ctx", scatter_dimension=0, tiled=True)
    xhat, rstd = norm_stats(x.astype(F32))
    gtok = gh + norm_back(gn1, xhat, rstd, gain1)
    small = dict(small, gain1=rows_sum(gn1 * xhat), shift1=rows_sum(gn1))
    row = jnp.zeros((1, z.width), F32)
    for name, key in (("b_q", "gq"), ("b_v", "gv")):
        r = row
        if z.full:
            r = lax.dynamic_update_slice(r, rows_sum(d[key + "_f"]), (0, i * z.full_width))
        if z.rest:
            r = r.at[:, z.main :].add(rows_sum(d[key + "_r"]))
        small[name] = r
    full = jnp.zeros((4, z.width, z.width), F32)
    if z.full:
        full = lax.dynamic_update_slice(full, d["gw_f"], (0, 0, i * z.full_width))
        full = lax.dynamic_update_slice(full, d["gwo_f"][None], (3, i * z.full_width, 0))
    if z.rest:
        full = full.at[:3, :, z.main :].add(d["gw_r"])
        full = full.at[3, z.main :, :].add(d["gwo_r"])
    gw = lax.psum_scatter(full.reshape(4 * z.width, z.width).astype(BF16), ("seq", "ctx"), scatter_dimension=0, tiled=True)
    b_up_all = lax.all_gather(lax.psum(small.pop("b_up"), "ctx")[0], "seq", axis=0, tiled=True)
    names = list(small)
    tot = lax.psum(jnp.concatenate([small[n] for n in names]), ("seq", "ctx"))
    return gtok, gw.astype(F32), {n: tot[j : j + 1] for j, n in enumerate(names)}, b_up_all


MESH = pl.DeviceIdType.MESH
DMA = pltpu.SemaphoreType.DMA
VMEM_LIMIT = 56 << 20


def rcopy(src, dst, ssem, rsem, **dev):
    return pltpu.make_async_remote_copy(
        src_ref=src, dst_ref=dst, send_sem=ssem, recv_sem=rsem, device_id=dev, device_id_type=MESH
    )


def greet(ctx_peers, seq_peers, wait=True):
    sem = pltpu.get_barrier_semaphore()
    for p in ctx_peers:
        pl.semaphore_signal(sem, inc=1, device_id={"ctx": p}, device_id_type=MESH)
    for p in seq_peers:
        pl.semaphore_signal(sem, inc=1, device_id={"seq": p}, device_id_type=MESH)
    if wait:
        met(len(ctx_peers) + len(seq_peers))


def met(count):
    pl.semaphore_wait(pltpu.get_barrier_semaphore(), count)


class Place:
    def __init__(self, z):
        self.k, self.s = lax.axis_index("ctx"), lax.axis_index("seq")
        self.chips = z.ctx // 2
        self.core = lax.rem(self.k, 2)
        self.chip = self.k // 2
        self.sib = self.k + 1 - 2 * self.core
        self.ring = [lax.rem(self.chip + i, self.chips) for i in range(self.chips)]
        self.same = [2 * q + self.core for q in self.ring]
        self.back = [2 * lax.rem(self.chip + self.chips - i, self.chips) + self.core for i in range(self.chips)]
        self.seqs = [lax.rem(self.s + i, z.seq) for i in range(z.seq)]
        self.seqs_back = [lax.rem(self.s + z.seq - i, z.seq) for i in range(z.seq)]


def call(body, name, outs, ins, scratch, cid, in_spaces, out_spaces, cost=None):
    spaces = {"v": pltpu.VMEM, "a": pl.ANY}
    return pl.pallas_call(
        body,
        name=name,
        out_shape=outs,
        in_specs=[pl.BlockSpec(memory_space=spaces[c]) for c in in_spaces],
        out_specs=[pl.BlockSpec(memory_space=spaces[c]) for c in out_spaces],
        scratch_shapes=scratch,
        compiler_params=pltpu.CompilerParams(
            collective_id=cid, has_side_effects=True, vmem_limit_bytes=VMEM_LIMIT
        ),
        cost_estimate=cost,
    )(*ins)


def sds(shape, dtype=BF16):
    return jax.ShapeDtypeStruct(shape, dtype)


class CtxGather:
    def __init__(self, at, own, dst, sems):
        self.at, self.own, self.dst, self.sems = at, own, dst, sems

    def send(self):
        at, ss, rs = self.at, self.sems[0], self.sems[1]
        for i in range(1, at.chips):
            rcopy(self.own, self.dst.at[at.k], ss.at[i], rs.at[i], ctx=at.same[i]).start()
        rcopy(self.own, self.dst.at[at.k], ss.at[0], rs.at[0], ctx=at.sib).start()
        pltpu.make_async_copy(self.own, self.dst.at[at.k], self.sems[4]).start()

    def forward(self, i):
        at, ss, rs, fs, fr = self.at, *self.sems[:4]
        src = at.back[i]
        rcopy(self.own, self.dst.at[src], ss.at[i], rs.at[i], ctx=at.same[i]).wait_recv()
        rcopy(self.dst.at[src], self.dst.at[src], fs.at[i], fr.at[i], ctx=at.sib).start()

    def finish(self):
        at, ss, rs, fs, fr = self.at, *self.sems[:4]
        pltpu.make_async_copy(self.own, self.dst.at[at.k], self.sems[4]).wait()
        rcopy(self.own, self.dst.at[at.k], ss.at[0], rs.at[0], ctx=at.sib).wait()
        for i in range(1, at.chips):
            rcopy(self.own, self.dst.at[at.k], ss.at[i], rs.at[i], ctx=at.same[i]).wait_send()
            rcopy(self.own, self.dst.at[at.k], fs.at[i], fr.at[i], ctx=at.sib).wait()

    @staticmethod
    def scratch(z):
        n = z.ctx // 2
        return [DMA((n,)), DMA((n,)), DMA((n,)), DMA((n,)), DMA]


def kernel_a(z, x, up, w, wr, pk, xa, ua, wf, wo2, wol, pa, *sems):
    at = Place(z)
    k, s, C = at.k, at.s, z.ctx
    g = CtxGather(at, x, xa, sems[:5])
    mz_s, mz_r, rz_s, rz_r, mx_s, mx_r, us, ur, oz_s, oz_r, ox_s, ox_r, loc, pz_s, pz_r, px_s, px_r = sems[5:]
    others = [lax.rem(k + i, C) for i in range(1, C)]
    greet(others, at.seqs[1:])
    last0 = z.main - (C - 1) * z.shard
    lastrows = w.at[pl.ds(last0, z.rest_width)]

    def cols(j):
        return w.at[:, pl.ds(pl.multiple_of(j * z.full_width, z.full_width), z.full_width)]

    def main(m, j):
        return wf.at[m, j, :, pl.ds(0, z.full_width)]

    def tail(m, j):
        return wf.at[m, j, :, pl.ds(z.full_width, z.full_width)]

    for i in range(1, C):
        rcopy(pk, pa.at[s, k], pz_s.at[i], pz_r.at[i], ctx=others[i - 1]).start()
    pltpu.make_async_copy(pk, pa.at[s, k], loc.at[3]).start()

    @pl.when(s < 3)
    def _():
        for i in range(1, C):
            j = lax.rem(k + i, C)
            rcopy(cols(j), main(s, k), mz_s.at[i], mz_r.at[k], ctx=j).start()
            rcopy(wr, tail(s, k), rz_s.at[i], rz_r.at[k], ctx=j).start()
        pltpu.make_async_copy(cols(k), main(s, k), loc.at[0]).start()
        pltpu.make_async_copy(wr, tail(s, k), loc.at[1]).start()

    @pl.when(s == 3)
    def _():
        @pl.when(k < C - 1)
        def _():
            rcopy(w, wo2.at[0], oz_s.at[0], oz_r.at[0], ctx=lax.rem(k + 1, C)).start()

        @pl.when(k == C - 1)
        def _():
            for i in range(1, C):
                rcopy(lastrows, wol, oz_s.at[i], oz_r.at[1], ctx=lax.rem(k + i, C)).start()
            pltpu.make_async_copy(lastrows, wol, loc.at[1]).start()

        pltpu.make_async_copy(w, wo2.at[1], loc.at[0]).start()
        for i in range(1, 4):
            rcopy(w, wo2.at[1], ox_s.at[0, i], ox_r.at[0], seq=at.seqs[i]).start()

    g.send()
    for i in range(1, z.seq):
        rcopy(up, ua.at[s], us.at[i], ur.at[i], seq=at.seqs[i]).start()
    pltpu.make_async_copy(up, ua.at[s], loc.at[2]).start()

    for i in range(1, C):
        rcopy(pk, pa.at[s, lax.rem(k + C - i, C)], pz_s.at[i], pz_r.at[i], ctx=k).wait_recv()
    pltpu.make_async_copy(pk, pa.at[s, k], loc.at[3]).wait()
    for i in range(1, z.seq):
        rcopy(pa.at[s], pa.at[s], px_s.at[i], px_r.at[i], seq=at.seqs[i]).start()

    @pl.when(s < 3)
    def _():
        for n in range(C):
            src = lax.rem(k + C - n, C)
            if n == 0:
                pltpu.make_async_copy(cols(k), main(s, k), loc.at[0]).wait()
                pltpu.make_async_copy(wr, tail(s, k), loc.at[1]).wait()
            else:
                rcopy(cols(k), main(s, src), mz_s.at[0], mz_r.at[src], ctx=k).wait_recv()
                rcopy(wr, tail(s, src), rz_s.at[0], rz_r.at[src], ctx=k).wait_recv()
            for i in range(1, 4):
                to = at.seqs[i]
                rcopy(wf.at[s, src], wf.at[s, src], mx_s.at[n, i], mx_r.at[s, src], seq=to).start()

    @pl.when(s == 3)
    def _():
        pltpu.make_async_copy(w, wo2.at[1], loc.at[0]).wait()

        @pl.when(k > 0)
        def _():
            rcopy(w, wo2.at[0], oz_s.at[0], oz_r.at[0], ctx=k).wait_recv()
            for i in range(1, 4):
                rcopy(wo2.at[0], wo2.at[0], ox_s.at[1, i], ox_r.at[1], seq=at.seqs[i]).start()

        @pl.when(k < C - 1)
        def _():
            rcopy(lastrows, wol, oz_s.at[1], oz_r.at[1], ctx=k).wait_recv()

        @pl.when(k == C - 1)
        def _():
            pltpu.make_async_copy(lastrows, wol, loc.at[1]).wait()

        for i in range(1, 4):
            rcopy(wol, wol, ox_s.at[2, i], ox_r.at[2], seq=at.seqs[i]).start()

    for i in range(1, at.chips):
        g.forward(i)
    g.finish()
    pltpu.make_async_copy(up, ua.at[s], loc.at[2]).wait()
    for i in range(1, z.seq):
        rcopy(up, ua.at[s], us.at[i], ur.at[i], seq=at.seqs[i]).wait()

    for i in range(1, C):
        rcopy(pk, pa.at[s, k], pz_s.at[i], pz_r.at[i], ctx=k).wait_send()
    for i in range(1, z.seq):
        rcopy(pa.at[s], pa.at[at.seqs_back[i]], px_s.at[i], px_r.at[i], seq=s).wait()

    for m in range(3):
        @pl.when(s != m)
        def _():
            for src in range(C):
                rcopy(wf.at[m, src], wf.at[m, src], mx_s.at[0, 0], mx_r.at[m, src], seq=s).wait_recv()

    @pl.when(s != 3)
    def _():
        rcopy(w, wo2.at[1], ox_s.at[0, 0], ox_r.at[0], seq=s).wait_recv()

        @pl.when(k > 0)
        def _():
            rcopy(w, wo2.at[0], ox_s.at[1, 0], ox_r.at[1], seq=s).wait_recv()

        rcopy(wol, wol, ox_s.at[2, 0], ox_r.at[2], seq=s).wait_recv()

    @pl.when(s < 3)
    def _():
        for i in range(1, C):
            rcopy(cols(k), main(s, k), mz_s.at[i], mz_r.at[k], ctx=k).wait_send()
            rcopy(wr, tail(s, k), rz_s.at[i], rz_r.at[k], ctx=k).wait_send()
        for n in range(C):
            for i in range(1, 4):
                rcopy(wf.at[s, k], wf.at[s, k], mx_s.at[n, i], mx_r.at[s, k], seq=s).wait_send()

    @pl.when(s == 3)
    def _():
        @pl.when(k < C - 1)
        def _():
            rcopy(w, wo2.at[0], oz_s.at[0], oz_r.at[0], ctx=k).wait_send()

        @pl.when(k == C - 1)
        def _():
            for i in range(1, C):
                rcopy(lastrows, wol, oz_s.at[i], oz_r.at[1], ctx=k).wait_send()

        for i in range(1, 4):
            rcopy(w, wo2.at[1], ox_s.at[0, i], ox_r.at[0], seq=s).wait_send()

            @pl.when(k > 0)
            def _():
                rcopy(wo2.at[0], wo2.at[0], ox_s.at[1, i], ox_r.at[1], seq=s).wait_send()

            rcopy(wol, wol, ox_s.at[2, i], ox_r.at[2], seq=s).wait_send()


def stage_a_kernel(z, x, up, w, pk):
    C, k = z.ctx, lax.axis_index("ctx")
    outs = [
        sds((C, z.rows, z.width)), sds((z.seq, z.rows, z.width)), sds((3, C, z.shard, 2 * z.full_width)),
        sds((2, z.shard, z.width)), sds((z.rest_width, z.width)),
        sds((z.seq, C) + pk.shape),
    ]
    scratch = CtxGather.scratch(z) + [
        DMA((C,)), DMA((C,)), DMA((C,)), DMA((C,)), DMA((C, 4)), DMA((3, C)),
        DMA((4,)), DMA((4,)), DMA((C,)), DMA((2,)), DMA((3, 4)), DMA((3,)), DMA((4,)),
        DMA((C,)), DMA((C,)), DMA((z.seq,)), DMA((z.seq,)),
    ]
    wr = jnp.pad(w[:, z.main :], ((0, 0), (0, z.full_width - z.rest_width)))
    xa, ua, wf, wo2, wol, pa = call(
        partial(kernel_a, z), "gather_in", outs, (x, up, w, wr, pk), scratch, 0, "a" * 5, "a" * 6
    )
    wo_f = lax.dynamic_slice_in_dim(
        wo2.reshape(2 * z.shard, z.width), z.shard - (z.shard - z.full_width) * k, z.full_width
    )
    return (
        xa.reshape(z.slot, z.width), ua.reshape(z.seq * z.rows, z.width), wf.reshape(3, z.width, 2 * z.full_width), wo_f, wol, pa,
    )


def matmul(a, b, ca=1, cb=0):
    return lax.dot_general(a, b, (((ca,), (cb,)), ((), ())), preferred_element_type=F32)


def block(z, d):
    return pl.ds(pl.multiple_of(d * z.rows, z.rows), z.rows)


class CtxReduce:
    def __init__(self, at, part, bufs):
        self.at, self.part = at, part
        self.sb, self.sr, self.zb, self.zr, self.ss, self.sn, self.zs, self.zn = bufs

    def sib(self, t):
        return rcopy(self.sb.at[t], self.sr.at[t], self.ss.at[t], self.sn.at[t], ctx=self.at.sib)

    def far(self, t):
        return rcopy(self.zb.at[t], self.zr.at[t], self.zs.at[t], self.zn.at[t], ctx=self.at.same[t])

    def start(self):
        at = self.at
        order = list(range(1, at.chips)) + [0]
        for t in order:
            self.sb[t] = self.part(2 * at.ring[t] + 1 - at.core).astype(BF16)
            self.sib(t).start()
        for t in order[:-1]:
            mine = self.part(at.same[t])
            self.sib(t).wait_recv()
            self.zb[t] = (mine + self.sr[t].astype(F32)).astype(BF16)
            self.far(t).start()

    def finish(self, own=None):
        at = self.at
        total = self.part(at.k) if own is None else own
        self.sib(0).wait_recv()
        total = total + self.sr[0].astype(F32)
        for t in range(1, at.chips):
            self.far(t).wait_recv()
            total = total + self.zr[t].astype(F32)
        return total

    def close(self):
        for t in range(self.at.chips):
            self.sib(t).wait_send()
            if t:
                self.far(t).wait_send()

    @staticmethod
    def scratch(z):
        n = z.ctx // 2
        return [pltpu.VMEM((n, z.rows, z.width), BF16)] * 4 + [DMA((n,))] * 4


NEG = -1e30


def turn(v):
    return jnp.transpose(v.astype(F32)).astype(BF16)


def of_head(v, h, head):
    lane = lax.broadcasted_iota(jnp.int32, v.shape, 1) // head
    return jnp.where(lane == h, v.astype(F32), 0.0)


def attend_block(heads, k, v_t, q, mask, head, p_ref):
    parts = []
    for h in range(heads):
        qh = (of_head(q, h, head) * head ** -0.5).astype(BF16)
        s = matmul(k, qh, 1, 1) + mask
        e = jnp.exp(s - jnp.max(s, axis=0, keepdims=True))
        p = (e * (1.0 / jnp.sum(e, axis=0, keepdims=True))).astype(BF16)
        p_ref[h] = p
        parts.append(matmul(v_t[h * head : (h + 1) * head], p))
    o_t = parts[0] if len(parts) == 1 else jnp.concatenate(parts, axis=0)
    return jnp.transpose(o_t).astype(BF16)


def kernel_bc(z, qb, xa, gain, shift, w, bq, bv, kpos, qpos, wo_f, wo_r, x, b_o, gain2, shift2,
              n1o, qo, ko, vo, p_fo, p_ro, o_fo, o_r, hid, xh, rs_o, n2a,
              n1, q, k, v, p_f, p_r, o_f, vt, vrt, n2, wb, ns, nr, *bufs):
    at = Place(z)
    FW, RW, nq = z.full_width, z.rest_width, z.slot // qb
    greet([at.sib] + at.same[1:], at.seqs[1:], False)

    def rows(j, _):
        r = block(z, j)
        n1[r] = (norm_stats(xa[r].astype(F32))[0] * gain[...] + shift[...]).astype(BF16)
        return 0

    lax.fori_loop(0, z.ctx, rows, 0)
    q[...] = (matmul(n1[...], w[0]) + bq[...]).astype(BF16)
    k[...] = matmul(n1[...], w[1]).astype(BF16)
    v[...] = (matmul(n1[...], w[2]) + bv[...]).astype(BF16)
    backs = [pltpu.make_async_copy(a, b, wb.at[i]) for i, (a, b) in enumerate(((n1, n1o), (q, qo), (k, ko), (v, vo)))]
    for c in backs:
        c.start()
    vt[...] = turn(v[:, 0:FW])
    vrt[...] = turn(v[:, FW : 2 * FW])[0:RW]
    mine = block(z, at.k)

    def steps(j, _):
        r = pl.ds(pl.multiple_of(j * qb, qb), qb)
        mask = jnp.where(kpos[...] <= qpos[:, r], 0.0, NEG)
        o_f[r] = attend_block(z.full, k[:, 0:FW], vt[...], q[r, 0:FW], mask, z.head, p_f.at[j])
        return 0

    lax.fori_loop(0, nq, steps, 0)
    mask = jnp.where(kpos[...] <= qpos[:, mine], 0.0, NEG)
    o_r[...] = attend_block(z.rest, k[:, FW : 2 * FW], vrt[...], q[mine, FW : 2 * FW], mask, z.head, p_r)
    more = [pltpu.make_async_copy(a, b, wb.at[4 + i]) for i, (a, b) in enumerate(((p_f, p_fo), (p_r, p_ro), (o_f, o_fo)))]
    for c in more:
        c.start()
    met(at.chips + z.seq - 1)
    red = CtxReduce(at, lambda d: matmul(o_f[block(z, d)], wo_f[...]), bufs)
    red.start()
    own = matmul(o_r[...], wo_r[...]) + b_o[...] + x[...].astype(F32)
    hidden = red.finish() + own
    xhat, rstd = norm_stats(hidden)
    n2[...] = (xhat * gain2[...] + shift2[...]).astype(BF16)
    copies = [rcopy(n2, n2a.at[at.s], ns.at[i], nr.at[i], seq=at.seqs[i]) for i in (2, 1, 3)]
    for c in copies:
        c.start()
    n2a[at.s] = n2[...]
    hid[...] = hidden
    xh[...] = xhat
    rs_o[...] = jnp.broadcast_to(rstd, rs_o.shape)
    red.close()
    for c in backs + more:
        c.wait()
    for c in copies:
        c.wait()


def stage_bc_kernel(z, x_all, w, gain, shift, bq, bv, pos, length, wo_f, wo_r, x, prm):
    N, D, FW, RW, R, S, qb = z.slot, z.width, z.full_width, z.rest_width, z.rows, z.seq, 256
    nq, W2 = N // qb, 2 * FW
    kpos = jnp.where(pos < length, pos, 1 << 30)[:, None]
    ins = (x_all, gain, shift, w, bq, bv, kpos, pos[None, :], wo_f, wo_r, x, prm["b_o"], prm["gain2"], prm["shift2"])
    names = ("n1", "q", "k", "v", "p_f", "p_r", "o_f", "o_r", "hid", "xh", "rs", "n2a")
    big = [(N, D), (N, W2), (N, W2), (N, W2), (nq, z.full, N, qb), (z.rest, N, R), (N, FW)]
    outs = [sds(s) for s in big] + [sds((R, RW)), sds((R, D), F32), sds((R, D), F32), sds((R, 128), F32), sds((S, R, D))]
    V = pltpu.VMEM
    scratch = [V(s, BF16) for s in big] + [V((FW, N), BF16), V((RW, N), BF16), V((R, D), BF16), DMA((7,)), DMA((S,)), DMA((S,))]
    out = call(partial(kernel_bc, z, qb), "attention", outs, ins, scratch + CtxReduce.scratch(z), 1, "v" * 14, "a" * 7 + "v" * 5)
    return dict(zip(names, out))


def ff_block(z, j):
    return pl.ds(pl.multiple_of(j * z.shard, 8), z.shard)


def kernel_f(z, n2h, uah, uph, dnh, b_up, hid, xh, rs_i, gain2, b_down, live, out, gh_o, gb_o, sm, bu, gba, ffr,
             n2, ua, up_t, down, act, gpre, gsend, grecv, fsend, frecv, g32, fs, fr, ld, gs, gr, cs, cr, ps, pr, wb, *gsem):
    at = Place(z)
    S, R, D, C = z.seq, z.rows, z.width, z.ctx
    units, step = up_t.shape[0], 256
    greet([at.sib] + at.same[1:], at.seqs[1:], False)
    chunks = [slice(c0, min(c0 + step, units)) for c0 in range(0, units, step)]
    loads = [pltpu.make_async_copy(n2h, n2, ld.at[0]), pltpu.make_async_copy(uah, ua, ld.at[1])]
    for i, c in enumerate(chunks):
        loads.append(pltpu.make_async_copy(uph.at[c], up_t.at[c], ld.at[2 + 2 * i]))
        loads.append(pltpu.make_async_copy(dnh.at[c], down.at[c], ld.at[3 + 2 * i]))
    for c in loads:
        c.start()
    loads[0].wait()
    loads[1].wait()
    for i, c in enumerate(chunks):
        loads[2 + 2 * i].wait()
        pre = matmul(n2[...], up_t[c], 1, 1) + b_up[:, c]
        loads[3 + 2 * i].wait()
        gact = matmul(ua[...], down[c], 1, 1)
        cdf = 0.5 * (1.0 + lax.erf(pre * (0.5 ** 0.5)))
        act[:, c] = (pre * cdf).astype(BF16)
        dgelu = cdf + pre * jnp.exp(-0.5 * pre * pre) * (1.0 / math.sqrt(2.0 * math.pi))
        g = (gact * dgelu).astype(BF16)
        gpre[:, c] = g
        bu[:, c] = jnp.sum(g.astype(F32), axis=0, keepdims=True)
    met(at.chips + S - 1)

    def gcopy(i):
        return rcopy(gsend.at[i], grecv.at[i], gs.at[i], gr.at[i], seq=at.seqs[i])

    def fcopy(i):
        return rcopy(fsend.at[i], frecv.at[i], cs.at[i], cr.at[i], seq=at.seqs[i])

    def pair(t, u):
        return rcopy(fs.at[t, u], fr.at[t, u], ps.at[t, u], pr.at[t, u], ctx=at.sib)

    def weight_grad(u, left, right):
        for c in chunks:
            g32[u, c] = matmul(left[:, c], right[...], 0, 0)
        for t in range(4):
            fs[t, u] = g32[u, ff_block(z, 2 * at.ring[t] + 1 - at.core)].astype(BF16)
            pair(t, u).start()

    def both(u):
        for t in range(4):
            pair(t, u).wait_recv()
            fr[t, u] = (g32[u, ff_block(z, at.same[t])] + fr[t, u].astype(F32)).astype(BF16)
            pltpu.make_async_copy(fr.at[t, u], ffr.at[t, u], wb.at[t, u]).start()

    for i in (2, 1, 3):
        gsend[i] = matmul(gpre[block(z, at.seqs[i])], up_t[...]).astype(BF16)
        gcopy(i).start()
    mine = block(z, at.s)
    gn2 = matmul(gpre[mine], up_t[...])
    weight_grad(0, gpre, n2)
    for i in range(1, S):
        gcopy(i).wait_recv()
        gn2 = gn2 + grecv[i].astype(F32)
    xhat = xh[...]
    up_own = ua[mine].astype(F32)
    gh = up_own + norm_back(gn2, xhat, rs_i[:, :1], gain2[...])
    gb_o[...] = gh.astype(BF16)
    gat = CtxGather(at, gb_o, gba, gsem)
    gat.send()
    gh_o[...] = gh
    sm[0:1] = jnp.sum(gn2 * xhat, axis=0, keepdims=True)
    sm[1:2] = jnp.sum(gn2, axis=0, keepdims=True)
    sm[2:3] = jnp.sum(gb_o[...].astype(F32), axis=0, keepdims=True)
    sm[3:4] = jnp.sum(up_own, axis=0, keepdims=True)
    for i in (2, 1, 3):
        fsend[i] = matmul(act[block(z, at.seqs[i])], down[...]).astype(BF16)
        fcopy(i).start()
    ff = matmul(act[mine], down[...])
    weight_grad(1, act, ua)
    both(0)
    for i in (1, 3):
        gat.forward(i)
    both(1)
    for i in range(1, S):
        fcopy(i).wait_recv()
        ff = ff + frecv[i].astype(F32)
    out[...] = (live[:, :1] * (hid[...] + ff + b_down[...])).astype(BF16)
    gat.forward(2)
    gat.finish()
    for t in range(4):
        for u in range(2):
            pair(t, u).wait_send()
            pltpu.make_async_copy(fr.at[t, u], ffr.at[t, u], wb.at[t, u]).wait()
    for i in range(1, S):
        gcopy(i).wait_send()
        fcopy(i).wait_send()


def stage_f_kernel(z, n2a, ua, up_t, down, prm, hid, xh, rs, live):
    R, D, S, U, C, SH = z.rows, z.width, z.seq, up_t.shape[0], z.ctx, z.shard
    outs = [sds((R, D)), sds((R, D), F32), sds((R, D)), sds((4, D), F32), sds((1, U), F32), sds((C, R, D)), sds((4, 2, SH, D))]
    V = pltpu.VMEM
    scratch = [
        V((S * R, D), BF16), V((S * R, D), BF16), V((U, D), BF16), V((U, D), BF16), V((S * R, U), BF16), V((S * R, U), BF16),
        *[V((S, R, D), BF16) for _ in range(4)], V((2, U, D), F32), V((4, 2, SH, D), BF16), V((4, 2, SH, D), BF16),
        DMA((2 + 2 * -(-U // 256),)), *[DMA((S,)) for _ in range(4)], DMA((4, 2)), DMA((4, 2)), DMA((4, 2)),
        *CtxGather.scratch(z),
    ]
    return call(
        partial(kernel_f, z), "feed_forward", outs,
        (n2a.reshape(S * R, D), ua, up_t, down, prm["b_up"], hid, xh, rs, prm["gain2"], prm["b_down"],
         jnp.broadcast_to(live, (R, 128))), scratch, 2, "aaaa" + "v" * 7, "v" * 5 + "aa",
    )


class SmallSum:
    def __init__(self, at, buf, rsib, rchip, rseq, sems):
        self.at, self.buf, self.rsib, self.rchip, self.rseq = at, buf, rsib, rchip, rseq
        self.s0, self.r0, self.s1, self.r1, self.s2, self.r2 = sems

    def sib(self):
        return rcopy(self.buf.at[0], self.rsib, self.s0, self.r0, ctx=self.at.sib)

    def chip(self, i):
        return rcopy(self.buf.at[1], self.rchip.at[i], self.s1.at[i], self.r1.at[i], ctx=self.at.same[i])

    def line(self, i):
        return rcopy(self.buf.at[2], self.rseq.at[i], self.s2.at[i], self.r2.at[i], seq=self.at.seqs[i])

    def first(self, value):
        self.buf[0] = value
        self.sib().start()

    def second(self):
        self.sib().wait_recv()
        self.buf[1] = self.buf[0] + self.rsib[...]
        for i in range(1, self.at.chips):
            self.chip(i).start()

    def third(self):
        total = self.buf[1]
        for i in range(1, self.at.chips):
            self.chip(i).wait_recv()
            total = total + self.rchip[i]
        self.buf[2] = total
        for i in range(1, len(self.at.seqs)):
            self.line(i).start()

    def last(self):
        total = self.buf[2]
        for i in range(1, len(self.at.seqs)):
            self.line(i).wait_recv()
            total = total + self.rseq[i]
        return total

    def close(self):
        self.sib().wait_send()
        for i in range(1, self.at.chips):
            self.chip(i).wait_send()
        for i in range(1, len(self.at.seqs)):
            self.line(i).wait_send()

    @staticmethod
    def scratch(z, rows):
        n, shape = z.ctx // 2, (rows, z.width)
        return [
            pltpu.VMEM((3,) + shape, F32), pltpu.VMEM(shape, F32), pltpu.VMEM((n,) + shape, F32),
            pltpu.VMEM((z.seq,) + shape, F32), DMA, DMA, DMA((n,)), DMA((n,)), DMA((z.seq,)), DMA((z.seq,)),
        ]


def attend_block_back(heads, k_t, v, q, go, p_ref, head, gk, gv):
    parts = []
    for h in range(heads):
        goh = of_head(go, h, head).astype(BF16)
        p = p_ref[h]
        pf = p.astype(F32)
        gp = matmul(v, goh, 1, 1)
        delta = jnp.sum(gp * pf, axis=0, keepdims=True)
        gs = (pf * (gp - delta)).astype(BF16)
        gk[...] += matmul(gs, of_head(q, h, head).astype(BF16))
        gv[...] += matmul(p, goh)
        parts.append(matmul(k_t[h * head : (h + 1) * head], gs))
    g_t = parts[0] if len(parts) == 1 else jnp.concatenate(parts, axis=0)
    return (jnp.transpose(g_t) * head ** -0.5).astype(BF16)


def kernel_de(z, qb, gbah, kh, oh, vh, qh, pfh, prh, wh, n1h, xah, ffr,
              wo_f, wo_r, o_r, x, gh, gain1, sm4, bu,
              gtok, ga, gud, tot, bup,
              gba, k, o_f, v, q, p_f, p_r, w, n1, xa, ld,
              go, kt, krt, gk, gv, gkr, gvr, gcat, gw, gwo, gwor, sums, ffz, ffo, fz_s, fz_r, fo,
              rf, ro, ror, sf_s, sf_r, so_s, so_r, sor_s, sor_r,
              zs, zr, land, landr, zs_s, zs_r, zr_s, zr_r,
              buf32, obs, obn, orrs, orr, ob_s, ob_r, orr_s, orr_r, *rest):
    at = Place(z)
    s, me, C, S, FW, RW, SH, D = at.s, at.k, z.ctx, z.seq, z.full_width, z.rest_width, z.shard, z.width
    bufs, small = rest[:8], rest[8:]
    scale, top = z.head ** -0.5, TOP(z)
    mine = block(z, me)
    greet([lax.rem(me + i, C) for i in range(1, C)], at.seqs[1:], False)
    pairs = ((gbah, gba), (kh, k), (oh, o_f), (vh, v), (qh, q), (pfh, p_f), (prh, p_r), (wh, w), (n1h, n1), (xah, xa))
    loads = [pltpu.make_async_copy(a, b, ld.at[i]) for i, (a, b) in enumerate(pairs)]
    for c in loads:
        c.start()
    ownff = pltpu.make_async_copy(ffr.at[0], ffo, fo)
    ownff.start()
    met(C + S - 2)

    def fz(t):
        return rcopy(ffr.at[t], ffz.at[t], fz_s.at[t], fz_r.at[t], ctx=at.same[t])

    for t in (2, 1, 3):
        fz(t).start()

    gk[...] = jnp.zeros_like(gk)
    gv[...] = jnp.zeros_like(gv)
    gkr[...] = jnp.zeros_like(gkr)
    gvr[...] = jnp.zeros_like(gvr)
    gcat[0, :, FW:] = jnp.zeros((z.slot, FW), BF16)
    for c in loads[:3]:
        c.wait()
    go[...] = matmul(gba[...], wo_f[...], 1, 1).astype(BF16)
    kt[...] = turn(k[:, 0:FW])
    krt[...] = turn(k[:, FW : 2 * FW])[0:RW]
    gwo[...] = matmul(o_f[...], gba[...], 0, 0).astype(BF16)
    gwor[...] = matmul(o_r[...], gba[mine], 0, 0).astype(BF16)

    def up(ref, dst, ssem, rsem, i, m=None):
        return rcopy(ref if m is None else ref.at[m], dst.at[i], ssem.at[i], rsem.at[i], seq=at.seqs[i])

    for i in range(1, S):
        @pl.when(at.seqs[i] == 3)
        def _():
            up(gwo, ro, so_s, so_r, i).start()
            up(gwor, ror, sor_s, sor_r, i).start()

    for c in loads[3:6]:
        c.wait()

    def steps(j, _):
        r = pl.ds(pl.multiple_of(j * qb, qb), qb)
        gcat[0, r, 0:FW] = attend_block_back(z.full, kt[...], v[:, 0:FW], q[r, 0:FW], go[r], p_f.at[j], z.head, gk, gv)
        return 0

    lax.fori_loop(0, z.slot // qb, steps, 0)
    loads[6].wait()
    gor = matmul(gba[mine], wo_r[...], 1, 1).astype(BF16)
    gor = jnp.concatenate([gor, jnp.zeros((z.rows, FW - RW), BF16)], axis=1)
    gcat[0, mine, FW : FW + RW] = attend_block_back(
        z.rest, krt[...], v[:, FW : 2 * FW], q[mine, FW : 2 * FW], gor, p_r, z.head, gkr, gvr)
    gcat[1, :, 0:FW] = (gk[...] * scale).astype(BF16)
    gcat[1, :, FW:] = (gkr[...] * scale).astype(BF16)
    gcat[2, :, 0:FW] = gv[...].astype(BF16)
    gcat[2, :, FW:] = gvr[...].astype(BF16)
    for c in loads[7:10]:
        c.wait()

    sums[...] = jnp.zeros_like(sums)

    def part(d):
        r = block(z, d)
        total = matmul(gcat[0, r], w[0], 1, 1) + matmul(gcat[1, r], w[1], 1, 1) + matmul(gcat[2, r], w[2], 1, 1)
        sums[8:9] += jnp.sum(total * norm_stats(xa[r].astype(F32))[0], axis=0, keepdims=True)
        sums[9:10] += jnp.sum(total, axis=0, keepdims=True)
        return total

    red = CtxReduce(at, part, bufs)
    red.start()
    own = part(me)

    def cols(m):
        a = jnp.sum(gcat[m].astype(F32), axis=0, keepdims=True)
        return jnp.concatenate([jnp.where(me == c, a[:, 0:FW], 0.0) for c in range(C)] + [a[:, FW : FW + RW]], axis=1)

    sums[0:4] = sm4[...]
    sums[4:5] = cols(0)
    sums[5:6] = cols(2)
    sums[6:7] = bu[...]
    se = SmallSum(at, *small[:4], small[4:])
    se.first(sums[...])

    for m in range(3):
        gw[m] = matmul(n1[...], gcat[m], 0, 0).astype(BF16).reshape(C, SH, 2 * FW)
    for i in range(1, S):
        m = at.seqs[i]

        @pl.when(m < 3)
        def _():
            up(gw, rf, sf_s, sf_r, i, m).start()

    se.second()

    def zf(i):
        return rcopy(zs.at[lax.rem(me + i, C)], land.at[i], zs_s.at[i], zs_r.at[i], ctx=lax.rem(me + i, C))

    def zrr(i):
        return rcopy(zr.at[lax.rem(me + i, C)], landr.at[i], zr_s.at[i], zr_r.at[i], ctx=lax.rem(me + i, C))

    def shift():
        return rcopy(obs, obn, ob_s, ob_r, ctx=lax.rem(me + C - 1, C))

    def tail(i):
        return rcopy(orrs, orr.at[i], orr_s, orr_r.at[i], ctx=C - 1)

    @pl.when(s < 3)
    def _():
        for i in range(1, S):
            up(gw, rf, sf_s, sf_r, i, 0).wait_recv()

        def add(j, _):
            t = gw[s, j].astype(F32)
            for i in range(1, S):
                t = t + rf[i, j].astype(F32)
            zs[j] = t[:, 0:FW].astype(BF16)
            u = t[:, FW : FW + RW]
            zr[j] = jnp.concatenate([u[:top], jnp.concatenate([u[top:], jnp.zeros((2 * top - SH, RW), F32)], axis=0)], axis=1).astype(BF16)
            return 0

        lax.fori_loop(0, C, add, 0)
        for i in range(1, C):
            zf(i).start()
            zrr(i).start()

    @pl.when(s == 3)
    def _():
        for i in range(1, S):
            up(gwo, ro, so_s, so_r, i).wait_recv()
            up(gwor, ror, sor_s, sor_r, i).wait_recv()
        t, u = gwo[...].astype(F32), gwor[...].astype(F32)
        for i in range(1, S):
            t = t + ro[i].astype(F32)
            u = u + ror[i].astype(F32)
        buf32[pl.ds(0, FW)] = t
        obs[...] = t.astype(BF16)
        orrs[...] = u.astype(BF16)

        @pl.when(me > 0)
        def _():
            shift().start()

        for i in range(C - 1):
            @pl.when(me == i)
            def _():
                tail(i).start()

    se.third()

    ownff.wait()
    for t in (1, 3, 2):
        fz(t).wait_recv()
    for u in range(2):
        total = ffo[u].astype(F32)
        for t in (1, 3, 2):
            total = total + ffz[t, u].astype(F32)
        gud[u] = total

    xhat, rstd = norm_stats(x[...].astype(F32))
    gn1 = red.finish(own)
    gtok[...] = gh[...] + norm_back(gn1, xhat, rstd, gain1[...])

    @pl.when(s < 3)
    def _():
        ga[:, pl.ds(pl.multiple_of(me * FW, FW), FW)] = zs[me].astype(F32)
        remain = zr[me].astype(F32)
        for i in range(1, C):
            zf(i).wait_recv()
            zrr(i).wait_recv()
            j = lax.rem(me + C - i, C)
            ga[:, pl.ds(pl.multiple_of(j * FW, FW), FW)] = land[i].astype(F32)
            remain = remain + landr[i].astype(F32)
        ga[0:top, z.main :] = remain[:, 0:RW]
        ga[top:SH, z.main :] = remain[0 : SH - top, RW : 2 * RW]
        for i in range(1, C):
            zf(i).wait_send()
            zrr(i).wait_send()

    @pl.when(s == 3)
    def _():
        @pl.when(me < C - 1)
        def _():
            shift().wait_recv()
            buf32[pl.ds(FW, FW)] = obn[...].astype(F32)

        @pl.when(me == C - 1)
        def _():
            u = orrs[...].astype(F32)
            for i in range(C - 1):
                tail(i).wait_recv()
                u = u + orr[i].astype(F32)
            buf32[pl.ds(FW, RW)] = u

        ga[...] = buf32[pl.ds(pl.multiple_of((SH - FW) * me, 8), SH)]

        @pl.when(me > 0)
        def _():
            shift().wait_send()

        @pl.when(me < C - 1)
        def _():
            tail(0).wait_send()

    tot[...] = se.last()
    bup[s] = se.buf[2, 6:7]
    for i in range(1, S):
        bup[at.seqs_back[i]] = se.rseq[i, 6:7]
    red.close()
    se.close()
    for t in (1, 2, 3):
        fz(t).wait_send()
    for i in range(1, S):
        m = at.seqs[i]

        @pl.when(m < 3)
        def _():
            up(gw, rf, sf_s, sf_r, i, m).wait_send()

        @pl.when(m == 3)
        def _():
            up(gwo, ro, so_s, so_r, i).wait_send()
            up(gwor, ror, sor_s, sor_r, i).wait_send()


def TOP(z):
    return -(-z.shard // 16) * 8


def stage_de_kernel(z, b, gba, ffr, wo_f, wo_r, w, x_all, x, gh, gain1, sm4, bu):
    C, S, D, FW, RW, SH, N, R, qb = z.ctx, z.seq, z.width, z.full_width, z.rest_width, z.shard, z.slot, z.rows, 256
    nq, W2, top = N // qb, 2 * FW, TOP(z)
    outs = [sds((R, D), F32), sds((SH, D), F32), sds((2, SH, D), F32), sds((10, D), F32), sds((S, 1, D), F32)]
    V = pltpu.VMEM
    scratch = [
        V((N, D), BF16), V((N, W2), BF16), V((N, FW), BF16), V((N, W2), BF16), V((N, W2), BF16), V((nq, z.full, N, qb), BF16),
        V((z.rest, N, R), BF16), V((3, D, W2), BF16), V((N, D), BF16), V((N, D), BF16), DMA((10,)),
        V((N, FW), BF16), V((FW, N), BF16), V((RW, N), BF16), *[V((N, FW), F32) for _ in range(4)],
        V((3, N, W2), BF16), V((3, C, SH, W2), BF16), V((FW, D), BF16), V((RW, D), BF16), V((10, D), F32),
        V((4, 2, SH, D), BF16), V((2, SH, D), BF16), DMA((4,)), DMA((4,)), DMA,
        V((S, C, SH, W2), BF16), V((S, FW, D), BF16), V((S, RW, D), BF16), *[DMA((S,)) for _ in range(6)],
        V((C, SH, FW), BF16), V((C, top, 2 * RW), BF16), V((C, SH, FW), BF16), V((C, top, 2 * RW), BF16),
        *[DMA((C,)) for _ in range(4)],
        V((2 * FW, D), F32), V((FW, D), BF16), V((FW, D), BF16), V((RW, D), BF16), V((C, RW, D), BF16),
        DMA, DMA, DMA, DMA((C,)),
        *CtxReduce.scratch(z), *SmallSum.scratch(z, 10),
    ]
    gtok, ga, gud, tot, bup = call(
        partial(kernel_de, z, qb), "attention_back", outs,
        (gba, b["k"], b["o_f"], b["v"], b["q"], b["p_f"], b["p_r"], w, b["n1"], x_all, ffr,
         wo_f, wo_r, b["o_r"], x, gh, gain1, sm4, bu),
        scratch, 4, "a" * 11 + "v" * 8, "v" * 5,
    )
    names = ("gain2", "shift2", "b_o", "b_down", "b_q", "b_v", None, None, "gain1", "shift1")
    return gtok, ga, gud, {n: tot[j : j + 1] for j, n in enumerate(names) if n}, bup.reshape(-1)


def shards(tokens, lengths, block_order, attention_weights, up_weights, down_weights, norm_gains, biases, cotangent):
    z = Sizes(tokens.shape[1], tokens.shape[2], block_order.shape[0])
    i, s = lax.axis_index("ctx"), lax.axis_index("seq")
    D = z.width
    x, cot = tokens[0], cotangent[0]
    length = lengths[0]
    pos = (block_order[:, None] * z.block_len + jnp.arange(z.block_len, dtype=jnp.int32)[None, :]).reshape(z.slot)
    my_pos = lax.dynamic_slice_in_dim(pos, i * z.rows, z.rows)
    live = (my_pos < length).astype(F32)[:, None]
    n_g, n_b = norm_gains.shape[0], biases.shape[0]
    lanes = -(-(n_g + n_b) // 1024) * 8
    packed = jnp.pad(jnp.concatenate([norm_gains, biases]), (0, lanes * 128 - n_g - n_b)).reshape(lanes, 128)
    upstream = (live * cot.astype(F32)).astype(BF16)
    fast = z.ctx == 8 and z.seq == 4 and 0 < z.width - z.main <= z.shard and z.ctx * up_weights.shape[1] == z.width and z.slot * D * 2 <= (4 << 20)
    if fast:
        x_all, ua, w3, wo_f, wo_r, both = stage_a_kernel(z, x, upstream, attention_weights, packed)
    else:
        x_all, wf, wr, wo_f, wo_r = stage_a(z, x, attention_weights)
        ua = lax.all_gather(upstream, "seq", axis=0, tiled=True)
        both = lax.all_gather(packed, ("seq", "ctx"), axis=0)
    both = both.reshape(z.seq * z.ctx, lanes * 128)
    gains = both[:, :n_g].reshape(-1).astype(F32)
    bias = both[:, n_g : n_g + n_b].reshape(-1).astype(F32)
    row = lambda v: v[None, :]
    piece = [row(bias[j * D : (j + 1) * D]) for j in range(6)]
    gain1, gain2 = row(gains[:D]), row(gains[D:])
    b_up = row(lax.dynamic_slice_in_dim(bias[6 * D :], s * (z.ctx * up_weights.shape[1]), z.ctx * up_weights.shape[1]))
    prm = dict(gain2=gain2, shift2=piece[4], b_o=piece[3], b_down=piece[5], b_up=b_up)
    fslice = lambda v: lax.dynamic_slice(v, (0, i * z.full_width), (1, z.full_width))
    up_t = lax.all_gather(up_weights.T, "ctx", axis=0, tiled=True)
    down = lax.all_gather(down_weights, "ctx", axis=0, tiled=True)

    if fast:
        wide = lambda v: jnp.concatenate([fslice(v), v[:, z.main :], jnp.zeros((1, z.full_width - z.rest_width), F32)], axis=1)
        b = stage_bc_kernel(z, x_all, w3, gain1, piece[0], wide(piece[1]), wide(piece[2]), pos, length, wo_f, wo_r, x, prm)
        output, gh, gb, sm4, bu, gba, ffr = stage_f_kernel(z, b["n2a"], ua, up_t, down, prm, b["hid"], b["xh"], b["rs"], live)
        gtok, gw, gud, tot, b_up_all = stage_de_kernel(
            z, b, gba.reshape(z.slot, D), ffr, wo_f, wo_r, w3, x_all, x, gh, gain1, sm4, bu)
        g_up_own, g_down_own = gud[0].T, gud[1]
    else:
        b = stage_b(z, x_all, wf, wr, gain1, piece[0], fslice(piece[1]), piece[1][:, z.main :],
                    fslice(piece[2]), piece[2][:, z.main :], pos, length)
        output, gh, gb, g_up_t, g_down, small = stage_c(z, b, wo_f, wo_r, x, upstream, ua, live, up_t, down, prm)
        g_up_own = lax.psum_scatter(g_up_t, "ctx", scatter_dimension=0, tiled=True).astype(F32).T
        g_down_own = lax.psum_scatter(g_down, "ctx", scatter_dimension=0, tiled=True).astype(F32)
        gba = lax.all_gather(gb, "ctx", axis=0, tiled=True) if z.full else None
        d = stage_d(z, b, gb, gba, wo_f, wo_r)
        gtok, gw, tot, b_up_all = stage_e(z, d, wf, wr, x, gh, gain1, small)
    me = s * z.ctx + i
    g_gain = lax.dynamic_slice_in_dim(jnp.concatenate([tot["gain1"][0], tot["gain2"][0]]), me * n_g, n_g)
    g_bias = lax.dynamic_slice_in_dim(jnp.concatenate([tot[n][0] for n in ("shift1", "b_q", "b_v", "b_o", "shift2", "b_down")] + [b_up_all]), me * n_b, n_b)
    return output[None], gtok[None], gw, g_up_own, g_down_own, g_gain, g_bias


def solution(mesh):
    in_specs = (
        P("seq", "ctx", None), P("seq"), P(), P(("seq", "ctx"), None), P(None, ("seq", "ctx")),
        P(("seq", "ctx"), None), P(("seq", "ctx")), P(("seq", "ctx")), P("seq", "ctx", None),
    )
    out_specs = (
        P("seq", "ctx", None), P("seq", "ctx", None), P(("seq", "ctx"), None), P(None, ("seq", "ctx")),
        P(("seq", "ctx"), None), P(("seq", "ctx")), P(("seq", "ctx")),
    )
    return jax.shard_map(shards, mesh=mesh, in_specs=in_specs, out_specs=out_specs, check_vma=False)
```

```python
import math
from functools import partial

import jax
import jax.numpy as jnp
from jax import lax
from jax.experimental import pallas as pl
from jax.experimental.pallas import tpu as pltpu
from jax.sharding import PartitionSpec as P

HEADS = 17
EPS = 1e-05
F32 = jnp.float32
BF16 = jnp.bfloat16


def norm_stats(values):
    centre = values - jnp.mean(values, axis=-1, keepdims=True)
    rstd = lax.rsqrt(jnp.mean(centre * centre, axis=-1, keepdims=True) + EPS)
    return centre * rstd, rstd


def norm_back(grad, xhat, rstd, gain):
    e = grad * gain
    mean_e = jnp.mean(e, axis=-1, keepdims=True)
    mean_ex = jnp.mean(e * xhat, axis=-1, keepdims=True)
    return (e - mean_e - xhat * mean_ex) * rstd


def dot(a, b, ca, cb):
    return lax.dot_general(a, b, (((ca,), (cb,)), ((), ())), preferred_element_type=F32)


def rows_sum(v):
    return jnp.sum(v.astype(F32), axis=0, keepdims=True)


class Sizes:
    def __init__(self, rows, width, block_count):
        self.rows, self.width = rows, width
        self.ctx, self.seq = lax.axis_size("ctx"), lax.axis_size("seq")
        self.slot = rows * self.ctx
        self.block_len = self.slot // block_count
        self.head = width // HEADS
        self.full = HEADS // self.ctx
        self.full_width = self.full * self.head
        self.main = self.full_width * self.ctx
        self.rest = HEADS - self.full * self.ctx
        self.rest_width = self.rest * self.head
        self.shard = width // self.ctx


def stage_a(z, x, w):
    k = lax.axis_index("ctx")
    x_all = lax.all_gather(x, "ctx", axis=0, tiled=True)
    w_all = lax.all_gather(w, "seq", axis=0)
    wm = w_all[:3, :, : z.main].reshape(3, z.shard, z.ctx, z.full_width)
    wf = lax.all_to_all(wm, "ctx", split_axis=2, concat_axis=1, tiled=True).reshape(
        3, z.width, z.full_width
    )
    wr = lax.all_gather(w_all[:3, :, z.main :], "ctx", axis=1, tiled=True)
    wo = lax.all_gather(w_all[3], "ctx", axis=0, tiled=True)
    wo_f = lax.dynamic_slice_in_dim(wo, k * z.full_width, z.full_width)
    wo_r = wo[z.main :]
    return x_all, wf, wr, wo_f, wo_r


def heads_of(v, h):
    return v.reshape(v.shape[0], -1, h).transpose(1, 0, 2)


def attend(z, q, k, v, qpos, kpos, length):
    s = jnp.einsum("hqd,hkd->hkq", heads_of(q, z.head), heads_of(k, z.head), preferred_element_type=F32)
    s = s * (z.head ** -0.5)
    seen = (kpos[:, None] <= qpos[None, :]) & (kpos[:, None] < length)
    s = jnp.where(seen[None], s, -1e30)
    e = jnp.exp(s - jnp.max(s, axis=1, keepdims=True))
    p = (e / jnp.sum(e, axis=1, keepdims=True)).astype(BF16)
    o = jnp.einsum("hkq,hkd->qhd", p, heads_of(v, z.head), preferred_element_type=F32)
    return p, o.reshape(q.shape).astype(BF16)


def stage_b(z, x_all, wf, wr, gain, shift, bq_f, bq_r, bv_f, bv_r, pos, length):
    i = lax.axis_index("ctx")
    n1 = (norm_stats(x_all.astype(F32))[0] * gain + shift).astype(BF16)
    mine = lax.dynamic_slice_in_dim(n1, i * z.rows, z.rows)
    qpos = lax.dynamic_slice_in_dim(pos, i * z.rows, z.rows)
    out = dict(n1=n1)
    if z.full:
        q = (dot(n1, wf[0], 1, 0) + bq_f).astype(BF16)
        k = dot(n1, wf[1], 1, 0).astype(BF16)
        v = (dot(n1, wf[2], 1, 0) + bv_f).astype(BF16)
        p, o = attend(z, q, k, v, pos, pos, length)
        out.update(q_f=q, k_f=k, v_f=v, p_f=p, o_f=o)
    if z.rest:
        q = (dot(mine, wr[0], 1, 0) + bq_r).astype(BF16)
        k = dot(n1, wr[1], 1, 0).astype(BF16)
        v = (dot(n1, wr[2], 1, 0) + bv_r).astype(BF16)
        p, o = attend(z, q, k, v, qpos, pos, length)
        out.update(q_r=q, k_r=k, v_r=v, p_r=p, o_r=o)
    return out


def stage_c(z, b, wo_f, wo_r, x, upstream, ua, live, up_t, down, prm):
    branch = prm["b_o"]
    if z.full:
        part = dot(b["o_f"], wo_f, 1, 0).astype(BF16)
        branch = branch + lax.psum_scatter(part.astype(F32), "ctx", scatter_dimension=0, tiled=True)
    if z.rest:
        branch = branch + dot(b["o_r"], wo_r, 1, 0)
    hidden = x.astype(F32) + branch
    xhat, rstd = norm_stats(hidden)
    n2 = (xhat * prm["gain2"] + prm["shift2"]).astype(BF16)
    n2a = lax.all_gather(n2, "seq", axis=0, tiled=True)
    pre = dot(n2a, up_t, 1, 1) + prm["b_up"]
    cdf = 0.5 * (1.0 + lax.erf(pre * (0.5 ** 0.5)))
    act = (pre * cdf).astype(BF16)
    dgelu = cdf + pre * jnp.exp(-0.5 * pre * pre) * (1.0 / math.sqrt(2.0 * math.pi))
    gact = dot(ua, down, 1, 1)
    gpre = (gact * dgelu).astype(BF16)
    gn2p = dot(gpre, up_t, 1, 0).astype(BF16)
    gn2 = lax.psum_scatter(gn2p.astype(F32), "seq", scatter_dimension=0, tiled=True)
    ffp = dot(act, down, 1, 0).astype(BF16)
    ff = lax.psum_scatter(ffp.astype(F32), "seq", scatter_dimension=0, tiled=True)
    output = (live * (hidden + ff + prm["b_down"])).astype(BF16)
    g_up_t = dot(gpre, n2a, 0, 0).astype(BF16)
    g_down = dot(act, ua, 0, 0).astype(BF16)
    gh = upstream.astype(F32) + norm_back(gn2, xhat, rstd, prm["gain2"])
    gb = gh.astype(BF16)
    small = dict(gain2=rows_sum(gn2 * xhat), shift2=rows_sum(gn2), b_o=rows_sum(gb),
                 b_down=rows_sum(upstream), b_up=rows_sum(gpre))
    return output, gh, gb, g_up_t, g_down, small


def attend_back(z, q, k, v, p, go):
    gp = jnp.einsum("hqd,hkd->hkq", heads_of(go, z.head), heads_of(v, z.head), preferred_element_type=F32)
    pf = p.astype(F32)
    delta = jnp.sum(gp * pf, axis=1, keepdims=True)
    gs = (pf * (gp - delta)).astype(BF16)
    sc = z.head ** -0.5
    gq = jnp.einsum("hkq,hkd->qhd", gs, heads_of(k, z.head), preferred_element_type=F32) * sc
    gk = jnp.einsum("hkq,hqd->khd", gs, heads_of(q, z.head), preferred_element_type=F32) * sc
    gv = jnp.einsum("hkq,hqd->khd", p, heads_of(go, z.head), preferred_element_type=F32)
    return gq.reshape(q.shape).astype(BF16), gk.reshape(k.shape).astype(BF16), gv.reshape(v.shape).astype(BF16)


def stage_d(z, b, gb, gba, wo_f, wo_r):
    i = lax.axis_index("ctx")
    n1 = b["n1"]
    mine = lax.dynamic_slice_in_dim(n1, i * z.rows, z.rows)
    out = {}
    if z.full:
        go = dot(gba, wo_f, 1, 1).astype(BF16)
        gq, gk, gv = attend_back(z, b["q_f"], b["k_f"], b["v_f"], b["p_f"], go)
        out.update(gq_f=gq, gk_f=gk, gv_f=gv, gwo_f=dot(b["o_f"], gba, 0, 0))
        out["gw_f"] = jnp.stack([dot(n1, g, 0, 0) for g in (gq, gk, gv)])
    if z.rest:
        go = dot(gb, wo_r, 1, 1).astype(BF16)
        gq, gk, gv = attend_back(z, b["q_r"], b["k_r"], b["v_r"], b["p_r"], go)
        out.update(gq_r=gq, gk_r=gk, gv_r=gv, gwo_r=dot(b["o_r"], gb, 0, 0))
        out["gw_r"] = jnp.stack([dot(mine, gq, 0, 0), dot(n1, gk, 0, 0), dot(n1, gv, 0, 0)])
    return out


def stage_e(z, d, wf, wr, x, gh, gain1, small):
    i, s = lax.axis_index("ctx"), lax.axis_index("seq")
    part = 0.0
    own = 0.0
    if z.full:
        part = part + dot(d["gq_f"], wf[0], 1, 1) + dot(d["gk_f"], wf[1], 1, 1) + dot(d["gv_f"], wf[2], 1, 1)
    if z.rest:
        part = part + dot(d["gk_r"], wr[1], 1, 1) + dot(d["gv_r"], wr[2], 1, 1)
        own = own + dot(d["gq_r"], wr[0], 1, 1)
    gn1 = own + lax.psum_scatter(part.astype(BF16).astype(F32), "ctx", scatter_dimension=0, tiled=True)
    xhat, rstd = norm_stats(x.astype(F32))
    gtok = gh + norm_back(gn1, xhat, rstd, gain1)
    small = dict(small, gain1=rows_sum(gn1 * xhat), shift1=rows_sum(gn1))
    row = jnp.zeros((1, z.width), F32)
    for name, key in (("b_q", "gq"), ("b_v", "gv")):
        r = row
        if z.full:
            r = lax.dynamic_update_slice(r, rows_sum(d[key + "_f"]), (0, i * z.full_width))
        if z.rest:
            r = r.at[:, z.main :].add(rows_sum(d[key + "_r"]))
        small[name] = r
    full = jnp.zeros((4, z.width, z.width), F32)
    if z.full:
        full = lax.dynamic_update_slice(full, d["gw_f"], (0, 0, i * z.full_width))
        full = lax.dynamic_update_slice(full, d["gwo_f"][None], (3, i * z.full_width, 0))
    if z.rest:
        full = full.at[:3, :, z.main :].add(d["gw_r"])
        full = full.at[3, z.main :, :].add(d["gwo_r"])
    gw = lax.psum_scatter(full.reshape(4 * z.width, z.width).astype(BF16), ("seq", "ctx"), scatter_dimension=0, tiled=True)
    b_up_all = lax.all_gather(lax.psum(small.pop("b_up"), "ctx")[0], "seq", axis=0, tiled=True)
    names = list(small)
    tot = lax.psum(jnp.concatenate([small[n] for n in names]), ("seq", "ctx"))
    return gtok, gw.astype(F32), {n: tot[j : j + 1] for j, n in enumerate(names)}, b_up_all


MESH = pl.DeviceIdType.MESH
DMA = pltpu.SemaphoreType.DMA
VMEM_LIMIT = 56 << 20


def rcopy(src, dst, ssem, rsem, **dev):
    return pltpu.make_async_remote_copy(
        src_ref=src, dst_ref=dst, send_sem=ssem, recv_sem=rsem, device_id=dev, device_id_type=MESH
    )


def greet(ctx_peers, seq_peers, wait=True):
    sem = pltpu.get_barrier_semaphore()
    for p in ctx_peers:
        pl.semaphore_signal(sem, inc=1, device_id={"ctx": p}, device_id_type=MESH)
    for p in seq_peers:
        pl.semaphore_signal(sem, inc=1, device_id={"seq": p}, device_id_type=MESH)
    if wait:
        met(len(ctx_peers) + len(seq_peers))


def met(count):
    pl.semaphore_wait(pltpu.get_barrier_semaphore(), count)


class Place:
    def __init__(self, z):
        self.k, self.s = lax.axis_index("ctx"), lax.axis_index("seq")
        self.chips, self.ctx = z.ctx // 2, z.ctx
        self.core = lax.rem(self.k, 2)
        self.chip = self.k // 2
        self.sib = self.k + 1 - 2 * self.core
        self.edge = (self.chip == 0) | (self.chip == self.chips - 1)
        self.ring = [lax.rem(self.chip + i, self.chips) for i in range(self.chips)]
        self.same = [2 * q + self.core for q in self.ring]
        self.back = [2 * lax.rem(self.chip + self.chips - i, self.chips) + self.core for i in range(self.chips)]
        self.seqs = [lax.rem(self.s + i, z.seq) for i in range(z.seq)]
        self.seqs_back = [lax.rem(self.s + z.seq - i, z.seq) for i in range(z.seq)]


def call(body, name, outs, ins, scratch, cid, in_spaces, out_spaces, cost=None):
    spaces = {"v": pltpu.VMEM, "a": pl.ANY}
    return pl.pallas_call(
        body,
        name=name,
        out_shape=outs,
        in_specs=[pl.BlockSpec(memory_space=spaces[c]) for c in in_spaces],
        out_specs=[pl.BlockSpec(memory_space=spaces[c]) for c in out_spaces],
        scratch_shapes=scratch,
        compiler_params=pltpu.CompilerParams(
            collective_id=cid, has_side_effects=True, vmem_limit_bytes=VMEM_LIMIT
        ),
        cost_estimate=cost,
    )(*ins)


def sds(shape, dtype=BF16):
    return jax.ShapeDtypeStruct(shape, dtype)


class CtxGather:
    def __init__(self, at, own, dst, sems):
        self.at, self.own, self.dst, self.sems = at, own, dst, sems

    def send(self):
        at, ss, rs = self.at, self.sems[0], self.sems[1]
        for i in range(1, at.chips):
            rcopy(self.own, self.dst.at[at.k], ss.at[i], rs.at[i], ctx=at.same[i]).start()
        rcopy(self.own, self.dst.at[at.k], ss.at[0], rs.at[0], ctx=at.sib).start()
        pltpu.make_async_copy(self.own, self.dst.at[at.k], self.sems[4]).start()

    def forward(self, i):
        at, ss, rs, fs, fr = self.at, *self.sems[:4]
        src = at.back[i]
        rcopy(self.own, self.dst.at[src], ss.at[i], rs.at[i], ctx=at.same[i]).wait_recv()
        rcopy(self.dst.at[src], self.dst.at[src], fs.at[i], fr.at[i], ctx=at.sib).start()

    def finish(self):
        at, ss, rs, fs, fr = self.at, *self.sems[:4]
        pltpu.make_async_copy(self.own, self.dst.at[at.k], self.sems[4]).wait()
        rcopy(self.own, self.dst.at[at.k], ss.at[0], rs.at[0], ctx=at.sib).wait()
        for i in range(1, at.chips):
            rcopy(self.own, self.dst.at[at.k], ss.at[i], rs.at[i], ctx=at.same[i]).wait_send()
            rcopy(self.own, self.dst.at[at.k], fs.at[i], fr.at[i], ctx=at.sib).wait()

    @staticmethod
    def scratch(z):
        n = z.ctx // 2
        return [DMA((n,)), DMA((n,)), DMA((n,)), DMA((n,)), DMA]


def matmul(a, b, ca=1, cb=0):
    return lax.dot_general(a, b, (((ca,), (cb,)), ((), ())), preferred_element_type=F32)


def block(z, d):
    return pl.ds(pl.multiple_of(d * z.rows, z.rows), z.rows)


class CtxReduce:
    def __init__(self, at, part, bufs):
        self.at, self.part = at, part
        self.sb, self.sr, self.zb, self.zr, self.ss, self.sn, self.zs, self.zn = bufs

    def sib(self, t):
        return rcopy(self.sb.at[t], self.sr.at[t], self.ss.at[t], self.sn.at[t], ctx=self.at.sib)

    def far(self, t):
        return rcopy(self.zb.at[t], self.zr.at[t], self.zs.at[t], self.zn.at[t], ctx=self.at.same[t])

    def start(self):
        at = self.at
        order = list(range(1, at.chips)) + [0]
        for t in order:
            self.sb[t] = self.part(2 * at.ring[t] + 1 - at.core).astype(BF16)
            self.sib(t).start()
        for t in order[:-1]:
            mine = self.part(at.same[t])
            self.sib(t).wait_recv()
            self.zb[t] = (mine + self.sr[t].astype(F32)).astype(BF16)
            self.far(t).start()

    def finish(self, own=None):
        at = self.at
        total = self.part(at.k) if own is None else own
        self.sib(0).wait_recv()
        total = total + self.sr[0].astype(F32)
        for t in range(1, at.chips):
            self.far(t).wait_recv()
            total = total + self.zr[t].astype(F32)
        return total

    def close(self):
        for t in range(self.at.chips):
            self.sib(t).wait_send()
            if t:
                self.far(t).wait_send()

    @staticmethod
    def scratch(z):
        n = z.ctx // 2
        return [pltpu.VMEM((n, z.rows, z.width), BF16)] * 4 + [DMA((n,))] * 4


NEG = -1e30


def turn(v):
    return jnp.transpose(v.astype(F32)).astype(BF16)


def of_head(v, h, head):
    lane = lax.broadcasted_iota(jnp.int32, v.shape, 1) // head
    return jnp.where(lane == h, v.astype(F32), 0.0)


def attend_block(heads, k, v_t, q, mask, head, p_ref):
    parts = []
    for h in range(heads):
        qh = (of_head(q, h, head) * head ** -0.5).astype(BF16)
        s = matmul(k, qh, 1, 1) + mask
        e = jnp.exp(s - jnp.max(s, axis=0, keepdims=True))
        p = (e * (1.0 / jnp.sum(e, axis=0, keepdims=True))).astype(BF16)
        p_ref[h] = p
        parts.append(matmul(v_t[h * head : (h + 1) * head], p))
    o_t = parts[0] if len(parts) == 1 else jnp.concatenate(parts, axis=0)
    return jnp.transpose(o_t).astype(BF16)


class FarGather:
    def __init__(self, at, own, dst, sems):
        self.at, self.own, self.dst = at, own, dst
        self.ss, self.rs, self.fs, self.fr, self.lo, self.ho = sems

    def each(self):
        return range(len(self.own))

    def to(self, u, i):
        return rcopy(self.own[u], self.dst[u].at[self.at.k], self.ss.at[u, i], self.rs.at[u, i], ctx=self.at.same[i])

    def side(self, u, i):
        b = self.dst[u].at[self.at.back[i]]
        return rcopy(b, b, self.fs.at[u, i], self.fr.at[u, i], ctx=self.at.sib)

    def hop(self, u, i, step):
        b = self.dst[u].at[self.at.back[i]]
        return rcopy(b, b, self.ho.at[u], self.rs.at[u, 2], ctx=lax.rem(self.at.k + step + self.at.ctx, self.at.ctx))

    def local(self, u):
        return pltpu.make_async_copy(self.own[u], self.dst[u].at[self.at.k], self.lo.at[u])

    def sibling(self, u):
        return rcopy(self.own[u], self.dst[u].at[self.at.k], self.fs.at[u, 0], self.fr.at[u, 0], ctx=self.at.sib)

    def start(self):
        at = self.at
        for u in self.each():
            self.to(u, 1).start()
            self.to(u, 3).start()
            self.local(u).start()
            self.sibling(u).start()

        @pl.when(at.edge)
        def _():
            for u in self.each():
                self.to(u, 2).start()

    def relay(self):
        @pl.when(self.at.chip == 1)
        def _():
            for u in self.each():
                self.to(u, 3).wait_recv()
                self.hop(u, 3, -2).start()

        @pl.when(self.at.chip == 2)
        def _():
            for u in self.each():
                self.to(u, 1).wait_recv()
                self.hop(u, 1, 2).start()

    def forward(self):
        for i in (1, 3, 2):
            for u in self.each():
                if i == 2:
                    self.to(u, i).wait_recv()
                else:
                    @pl.when(self.at.chip != (2 if i == 1 else 1))
                    def _():
                        self.to(u, i).wait_recv()
                self.side(u, i).start()

    def finish(self):
        for u in self.each():
            self.local(u).wait()
            self.sibling(u).wait()
            for i in (1, 3, 2):
                self.side(u, i).wait()
            self.to(u, 1).wait_send()
            self.to(u, 3).wait_send()

            @pl.when(self.at.edge)
            def _():
                self.to(u, 2).wait_send()

            @pl.when(~self.at.edge)
            def _():
                self.hop(u, 1, 2).wait_send()

    @staticmethod
    def scratch(z):
        return [DMA((2, 4)), DMA((2, 4)), DMA((2, 4)), DMA((2, 4)), DMA((2,)), DMA((2,))]


def place_rows(flat, piece, offset):
    wide = piece.shape[1] + 128
    base, shift = offset // 128 * 128, offset % 128
    padded = jnp.concatenate([piece, jnp.zeros((8, 128), F32)], axis=1)
    flat[:, base : base + wide] += pltpu.roll(padded, shift, 1) if shift else padded


def take_row(flat, start, width):
    base, shift = start // 128 * 128, start % 128
    wide = -(-(shift + width) // 128) * 128
    v = flat[:, base : base + wide]
    if shift:
        v = pltpu.roll(v, wide - shift, 1)
    return v[0:1, 0:width]


def kernel_first(z, n_g, n_b, qb, order, length, xt, ct, wv, w, pk, upw, dnw,
                 ua, wf, wo2, wol, upa, dna, xao, n1o, qo, ko, vo, p_fo, p_ro, o_fo,
                 prm, live, wo_f, o_r, hid, xh, rs_o, n2a,
                 x, up, wr, pa, xa, n1, q, k, v, p_f, p_r, o_f, vt, vrt, wvm, wo_r, kp, qp, gflat, bflat, n2,
                 mz_s, mz_r, rz_s, rz_r, mx_s, mx_r, us, ur, oz_s, oz_r, ox_s, ox_r, loc, pz_s, pz_r, px_s, px_r, wl, wb, ns, nr, *rest):
    at = Place(z)
    me, s, C, S, FW, RW, SH, D, R, N = at.k, at.s, z.ctx, z.seq, z.full_width, z.rest_width, z.shard, z.width, z.rows, z.slot
    ffg = FarGather(at, (upw, dnw), (upa, dna), rest[:6])
    tok = CtxGather(at, x, xa, rest[6:11])
    bufs = rest[11:]
    others = [lax.rem(me + i, C) for i in range(1, C)]
    greet(others, at.seqs[1:], False)

    x[...] = jnp.transpose(xt[...].astype(F32)).astype(BF16)
    half, lens = z.block_len, length[0]
    row = lax.broadcasted_iota(jnp.int32, (R, 128), 0)
    where = jnp.where(row < half, order[2 * me] * half + row, order[2 * me + 1] * half + row - half)
    live[...] = jnp.where(where < lens, 1.0, 0.0)
    up[...] = (jnp.transpose(ct[...].astype(F32)) * live[:, 0:1]).astype(BF16)
    wr[...] = jnp.zeros_like(wr)
    wr[:, 0:RW] = wv[:, z.main :]
    met(C + S - 2)

    def rows_of(j):
        return pl.ds(pl.multiple_of(j * SH, 8), SH)

    def cols(j):
        return wv.at[:, pl.ds(pl.multiple_of(j * FW, FW), FW)]

    def main(m, j):
        return wf.at[m, rows_of(j), pl.ds(0, FW)]

    def tail(m, j):
        return wf.at[m, rows_of(j), pl.ds(FW, FW)]

    def both(m, j):
        return wf.at[m, rows_of(j)]

    before, after = wo2.at[pl.ds(0, SH)], wo2.at[pl.ds(SH, SH)]
    lastrows = w.at[pl.ds(z.main - (C - 1) * SH, RW)]

    for i in range(1, C):
        rcopy(pk, pa.at[s, me], pz_s.at[i], pz_r.at[i], ctx=others[i - 1]).start()
    pltpu.make_async_copy(pk, pa.at[s, me], loc.at[3]).start()

    @pl.when(s < 3)
    def _():
        for i in range(1, C):
            j = lax.rem(me + i, C)
            rcopy(cols(j), main(s, me), mz_s.at[i], mz_r.at[me], ctx=j).start()
            rcopy(wr, tail(s, me), rz_s.at[i], rz_r.at[me], ctx=j).start()
        pltpu.make_async_copy(cols(me), main(s, me), loc.at[0]).start()
        pltpu.make_async_copy(wr, tail(s, me), loc.at[1]).start()

    @pl.when(s == 3)
    def _():
        @pl.when(me < C - 1)
        def _():
            rcopy(w, before, oz_s.at[0], oz_r.at[0], ctx=lax.rem(me + 1, C)).start()

        @pl.when(me == C - 1)
        def _():
            for i in range(1, C):
                rcopy(lastrows, wol, oz_s.at[i], oz_r.at[1], ctx=lax.rem(me + i, C)).start()
            pltpu.make_async_copy(lastrows, wol, loc.at[1]).start()

        pltpu.make_async_copy(w, after, loc.at[0]).start()
        for i in range(1, 4):
            rcopy(w, after, ox_s.at[0, i], ox_r.at[0], seq=at.seqs[i]).start()

    tok.send()

    for i in range(1, C):
        rcopy(pk, pa.at[s, lax.rem(me + C - i, C)], pz_s.at[i], pz_r.at[i], ctx=me).wait_recv()
    pltpu.make_async_copy(pk, pa.at[s, me], loc.at[3]).wait()
    for i in range(1, S):
        rcopy(pa.at[s], pa.at[s], px_s.at[i], px_r.at[i], seq=at.seqs[i]).start()

    for b in range(N // half):
        p = order[b] * half + lax.broadcasted_iota(jnp.int32, (half, 128), 0)
        kp[b * half : (b + 1) * half] = jnp.where(p < lens, p, 1 << 30)
    lane = lax.broadcasted_iota(jnp.int32, (8, 128), 1)
    for b in range(N // 128):
        qp[:, b * 128 : (b + 1) * 128] = jnp.where(
            lane < half, order[2 * b] * half + lane, order[2 * b + 1] * half + lane - half)

    @pl.when(s < 3)
    def _():
        for n in range(C):
            src = lax.rem(me + C - n, C)
            if n == 0:
                pltpu.make_async_copy(cols(me), main(s, me), loc.at[0]).wait()
                pltpu.make_async_copy(wr, tail(s, me), loc.at[1]).wait()
            else:
                rcopy(cols(me), main(s, src), mz_s.at[0], mz_r.at[src], ctx=me).wait_recv()
                rcopy(wr, tail(s, src), rz_s.at[0], rz_r.at[src], ctx=me).wait_recv()
            for i in range(1, 4):
                rcopy(both(s, src), both(s, src), mx_s.at[n, i], mx_r.at[s, src], seq=at.seqs[i]).start()

    @pl.when(s == 3)
    def _():
        pltpu.make_async_copy(w, after, loc.at[0]).wait()

        @pl.when(me > 0)
        def _():
            rcopy(w, before, oz_s.at[0], oz_r.at[0], ctx=me).wait_recv()
            for i in range(1, 4):
                rcopy(before, before, ox_s.at[1, i], ox_r.at[1], seq=at.seqs[i]).start()

        @pl.when(me < C - 1)
        def _():
            rcopy(lastrows, wol, oz_s.at[1], oz_r.at[1], ctx=me).wait_recv()

        @pl.when(me == C - 1)
        def _():
            pltpu.make_async_copy(lastrows, wol, loc.at[1]).wait()

        for i in range(1, 4):
            rcopy(wol, wol, ox_s.at[2, i], ox_r.at[2], seq=at.seqs[i]).start()

    for i in range(1, S):
        rcopy(pa.at[s], pa.at[at.seqs_back[i]], px_s.at[i], px_r.at[i], seq=s).wait()
    gflat[...] = jnp.zeros_like(gflat)
    bflat[...] = jnp.zeros_like(bflat)
    for d in range(S * C):
        t = pa[d // C, d % C].astype(F32)
        place_rows(gflat, jnp.broadcast_to(t[0:1], (8, 128)), d * n_g)
        place_rows(bflat, jnp.broadcast_to(jnp.concatenate([t[1:2], t[2:3], t[3:4]], axis=1), (8, 384)), d * n_b)
    for j in range(2):
        prm[j : j + 1] = take_row(gflat, j * D, D)
    for j in range(10):
        prm[2 + j : 3 + j] = take_row(bflat, j * D, D)

    for i in range(1, at.chips):
        tok.forward(i)
    ffg.start()
    for i in range(1, S):
        rcopy(up, ua.at[s], us.at[i], ur.at[i], seq=at.seqs[i]).start()
    pltpu.make_async_copy(up, ua.at[s], loc.at[2]).start()
    tok.finish()

    def norm_rows(j, _):
        n1[block(z, j)] = (norm_stats(xa[j].astype(F32))[0] * prm[0:1] + prm[2:3]).astype(BF16)
        return 0

    lax.fori_loop(0, C, norm_rows, 0)

    for m in range(3):
        @pl.when(s != m)
        def _():
            for src in range(C):
                rcopy(both(m, src), both(m, src), mx_s.at[0, 0], mx_r.at[m, src], seq=s).wait_recv()
    wload = [pltpu.make_async_copy(wf.at[m], wvm.at[m], wl.at[m]) for m in range(3)]
    for c in wload:
        c.start()

    @pl.when(s != 3)
    def _():
        rcopy(w, after, ox_s.at[0, 0], ox_r.at[0], seq=s).wait_recv()

        @pl.when(me > 0)
        def _():
            rcopy(w, before, ox_s.at[1, 0], ox_r.at[1], seq=s).wait_recv()

        rcopy(wol, wol, ox_s.at[2, 0], ox_r.at[2], seq=s).wait_recv()

    wload += [
        pltpu.make_async_copy(wo2.at[pl.ds(pl.multiple_of(SH - (SH - FW) * me, 8), FW)], wo_f, wl.at[3]),
        pltpu.make_async_copy(wol, wo_r, wl.at[4]),
    ]
    wload[3].start()
    wload[4].start()

    def bias(j):
        a = prm[j : j + 1]
        own = jnp.zeros((1, FW), F32)
        for c in range(C):
            own = own + jnp.where(me == c, a[:, c * FW : (c + 1) * FW], 0.0)
        return jnp.concatenate([own, a[:, z.main :], jnp.zeros((1, FW - RW), F32)], axis=1)

    wload[0].wait()
    q[...] = (matmul(n1[...], wvm[0]) + bias(3)).astype(BF16)
    wload[1].wait()
    k[...] = matmul(n1[...], wvm[1]).astype(BF16)
    wload[2].wait()
    v[...] = (matmul(n1[...], wvm[2]) + bias(4)).astype(BF16)
    backs = [pltpu.make_async_copy(a, b, wb.at[i]) for i, (a, b) in enumerate(((n1, n1o), (q, qo), (k, ko), (v, vo), (xa, xao)))]
    for c in backs:
        c.start()
    vt[...] = turn(v[:, 0:FW])
    vrt[...] = turn(v[:, FW : 2 * FW])[0:RW]
    mine = block(z, me)
    ffg.relay()

    def steps(j, _):
        r = pl.ds(pl.multiple_of(j * qb, qb), qb)
        mask = jnp.where(jnp.concatenate([kp[...]] * (qb // 128), axis=1) <= qp[0:1, r], 0.0, NEG)
        o_f[r] = attend_block(z.full, k[:, 0:FW], vt[...], q[r, 0:FW], mask, z.head, p_f.at[j])
        return 0

    lax.fori_loop(0, N // qb, steps, 0)
    mask = jnp.where(kp[...] <= qp[0:1, mine], 0.0, NEG)
    o_r[...] = attend_block(z.rest, k[:, FW : 2 * FW], vrt[...], q[mine, FW : 2 * FW], mask, z.head, p_r)
    more = [pltpu.make_async_copy(a, b, wb.at[5 + i]) for i, (a, b) in enumerate(((p_f, p_fo), (p_r, p_ro), (o_f, o_fo)))]
    for c in more:
        c.start()
    wload[3].wait()
    wload[4].wait()
    red = CtxReduce(at, lambda d: matmul(o_f[block(z, d)], wo_f[...]), bufs)
    red.start()
    ffg.forward()
    own = matmul(o_r[...], wo_r[...]) + prm[5:6] + x[...].astype(F32)
    hidden = red.finish() + own
    xhat, rstd = norm_stats(hidden)
    n2[...] = (xhat * prm[1:2] + prm[6:7]).astype(BF16)
    copies = [rcopy(n2, n2a.at[s], ns.at[i], nr.at[i], seq=at.seqs[i]) for i in (2, 1, 3)]
    for c in copies:
        c.start()
    n2a[s] = n2[...]
    hid[...] = hidden
    xh[...] = xhat
    rs_o[...] = jnp.broadcast_to(rstd, rs_o.shape)

    red.close()
    ffg.finish()
    pltpu.make_async_copy(up, ua.at[s], loc.at[2]).wait()
    for i in range(1, S):
        rcopy(up, ua.at[s], us.at[i], ur.at[i], seq=at.seqs[i]).wait()
    for i in range(1, C):
        rcopy(pk, pa.at[s, me], pz_s.at[i], pz_r.at[i], ctx=me).wait_send()

    @pl.when(s < 3)
    def _():
        for i in range(1, C):
            rcopy(cols(me), main(s, me), mz_s.at[i], mz_r.at[me], ctx=me).wait_send()
            rcopy(wr, tail(s, me), rz_s.at[i], rz_r.at[me], ctx=me).wait_send()
        for n in range(C):
            for i in range(1, 4):
                rcopy(both(s, me), both(s, me), mx_s.at[n, i], mx_r.at[s, me], seq=s).wait_send()

    @pl.when(s == 3)
    def _():
        @pl.when(me < C - 1)
        def _():
            rcopy(w, before, oz_s.at[0], oz_r.at[0], ctx=me).wait_send()

        @pl.when(me == C - 1)
        def _():
            for i in range(1, C):
                rcopy(lastrows, wol, oz_s.at[i], oz_r.at[1], ctx=me).wait_send()

        for i in range(1, 4):
            rcopy(w, after, ox_s.at[0, i], ox_r.at[0], seq=s).wait_send()

            @pl.when(me > 0)
            def _():
                rcopy(before, before, ox_s.at[1, i], ox_r.at[1], seq=s).wait_send()

            rcopy(wol, wol, ox_s.at[2, i], ox_r.at[2], seq=s).wait_send()

    for c in backs + more:
        c.wait()
    for c in copies:
        c.wait()


def stage_first_kernel(z, tokens, lengths, block_order, w, up_weights, down_weights, norm_gains, biases, cotangent):
    N, D, FW, RW, R, S, C, SH, qb = z.slot, z.width, z.full_width, z.rest_width, z.rows, z.seq, z.ctx, z.shard, 256
    nq, W2 = N // qb, 2 * FW
    n_g, n_b = norm_gains.shape[0], biases.shape[0]
    pk = jnp.concatenate([jnp.pad(norm_gains, (0, 128 - n_g)), jnp.pad(biases, (0, 896 - n_b))]).reshape(8, 128)
    ins = (block_order, lengths, tokens[0].T, cotangent[0].T, w, w, pk, up_weights.T, down_weights)
    shapes = dict(
        ua=(S, R, D), w3=(3, D, W2), wo2=(2 * SH, D), wo_r=(RW, D), up_t=(C, SH, D), down=(C, SH, D), xa=(C, R, D), n1=(N, D), q=(N, W2),
        k=(N, W2), v=(N, W2), p_f=(nq, z.full, N, qb), p_r=(z.rest, N, R), o_f=(N, FW))
    wide = dict(prm=(12, D), live=(R, 128), wo_f=(FW, D), o_r=(R, RW), hid=(R, D), xh=(R, D), rs=(R, 128), n2a=(S, R, D))
    low = ("wo_f", "o_r", "n2a")
    outs = [sds(a) for a in shapes.values()] + [sds(a, BF16 if n in low else F32) for n, a in wide.items()]
    V = pltpu.VMEM
    scratch = [
        V((R, D), BF16), V((R, D), BF16), V((SH, FW), BF16), V((S, C, 8, 128), BF16), V((C, R, D), BF16), V((N, D), BF16),
        V((N, W2), BF16), V((N, W2), BF16), V((N, W2), BF16), V((nq, z.full, N, qb), BF16), V((z.rest, N, R), BF16), V((N, FW), BF16),
        V((FW, N), BF16), V((RW, N), BF16), V((3, D, W2), BF16), V((RW, D), BF16), V((N, 128), jnp.int32), V((8, N), jnp.int32),
        V((8, -(-2 * D // 128) * 128 + 256), F32), V((8, -(-10 * D // 128) * 128 + 512), F32), V((R, D), BF16),
        DMA((C,)), DMA((C,)), DMA((C,)), DMA((C,)), DMA((C, 4)), DMA((3, C)), DMA((4,)), DMA((4,)), DMA((C,)), DMA((2,)), DMA((3, 4)),
        DMA((3,)), DMA((4,)), DMA((C,)), DMA((C,)), DMA((S,)), DMA((S,)), DMA((5,)), DMA((8,)), DMA((S,)), DMA((S,)),
        *FarGather.scratch(z), *CtxGather.scratch(z), *CtxReduce.scratch(z),
    ]
    spaces = {"v": pltpu.VMEM, "a": pl.ANY, "s": pltpu.SMEM}
    out = pl.pallas_call(
        partial(kernel_first, z, n_g, n_b, qb), name="first_half", out_shape=outs,
        in_specs=[pl.BlockSpec(memory_space=spaces[c]) for c in "ssvvvaaaa"],
        out_specs=[pl.BlockSpec(memory_space=spaces[c]) for c in "a" * 14 + "v" * 8],
        scratch_shapes=scratch,
        compiler_params=pltpu.CompilerParams(collective_id=0, has_side_effects=True, vmem_limit_bytes=VMEM_LIMIT),
    )(*ins)
    return dict(zip(tuple(shapes) + tuple(wide), out))


def ff_block(z, j):
    return pl.ds(pl.multiple_of(j * z.shard, 8), z.shard)


def kernel_f(z, n2h, uah, uph, dnh, prm, hid, xh, rs_i, live, out, gh_o, gb_o, sm, bu, gba, ffr,
             n2, ua, up_t, down, act, gpre, gsend, grecv, fsend, frecv, g32, fs, fr, ld, gs, gr, cs, cr, ps, pr, wb, *gsem):
    at = Place(z)
    S, R, D, C = z.seq, z.rows, z.width, z.ctx
    units, step = up_t.shape[0], 256
    b_up = prm[pl.ds(8 + at.s, 1)]
    greet([at.sib] + at.same[1:], at.seqs[1:], False)
    chunks = [slice(c0, min(c0 + step, units)) for c0 in range(0, units, step)]
    loads = [pltpu.make_async_copy(n2h, n2, ld.at[0]), pltpu.make_async_copy(uah, ua, ld.at[1])]
    for i, c in enumerate(chunks):
        loads.append(pltpu.make_async_copy(uph.at[c], up_t.at[c], ld.at[2 + 2 * i]))
        loads.append(pltpu.make_async_copy(dnh.at[c], down.at[c], ld.at[3 + 2 * i]))
    for c in loads:
        c.start()
    loads[0].wait()
    loads[1].wait()
    for i, c in enumerate(chunks):
        loads[2 + 2 * i].wait()
        pre = matmul(n2[...], up_t[c], 1, 1) + b_up[:, c]
        loads[3 + 2 * i].wait()
        gact = matmul(ua[...], down[c], 1, 1)
        cdf = 0.5 * (1.0 + lax.erf(pre * (0.5 ** 0.5)))
        act[:, c] = (pre * cdf).astype(BF16)
        dgelu = cdf + pre * jnp.exp(-0.5 * pre * pre) * (1.0 / math.sqrt(2.0 * math.pi))
        g = (gact * dgelu).astype(BF16)
        gpre[:, c] = g
        bu[:, c] = jnp.sum(g.astype(F32), axis=0, keepdims=True)
    met(at.chips + S - 1)

    def gcopy(i):
        return rcopy(gsend.at[i], grecv.at[i], gs.at[i], gr.at[i], seq=at.seqs[i])

    def fcopy(i):
        return rcopy(fsend.at[i], frecv.at[i], cs.at[i], cr.at[i], seq=at.seqs[i])

    def pair(t, u):
        return rcopy(fs.at[t, u], fr.at[t, u], ps.at[t, u], pr.at[t, u], ctx=at.sib)

    def weight_grad(u, left, right):
        for c in chunks:
            g32[u, c] = matmul(left[:, c], right[...], 0, 0)
        for t in range(4):
            fs[t, u] = g32[u, ff_block(z, 2 * at.ring[t] + 1 - at.core)].astype(BF16)
            pair(t, u).start()

    def both(u):
        for t in range(4):
            pair(t, u).wait_recv()
            fr[t, u] = (g32[u, ff_block(z, at.same[t])] + fr[t, u].astype(F32)).astype(BF16)
            pltpu.make_async_copy(fr.at[t, u], ffr.at[t, u], wb.at[t, u]).start()

    for i in (2, 1, 3):
        gsend[i] = matmul(gpre[block(z, at.seqs[i])], up_t[...]).astype(BF16)
        gcopy(i).start()
    mine = block(z, at.s)
    gn2 = matmul(gpre[mine], up_t[...])
    weight_grad(0, gpre, n2)
    for i in range(1, S):
        gcopy(i).wait_recv()
        gn2 = gn2 + grecv[i].astype(F32)
    xhat = xh[...]
    up_own = ua[mine].astype(F32)
    gh = up_own + norm_back(gn2, xhat, rs_i[:, :1], prm[1:2])
    gb_o[...] = gh.astype(BF16)
    gat = CtxGather(at, gb_o, gba, gsem)
    gat.send()
    gh_o[...] = gh
    sm[0:1] = jnp.sum(gn2 * xhat, axis=0, keepdims=True)
    sm[1:2] = jnp.sum(gn2, axis=0, keepdims=True)
    sm[2:3] = jnp.sum(gb_o[...].astype(F32), axis=0, keepdims=True)
    sm[3:4] = jnp.sum(up_own, axis=0, keepdims=True)
    for i in (2, 1, 3):
        fsend[i] = matmul(act[block(z, at.seqs[i])], down[...]).astype(BF16)
        fcopy(i).start()
    ff = matmul(act[mine], down[...])
    weight_grad(1, act, ua)
    both(0)
    for i in (1, 3):
        gat.forward(i)
    both(1)
    for i in range(1, S):
        fcopy(i).wait_recv()
        ff = ff + frecv[i].astype(F32)
    out[...] = jnp.transpose(live[:, :1] * (hid[...] + ff + prm[7:8])).astype(BF16)
    gat.forward(2)
    gat.finish()
    for t in range(4):
        for u in range(2):
            pair(t, u).wait_send()
            pltpu.make_async_copy(fr.at[t, u], ffr.at[t, u], wb.at[t, u]).wait()
    for i in range(1, S):
        gcopy(i).wait_send()
        fcopy(i).wait_send()


def stage_f_kernel(z, b):
    R, D, S, U, C, SH = z.rows, z.width, z.seq, z.ctx * z.shard, z.ctx, z.shard
    outs = [sds((D, R)), sds((R, D), F32), sds((R, D)), sds((4, D), F32), sds((1, U), F32), sds((C, R, D)), sds((4, 2, SH, D))]
    V = pltpu.VMEM
    scratch = [
        V((S * R, D), BF16), V((S * R, D), BF16), V((U, D), BF16), V((U, D), BF16), V((S * R, U), BF16), V((S * R, U), BF16),
        *[V((S, R, D), BF16) for _ in range(4)], V((2, U, D), F32), V((4, 2, SH, D), BF16), V((4, 2, SH, D), BF16),
        DMA((2 + 2 * -(-U // 256),)), *[DMA((S,)) for _ in range(4)], DMA((4, 2)), DMA((4, 2)), DMA((4, 2)),
        *CtxGather.scratch(z),
    ]
    return call(
        partial(kernel_f, z), "feed_forward", outs,
        (b["n2a"].reshape(S * R, D), b["ua"].reshape(S * R, D), b["up_t"].reshape(U, D), b["down"].reshape(U, D),
         b["prm"], b["hid"], b["xh"], b["rs"], b["live"]), scratch, 2, "aaaa" + "v" * 5, "v" * 5 + "aa",
    )


class SmallSum:
    def __init__(self, at, buf, rsib, rchip, rseq, sems):
        self.at, self.buf, self.rsib, self.rchip, self.rseq = at, buf, rsib, rchip, rseq
        self.s0, self.r0, self.s1, self.r1, self.s2, self.r2 = sems

    def sib(self):
        return rcopy(self.buf.at[0], self.rsib, self.s0, self.r0, ctx=self.at.sib)

    def chip(self, i):
        return rcopy(self.buf.at[1], self.rchip.at[i], self.s1.at[i], self.r1.at[i], ctx=self.at.same[i])

    def line(self, i):
        return rcopy(self.buf.at[2], self.rseq.at[i], self.s2.at[i], self.r2.at[i], seq=self.at.seqs[i])

    def first(self, value):
        self.buf[0] = value
        self.sib().start()

    def second(self):
        self.sib().wait_recv()
        self.buf[1] = self.buf[0] + self.rsib[...]
        for i in range(1, self.at.chips):
            self.chip(i).start()

    def third(self):
        total = self.buf[1]
        for i in range(1, self.at.chips):
            self.chip(i).wait_recv()
            total = total + self.rchip[i]
        self.buf[2] = total
        for i in range(1, len(self.at.seqs)):
            self.line(i).start()

    def last(self):
        total = self.buf[2]
        for i in range(1, len(self.at.seqs)):
            self.line(i).wait_recv()
            total = total + self.rseq[i]
        return total

    def close(self):
        self.sib().wait_send()
        for i in range(1, self.at.chips):
            self.chip(i).wait_send()
        for i in range(1, len(self.at.seqs)):
            self.line(i).wait_send()

    @staticmethod
    def scratch(z, rows):
        n, shape = z.ctx // 2, (rows, z.width)
        return [
            pltpu.VMEM((3,) + shape, F32), pltpu.VMEM(shape, F32), pltpu.VMEM((n,) + shape, F32),
            pltpu.VMEM((z.seq,) + shape, F32), DMA, DMA, DMA((n,)), DMA((n,)), DMA((z.seq,)), DMA((z.seq,)),
        ]


def attend_block_back(heads, k_t, v, q, go, p_ref, head, gk, gv):
    parts = []
    for h in range(heads):
        goh = of_head(go, h, head).astype(BF16)
        p = p_ref[h]
        pf = p.astype(F32)
        gp = matmul(v, goh, 1, 1)
        delta = jnp.sum(gp * pf, axis=0, keepdims=True)
        gs = (pf * (gp - delta)).astype(BF16)
        gk[...] += matmul(gs, of_head(q, h, head).astype(BF16))
        gv[...] += matmul(p, goh)
        parts.append(matmul(k_t[h * head : (h + 1) * head], gs))
    g_t = parts[0] if len(parts) == 1 else jnp.concatenate(parts, axis=0)
    return (jnp.transpose(g_t) * head ** -0.5).astype(BF16)


def kernel_de(z, qb, gbah, kh, oh, vh, qh, pfh, prh, wh, n1h, xah, ffr,
              wo_f, wo_r, o_r, gh, prm, sm4, bu,
              gtok, ga, gup, gdn, tot, bup,
              gba, k, o_f, v, q, p_f, p_r, w, n1, xa, ld,
              go, kt, krt, gk, gv, gkr, gvr, gcat, gw, gwr, gwo, gwor, sums, ffz, ffo, comb, mid, fz_s, fz_r, fo, fm,
              rf, rr, ro, ror, sf_s, sf_r, sr_s, sr_r, so_s, so_r, sor_s, sor_r,
              zs, zr, land, landr, zs_s, zs_r, zr_s, zr_r,
              buf32, obs, obn, orrs, orr, ob_s, ob_r, orr_s, orr_r, *rest):
    at = Place(z)
    s, me, C, S, FW, RW, SH, D = at.s, at.k, z.ctx, z.seq, z.full_width, z.rest_width, z.shard, z.width
    bufs, small = rest[:8], rest[8:]
    scale, top = z.head ** -0.5, TOP(z)
    mine = block(z, me)
    greet([lax.rem(me + i, C) for i in range(1, C)], at.seqs[1:], False)
    pairs = ((gbah, gba), (kh, k), (oh, o_f), (vh, v), (qh, q), (pfh, p_f), (prh, p_r), (wh, w), (n1h, n1), (xah, xa))
    loads = [pltpu.make_async_copy(a, b, ld.at[i]) for i, (a, b) in enumerate(pairs)]
    for c in loads:
        c.start()
    ownff = pltpu.make_async_copy(ffr.at[0], ffo, fo.at[0])
    ownff.start()
    farff = pltpu.make_async_copy(ffr.at[2], comb, fo.at[1])
    farff.start()
    met(C + S - 2)

    def fz(t):
        return rcopy(ffr.at[t], ffz.at[t], fz_s.at[t], fz_r.at[t], ctx=at.same[t])

    def via(t):
        return rcopy(ffr.at[t], mid, fm.at[0], fm.at[1], ctx=at.same[4 - t])

    def across():
        return rcopy(comb, ffz.at[2], fz_s.at[2], fz_r.at[2], ctx=at.same[2])

    @pl.when(at.chip == 0)
    def _():
        via(3).start()

    @pl.when(at.chip == 3)
    def _():
        via(1).start()

    @pl.when(~at.edge)
    def _():
        fz(1).start()
        fz(3).start()

    gk[...] = jnp.zeros_like(gk)
    gv[...] = jnp.zeros_like(gv)
    gkr[...] = jnp.zeros_like(gkr)
    gvr[...] = jnp.zeros_like(gvr)
    gcat[0, :, FW:] = jnp.zeros((z.slot, FW), BF16)
    for c in loads[:3]:
        c.wait()
    go[...] = matmul(gba[...], wo_f[...], 1, 1).astype(BF16)
    kt[...] = turn(k[:, 0:FW])
    krt[...] = turn(k[:, FW : 2 * FW])[0:RW]
    gwo[...] = matmul(o_f[...], gba[...], 0, 0).astype(BF16)
    gwor[...] = matmul(o_r[...], gba[mine], 0, 0).astype(BF16)

    def up(ref, dst, ssem, rsem, i, m=None):
        return rcopy(ref if m is None else ref.at[m], dst.at[i], ssem.at[i], rsem.at[i], seq=at.seqs[i])

    for i in range(1, S):
        @pl.when(at.seqs[i] == 3)
        def _():
            up(gwo, ro, so_s, so_r, i).start()
            up(gwor, ror, sor_s, sor_r, i).start()

    for c in loads[3:6]:
        c.wait()

    def steps(j, _):
        r = pl.ds(pl.multiple_of(j * qb, qb), qb)
        gcat[0, r, 0:FW] = attend_block_back(z.full, kt[...], v[:, 0:FW], q[r, 0:FW], go[r], p_f.at[j], z.head, gk, gv)
        return 0

    lax.fori_loop(0, z.slot // qb, steps, 0)

    farff.wait()

    @pl.when(at.chip == 0)
    def _():
        via(3).wait_send()
        fz(1).start()

    @pl.when(at.chip == 3)
    def _():
        via(1).wait_send()
        fz(3).start()

    @pl.when(~at.edge)
    def _():
        via(1).wait_recv()
        for u in range(2):
            comb[u] = (comb[u].astype(F32) + mid[u].astype(F32)).astype(BF16)

    across().start()
    loads[6].wait()
    gor = matmul(gba[mine], wo_r[...], 1, 1).astype(BF16)
    gor = jnp.concatenate([gor, jnp.zeros((z.rows, FW - RW), BF16)], axis=1)
    gcat[0, mine, FW : FW + RW] = attend_block_back(
        z.rest, krt[...], v[:, FW : 2 * FW], q[mine, FW : 2 * FW], gor, p_r, z.head, gkr, gvr)
    gcat[1, :, 0:FW] = (gk[...] * scale).astype(BF16)
    gcat[1, :, FW:] = (gkr[...] * scale).astype(BF16)
    gcat[2, :, 0:FW] = gv[...].astype(BF16)
    gcat[2, :, FW:] = gvr[...].astype(BF16)
    for c in loads[7:10]:
        c.wait()

    for m in (2, 1, 0):
        g = matmul(n1[...], gcat[m], 0, 0).reshape(C, SH, 2 * FW)
        gw[m] = g[:, :, 0:FW].astype(BF16)
        g = g[:, :, FW : FW + RW]
        low = jnp.concatenate([g[:, top:], jnp.zeros((C, 2 * top - SH, RW), F32)], axis=1)
        gwr[m] = jnp.concatenate([g[:, :top], low], axis=2).astype(BF16)
    for i in (2, 1, 3):
        m = at.seqs[i]

        @pl.when(m < 3)
        def _():
            up(gw, rf, sf_s, sf_r, i, m).start()
            up(gwr, rr, sr_s, sr_r, i, m).start()

    sums[...] = jnp.zeros_like(sums)

    def part(d):
        r = block(z, d)
        total = matmul(gcat[0, r], w[0], 1, 1) + matmul(gcat[1, r], w[1], 1, 1) + matmul(gcat[2, r], w[2], 1, 1)
        sums[8:9] += jnp.sum(total * norm_stats(xa[r].astype(F32))[0], axis=0, keepdims=True)
        sums[9:10] += jnp.sum(total, axis=0, keepdims=True)
        return total

    red = CtxReduce(at, part, bufs)
    red.start()
    own = part(me)

    def cols(m):
        a = jnp.sum(gcat[m].astype(F32), axis=0, keepdims=True)
        return jnp.concatenate([jnp.where(me == c, a[:, 0:FW], 0.0) for c in range(C)] + [a[:, FW : FW + RW]], axis=1)

    sums[0:4] = sm4[...]
    sums[4:5] = cols(0)
    sums[5:6] = cols(2)
    sums[6:7] = bu[...]
    se = SmallSum(at, *small[:4], small[4:])
    se.first(sums[...])

    se.second()

    def zf(i):
        return rcopy(zs.at[lax.rem(me + i, C)], land.at[i], zs_s.at[i], zs_r.at[i], ctx=lax.rem(me + i, C))

    def zrr(i):
        return rcopy(zr.at[lax.rem(me + i, C)], landr.at[i], zr_s.at[i], zr_r.at[i], ctx=lax.rem(me + i, C))

    def shift():
        return rcopy(obs, obn, ob_s, ob_r, ctx=lax.rem(me + C - 1, C))

    def tail(i):
        return rcopy(orrs, orr.at[i], orr_s, orr_r.at[i], ctx=C - 1)

    @pl.when(s < 3)
    def _():
        for i in range(1, S):
            up(gw, rf, sf_s, sf_r, i, 0).wait_recv()
            up(gwr, rr, sr_s, sr_r, i, 0).wait_recv()

        def add(j, _):
            t, u = gw[s, j].astype(F32), gwr[s, j].astype(F32)
            for i in range(1, S):
                t = t + rf[i, j].astype(F32)
                u = u + rr[i, j].astype(F32)
            zs[j] = t.astype(BF16)
            zr[j] = u.astype(BF16)
            return 0

        lax.fori_loop(0, C, add, 0)
        for i in range(1, C):
            zf(i).start()
            zrr(i).start()

    @pl.when(s == 3)
    def _():
        for i in range(1, S):
            up(gwo, ro, so_s, so_r, i).wait_recv()
            up(gwor, ror, sor_s, sor_r, i).wait_recv()
        t, u = gwo[...].astype(F32), gwor[...].astype(F32)
        for i in range(1, S):
            t = t + ro[i].astype(F32)
            u = u + ror[i].astype(F32)
        buf32[pl.ds(0, FW)] = t
        obs[...] = t.astype(BF16)
        orrs[...] = u.astype(BF16)

        @pl.when(me > 0)
        def _():
            shift().start()

        for i in range(C - 1):
            @pl.when(me == i)
            def _():
                tail(i).start()

    se.third()

    ownff.wait()
    across().wait_recv()
    for u, g in enumerate((gup, gdn)):
        g[...] = ffo[u].astype(F32) + ffz[2, u].astype(F32)
    for t in (1, 3):
        @pl.when(at.chip != (0 if t == 1 else 3))
        def _():
            fz(t).wait_recv()
            for u, g in enumerate((gup, gdn)):
                g[...] += ffz[t, u].astype(F32)

    xhat, rstd = norm_stats(xa[mine].astype(F32))
    gn1 = red.finish(own)
    gtok[...] = jnp.transpose(gh[...] + norm_back(gn1, xhat, rstd, prm[0:1]))

    @pl.when(s < 3)
    def _():
        ga[:, pl.ds(pl.multiple_of(me * FW, FW), FW)] = zs[me].astype(F32)
        remain = zr[me].astype(F32)
        for i in range(1, C):
            zf(i).wait_recv()
            zrr(i).wait_recv()
            j = lax.rem(me + C - i, C)
            ga[:, pl.ds(pl.multiple_of(j * FW, FW), FW)] = land[i].astype(F32)
            remain = remain + landr[i].astype(F32)
        ga[0:top, z.main :] = remain[:, 0:RW]
        ga[top:SH, z.main :] = remain[0 : SH - top, RW : 2 * RW]
        for i in range(1, C):
            zf(i).wait_send()
            zrr(i).wait_send()

    @pl.when(s == 3)
    def _():
        @pl.when(me < C - 1)
        def _():
            shift().wait_recv()
            buf32[pl.ds(FW, FW)] = obn[...].astype(F32)

        @pl.when(me == C - 1)
        def _():
            u = orrs[...].astype(F32)
            for i in range(C - 1):
                tail(i).wait_recv()
                u = u + orr[i].astype(F32)
            buf32[pl.ds(FW, RW)] = u

        ga[...] = buf32[pl.ds(pl.multiple_of((SH - FW) * me, 8), SH)]

        @pl.when(me > 0)
        def _():
            shift().wait_send()

        @pl.when(me < C - 1)
        def _():
            tail(0).wait_send()

    tot[...] = se.last()
    bup[s] = se.buf[2, 6:7]
    for i in range(1, S):
        bup[at.seqs_back[i]] = se.rseq[i, 6:7]
    red.close()
    se.close()
    across().wait_send()

    @pl.when(at.chip != 3)
    def _():
        fz(1).wait_send()

    @pl.when(at.chip != 0)
    def _():
        fz(3).wait_send()
    for i in range(1, S):
        m = at.seqs[i]

        @pl.when(m < 3)
        def _():
            up(gw, rf, sf_s, sf_r, i, m).wait_send()
            up(gwr, rr, sr_s, sr_r, i, m).wait_send()

        @pl.when(m == 3)
        def _():
            up(gwo, ro, so_s, so_r, i).wait_send()
            up(gwor, ror, sor_s, sor_r, i).wait_send()


def TOP(z):
    return -(-z.shard // 16) * 8


def stage_de_kernel(z, b, gba, ffr, gh, sm4, bu):
    C, S, D, FW, RW, SH, N, R, qb = z.ctx, z.seq, z.width, z.full_width, z.rest_width, z.shard, z.slot, z.rows, 256
    nq, W2, top = N // qb, 2 * FW, TOP(z)
    outs = [sds((D, R), F32), sds((SH, D), F32), sds((SH, D), F32), sds((SH, D), F32), sds((10, D), F32), sds((S, 1, D), F32)]
    V = pltpu.VMEM
    scratch = [
        V((N, D), BF16), V((N, W2), BF16), V((N, FW), BF16), V((N, W2), BF16), V((N, W2), BF16), V((nq, z.full, N, qb), BF16),
        V((z.rest, N, R), BF16), V((3, D, W2), BF16), V((N, D), BF16), V((N, D), BF16), DMA((10,)),
        V((N, FW), BF16), V((FW, N), BF16), V((RW, N), BF16), *[V((N, FW), F32) for _ in range(4)],
        V((3, N, W2), BF16), V((3, C, SH, FW), BF16), V((3, C, top, 2 * RW), BF16), V((FW, D), BF16), V((RW, D), BF16), V((10, D), F32),
        V((4, 2, SH, D), BF16), V((2, SH, D), BF16), V((2, SH, D), BF16), V((2, SH, D), BF16), DMA((4,)), DMA((4,)), DMA((2,)), DMA((2,)),
        V((S, C, SH, FW), BF16), V((S, C, top, 2 * RW), BF16), V((S, FW, D), BF16), V((S, RW, D), BF16), *[DMA((S,)) for _ in range(8)],
        V((C, SH, FW), BF16), V((C, top, 2 * RW), BF16), V((C, SH, FW), BF16), V((C, top, 2 * RW), BF16),
        *[DMA((C,)) for _ in range(4)],
        V((2 * FW, D), F32), V((FW, D), BF16), V((FW, D), BF16), V((RW, D), BF16), V((C, RW, D), BF16),
        DMA, DMA, DMA, DMA((C,)),
        *CtxReduce.scratch(z), *SmallSum.scratch(z, 10),
    ]
    gtok, ga, gup, gdn, tot, bup = call(
        partial(kernel_de, z, qb), "attention_back", outs,
        (gba.reshape(N, D), b["k"], b["o_f"], b["v"], b["q"], b["p_f"], b["p_r"], b["w3"], b["n1"], b["xa"].reshape(N, D), ffr,
         b["wo_f"], b["wo_r"], b["o_r"], gh, b["prm"], sm4, bu),
        scratch, 4, "a" * 11 + "v" * 7, "v" * 6,
    )
    names = ("gain2", "shift2", "b_o", "b_down", "b_q", "b_v", None, None, "gain1", "shift1")
    return gtok, ga, gup, gdn, {n: tot[j : j + 1] for j, n in enumerate(names) if n}, bup.reshape(-1)


def shards(tokens, lengths, block_order, attention_weights, up_weights, down_weights, norm_gains, biases, cotangent):
    z = Sizes(tokens.shape[1], tokens.shape[2], block_order.shape[0])
    i, s = lax.axis_index("ctx"), lax.axis_index("seq")
    me, D = s * z.ctx + i, z.width
    n_g, n_b = norm_gains.shape[0], biases.shape[0]
    fast = (
        z.ctx == 8 and z.seq == 4 and 0 < D - z.main <= z.shard and z.rest == 1 and z.full_width == 128
        and z.ctx * up_weights.shape[1] == D and z.rows == 2 * z.block_len and n_g <= 128 and n_b <= 384
    )
    if fast:
        b = stage_first_kernel(
            z, tokens, lengths, block_order, attention_weights, up_weights, down_weights, norm_gains, biases, cotangent)
        output, gh, _, sm4, bu, gba, ffr = stage_f_kernel(z, b)
        gtok, gw, g_up_own, g_down_own, tot, b_up_all = stage_de_kernel(z, b, gba, ffr, gh, sm4, bu)
        output, gtok, g_up_own = output.T, gtok.T, g_up_own.T
    else:
        x, cot, length = tokens[0], cotangent[0], lengths[0]
        pos = (block_order[:, None] * z.block_len + jnp.arange(z.block_len, dtype=jnp.int32)[None, :]).reshape(z.slot)
        my_pos = lax.dynamic_slice_in_dim(pos, i * z.rows, z.rows)
        live = (my_pos < length).astype(F32)[:, None]
        lanes = -(-(n_g + n_b) // 1024) * 8
        packed = jnp.pad(jnp.concatenate([norm_gains, biases]), (0, lanes * 128 - n_g - n_b)).reshape(lanes, 128)
        upstream = (live * cot.astype(F32)).astype(BF16)
        x_all, wf, wr, wo_f, wo_r = stage_a(z, x, attention_weights)
        ua = lax.all_gather(upstream, "seq", axis=0, tiled=True)
        both = lax.all_gather(packed, ("seq", "ctx"), axis=0).reshape(z.seq * z.ctx, lanes * 128)
        gains = both[:, :n_g].reshape(-1).astype(F32)
        bias = both[:, n_g : n_g + n_b].reshape(-1).astype(F32)
        row = lambda v: v[None, :]
        piece = [row(bias[j * D : (j + 1) * D]) for j in range(6)]
        gain1, gain2 = row(gains[:D]), row(gains[D:])
        units = z.ctx * up_weights.shape[1]
        b_up = row(lax.dynamic_slice_in_dim(bias[6 * D :], s * units, units))
        prm = dict(gain2=gain2, shift2=piece[4], b_o=piece[3], b_down=piece[5], b_up=b_up)
        fslice = lambda v: lax.dynamic_slice(v, (0, i * z.full_width), (1, z.full_width))
        up_t = lax.all_gather(up_weights.T, "ctx", axis=0, tiled=True)
        down = lax.all_gather(down_weights, "ctx", axis=0, tiled=True)
        b = stage_b(z, x_all, wf, wr, gain1, piece[0], fslice(piece[1]), piece[1][:, z.main :],
                    fslice(piece[2]), piece[2][:, z.main :], pos, length)
        output, gh, gb, g_up_t, g_down, small = stage_c(z, b, wo_f, wo_r, x, upstream, ua, live, up_t, down, prm)
        g_up_own = lax.psum_scatter(g_up_t, "ctx", scatter_dimension=0, tiled=True).astype(F32).T
        g_down_own = lax.psum_scatter(g_down, "ctx", scatter_dimension=0, tiled=True).astype(F32)
        gba = lax.all_gather(gb, "ctx", axis=0, tiled=True) if z.full else None
        d = stage_d(z, b, gb, gba, wo_f, wo_r)
        gtok, gw, tot, b_up_all = stage_e(z, d, wf, wr, x, gh, gain1, small)
    g_gain = lax.dynamic_slice_in_dim(jnp.concatenate([tot["gain1"][0], tot["gain2"][0]]), me * n_g, n_g)
    g_bias = lax.dynamic_slice_in_dim(jnp.concatenate([tot[n][0] for n in ("shift1", "b_q", "b_v", "b_o", "shift2", "b_down")] + [b_up_all]), me * n_b, n_b)
    return output[None], gtok[None], gw, g_up_own, g_down_own, g_gain, g_bias


def solution(mesh):
    in_specs = (
        P("seq", "ctx", None), P("seq"), P(), P(("seq", "ctx"), None), P(None, ("seq", "ctx")),
        P(("seq", "ctx"), None), P(("seq", "ctx")), P(("seq", "ctx")), P("seq", "ctx", None),
    )
    out_specs = (
        P("seq", "ctx", None), P("seq", "ctx", None), P(("seq", "ctx"), None), P(None, ("seq", "ctx")),
        P(("seq", "ctx"), None), P(("seq", "ctx")), P(("seq", "ctx")),
    )
    return jax.shard_map(shards, mesh=mesh, in_specs=in_specs, out_specs=out_specs, check_vma=False)
```

```python
import math
from functools import partial

import jax
import jax.numpy as jnp
from jax import lax
from jax.experimental import pallas as pl
from jax.experimental.pallas import tpu as pltpu
from jax.sharding import PartitionSpec as P

HEADS = 17
EPS = 1e-05
F32 = jnp.float32
BF16 = jnp.bfloat16


def norm_stats(values):
    centre = values - jnp.mean(values, axis=-1, keepdims=True)
    rstd = lax.rsqrt(jnp.mean(centre * centre, axis=-1, keepdims=True) + EPS)
    return centre * rstd, rstd


def norm_back(grad, xhat, rstd, gain):
    e = grad * gain
    mean_e = jnp.mean(e, axis=-1, keepdims=True)
    mean_ex = jnp.mean(e * xhat, axis=-1, keepdims=True)
    return (e - mean_e - xhat * mean_ex) * rstd


def dot(a, b, ca, cb):
    return lax.dot_general(a, b, (((ca,), (cb,)), ((), ())), preferred_element_type=F32)


def rows_sum(v):
    return jnp.sum(v.astype(F32), axis=0, keepdims=True)


class Sizes:
    def __init__(self, rows, width, block_count):
        self.rows, self.width = rows, width
        self.ctx, self.seq = lax.axis_size("ctx"), lax.axis_size("seq")
        self.slot = rows * self.ctx
        self.block_len = self.slot // block_count
        self.head = width // HEADS
        self.full = HEADS // self.ctx
        self.full_width = self.full * self.head
        self.main = self.full_width * self.ctx
        self.rest = HEADS - self.full * self.ctx
        self.rest_width = self.rest * self.head
        self.shard = width // self.ctx


def stage_a(z, x, w):
    k = lax.axis_index("ctx")
    x_all = lax.all_gather(x, "ctx", axis=0, tiled=True)
    w_all = lax.all_gather(w, "seq", axis=0)
    wm = w_all[:3, :, : z.main].reshape(3, z.shard, z.ctx, z.full_width)
    wf = lax.all_to_all(wm, "ctx", split_axis=2, concat_axis=1, tiled=True).reshape(
        3, z.width, z.full_width
    )
    wr = lax.all_gather(w_all[:3, :, z.main :], "ctx", axis=1, tiled=True)
    wo = lax.all_gather(w_all[3], "ctx", axis=0, tiled=True)
    wo_f = lax.dynamic_slice_in_dim(wo, k * z.full_width, z.full_width)
    wo_r = wo[z.main :]
    return x_all, wf, wr, wo_f, wo_r


def heads_of(v, h):
    return v.reshape(v.shape[0], -1, h).transpose(1, 0, 2)


def attend(z, q, k, v, qpos, kpos, length):
    s = jnp.einsum("hqd,hkd->hkq", heads_of(q, z.head), heads_of(k, z.head), preferred_element_type=F32)
    s = s * (z.head ** -0.5)
    seen = (kpos[:, None] <= qpos[None, :]) & (kpos[:, None] < length)
    s = jnp.where(seen[None], s, -1e30)
    e = jnp.exp(s - jnp.max(s, axis=1, keepdims=True))
    p = (e / jnp.sum(e, axis=1, keepdims=True)).astype(BF16)
    o = jnp.einsum("hkq,hkd->qhd", p, heads_of(v, z.head), preferred_element_type=F32)
    return p, o.reshape(q.shape).astype(BF16)


def stage_b(z, x_all, wf, wr, gain, shift, bq_f, bq_r, bv_f, bv_r, pos, length):
    i = lax.axis_index("ctx")
    n1 = (norm_stats(x_all.astype(F32))[0] * gain + shift).astype(BF16)
    mine = lax.dynamic_slice_in_dim(n1, i * z.rows, z.rows)
    qpos = lax.dynamic_slice_in_dim(pos, i * z.rows, z.rows)
    out = dict(n1=n1)
    if z.full:
        q = (dot(n1, wf[0], 1, 0) + bq_f).astype(BF16)
        k = dot(n1, wf[1], 1, 0).astype(BF16)
        v = (dot(n1, wf[2], 1, 0) + bv_f).astype(BF16)
        p, o = attend(z, q, k, v, pos, pos, length)
        out.update(q_f=q, k_f=k, v_f=v, p_f=p, o_f=o)
    if z.rest:
        q = (dot(mine, wr[0], 1, 0) + bq_r).astype(BF16)
        k = dot(n1, wr[1], 1, 0).astype(BF16)
        v = (dot(n1, wr[2], 1, 0) + bv_r).astype(BF16)
        p, o = attend(z, q, k, v, qpos, pos, length)
        out.update(q_r=q, k_r=k, v_r=v, p_r=p, o_r=o)
    return out


def stage_c(z, b, wo_f, wo_r, x, upstream, ua, live, up_t, down, prm):
    branch = prm["b_o"]
    if z.full:
        part = dot(b["o_f"], wo_f, 1, 0).astype(BF16)
        branch = branch + lax.psum_scatter(part.astype(F32), "ctx", scatter_dimension=0, tiled=True)
    if z.rest:
        branch = branch + dot(b["o_r"], wo_r, 1, 0)
    hidden = x.astype(F32) + branch
    xhat, rstd = norm_stats(hidden)
    n2 = (xhat * prm["gain2"] + prm["shift2"]).astype(BF16)
    n2a = lax.all_gather(n2, "seq", axis=0, tiled=True)
    pre = dot(n2a, up_t, 1, 1) + prm["b_up"]
    cdf = 0.5 * (1.0 + lax.erf(pre * (0.5 ** 0.5)))
    act = (pre * cdf).astype(BF16)
    dgelu = cdf + pre * jnp.exp(-0.5 * pre * pre) * (1.0 / math.sqrt(2.0 * math.pi))
    gact = dot(ua, down, 1, 1)
    gpre = (gact * dgelu).astype(BF16)
    gn2p = dot(gpre, up_t, 1, 0).astype(BF16)
    gn2 = lax.psum_scatter(gn2p.astype(F32), "seq", scatter_dimension=0, tiled=True)
    ffp = dot(act, down, 1, 0).astype(BF16)
    ff = lax.psum_scatter(ffp.astype(F32), "seq", scatter_dimension=0, tiled=True)
    output = (live * (hidden + ff + prm["b_down"])).astype(BF16)
    g_up_t = dot(gpre, n2a, 0, 0).astype(BF16)
    g_down = dot(act, ua, 0, 0).astype(BF16)
    gh = upstream.astype(F32) + norm_back(gn2, xhat, rstd, prm["gain2"])
    gb = gh.astype(BF16)
    small = dict(gain2=rows_sum(gn2 * xhat), shift2=rows_sum(gn2), b_o=rows_sum(gb),
                 b_down=rows_sum(upstream), b_up=rows_sum(gpre))
    return output, gh, gb, g_up_t, g_down, small


def attend_back(z, q, k, v, p, go):
    gp = jnp.einsum("hqd,hkd->hkq", heads_of(go, z.head), heads_of(v, z.head), preferred_element_type=F32)
    pf = p.astype(F32)
    delta = jnp.sum(gp * pf, axis=1, keepdims=True)
    gs = (pf * (gp - delta)).astype(BF16)
    sc = z.head ** -0.5
    gq = jnp.einsum("hkq,hkd->qhd", gs, heads_of(k, z.head), preferred_element_type=F32) * sc
    gk = jnp.einsum("hkq,hqd->khd", gs, heads_of(q, z.head), preferred_element_type=F32) * sc
    gv = jnp.einsum("hkq,hqd->khd", p, heads_of(go, z.head), preferred_element_type=F32)
    return gq.reshape(q.shape).astype(BF16), gk.reshape(k.shape).astype(BF16), gv.reshape(v.shape).astype(BF16)


def stage_d(z, b, gb, gba, wo_f, wo_r):
    i = lax.axis_index("ctx")
    n1 = b["n1"]
    mine = lax.dynamic_slice_in_dim(n1, i * z.rows, z.rows)
    out = {}
    if z.full:
        go = dot(gba, wo_f, 1, 1).astype(BF16)
        gq, gk, gv = attend_back(z, b["q_f"], b["k_f"], b["v_f"], b["p_f"], go)
        out.update(gq_f=gq, gk_f=gk, gv_f=gv, gwo_f=dot(b["o_f"], gba, 0, 0))
        out["gw_f"] = jnp.stack([dot(n1, g, 0, 0) for g in (gq, gk, gv)])
    if z.rest:
        go = dot(gb, wo_r, 1, 1).astype(BF16)
        gq, gk, gv = attend_back(z, b["q_r"], b["k_r"], b["v_r"], b["p_r"], go)
        out.update(gq_r=gq, gk_r=gk, gv_r=gv, gwo_r=dot(b["o_r"], gb, 0, 0))
        out["gw_r"] = jnp.stack([dot(mine, gq, 0, 0), dot(n1, gk, 0, 0), dot(n1, gv, 0, 0)])
    return out


def stage_e(z, d, wf, wr, x, gh, gain1, small):
    i, s = lax.axis_index("ctx"), lax.axis_index("seq")
    part = 0.0
    own = 0.0
    if z.full:
        part = part + dot(d["gq_f"], wf[0], 1, 1) + dot(d["gk_f"], wf[1], 1, 1) + dot(d["gv_f"], wf[2], 1, 1)
    if z.rest:
        part = part + dot(d["gk_r"], wr[1], 1, 1) + dot(d["gv_r"], wr[2], 1, 1)
        own = own + dot(d["gq_r"], wr[0], 1, 1)
    gn1 = own + lax.psum_scatter(part.astype(BF16).astype(F32), "ctx", scatter_dimension=0, tiled=True)
    xhat, rstd = norm_stats(x.astype(F32))
    gtok = gh + norm_back(gn1, xhat, rstd, gain1)
    small = dict(small, gain1=rows_sum(gn1 * xhat), shift1=rows_sum(gn1))
    row = jnp.zeros((1, z.width), F32)
    for name, key in (("b_q", "gq"), ("b_v", "gv")):
        r = row
        if z.full:
            r = lax.dynamic_update_slice(r, rows_sum(d[key + "_f"]), (0, i * z.full_width))
        if z.rest:
            r = r.at[:, z.main :].add(rows_sum(d[key + "_r"]))
        small[name] = r
    full = jnp.zeros((4, z.width, z.width), F32)
    if z.full:
        full = lax.dynamic_update_slice(full, d["gw_f"], (0, 0, i * z.full_width))
        full = lax.dynamic_update_slice(full, d["gwo_f"][None], (3, i * z.full_width, 0))
    if z.rest:
        full = full.at[:3, :, z.main :].add(d["gw_r"])
        full = full.at[3, z.main :, :].add(d["gwo_r"])
    gw = lax.psum_scatter(full.reshape(4 * z.width, z.width).astype(BF16), ("seq", "ctx"), scatter_dimension=0, tiled=True)
    b_up_all = lax.all_gather(lax.psum(small.pop("b_up"), "ctx")[0], "seq", axis=0, tiled=True)
    names = list(small)
    tot = lax.psum(jnp.concatenate([small[n] for n in names]), ("seq", "ctx"))
    return gtok, gw.astype(F32), {n: tot[j : j + 1] for j, n in enumerate(names)}, b_up_all


MESH = pl.DeviceIdType.MESH
DMA = pltpu.SemaphoreType.DMA
VMEM_LIMIT = 56 << 20


def rcopy(src, dst, ssem, rsem, **dev):
    return pltpu.make_async_remote_copy(
        src_ref=src, dst_ref=dst, send_sem=ssem, recv_sem=rsem, device_id=dev, device_id_type=MESH
    )


def greet(ctx_peers, seq_peers, wait=True):
    sem = pltpu.get_barrier_semaphore()
    for p in ctx_peers:
        pl.semaphore_signal(sem, inc=1, device_id={"ctx": p}, device_id_type=MESH)
    for p in seq_peers:
        pl.semaphore_signal(sem, inc=1, device_id={"seq": p}, device_id_type=MESH)
    if wait:
        met(len(ctx_peers) + len(seq_peers))


def met(count):
    pl.semaphore_wait(pltpu.get_barrier_semaphore(), count)


class Place:
    def __init__(self, z):
        self.k, self.s = lax.axis_index("ctx"), lax.axis_index("seq")
        self.chips, self.ctx = z.ctx // 2, z.ctx
        self.core = lax.rem(self.k, 2)
        self.chip = self.k // 2
        self.sib = self.k + 1 - 2 * self.core
        self.edge = (self.chip == 0) | (self.chip == self.chips - 1)
        self.ring = [lax.rem(self.chip + i, self.chips) for i in range(self.chips)]
        self.same = [2 * q + self.core for q in self.ring]
        self.back = [2 * lax.rem(self.chip + self.chips - i, self.chips) + self.core for i in range(self.chips)]
        self.seqs = [lax.rem(self.s + i, z.seq) for i in range(z.seq)]
        self.seqs_back = [lax.rem(self.s + z.seq - i, z.seq) for i in range(z.seq)]


def call(body, name, outs, ins, scratch, cid, in_spaces, out_spaces, cost=None):
    spaces = {"v": pltpu.VMEM, "a": pl.ANY}
    return pl.pallas_call(
        body,
        name=name,
        out_shape=outs,
        in_specs=[pl.BlockSpec(memory_space=spaces[c]) for c in in_spaces],
        out_specs=[pl.BlockSpec(memory_space=spaces[c]) for c in out_spaces],
        scratch_shapes=scratch,
        compiler_params=pltpu.CompilerParams(
            collective_id=cid, has_side_effects=True, vmem_limit_bytes=VMEM_LIMIT
        ),
        cost_estimate=cost,
    )(*ins)


def sds(shape, dtype=BF16):
    return jax.ShapeDtypeStruct(shape, dtype)


class CtxGather:
    def __init__(self, at, own, dst, sems):
        self.at, self.own, self.dst = at, own, dst
        self.ss, self.rs, self.fs, self.fr, self.lo, self.ho = sems

    def to(self, i):
        return rcopy(self.own, self.dst.at[self.at.k], self.ss.at[i], self.rs.at[i], ctx=self.at.same[i])

    def side(self, i):
        b = self.dst.at[self.at.back[i]]
        return rcopy(b, b, self.fs.at[i], self.fr.at[i], ctx=self.at.sib)

    def hop(self, i, step):
        b = self.dst.at[self.at.back[i]]
        return rcopy(b, b, self.ho, self.rs.at[2], ctx=lax.rem(self.at.k + step + self.at.ctx, self.at.ctx))

    def sibling(self):
        return rcopy(self.own, self.dst.at[self.at.k], self.fs.at[0], self.fr.at[0], ctx=self.at.sib)

    def local(self):
        return pltpu.make_async_copy(self.own, self.dst.at[self.at.k], self.lo)

    def send(self):
        @pl.when(self.at.chip != 3)
        def _():
            self.to(1).start()

        @pl.when(self.at.chip != 0)
        def _():
            self.to(3).start()

        self.sibling().start()
        self.local().start()

    def send_rest(self):
        @pl.when(self.at.chip == 0)
        def _():
            self.to(1).wait_send()
            self.to(3).start()
            self.to(2).start()

        @pl.when(self.at.chip == 3)
        def _():
            self.to(3).wait_send()
            self.to(1).start()
            self.to(2).start()

        @pl.when(self.at.chip == 1)
        def _():
            self.to(3).wait_recv()
            self.hop(3, -2).start()

        @pl.when(self.at.chip == 2)
        def _():
            self.to(1).wait_recv()
            self.hop(1, 2).start()

    def forward(self, i):
        if i == 2:
            self.to(i).wait_recv()
        else:
            @pl.when(self.at.chip != (2 if i == 1 else 1))
            def _():
                self.to(i).wait_recv()
        self.side(i).start()

    def finish(self):
        self.local().wait()
        self.sibling().wait()
        for i in (1, 3, 2):
            self.side(i).wait()

        @pl.when(self.at.chip != 0)
        def _():
            self.to(1).wait_send()

        @pl.when(self.at.chip != 3)
        def _():
            self.to(3).wait_send()

        @pl.when(self.at.edge)
        def _():
            self.to(2).wait_send()

        @pl.when(~self.at.edge)
        def _():
            self.hop(1, 2).wait_send()

    @staticmethod
    def scratch(z):
        return [DMA((4,)), DMA((4,)), DMA((4,)), DMA((4,)), DMA, DMA]


class DirectGather:
    def __init__(self, at, own, dst, sems):
        self.at, self.own, self.dst, self.sems = at, own, dst, sems

    def send(self):
        at, ss, rs = self.at, self.sems[0], self.sems[1]
        for i in range(1, at.chips):
            rcopy(self.own, self.dst.at[at.k], ss.at[i], rs.at[i], ctx=at.same[i]).start()
        rcopy(self.own, self.dst.at[at.k], ss.at[0], rs.at[0], ctx=at.sib).start()
        pltpu.make_async_copy(self.own, self.dst.at[at.k], self.sems[4]).start()

    def forward(self, i):
        at, ss, rs, fs, fr = self.at, *self.sems[:4]
        src = at.back[i]
        rcopy(self.own, self.dst.at[src], ss.at[i], rs.at[i], ctx=at.same[i]).wait_recv()
        rcopy(self.dst.at[src], self.dst.at[src], fs.at[i], fr.at[i], ctx=at.sib).start()

    def finish(self):
        at, ss, rs, fs, fr = self.at, *self.sems[:4]
        pltpu.make_async_copy(self.own, self.dst.at[at.k], self.sems[4]).wait()
        rcopy(self.own, self.dst.at[at.k], ss.at[0], rs.at[0], ctx=at.sib).wait()
        for i in range(1, at.chips):
            rcopy(self.own, self.dst.at[at.k], ss.at[i], rs.at[i], ctx=at.same[i]).wait_send()
            rcopy(self.own, self.dst.at[at.k], fs.at[i], fr.at[i], ctx=at.sib).wait()

    @staticmethod
    def scratch(z):
        n = z.ctx // 2
        return [DMA((n,)), DMA((n,)), DMA((n,)), DMA((n,)), DMA]


def matmul(a, b, ca=1, cb=0):
    return lax.dot_general(a, b, (((ca,), (cb,)), ((), ())), preferred_element_type=F32)


def block(z, d):
    return pl.ds(pl.multiple_of(d * z.rows, z.rows), z.rows)


class CtxReduce:
    def __init__(self, at, part, bufs):
        self.at, self.part = at, part
        self.sb, self.sr, self.zb, self.zr, self.mid, self.ss, self.sn, self.zs, self.zn, self.ms, self.mn = bufs
        self.first = jnp.where(at.chip == 3, 1, 3)
        self.second = 4 - self.first

    def core_at(self, t):
        return 2 * lax.rem(self.at.chip + t, 4) + self.at.core

    def sib(self, t):
        return rcopy(self.sb.at[t], self.sr.at[t], self.ss.at[t], self.sn.at[t], ctx=self.at.sib)

    def far(self, t):
        return rcopy(self.zb.at[t], self.zr.at[t], self.zs.at[t], self.zn.at[t], ctx=self.core_at(t))

    def via(self):
        return rcopy(self.zb.at[self.first], self.mid, self.ms, self.mn, ctx=self.core_at(self.second))

    def start(self):
        at = self.at
        for t in (self.first, self.second, 2, 0):
            self.sb[t] = self.part(self.core_at(t) + 1 - 2 * at.core).astype(BF16)
            self.sib(t).start()
        for n, t in enumerate((self.first, self.second, 2)):
            mine = self.part(self.core_at(t))
            self.sib(t).wait_recv()
            mine = mine + self.sr[t].astype(F32)
            self.zb[t] = mine.astype(BF16)
            if n < 2:
                @pl.when(~at.edge)
                def _():
                    self.far(t).start()
            if n == 0:
                @pl.when(at.edge)
                def _():
                    self.via().start()
            if n == 2:
                @pl.when(at.edge)
                def _():
                    self.via().wait_send()
                    self.far(self.second).start()

                @pl.when(~at.edge)
                def _():
                    self.via().wait_recv()
                    self.zb[2] = (mine + self.mid[...].astype(F32)).astype(BF16)

                self.far(2).start()

    def finish(self, own=None):
        at = self.at
        total = self.part(at.k) if own is None else own
        self.sib(0).wait_recv()
        total = total + self.sr[0].astype(F32)
        for t in (1, 3, 2):
            if t == 2:
                self.far(2).wait_recv()
            else:
                none = at.chip == (0 if t == 1 else 3)

                @pl.when(none)
                def _():
                    self.zr[t] = jnp.zeros(self.zr.shape[1:], BF16)

                @pl.when(~none)
                def _():
                    self.far(t).wait_recv()
            total = total + self.zr[t].astype(F32)
        return total

    def close(self):
        for t in range(4):
            self.sib(t).wait_send()
        self.far(2).wait_send()
        self.far(self.second).wait_send()

        @pl.when(~self.at.edge)
        def _():
            self.far(self.first).wait_send()

    @staticmethod
    def scratch(z):
        return [pltpu.VMEM((4, z.rows, z.width), BF16)] * 4 + [pltpu.VMEM((z.rows, z.width), BF16)] + [DMA((4,))] * 4 + [DMA, DMA]


NEG = -1e30


def turn(v):
    return jnp.transpose(v.astype(F32)).astype(BF16)


def of_head(v, h, head):
    lane = lax.broadcasted_iota(jnp.int32, v.shape, 1) // head
    return jnp.where(lane == h, v.astype(F32), 0.0)


def attend_block(heads, k, v_t, q, mask, head, p_ref):
    parts = []
    for h in range(heads):
        qh = (of_head(q, h, head) * head ** -0.5).astype(BF16)
        s = matmul(k, qh, 1, 1) + mask
        e = jnp.exp(s - jnp.max(s, axis=0, keepdims=True))
        p = (e * (1.0 / jnp.sum(e, axis=0, keepdims=True))).astype(BF16)
        p_ref[h] = p
        parts.append(matmul(v_t[h * head : (h + 1) * head], p))
    o_t = parts[0] if len(parts) == 1 else jnp.concatenate(parts, axis=0)
    return jnp.transpose(o_t).astype(BF16)


class FarGather:
    def __init__(self, at, own, dst, sems):
        self.at, self.own, self.dst = at, own, dst
        self.ss, self.rs, self.fs, self.fr, self.lo, self.ho = sems

    def each(self):
        return range(len(self.own))

    def to(self, u, i):
        return rcopy(self.own[u], self.dst[u].at[self.at.k], self.ss.at[u, i], self.rs.at[u, i], ctx=self.at.same[i])

    def side(self, u, i):
        b = self.dst[u].at[self.at.back[i]]
        return rcopy(b, b, self.fs.at[u, i], self.fr.at[u, i], ctx=self.at.sib)

    def hop(self, u, i, step):
        b = self.dst[u].at[self.at.back[i]]
        return rcopy(b, b, self.ho.at[u], self.rs.at[u, 2], ctx=lax.rem(self.at.k + step + self.at.ctx, self.at.ctx))

    def local(self, u):
        return pltpu.make_async_copy(self.own[u], self.dst[u].at[self.at.k], self.lo.at[u])

    def sibling(self, u):
        return rcopy(self.own[u], self.dst[u].at[self.at.k], self.fs.at[u, 0], self.fr.at[u, 0], ctx=self.at.sib)

    def start(self):
        for u in self.each():
            @pl.when(self.at.chip != 3)
            def _():
                self.to(u, 1).start()

            @pl.when(self.at.chip != 0)
            def _():
                self.to(u, 3).start()

            self.local(u).start()
            self.sibling(u).start()

    def relay(self):
        for chip, near in ((0, 1), (3, 3)):
            @pl.when(self.at.chip == chip)
            def _():
                for u in self.each():
                    self.to(u, near).wait_send()
                    self.to(u, 4 - near).start()
                    self.to(u, 2).start()

        for chip, near, step in ((1, 3, -2), (2, 1, 2)):
            @pl.when(self.at.chip == chip)
            def _():
                for u in self.each():
                    self.to(u, near).wait_recv()
                    self.hop(u, near, step).start()

    def forward(self):
        for i in (1, 3, 2):
            for u in self.each():
                if i == 2:
                    self.to(u, i).wait_recv()
                else:
                    @pl.when(self.at.chip != (2 if i == 1 else 1))
                    def _():
                        self.to(u, i).wait_recv()
                self.side(u, i).start()

    def finish(self):
        for u in self.each():
            self.local(u).wait()
            self.sibling(u).wait()
            for i in (1, 3, 2):
                self.side(u, i).wait()

            @pl.when(self.at.chip != 0)
            def _():
                self.to(u, 1).wait_send()

            @pl.when(self.at.chip != 3)
            def _():
                self.to(u, 3).wait_send()

            @pl.when(self.at.edge)
            def _():
                self.to(u, 2).wait_send()

            @pl.when(~self.at.edge)
            def _():
                self.hop(u, 1, 2).wait_send()

    @staticmethod
    def scratch(z):
        return [DMA((2, 4)), DMA((2, 4)), DMA((2, 4)), DMA((2, 4)), DMA((2,)), DMA((2,))]


def place_rows(flat, piece, offset):
    wide = piece.shape[1] + 128
    base, shift = offset // 128 * 128, offset % 128
    padded = jnp.concatenate([piece, jnp.zeros((8, 128), F32)], axis=1)
    flat[:, base : base + wide] += pltpu.roll(padded, shift, 1) if shift else padded


def take_row(flat, start, width):
    base, shift = start // 128 * 128, start % 128
    wide = -(-(shift + width) // 128) * 128
    v = flat[:, base : base + wide]
    if shift:
        v = pltpu.roll(v, wide - shift, 1)
    return v[0:1, 0:width]


def kernel_first(z, n_g, n_b, qb, order, length, xt, ct, wv, w, pk, upw, dnw,
                 ua, wf, wo2, wol, upa, dna, xao, n1o, qo, ko, vo, p_fo, p_ro, o_fo,
                 prm, live, wo_f, o_r, hid, xh, rs_o, n2a,
                 x, up, wr, pa, xa, n1, q, k, v, p_f, p_r, o_f, vt, vrt, wvm, wo_r, kp, qp, gflat, bflat, n2,
                 mz_s, mz_r, rz_s, rz_r, mx_s, mx_r, us, ur, oz_s, oz_r, ox_s, ox_r, loc, pz_s, pz_r, px_s, px_r, wl, wb, ns, nr, *rest):
    at = Place(z)
    me, s, C, S, FW, RW, SH, D, R, N = at.k, at.s, z.ctx, z.seq, z.full_width, z.rest_width, z.shard, z.width, z.rows, z.slot
    ffg = FarGather(at, (upw, dnw), (upa, dna), rest[:6])
    tok = CtxGather(at, x, xa, rest[6:12])
    bufs = rest[12:]
    others = [lax.rem(me + i, C) for i in range(1, C)]
    greet(others, at.seqs[1:], False)

    x[...] = jnp.transpose(xt[...].astype(F32)).astype(BF16)
    half, lens = z.block_len, length[0]
    row = lax.broadcasted_iota(jnp.int32, (R, 128), 0)
    where = jnp.where(row < half, order[2 * me] * half + row, order[2 * me + 1] * half + row - half)
    live[...] = jnp.where(where < lens, 1.0, 0.0)
    up[...] = (jnp.transpose(ct[...].astype(F32)) * live[:, 0:1]).astype(BF16)
    wr[...] = jnp.zeros_like(wr)
    wr[:, 0:RW] = wv[:, z.main :]
    met(C + S - 2)

    def rows_of(j):
        return pl.ds(pl.multiple_of(j * SH, 8), SH)

    def cols(j):
        return wv.at[:, pl.ds(pl.multiple_of(j * FW, FW), FW)]

    def main(m, j):
        return wf.at[m, rows_of(j), pl.ds(0, FW)]

    def tail(m, j):
        return wf.at[m, rows_of(j), pl.ds(FW, FW)]

    def both(m, j):
        return wf.at[m, rows_of(j)]

    before, after = wo2.at[pl.ds(0, SH)], wo2.at[pl.ds(SH, SH)]
    lastrows = w.at[pl.ds(z.main - (C - 1) * SH, RW)]

    for i in range(1, C):
        rcopy(pk, pa.at[s, me], pz_s.at[i], pz_r.at[i], ctx=others[i - 1]).start()
    pltpu.make_async_copy(pk, pa.at[s, me], loc.at[3]).start()

    @pl.when(s < 3)
    def _():
        for i in range(1, C):
            j = lax.rem(me + i, C)
            rcopy(cols(j), main(s, me), mz_s.at[i], mz_r.at[me], ctx=j).start()
            rcopy(wr, tail(s, me), rz_s.at[i], rz_r.at[me], ctx=j).start()
        pltpu.make_async_copy(cols(me), main(s, me), loc.at[0]).start()
        pltpu.make_async_copy(wr, tail(s, me), loc.at[1]).start()

    @pl.when(s == 3)
    def _():
        @pl.when(me < C - 1)
        def _():
            rcopy(w, before, oz_s.at[0], oz_r.at[0], ctx=lax.rem(me + 1, C)).start()

        @pl.when(me == C - 1)
        def _():
            for i in range(1, C):
                rcopy(lastrows, wol, oz_s.at[i], oz_r.at[1], ctx=lax.rem(me + i, C)).start()
            pltpu.make_async_copy(lastrows, wol, loc.at[1]).start()

        pltpu.make_async_copy(w, after, loc.at[0]).start()
        for i in range(1, 4):
            rcopy(w, after, ox_s.at[0, i], ox_r.at[0], seq=at.seqs[i]).start()

    for i in range(1, C):
        rcopy(pk, pa.at[s, lax.rem(me + C - i, C)], pz_s.at[i], pz_r.at[i], ctx=me).wait_recv()
    pltpu.make_async_copy(pk, pa.at[s, me], loc.at[3]).wait()
    for i in range(1, S):
        rcopy(pa.at[s], pa.at[s], px_s.at[i], px_r.at[i], seq=at.seqs[i]).start()

    for b in range(N // half):
        p = order[b] * half + lax.broadcasted_iota(jnp.int32, (half, 128), 0)
        kp[b * half : (b + 1) * half] = jnp.where(p < lens, p, 1 << 30)
    lane = lax.broadcasted_iota(jnp.int32, (8, 128), 1)
    for b in range(N // 128):
        qp[:, b * 128 : (b + 1) * 128] = jnp.where(
            lane < half, order[2 * b] * half + lane, order[2 * b + 1] * half + lane - half)

    @pl.when(s < 3)
    def _():
        for n in range(C):
            src = lax.rem(me + C - n, C)
            if n == 0:
                pltpu.make_async_copy(cols(me), main(s, me), loc.at[0]).wait()
                pltpu.make_async_copy(wr, tail(s, me), loc.at[1]).wait()
            else:
                rcopy(cols(me), main(s, src), mz_s.at[0], mz_r.at[src], ctx=me).wait_recv()
                rcopy(wr, tail(s, src), rz_s.at[0], rz_r.at[src], ctx=me).wait_recv()
            for i in range(1, 4):
                rcopy(both(s, src), both(s, src), mx_s.at[n, i], mx_r.at[s, src], seq=at.seqs[i]).start()

    @pl.when(s == 3)
    def _():
        pltpu.make_async_copy(w, after, loc.at[0]).wait()

        @pl.when(me > 0)
        def _():
            rcopy(w, before, oz_s.at[0], oz_r.at[0], ctx=me).wait_recv()
            for i in range(1, 4):
                rcopy(before, before, ox_s.at[1, i], ox_r.at[1], seq=at.seqs[i]).start()

        @pl.when(me < C - 1)
        def _():
            rcopy(lastrows, wol, oz_s.at[1], oz_r.at[1], ctx=me).wait_recv()

        @pl.when(me == C - 1)
        def _():
            pltpu.make_async_copy(lastrows, wol, loc.at[1]).wait()

        for i in range(1, 4):
            rcopy(wol, wol, ox_s.at[2, i], ox_r.at[2], seq=at.seqs[i]).start()

    tok.send()
    ffg.start()

    for i in range(1, S):
        rcopy(pa.at[s], pa.at[at.seqs_back[i]], px_s.at[i], px_r.at[i], seq=s).wait()
    gflat[...] = jnp.zeros_like(gflat)
    bflat[...] = jnp.zeros_like(bflat)
    for d in range(S * C):
        t = pa[d // C, d % C].astype(F32)
        place_rows(gflat, jnp.broadcast_to(t[0:1], (8, 128)), d * n_g)
        place_rows(bflat, jnp.broadcast_to(jnp.concatenate([t[1:2], t[2:3], t[3:4]], axis=1), (8, 384)), d * n_b)
    for j in range(2):
        prm[j : j + 1] = take_row(gflat, j * D, D)
    for j in range(10):
        prm[2 + j : 3 + j] = take_row(bflat, j * D, D)

    def norm_rows(j, src):
        n1[block(z, j)] = (norm_stats(src.astype(F32))[0] * prm[0:1] + prm[2:3]).astype(BF16)

    tok.send_rest()
    norm_rows(me, x[...])
    for i in (1, 3, 2):
        tok.forward(i)
        norm_rows(at.back[i], xa[at.back[i]])
    tok.finish()

    def norm_other(j, _):
        d = 2 * j + 1 - at.core
        norm_rows(d, xa[d])
        return 0

    lax.fori_loop(0, at.chips, norm_other, 0)
    ffg.relay()

    for m in range(3):
        @pl.when(s != m)
        def _():
            for src in range(C):
                rcopy(both(m, src), both(m, src), mx_s.at[0, 0], mx_r.at[m, src], seq=s).wait_recv()
    wload = [pltpu.make_async_copy(wf.at[m], wvm.at[m], wl.at[m]) for m in range(3)]
    for c in wload:
        c.start()

    @pl.when(s != 3)
    def _():
        rcopy(w, after, ox_s.at[0, 0], ox_r.at[0], seq=s).wait_recv()

        @pl.when(me > 0)
        def _():
            rcopy(w, before, ox_s.at[1, 0], ox_r.at[1], seq=s).wait_recv()

        rcopy(wol, wol, ox_s.at[2, 0], ox_r.at[2], seq=s).wait_recv()

    wload += [
        pltpu.make_async_copy(wo2.at[pl.ds(pl.multiple_of(SH - (SH - FW) * me, 8), FW)], wo_f, wl.at[3]),
        pltpu.make_async_copy(wol, wo_r, wl.at[4]),
    ]
    wload[3].start()
    wload[4].start()

    def bias(j):
        a = prm[j : j + 1]
        own = jnp.zeros((1, FW), F32)
        for c in range(C):
            own = own + jnp.where(me == c, a[:, c * FW : (c + 1) * FW], 0.0)
        return jnp.concatenate([own, a[:, z.main :], jnp.zeros((1, FW - RW), F32)], axis=1)

    wload[0].wait()
    q[...] = (matmul(n1[...], wvm[0]) + bias(3)).astype(BF16)
    wload[1].wait()
    k[...] = matmul(n1[...], wvm[1]).astype(BF16)
    wload[2].wait()
    v[...] = (matmul(n1[...], wvm[2]) + bias(4)).astype(BF16)
    backs = [pltpu.make_async_copy(a, b, wb.at[i]) for i, (a, b) in enumerate(((n1, n1o), (q, qo), (k, ko), (v, vo), (xa, xao)))]
    for c in backs:
        c.start()
    vt[...] = turn(v[:, 0:FW])
    vrt[...] = turn(v[:, FW : 2 * FW])[0:RW]
    mine = block(z, me)

    for i in range(1, S):
        rcopy(up, ua.at[s], us.at[i], ur.at[i], seq=at.seqs[i]).start()
    pltpu.make_async_copy(up, ua.at[s], loc.at[2]).start()

    def steps(j, _):
        r = pl.ds(pl.multiple_of(j * qb, qb), qb)
        mask = jnp.where(jnp.concatenate([kp[...]] * (qb // 128), axis=1) <= qp[0:1, r], 0.0, NEG)
        o_f[r] = attend_block(z.full, k[:, 0:FW], vt[...], q[r, 0:FW], mask, z.head, p_f.at[j])
        return 0

    lax.fori_loop(0, N // qb, steps, 0)
    mask = jnp.where(kp[...] <= qp[0:1, mine], 0.0, NEG)
    o_r[...] = attend_block(z.rest, k[:, FW : 2 * FW], vrt[...], q[mine, FW : 2 * FW], mask, z.head, p_r)
    more = [pltpu.make_async_copy(a, b, wb.at[5 + i]) for i, (a, b) in enumerate(((p_f, p_fo), (p_r, p_ro), (o_f, o_fo)))]
    for c in more:
        c.start()
    wload[3].wait()
    wload[4].wait()
    red = CtxReduce(at, lambda d: matmul(o_f[block(z, d)], wo_f[...]), bufs)
    red.start()
    ffg.forward()
    own = matmul(o_r[...], wo_r[...]) + prm[5:6] + x[...].astype(F32)
    hidden = red.finish() + own
    xhat, rstd = norm_stats(hidden)
    n2[...] = (xhat * prm[1:2] + prm[6:7]).astype(BF16)
    copies = [rcopy(n2, n2a.at[s], ns.at[i], nr.at[i], seq=at.seqs[i]) for i in (2, 1, 3)]
    for c in copies:
        c.start()
    n2a[s] = n2[...]
    hid[...] = hidden
    xh[...] = xhat
    rs_o[...] = jnp.broadcast_to(rstd, rs_o.shape)

    red.close()
    ffg.finish()
    pltpu.make_async_copy(up, ua.at[s], loc.at[2]).wait()
    for i in range(1, S):
        rcopy(up, ua.at[s], us.at[i], ur.at[i], seq=at.seqs[i]).wait()
    for i in range(1, C):
        rcopy(pk, pa.at[s, me], pz_s.at[i], pz_r.at[i], ctx=me).wait_send()

    @pl.when(s < 3)
    def _():
        for i in range(1, C):
            rcopy(cols(me), main(s, me), mz_s.at[i], mz_r.at[me], ctx=me).wait_send()
            rcopy(wr, tail(s, me), rz_s.at[i], rz_r.at[me], ctx=me).wait_send()
        for n in range(C):
            for i in range(1, 4):
                rcopy(both(s, me), both(s, me), mx_s.at[n, i], mx_r.at[s, me], seq=s).wait_send()

    @pl.when(s == 3)
    def _():
        @pl.when(me < C - 1)
        def _():
            rcopy(w, before, oz_s.at[0], oz_r.at[0], ctx=me).wait_send()

        @pl.when(me == C - 1)
        def _():
            for i in range(1, C):
                rcopy(lastrows, wol, oz_s.at[i], oz_r.at[1], ctx=me).wait_send()

        for i in range(1, 4):
            rcopy(w, after, ox_s.at[0, i], ox_r.at[0], seq=s).wait_send()

            @pl.when(me > 0)
            def _():
                rcopy(before, before, ox_s.at[1, i], ox_r.at[1], seq=s).wait_send()

            rcopy(wol, wol, ox_s.at[2, i], ox_r.at[2], seq=s).wait_send()

    for c in backs + more:
        c.wait()
    for c in copies:
        c.wait()


def stage_first_kernel(z, tokens, lengths, block_order, w, up_weights, down_weights, norm_gains, biases, cotangent):
    N, D, FW, RW, R, S, C, SH, qb = z.slot, z.width, z.full_width, z.rest_width, z.rows, z.seq, z.ctx, z.shard, 256
    nq, W2 = N // qb, 2 * FW
    n_g, n_b = norm_gains.shape[0], biases.shape[0]
    pk = jnp.concatenate([jnp.pad(norm_gains, (0, 128 - n_g)), jnp.pad(biases, (0, 896 - n_b))]).reshape(8, 128)
    ins = (block_order, lengths, tokens[0].T, cotangent[0].T, w, w, pk, up_weights.T, down_weights)
    shapes = dict(
        ua=(S, R, D), w3=(3, D, W2), wo2=(2 * SH, D), wo_r=(RW, D), up_t=(C, SH, D), down=(C, SH, D), xa=(C, R, D), n1=(N, D), q=(N, W2),
        k=(N, W2), v=(N, W2), p_f=(nq, z.full, N, qb), p_r=(z.rest, N, R), o_f=(N, FW))
    wide = dict(prm=(12, D), live=(R, 128), wo_f=(FW, D), o_r=(R, RW), hid=(R, D), xh=(R, D), rs=(R, 128), n2a=(S, R, D))
    low = ("wo_f", "o_r", "n2a")
    outs = [sds(a) for a in shapes.values()] + [sds(a, BF16 if n in low else F32) for n, a in wide.items()]
    V = pltpu.VMEM
    scratch = [
        V((R, D), BF16), V((R, D), BF16), V((SH, FW), BF16), V((S, C, 8, 128), BF16), V((C, R, D), BF16), V((N, D), BF16),
        V((N, W2), BF16), V((N, W2), BF16), V((N, W2), BF16), V((nq, z.full, N, qb), BF16), V((z.rest, N, R), BF16), V((N, FW), BF16),
        V((FW, N), BF16), V((RW, N), BF16), V((3, D, W2), BF16), V((RW, D), BF16), V((N, 128), jnp.int32), V((8, N), jnp.int32),
        V((8, -(-2 * D // 128) * 128 + 256), F32), V((8, -(-10 * D // 128) * 128 + 512), F32), V((R, D), BF16),
        DMA((C,)), DMA((C,)), DMA((C,)), DMA((C,)), DMA((C, 4)), DMA((3, C)), DMA((4,)), DMA((4,)), DMA((C,)), DMA((2,)), DMA((3, 4)),
        DMA((3,)), DMA((4,)), DMA((C,)), DMA((C,)), DMA((S,)), DMA((S,)), DMA((5,)), DMA((8,)), DMA((S,)), DMA((S,)),
        *FarGather.scratch(z), *CtxGather.scratch(z), *CtxReduce.scratch(z),
    ]
    spaces = {"v": pltpu.VMEM, "a": pl.ANY, "s": pltpu.SMEM}
    out = pl.pallas_call(
        partial(kernel_first, z, n_g, n_b, qb), name="first_half", out_shape=outs,
        in_specs=[pl.BlockSpec(memory_space=spaces[c]) for c in "ssvvvaaaa"],
        out_specs=[pl.BlockSpec(memory_space=spaces[c]) for c in "a" * 14 + "v" * 8],
        scratch_shapes=scratch,
        compiler_params=pltpu.CompilerParams(collective_id=0, has_side_effects=True, vmem_limit_bytes=VMEM_LIMIT),
    )(*ins)
    return dict(zip(tuple(shapes) + tuple(wide), out))


def ff_block(z, j):
    return pl.ds(pl.multiple_of(j * z.shard, 8), z.shard)


def kernel_f(z, n2h, uah, uph, dnh, prm, hid, xh, rs_i, live, out, gh_o, gb_o, sm, bu, gba, ffr,
             n2, ua, up_t, down, act, gpre, gsend, grecv, fsend, frecv, g32, fs, fr, ld, gs, gr, cs, cr, ps, pr, wb, *gsem):
    at = Place(z)
    S, R, D, C = z.seq, z.rows, z.width, z.ctx
    units, step = up_t.shape[0], 256
    b_up = prm[pl.ds(8 + at.s, 1)]
    greet([at.sib] + at.same[1:], at.seqs[1:], False)
    chunks = [slice(c0, min(c0 + step, units)) for c0 in range(0, units, step)]
    loads = [pltpu.make_async_copy(n2h, n2, ld.at[0]), pltpu.make_async_copy(uah, ua, ld.at[1])]
    for i, c in enumerate(chunks):
        loads.append(pltpu.make_async_copy(uph.at[c], up_t.at[c], ld.at[2 + 2 * i]))
        loads.append(pltpu.make_async_copy(dnh.at[c], down.at[c], ld.at[3 + 2 * i]))
    for c in loads:
        c.start()
    loads[0].wait()
    loads[1].wait()
    for i, c in enumerate(chunks):
        loads[2 + 2 * i].wait()
        pre = matmul(n2[...], up_t[c], 1, 1) + b_up[:, c]
        loads[3 + 2 * i].wait()
        gact = matmul(ua[...], down[c], 1, 1)
        cdf = 0.5 * (1.0 + lax.erf(pre * (0.5 ** 0.5)))
        act[:, c] = (pre * cdf).astype(BF16)
        dgelu = cdf + pre * jnp.exp(-0.5 * pre * pre) * (1.0 / math.sqrt(2.0 * math.pi))
        g = (gact * dgelu).astype(BF16)
        gpre[:, c] = g
        bu[:, c] = jnp.sum(g.astype(F32), axis=0, keepdims=True)
    met(at.chips + S - 1)

    def gcopy(i):
        return rcopy(gsend.at[i], grecv.at[i], gs.at[i], gr.at[i], seq=at.seqs[i])

    def fcopy(i):
        return rcopy(fsend.at[i], frecv.at[i], cs.at[i], cr.at[i], seq=at.seqs[i])

    def pair(t, u):
        return rcopy(fs.at[t, u], fr.at[t, u], ps.at[t, u], pr.at[t, u], ctx=at.sib)

    def weight_grad(u, left, right):
        for c in chunks:
            g32[u, c] = matmul(left[:, c], right[...], 0, 0)
        for t in range(4):
            fs[t, u] = g32[u, ff_block(z, 2 * at.ring[t] + 1 - at.core)].astype(BF16)
            pair(t, u).start()

    def both(u):
        for t in range(4):
            pair(t, u).wait_recv()
            fr[t, u] = (g32[u, ff_block(z, at.same[t])] + fr[t, u].astype(F32)).astype(BF16)
            pltpu.make_async_copy(fr.at[t, u], ffr.at[t, u], wb.at[t, u]).start()

    for i in (2, 1, 3):
        gsend[i] = matmul(gpre[block(z, at.seqs[i])], up_t[...]).astype(BF16)
        gcopy(i).start()
    mine = block(z, at.s)
    gn2 = matmul(gpre[mine], up_t[...])
    weight_grad(0, gpre, n2)
    for i in range(1, S):
        gcopy(i).wait_recv()
        gn2 = gn2 + grecv[i].astype(F32)
    xhat = xh[...]
    up_own = ua[mine].astype(F32)
    gh = up_own + norm_back(gn2, xhat, rs_i[:, :1], prm[1:2])
    gb_o[...] = gh.astype(BF16)
    gat = DirectGather(at, gb_o, gba, gsem)
    gat.send()
    gh_o[...] = gh
    sm[0:1] = jnp.sum(gn2 * xhat, axis=0, keepdims=True)
    sm[1:2] = jnp.sum(gn2, axis=0, keepdims=True)
    sm[2:3] = jnp.sum(gb_o[...].astype(F32), axis=0, keepdims=True)
    sm[3:4] = jnp.sum(up_own, axis=0, keepdims=True)
    for i in (2, 1, 3):
        fsend[i] = matmul(act[block(z, at.seqs[i])], down[...]).astype(BF16)
        fcopy(i).start()
    ff = matmul(act[mine], down[...])
    weight_grad(1, act, ua)
    both(0)
    for i in (1, 3):
        gat.forward(i)
    both(1)
    for i in range(1, S):
        fcopy(i).wait_recv()
        ff = ff + frecv[i].astype(F32)
    out[...] = jnp.transpose(live[:, :1] * (hid[...] + ff + prm[7:8])).astype(BF16)
    gat.forward(2)
    gat.finish()
    for t in range(4):
        for u in range(2):
            pair(t, u).wait_send()
            pltpu.make_async_copy(fr.at[t, u], ffr.at[t, u], wb.at[t, u]).wait()
    for i in range(1, S):
        gcopy(i).wait_send()
        fcopy(i).wait_send()


def stage_f_kernel(z, b):
    R, D, S, U, C, SH = z.rows, z.width, z.seq, z.ctx * z.shard, z.ctx, z.shard
    outs = [sds((D, R)), sds((R, D), F32), sds((R, D)), sds((4, D), F32), sds((1, U), F32), sds((C, R, D)), sds((4, 2, SH, D))]
    V = pltpu.VMEM
    scratch = [
        V((S * R, D), BF16), V((S * R, D), BF16), V((U, D), BF16), V((U, D), BF16), V((S * R, U), BF16), V((S * R, U), BF16),
        *[V((S, R, D), BF16) for _ in range(4)], V((2, U, D), F32), V((4, 2, SH, D), BF16), V((4, 2, SH, D), BF16),
        DMA((2 + 2 * -(-U // 256),)), *[DMA((S,)) for _ in range(4)], DMA((4, 2)), DMA((4, 2)), DMA((4, 2)),
        *DirectGather.scratch(z),
    ]
    return call(
        partial(kernel_f, z), "feed_forward", outs,
        (b["n2a"].reshape(S * R, D), b["ua"].reshape(S * R, D), b["up_t"].reshape(U, D), b["down"].reshape(U, D),
         b["prm"], b["hid"], b["xh"], b["rs"], b["live"]), scratch, 2, "aaaa" + "v" * 5, "v" * 5 + "aa",
    )


class SmallSum:
    def __init__(self, at, buf, rsib, rchip, rseq, sems):
        self.at, self.buf, self.rsib, self.rchip, self.rseq = at, buf, rsib, rchip, rseq
        self.s0, self.r0, self.s1, self.r1, self.s2, self.r2 = sems

    def sib(self):
        return rcopy(self.buf.at[0], self.rsib, self.s0, self.r0, ctx=self.at.sib)

    def chip(self, i):
        return rcopy(self.buf.at[1], self.rchip.at[i], self.s1.at[i], self.r1.at[i], ctx=self.at.same[i])

    def line(self, i):
        return rcopy(self.buf.at[2], self.rseq.at[i], self.s2.at[i], self.r2.at[i], seq=self.at.seqs[i])

    def first(self, value):
        self.buf[0] = value
        self.sib().start()

    def second(self):
        self.sib().wait_recv()
        self.buf[1] = self.buf[0] + self.rsib[...]
        for i in range(1, self.at.chips):
            self.chip(i).start()

    def third(self):
        total = self.buf[1]
        for i in range(1, self.at.chips):
            self.chip(i).wait_recv()
            total = total + self.rchip[i]
        self.buf[2] = total
        for i in range(1, len(self.at.seqs)):
            self.line(i).start()

    def last(self):
        total = self.buf[2]
        for i in range(1, len(self.at.seqs)):
            self.line(i).wait_recv()
            total = total + self.rseq[i]
        return total

    def close(self):
        self.sib().wait_send()
        for i in range(1, self.at.chips):
            self.chip(i).wait_send()
        for i in range(1, len(self.at.seqs)):
            self.line(i).wait_send()

    @staticmethod
    def scratch(z, rows):
        n, shape = z.ctx // 2, (rows, z.width)
        return [
            pltpu.VMEM((3,) + shape, F32), pltpu.VMEM(shape, F32), pltpu.VMEM((n,) + shape, F32),
            pltpu.VMEM((z.seq,) + shape, F32), DMA, DMA, DMA((n,)), DMA((n,)), DMA((z.seq,)), DMA((z.seq,)),
        ]


def attend_block_back(heads, k_t, v, q, go, p_ref, head, gk, gv):
    parts = []
    for h in range(heads):
        goh = of_head(go, h, head).astype(BF16)
        p = p_ref[h]
        pf = p.astype(F32)
        gp = matmul(v, goh, 1, 1)
        delta = jnp.sum(gp * pf, axis=0, keepdims=True)
        gs = (pf * (gp - delta)).astype(BF16)
        gk[...] += matmul(gs, of_head(q, h, head).astype(BF16))
        gv[...] += matmul(p, goh)
        parts.append(matmul(k_t[h * head : (h + 1) * head], gs))
    g_t = parts[0] if len(parts) == 1 else jnp.concatenate(parts, axis=0)
    return (jnp.transpose(g_t) * head ** -0.5).astype(BF16)


def kernel_de(z, qb, gbah, kh, oh, vh, qh, pfh, prh, wh, n1h, xah, ffr,
              wo_f, wo_r, o_r, gh, prm, sm4, bu,
              gtok, ga, gup, gdn, tot, bup,
              gba, k, o_f, v, q, p_f, p_r, w, n1, xa, ld,
              go, kt, krt, gk, gv, gkr, gvr, gcat, gw, gwr, gwo, gwor, sums, ffz, ffo, comb, mid, fz_s, fz_r, fo, fm,
              rf, rr, ro, ror, sf_s, sf_r, sr_s, sr_r, so_s, so_r, sor_s, sor_r,
              zs, zr, land, landr, zs_s, zs_r, zr_s, zr_r,
              buf32, obs, obn, orrs, orr, ob_s, ob_r, orr_s, orr_r, *rest):
    at = Place(z)
    s, me, C, S, FW, RW, SH, D = at.s, at.k, z.ctx, z.seq, z.full_width, z.rest_width, z.shard, z.width
    bufs, small = rest[:11], rest[11:]
    scale, top = z.head ** -0.5, TOP(z)
    mine = block(z, me)
    greet([lax.rem(me + i, C) for i in range(1, C)], at.seqs[1:], False)
    pairs = ((gbah, gba), (kh, k), (oh, o_f), (vh, v), (qh, q), (pfh, p_f), (prh, p_r), (wh, w), (n1h, n1), (xah, xa))
    loads = [pltpu.make_async_copy(a, b, ld.at[i]) for i, (a, b) in enumerate(pairs)]
    for c in loads:
        c.start()
    ownff = pltpu.make_async_copy(ffr.at[0], ffo, fo.at[0])
    ownff.start()
    farff = pltpu.make_async_copy(ffr.at[2], comb, fo.at[1])
    farff.start()
    met(C + S - 2)

    def fz(t):
        return rcopy(ffr.at[t], ffz.at[t], fz_s.at[t], fz_r.at[t], ctx=at.same[t])

    def via(t):
        return rcopy(ffr.at[t], mid, fm.at[0], fm.at[1], ctx=at.same[4 - t])

    def across():
        return rcopy(comb, ffz.at[2], fz_s.at[2], fz_r.at[2], ctx=at.same[2])

    @pl.when(at.chip == 0)
    def _():
        via(3).start()

    @pl.when(at.chip == 3)
    def _():
        via(1).start()

    @pl.when(~at.edge)
    def _():
        fz(1).start()
        fz(3).start()

    gk[...] = jnp.zeros_like(gk)
    gv[...] = jnp.zeros_like(gv)
    gkr[...] = jnp.zeros_like(gkr)
    gvr[...] = jnp.zeros_like(gvr)
    gcat[0, :, FW:] = jnp.zeros((z.slot, FW), BF16)
    for c in loads[:3]:
        c.wait()
    go[...] = matmul(gba[...], wo_f[...], 1, 1).astype(BF16)
    kt[...] = turn(k[:, 0:FW])
    krt[...] = turn(k[:, FW : 2 * FW])[0:RW]
    gwo[...] = matmul(o_f[...], gba[...], 0, 0).astype(BF16)
    gwor[...] = matmul(o_r[...], gba[mine], 0, 0).astype(BF16)

    def up(ref, dst, ssem, rsem, i, m=None):
        return rcopy(ref if m is None else ref.at[m], dst.at[i], ssem.at[i], rsem.at[i], seq=at.seqs[i])

    for i in range(1, S):
        @pl.when(at.seqs[i] == 3)
        def _():
            up(gwo, ro, so_s, so_r, i).start()
            up(gwor, ror, sor_s, sor_r, i).start()

    for c in loads[3:6]:
        c.wait()

    def steps(j, _):
        r = pl.ds(pl.multiple_of(j * qb, qb), qb)
        gcat[0, r, 0:FW] = attend_block_back(z.full, kt[...], v[:, 0:FW], q[r, 0:FW], go[r], p_f.at[j], z.head, gk, gv)
        return 0

    lax.fori_loop(0, z.slot // qb, steps, 0)

    farff.wait()

    @pl.when(at.chip == 0)
    def _():
        via(3).wait_send()
        fz(1).start()

    @pl.when(at.chip == 3)
    def _():
        via(1).wait_send()
        fz(3).start()

    @pl.when(~at.edge)
    def _():
        via(1).wait_recv()
        for u in range(2):
            comb[u] = (comb[u].astype(F32) + mid[u].astype(F32)).astype(BF16)

    across().start()
    loads[6].wait()
    gor = matmul(gba[mine], wo_r[...], 1, 1).astype(BF16)
    gor = jnp.concatenate([gor, jnp.zeros((z.rows, FW - RW), BF16)], axis=1)
    gcat[0, mine, FW : FW + RW] = attend_block_back(
        z.rest, krt[...], v[:, FW : 2 * FW], q[mine, FW : 2 * FW], gor, p_r, z.head, gkr, gvr)
    gcat[1, :, 0:FW] = (gk[...] * scale).astype(BF16)
    gcat[1, :, FW:] = (gkr[...] * scale).astype(BF16)
    gcat[2, :, 0:FW] = gv[...].astype(BF16)
    gcat[2, :, FW:] = gvr[...].astype(BF16)
    for c in loads[7:10]:
        c.wait()

    for m in (2, 1, 0):
        g = matmul(n1[...], gcat[m], 0, 0).reshape(C, SH, 2 * FW)
        gw[m] = g[:, :, 0:FW].astype(BF16)
        g = g[:, :, FW : FW + RW]
        low = jnp.concatenate([g[:, top:], jnp.zeros((C, 2 * top - SH, RW), F32)], axis=1)
        gwr[m] = jnp.concatenate([g[:, :top], low], axis=2).astype(BF16)
    for i in (2, 1, 3):
        m = at.seqs[i]

        @pl.when(m < 3)
        def _():
            up(gw, rf, sf_s, sf_r, i, m).start()
            up(gwr, rr, sr_s, sr_r, i, m).start()

    sums[...] = jnp.zeros_like(sums)

    def part(d):
        r = block(z, d)
        total = matmul(gcat[0, r], w[0], 1, 1) + matmul(gcat[1, r], w[1], 1, 1) + matmul(gcat[2, r], w[2], 1, 1)
        sums[8:9] += jnp.sum(total * norm_stats(xa[r].astype(F32))[0], axis=0, keepdims=True)
        sums[9:10] += jnp.sum(total, axis=0, keepdims=True)
        return total

    red = CtxReduce(at, part, bufs)
    red.start()
    own = part(me)

    def cols(m):
        a = jnp.sum(gcat[m].astype(F32), axis=0, keepdims=True)
        return jnp.concatenate([jnp.where(me == c, a[:, 0:FW], 0.0) for c in range(C)] + [a[:, FW : FW + RW]], axis=1)

    sums[0:4] = sm4[...]
    sums[4:5] = cols(0)
    sums[5:6] = cols(2)
    sums[6:7] = bu[...]
    se = SmallSum(at, *small[:4], small[4:])
    se.first(sums[...])

    se.second()

    def zf(i):
        return rcopy(zs.at[lax.rem(me + i, C)], land.at[i], zs_s.at[i], zs_r.at[i], ctx=lax.rem(me + i, C))

    def zrr(i):
        return rcopy(zr.at[lax.rem(me + i, C)], landr.at[i], zr_s.at[i], zr_r.at[i], ctx=lax.rem(me + i, C))

    def shift():
        return rcopy(obs, obn, ob_s, ob_r, ctx=lax.rem(me + C - 1, C))

    def tail(i):
        return rcopy(orrs, orr.at[i], orr_s, orr_r.at[i], ctx=C - 1)

    @pl.when(s < 3)
    def _():
        for i in range(1, S):
            up(gw, rf, sf_s, sf_r, i, 0).wait_recv()
            up(gwr, rr, sr_s, sr_r, i, 0).wait_recv()

        def add(j, _):
            t, u = gw[s, j].astype(F32), gwr[s, j].astype(F32)
            for i in range(1, S):
                t = t + rf[i, j].astype(F32)
                u = u + rr[i, j].astype(F32)
            zs[j] = t.astype(BF16)
            zr[j] = u.astype(BF16)
            return 0

        lax.fori_loop(0, C, add, 0)
        for i in range(1, C):
            zf(i).start()
            zrr(i).start()

    @pl.when(s == 3)
    def _():
        for i in range(1, S):
            up(gwo, ro, so_s, so_r, i).wait_recv()
            up(gwor, ror, sor_s, sor_r, i).wait_recv()
        t, u = gwo[...].astype(F32), gwor[...].astype(F32)
        for i in range(1, S):
            t = t + ro[i].astype(F32)
            u = u + ror[i].astype(F32)
        buf32[pl.ds(0, FW)] = t
        obs[...] = t.astype(BF16)
        orrs[...] = u.astype(BF16)

        @pl.when(me > 0)
        def _():
            shift().start()

        for i in range(C - 1):
            @pl.when(me == i)
            def _():
                tail(i).start()

    se.third()

    ownff.wait()
    across().wait_recv()
    for u, g in enumerate((gup, gdn)):
        g[...] = ffo[u].astype(F32) + ffz[2, u].astype(F32)
    for t in (1, 3):
        @pl.when(at.chip != (0 if t == 1 else 3))
        def _():
            fz(t).wait_recv()
            for u, g in enumerate((gup, gdn)):
                g[...] += ffz[t, u].astype(F32)

    xhat, rstd = norm_stats(xa[mine].astype(F32))
    gn1 = red.finish(own)
    gtok[...] = jnp.transpose(gh[...] + norm_back(gn1, xhat, rstd, prm[0:1]))

    @pl.when(s < 3)
    def _():
        ga[:, pl.ds(pl.multiple_of(me * FW, FW), FW)] = zs[me].astype(F32)
        remain = zr[me].astype(F32)
        for i in range(1, C):
            zf(i).wait_recv()
            zrr(i).wait_recv()
            j = lax.rem(me + C - i, C)
            ga[:, pl.ds(pl.multiple_of(j * FW, FW), FW)] = land[i].astype(F32)
            remain = remain + landr[i].astype(F32)
        ga[0:top, z.main :] = remain[:, 0:RW]
        ga[top:SH, z.main :] = remain[0 : SH - top, RW : 2 * RW]
        for i in range(1, C):
            zf(i).wait_send()
            zrr(i).wait_send()

    @pl.when(s == 3)
    def _():
        @pl.when(me < C - 1)
        def _():
            shift().wait_recv()
            buf32[pl.ds(FW, FW)] = obn[...].astype(F32)

        @pl.when(me == C - 1)
        def _():
            u = orrs[...].astype(F32)
            for i in range(C - 1):
                tail(i).wait_recv()
                u = u + orr[i].astype(F32)
            buf32[pl.ds(FW, RW)] = u

        ga[...] = buf32[pl.ds(pl.multiple_of((SH - FW) * me, 8), SH)]

        @pl.when(me > 0)
        def _():
            shift().wait_send()

        @pl.when(me < C - 1)
        def _():
            tail(0).wait_send()

    tot[...] = se.last()
    bup[s] = se.buf[2, 6:7]
    for i in range(1, S):
        bup[at.seqs_back[i]] = se.rseq[i, 6:7]
    red.close()
    se.close()
    across().wait_send()

    @pl.when(at.chip != 3)
    def _():
        fz(1).wait_send()

    @pl.when(at.chip != 0)
    def _():
        fz(3).wait_send()
    for i in range(1, S):
        m = at.seqs[i]

        @pl.when(m < 3)
        def _():
            up(gw, rf, sf_s, sf_r, i, m).wait_send()
            up(gwr, rr, sr_s, sr_r, i, m).wait_send()

        @pl.when(m == 3)
        def _():
            up(gwo, ro, so_s, so_r, i).wait_send()
            up(gwor, ror, sor_s, sor_r, i).wait_send()


def TOP(z):
    return -(-z.shard // 16) * 8


def stage_de_kernel(z, b, gba, ffr, gh, sm4, bu):
    C, S, D, FW, RW, SH, N, R, qb = z.ctx, z.seq, z.width, z.full_width, z.rest_width, z.shard, z.slot, z.rows, 256
    nq, W2, top = N // qb, 2 * FW, TOP(z)
    outs = [sds((D, R), F32), sds((SH, D), F32), sds((SH, D), F32), sds((SH, D), F32), sds((10, D), F32), sds((S, 1, D), F32)]
    V = pltpu.VMEM
    scratch = [
        V((N, D), BF16), V((N, W2), BF16), V((N, FW), BF16), V((N, W2), BF16), V((N, W2), BF16), V((nq, z.full, N, qb), BF16),
        V((z.rest, N, R), BF16), V((3, D, W2), BF16), V((N, D), BF16), V((N, D), BF16), DMA((10,)),
        V((N, FW), BF16), V((FW, N), BF16), V((RW, N), BF16), *[V((N, FW), F32) for _ in range(4)],
        V((3, N, W2), BF16), V((3, C, SH, FW), BF16), V((3, C, top, 2 * RW), BF16), V((FW, D), BF16), V((RW, D), BF16), V((10, D), F32),
        V((4, 2, SH, D), BF16), V((2, SH, D), BF16), V((2, SH, D), BF16), V((2, SH, D), BF16), DMA((4,)), DMA((4,)), DMA((2,)), DMA((2,)),
        V((S, C, SH, FW), BF16), V((S, C, top, 2 * RW), BF16), V((S, FW, D), BF16), V((S, RW, D), BF16), *[DMA((S,)) for _ in range(8)],
        V((C, SH, FW), BF16), V((C, top, 2 * RW), BF16), V((C, SH, FW), BF16), V((C, top, 2 * RW), BF16),
        *[DMA((C,)) for _ in range(4)],
        V((2 * FW, D), F32), V((FW, D), BF16), V((FW, D), BF16), V((RW, D), BF16), V((C, RW, D), BF16),
        DMA, DMA, DMA, DMA((C,)),
        *CtxReduce.scratch(z), *SmallSum.scratch(z, 10),
    ]
    gtok, ga, gup, gdn, tot, bup = call(
        partial(kernel_de, z, qb), "attention_back", outs,
        (gba.reshape(N, D), b["k"], b["o_f"], b["v"], b["q"], b["p_f"], b["p_r"], b["w3"], b["n1"], b["xa"].reshape(N, D), ffr,
         b["wo_f"], b["wo_r"], b["o_r"], gh, b["prm"], sm4, bu),
        scratch, 4, "a" * 11 + "v" * 7, "v" * 6,
    )
    names = ("gain2", "shift2", "b_o", "b_down", "b_q", "b_v", None, None, "gain1", "shift1")
    return gtok, ga, gup, gdn, {n: tot[j : j + 1] for j, n in enumerate(names) if n}, bup.reshape(-1)


def shards(tokens, lengths, block_order, attention_weights, up_weights, down_weights, norm_gains, biases, cotangent):
    z = Sizes(tokens.shape[1], tokens.shape[2], block_order.shape[0])
    i, s = lax.axis_index("ctx"), lax.axis_index("seq")
    me, D = s * z.ctx + i, z.width
    n_g, n_b = norm_gains.shape[0], biases.shape[0]
    fast = (
        z.ctx == 8 and z.seq == 4 and 0 < D - z.main <= z.shard and z.rest == 1 and z.full_width == 128
        and z.ctx * up_weights.shape[1] == D and z.rows == 2 * z.block_len and n_g <= 128 and n_b <= 384
    )
    if fast:
        b = stage_first_kernel(
            z, tokens, lengths, block_order, attention_weights, up_weights, down_weights, norm_gains, biases, cotangent)
        output, gh, _, sm4, bu, gba, ffr = stage_f_kernel(z, b)
        gtok, gw, g_up_own, g_down_own, tot, b_up_all = stage_de_kernel(z, b, gba, ffr, gh, sm4, bu)
        output, gtok, g_up_own = output.T, gtok.T, g_up_own.T
    else:
        x, cot, length = tokens[0], cotangent[0], lengths[0]
        pos = (block_order[:, None] * z.block_len + jnp.arange(z.block_len, dtype=jnp.int32)[None, :]).reshape(z.slot)
        my_pos = lax.dynamic_slice_in_dim(pos, i * z.rows, z.rows)
        live = (my_pos < length).astype(F32)[:, None]
        lanes = -(-(n_g + n_b) // 1024) * 8
        packed = jnp.pad(jnp.concatenate([norm_gains, biases]), (0, lanes * 128 - n_g - n_b)).reshape(lanes, 128)
        upstream = (live * cot.astype(F32)).astype(BF16)
        x_all, wf, wr, wo_f, wo_r = stage_a(z, x, attention_weights)
        ua = lax.all_gather(upstream, "seq", axis=0, tiled=True)
        both = lax.all_gather(packed, ("seq", "ctx"), axis=0).reshape(z.seq * z.ctx, lanes * 128)
        gains = both[:, :n_g].reshape(-1).astype(F32)
        bias = both[:, n_g : n_g + n_b].reshape(-1).astype(F32)
        row = lambda v: v[None, :]
        piece = [row(bias[j * D : (j + 1) * D]) for j in range(6)]
        gain1, gain2 = row(gains[:D]), row(gains[D:])
        units = z.ctx * up_weights.shape[1]
        b_up = row(lax.dynamic_slice_in_dim(bias[6 * D :], s * units, units))
        prm = dict(gain2=gain2, shift2=piece[4], b_o=piece[3], b_down=piece[5], b_up=b_up)
        fslice = lambda v: lax.dynamic_slice(v, (0, i * z.full_width), (1, z.full_width))
        up_t = lax.all_gather(up_weights.T, "ctx", axis=0, tiled=True)
        down = lax.all_gather(down_weights, "ctx", axis=0, tiled=True)
        b = stage_b(z, x_all, wf, wr, gain1, piece[0], fslice(piece[1]), piece[1][:, z.main :],
                    fslice(piece[2]), piece[2][:, z.main :], pos, length)
        output, gh, gb, g_up_t, g_down, small = stage_c(z, b, wo_f, wo_r, x, upstream, ua, live, up_t, down, prm)
        g_up_own = lax.psum_scatter(g_up_t, "ctx", scatter_dimension=0, tiled=True).astype(F32).T
        g_down_own = lax.psum_scatter(g_down, "ctx", scatter_dimension=0, tiled=True).astype(F32)
        gba = lax.all_gather(gb, "ctx", axis=0, tiled=True) if z.full else None
        d = stage_d(z, b, gb, gba, wo_f, wo_r)
        gtok, gw, tot, b_up_all = stage_e(z, d, wf, wr, x, gh, gain1, small)
    g_gain = lax.dynamic_slice_in_dim(jnp.concatenate([tot["gain1"][0], tot["gain2"][0]]), me * n_g, n_g)
    g_bias = lax.dynamic_slice_in_dim(jnp.concatenate([tot[n][0] for n in ("shift1", "b_q", "b_v", "b_o", "shift2", "b_down")] + [b_up_all]), me * n_b, n_b)
    return output[None], gtok[None], gw, g_up_own, g_down_own, g_gain, g_bias


def solution(mesh):
    in_specs = (
        P("seq", "ctx", None), P("seq"), P(), P(("seq", "ctx"), None), P(None, ("seq", "ctx")),
        P(("seq", "ctx"), None), P(("seq", "ctx")), P(("seq", "ctx")), P("seq", "ctx", None),
    )
    out_specs = (
        P("seq", "ctx", None), P("seq", "ctx", None), P(("seq", "ctx"), None), P(None, ("seq", "ctx")),
        P(("seq", "ctx"), None), P(("seq", "ctx")), P(("seq", "ctx")),
    )
    return jax.shard_map(shards, mesh=mesh, in_specs=in_specs, out_specs=out_specs, check_vma=False)
```

```python
import math
from functools import partial

import jax
import jax.numpy as jnp
from jax import lax
from jax.experimental import pallas as pl
from jax.experimental.pallas import tpu as pltpu
from jax.sharding import PartitionSpec as P

HEADS = 17
EPS = 1e-05
F32 = jnp.float32
BF16 = jnp.bfloat16


def norm_stats(values):
    centre = values - jnp.mean(values, axis=-1, keepdims=True)
    rstd = lax.rsqrt(jnp.mean(centre * centre, axis=-1, keepdims=True) + EPS)
    return centre * rstd, rstd


def norm_back(grad, xhat, rstd, gain):
    e = grad * gain
    mean_e = jnp.mean(e, axis=-1, keepdims=True)
    mean_ex = jnp.mean(e * xhat, axis=-1, keepdims=True)
    return (e - mean_e - xhat * mean_ex) * rstd


def dot(a, b, ca, cb):
    return lax.dot_general(a, b, (((ca,), (cb,)), ((), ())), preferred_element_type=F32)


def rows_sum(v):
    return jnp.sum(v.astype(F32), axis=0, keepdims=True)


class Sizes:
    def __init__(self, rows, width, block_count):
        self.rows, self.width = rows, width
        self.ctx, self.seq = lax.axis_size("ctx"), lax.axis_size("seq")
        self.slot = rows * self.ctx
        self.block_len = self.slot // block_count
        self.head = width // HEADS
        self.full = HEADS // self.ctx
        self.full_width = self.full * self.head
        self.main = self.full_width * self.ctx
        self.rest = HEADS - self.full * self.ctx
        self.rest_width = self.rest * self.head
        self.shard = width // self.ctx


def stage_a(z, x, w):
    k = lax.axis_index("ctx")
    x_all = lax.all_gather(x, "ctx", axis=0, tiled=True)
    w_all = lax.all_gather(w, "seq", axis=0)
    wm = w_all[:3, :, : z.main].reshape(3, z.shard, z.ctx, z.full_width)
    wf = lax.all_to_all(wm, "ctx", split_axis=2, concat_axis=1, tiled=True).reshape(
        3, z.width, z.full_width
    )
    wr = lax.all_gather(w_all[:3, :, z.main :], "ctx", axis=1, tiled=True)
    wo = lax.all_gather(w_all[3], "ctx", axis=0, tiled=True)
    wo_f = lax.dynamic_slice_in_dim(wo, k * z.full_width, z.full_width)
    wo_r = wo[z.main :]
    return x_all, wf, wr, wo_f, wo_r


def heads_of(v, h):
    return v.reshape(v.shape[0], -1, h).transpose(1, 0, 2)


def attend(z, q, k, v, qpos, kpos, length):
    s = jnp.einsum("hqd,hkd->hkq", heads_of(q, z.head), heads_of(k, z.head), preferred_element_type=F32)
    s = s * (z.head ** -0.5)
    seen = (kpos[:, None] <= qpos[None, :]) & (kpos[:, None] < length)
    s = jnp.where(seen[None], s, -1e30)
    e = jnp.exp(s - jnp.max(s, axis=1, keepdims=True))
    p = (e / jnp.sum(e, axis=1, keepdims=True)).astype(BF16)
    o = jnp.einsum("hkq,hkd->qhd", p, heads_of(v, z.head), preferred_element_type=F32)
    return p, o.reshape(q.shape).astype(BF16)


def stage_b(z, x_all, wf, wr, gain, shift, bq_f, bq_r, bv_f, bv_r, pos, length):
    i = lax.axis_index("ctx")
    n1 = (norm_stats(x_all.astype(F32))[0] * gain + shift).astype(BF16)
    mine = lax.dynamic_slice_in_dim(n1, i * z.rows, z.rows)
    qpos = lax.dynamic_slice_in_dim(pos, i * z.rows, z.rows)
    out = dict(n1=n1)
    if z.full:
        q = (dot(n1, wf[0], 1, 0) + bq_f).astype(BF16)
        k = dot(n1, wf[1], 1, 0).astype(BF16)
        v = (dot(n1, wf[2], 1, 0) + bv_f).astype(BF16)
        p, o = attend(z, q, k, v, pos, pos, length)
        out.update(q_f=q, k_f=k, v_f=v, p_f=p, o_f=o)
    if z.rest:
        q = (dot(mine, wr[0], 1, 0) + bq_r).astype(BF16)
        k = dot(n1, wr[1], 1, 0).astype(BF16)
        v = (dot(n1, wr[2], 1, 0) + bv_r).astype(BF16)
        p, o = attend(z, q, k, v, qpos, pos, length)
        out.update(q_r=q, k_r=k, v_r=v, p_r=p, o_r=o)
    return out


def stage_c(z, b, wo_f, wo_r, x, upstream, ua, live, up_t, down, prm):
    branch = prm["b_o"]
    if z.full:
        part = dot(b["o_f"], wo_f, 1, 0).astype(BF16)
        branch = branch + lax.psum_scatter(part.astype(F32), "ctx", scatter_dimension=0, tiled=True)
    if z.rest:
        branch = branch + dot(b["o_r"], wo_r, 1, 0)
    hidden = x.astype(F32) + branch
    xhat, rstd = norm_stats(hidden)
    n2 = (xhat * prm["gain2"] + prm["shift2"]).astype(BF16)
    n2a = lax.all_gather(n2, "seq", axis=0, tiled=True)
    pre = dot(n2a, up_t, 1, 1) + prm["b_up"]
    cdf = 0.5 * (1.0 + lax.erf(pre * (0.5 ** 0.5)))
    act = (pre * cdf).astype(BF16)
    dgelu = cdf + pre * jnp.exp(-0.5 * pre * pre) * (1.0 / math.sqrt(2.0 * math.pi))
    gact = dot(ua, down, 1, 1)
    gpre = (gact * dgelu).astype(BF16)
    gn2p = dot(gpre, up_t, 1, 0).astype(BF16)
    gn2 = lax.psum_scatter(gn2p.astype(F32), "seq", scatter_dimension=0, tiled=True)
    ffp = dot(act, down, 1, 0).astype(BF16)
    ff = lax.psum_scatter(ffp.astype(F32), "seq", scatter_dimension=0, tiled=True)
    output = (live * (hidden + ff + prm["b_down"])).astype(BF16)
    g_up_t = dot(gpre, n2a, 0, 0).astype(BF16)
    g_down = dot(act, ua, 0, 0).astype(BF16)
    gh = upstream.astype(F32) + norm_back(gn2, xhat, rstd, prm["gain2"])
    gb = gh.astype(BF16)
    small = dict(gain2=rows_sum(gn2 * xhat), shift2=rows_sum(gn2), b_o=rows_sum(gb),
                 b_down=rows_sum(upstream), b_up=rows_sum(gpre))
    return output, gh, gb, g_up_t, g_down, small


def attend_back(z, q, k, v, p, go):
    gp = jnp.einsum("hqd,hkd->hkq", heads_of(go, z.head), heads_of(v, z.head), preferred_element_type=F32)
    pf = p.astype(F32)
    delta = jnp.sum(gp * pf, axis=1, keepdims=True)
    gs = (pf * (gp - delta)).astype(BF16)
    sc = z.head ** -0.5
    gq = jnp.einsum("hkq,hkd->qhd", gs, heads_of(k, z.head), preferred_element_type=F32) * sc
    gk = jnp.einsum("hkq,hqd->khd", gs, heads_of(q, z.head), preferred_element_type=F32) * sc
    gv = jnp.einsum("hkq,hqd->khd", p, heads_of(go, z.head), preferred_element_type=F32)
    return gq.reshape(q.shape).astype(BF16), gk.reshape(k.shape).astype(BF16), gv.reshape(v.shape).astype(BF16)


def stage_d(z, b, gb, gba, wo_f, wo_r):
    i = lax.axis_index("ctx")
    n1 = b["n1"]
    mine = lax.dynamic_slice_in_dim(n1, i * z.rows, z.rows)
    out = {}
    if z.full:
        go = dot(gba, wo_f, 1, 1).astype(BF16)
        gq, gk, gv = attend_back(z, b["q_f"], b["k_f"], b["v_f"], b["p_f"], go)
        out.update(gq_f=gq, gk_f=gk, gv_f=gv, gwo_f=dot(b["o_f"], gba, 0, 0))
        out["gw_f"] = jnp.stack([dot(n1, g, 0, 0) for g in (gq, gk, gv)])
    if z.rest:
        go = dot(gb, wo_r, 1, 1).astype(BF16)
        gq, gk, gv = attend_back(z, b["q_r"], b["k_r"], b["v_r"], b["p_r"], go)
        out.update(gq_r=gq, gk_r=gk, gv_r=gv, gwo_r=dot(b["o_r"], gb, 0, 0))
        out["gw_r"] = jnp.stack([dot(mine, gq, 0, 0), dot(n1, gk, 0, 0), dot(n1, gv, 0, 0)])
    return out


def stage_e(z, d, wf, wr, x, gh, gain1, small):
    i, s = lax.axis_index("ctx"), lax.axis_index("seq")
    part = 0.0
    own = 0.0
    if z.full:
        part = part + dot(d["gq_f"], wf[0], 1, 1) + dot(d["gk_f"], wf[1], 1, 1) + dot(d["gv_f"], wf[2], 1, 1)
    if z.rest:
        part = part + dot(d["gk_r"], wr[1], 1, 1) + dot(d["gv_r"], wr[2], 1, 1)
        own = own + dot(d["gq_r"], wr[0], 1, 1)
    gn1 = own + lax.psum_scatter(part.astype(BF16).astype(F32), "ctx", scatter_dimension=0, tiled=True)
    xhat, rstd = norm_stats(x.astype(F32))
    gtok = gh + norm_back(gn1, xhat, rstd, gain1)
    small = dict(small, gain1=rows_sum(gn1 * xhat), shift1=rows_sum(gn1))
    row = jnp.zeros((1, z.width), F32)
    for name, key in (("b_q", "gq"), ("b_v", "gv")):
        r = row
        if z.full:
            r = lax.dynamic_update_slice(r, rows_sum(d[key + "_f"]), (0, i * z.full_width))
        if z.rest:
            r = r.at[:, z.main :].add(rows_sum(d[key + "_r"]))
        small[name] = r
    full = jnp.zeros((4, z.width, z.width), F32)
    if z.full:
        full = lax.dynamic_update_slice(full, d["gw_f"], (0, 0, i * z.full_width))
        full = lax.dynamic_update_slice(full, d["gwo_f"][None], (3, i * z.full_width, 0))
    if z.rest:
        full = full.at[:3, :, z.main :].add(d["gw_r"])
        full = full.at[3, z.main :, :].add(d["gwo_r"])
    gw = lax.psum_scatter(full.reshape(4 * z.width, z.width).astype(BF16), ("seq", "ctx"), scatter_dimension=0, tiled=True)
    b_up_all = lax.all_gather(lax.psum(small.pop("b_up"), "ctx")[0], "seq", axis=0, tiled=True)
    names = list(small)
    tot = lax.psum(jnp.concatenate([small[n] for n in names]), ("seq", "ctx"))
    return gtok, gw.astype(F32), {n: tot[j : j + 1] for j, n in enumerate(names)}, b_up_all


MESH = pl.DeviceIdType.MESH
DMA = pltpu.SemaphoreType.DMA
VMEM_LIMIT = 56 << 20


def rcopy(src, dst, ssem, rsem, **dev):
    return pltpu.make_async_remote_copy(
        src_ref=src, dst_ref=dst, send_sem=ssem, recv_sem=rsem, device_id=dev, device_id_type=MESH
    )


def greet(ctx_peers, seq_peers, wait=True):
    sem = pltpu.get_barrier_semaphore()
    for p in ctx_peers:
        pl.semaphore_signal(sem, inc=1, device_id={"ctx": p}, device_id_type=MESH)
    for p in seq_peers:
        pl.semaphore_signal(sem, inc=1, device_id={"seq": p}, device_id_type=MESH)
    if wait:
        met(len(ctx_peers) + len(seq_peers))


def met(count):
    pl.semaphore_wait(pltpu.get_barrier_semaphore(), count)


class Place:
    def __init__(self, z):
        self.k, self.s = lax.axis_index("ctx"), lax.axis_index("seq")
        self.chips, self.ctx = z.ctx // 2, z.ctx
        self.core = lax.rem(self.k, 2)
        self.chip = self.k // 2
        self.sib = self.k + 1 - 2 * self.core
        self.edge = (self.chip == 0) | (self.chip == self.chips - 1)
        self.ring = [lax.rem(self.chip + i, self.chips) for i in range(self.chips)]
        self.same = [2 * q + self.core for q in self.ring]
        self.back = [2 * lax.rem(self.chip + self.chips - i, self.chips) + self.core for i in range(self.chips)]
        self.seqs = [lax.rem(self.s + i, z.seq) for i in range(z.seq)]
        self.seqs_back = [lax.rem(self.s + z.seq - i, z.seq) for i in range(z.seq)]


def call(body, name, outs, ins, scratch, cid, in_spaces, out_spaces, cost=None):
    spaces = {"v": pltpu.VMEM, "a": pl.ANY}
    return pl.pallas_call(
        body,
        name=name,
        out_shape=outs,
        in_specs=[pl.BlockSpec(memory_space=spaces[c]) for c in in_spaces],
        out_specs=[pl.BlockSpec(memory_space=spaces[c]) for c in out_spaces],
        scratch_shapes=scratch,
        compiler_params=pltpu.CompilerParams(
            collective_id=cid, has_side_effects=True, vmem_limit_bytes=VMEM_LIMIT
        ),
        cost_estimate=cost,
    )(*ins)


def sds(shape, dtype=BF16):
    return jax.ShapeDtypeStruct(shape, dtype)


class CtxGather:
    def __init__(self, at, own, dst, sems):
        self.at, self.own, self.dst = at, own, dst
        self.ss, self.rs, self.fs, self.fr, self.lo, self.ho = sems

    def to(self, i):
        return rcopy(self.own, self.dst.at[self.at.k], self.ss.at[i], self.rs.at[i], ctx=self.at.same[i])

    def side(self, i):
        b = self.dst.at[self.at.back[i]]
        return rcopy(b, b, self.fs.at[i], self.fr.at[i], ctx=self.at.sib)

    def hop(self, i, step):
        b = self.dst.at[self.at.back[i]]
        return rcopy(b, b, self.ho, self.rs.at[2], ctx=lax.rem(self.at.k + step + self.at.ctx, self.at.ctx))

    def sibling(self):
        return rcopy(self.own, self.dst.at[self.at.k], self.fs.at[0], self.fr.at[0], ctx=self.at.sib)

    def local(self):
        return pltpu.make_async_copy(self.own, self.dst.at[self.at.k], self.lo)

    def send(self):
        @pl.when(self.at.chip != 3)
        def _():
            self.to(1).start()

        @pl.when(self.at.chip != 0)
        def _():
            self.to(3).start()

        self.sibling().start()
        self.local().start()

    def send_rest(self):
        @pl.when(self.at.chip == 0)
        def _():
            self.to(1).wait_send()
            self.to(3).start()
            self.to(2).start()

        @pl.when(self.at.chip == 3)
        def _():
            self.to(3).wait_send()
            self.to(1).start()
            self.to(2).start()

        @pl.when(self.at.chip == 1)
        def _():
            self.to(3).wait_recv()
            self.hop(3, -2).start()

        @pl.when(self.at.chip == 2)
        def _():
            self.to(1).wait_recv()
            self.hop(1, 2).start()

    def forward(self, i):
        if i == 2:
            self.to(i).wait_recv()
        else:
            @pl.when(self.at.chip != (2 if i == 1 else 1))
            def _():
                self.to(i).wait_recv()
        self.side(i).start()

    def finish(self):
        self.local().wait()
        self.sibling().wait()
        for i in (1, 3, 2):
            self.side(i).wait()

        @pl.when(self.at.chip != 0)
        def _():
            self.to(1).wait_send()

        @pl.when(self.at.chip != 3)
        def _():
            self.to(3).wait_send()

        @pl.when(self.at.edge)
        def _():
            self.to(2).wait_send()

        @pl.when(~self.at.edge)
        def _():
            self.hop(1, 2).wait_send()

    @staticmethod
    def scratch(z):
        return [DMA((4,)), DMA((4,)), DMA((4,)), DMA((4,)), DMA, DMA]


class DirectGather:
    def __init__(self, at, own, dst, sems):
        self.at, self.own, self.dst, self.sems = at, own, dst, sems

    def send(self):
        at, ss, rs = self.at, self.sems[0], self.sems[1]
        for i in range(1, at.chips):
            rcopy(self.own, self.dst.at[at.k], ss.at[i], rs.at[i], ctx=at.same[i]).start()
        rcopy(self.own, self.dst.at[at.k], ss.at[0], rs.at[0], ctx=at.sib).start()
        pltpu.make_async_copy(self.own, self.dst.at[at.k], self.sems[4]).start()

    def forward(self, i):
        at, ss, rs, fs, fr = self.at, *self.sems[:4]
        src = at.back[i]
        rcopy(self.own, self.dst.at[src], ss.at[i], rs.at[i], ctx=at.same[i]).wait_recv()
        rcopy(self.dst.at[src], self.dst.at[src], fs.at[i], fr.at[i], ctx=at.sib).start()

    def finish(self):
        at, ss, rs, fs, fr = self.at, *self.sems[:4]
        pltpu.make_async_copy(self.own, self.dst.at[at.k], self.sems[4]).wait()
        rcopy(self.own, self.dst.at[at.k], ss.at[0], rs.at[0], ctx=at.sib).wait()
        for i in range(1, at.chips):
            rcopy(self.own, self.dst.at[at.k], ss.at[i], rs.at[i], ctx=at.same[i]).wait_send()
            rcopy(self.own, self.dst.at[at.k], fs.at[i], fr.at[i], ctx=at.sib).wait()

    @staticmethod
    def scratch(z):
        n = z.ctx // 2
        return [DMA((n,)), DMA((n,)), DMA((n,)), DMA((n,)), DMA]


def matmul(a, b, ca=1, cb=0):
    return lax.dot_general(a, b, (((ca,), (cb,)), ((), ())), preferred_element_type=F32)


def block(z, d):
    return pl.ds(pl.multiple_of(d * z.rows, z.rows), z.rows)


class CtxReduce:
    def __init__(self, at, part, bufs):
        self.at, self.part = at, part
        self.sb, self.sr, self.zb, self.zr, self.mid, self.ss, self.sn, self.zs, self.zn, self.ms, self.mn = bufs
        self.first = jnp.where(at.chip == 3, 1, 3)
        self.second = 4 - self.first

    def core_at(self, t):
        return 2 * lax.rem(self.at.chip + t, 4) + self.at.core

    def sib(self, t):
        return rcopy(self.sb.at[t], self.sr.at[t], self.ss.at[t], self.sn.at[t], ctx=self.at.sib)

    def far(self, t):
        return rcopy(self.zb.at[t], self.zr.at[t], self.zs.at[t], self.zn.at[t], ctx=self.core_at(t))

    def via(self):
        return rcopy(self.zb.at[self.first], self.mid, self.ms, self.mn, ctx=self.core_at(self.second))

    def start(self):
        at = self.at
        for t in (self.first, self.second, 2, 0):
            self.sb[t] = self.part(self.core_at(t) + 1 - 2 * at.core).astype(BF16)
            self.sib(t).start()
        for n, t in enumerate((self.first, self.second, 2)):
            mine = self.part(self.core_at(t))
            self.sib(t).wait_recv()
            mine = mine + self.sr[t].astype(F32)
            self.zb[t] = mine.astype(BF16)
            if n < 2:
                @pl.when(~at.edge)
                def _():
                    self.far(t).start()
            if n == 0:
                @pl.when(at.edge)
                def _():
                    self.via().start()
            if n == 2:
                @pl.when(at.edge)
                def _():
                    self.via().wait_send()
                    self.far(self.second).start()

                @pl.when(~at.edge)
                def _():
                    self.via().wait_recv()
                    self.zb[2] = (mine + self.mid[...].astype(F32)).astype(BF16)

                self.far(2).start()

    def finish(self, own=None):
        at = self.at
        total = self.part(at.k) if own is None else own
        self.sib(0).wait_recv()
        total = total + self.sr[0].astype(F32)
        for t in (1, 3, 2):
            if t == 2:
                self.far(2).wait_recv()
            else:
                none = at.chip == (0 if t == 1 else 3)

                @pl.when(none)
                def _():
                    self.zr[t] = jnp.zeros(self.zr.shape[1:], BF16)

                @pl.when(~none)
                def _():
                    self.far(t).wait_recv()
            total = total + self.zr[t].astype(F32)
        return total

    def close(self):
        for t in range(4):
            self.sib(t).wait_send()
        self.far(2).wait_send()
        self.far(self.second).wait_send()

        @pl.when(~self.at.edge)
        def _():
            self.far(self.first).wait_send()

    @staticmethod
    def scratch(z):
        return [pltpu.VMEM((4, z.rows, z.width), BF16)] * 4 + [pltpu.VMEM((z.rows, z.width), BF16)] + [DMA((4,))] * 4 + [DMA, DMA]


NEG = -1e30


def turn(v):
    return jnp.transpose(v.astype(F32)).astype(BF16)


def of_head(v, h, head):
    lane = lax.broadcasted_iota(jnp.int32, v.shape, 1) // head
    return jnp.where(lane == h, v.astype(F32), 0.0)


def attend_block(heads, k, v_t, q, mask, head, p_ref):
    parts = []
    for h in range(heads):
        qh = (of_head(q, h, head) * head ** -0.5).astype(BF16)
        s = matmul(k, qh, 1, 1) + mask
        e = jnp.exp(s - jnp.max(s, axis=0, keepdims=True))
        p = (e * (1.0 / jnp.sum(e, axis=0, keepdims=True))).astype(BF16)
        p_ref[h] = p
        parts.append(matmul(v_t[h * head : (h + 1) * head], p))
    o_t = parts[0] if len(parts) == 1 else jnp.concatenate(parts, axis=0)
    return jnp.transpose(o_t).astype(BF16)


class FarGather:
    def __init__(self, at, own, dst, sems):
        self.at, self.own, self.dst = at, own, dst
        self.ss, self.rs, self.fs, self.fr, self.lo, self.ho = sems

    def each(self):
        return range(len(self.own))

    def to(self, u, i):
        return rcopy(self.own[u], self.dst[u].at[self.at.k], self.ss.at[u, i], self.rs.at[u, i], ctx=self.at.same[i])

    def side(self, u, i):
        b = self.dst[u].at[self.at.back[i]]
        return rcopy(b, b, self.fs.at[u, i], self.fr.at[u, i], ctx=self.at.sib)

    def hop(self, u, i, step):
        b = self.dst[u].at[self.at.back[i]]
        return rcopy(b, b, self.ho.at[u], self.rs.at[u, 2], ctx=lax.rem(self.at.k + step + self.at.ctx, self.at.ctx))

    def local(self, u):
        return pltpu.make_async_copy(self.own[u], self.dst[u].at[self.at.k], self.lo.at[u])

    def sibling(self, u):
        return rcopy(self.own[u], self.dst[u].at[self.at.k], self.fs.at[u, 0], self.fr.at[u, 0], ctx=self.at.sib)

    def start(self):
        for u in self.each():
            @pl.when(self.at.chip != 3)
            def _():
                self.to(u, 1).start()

            @pl.when(self.at.chip != 0)
            def _():
                self.to(u, 3).start()

            self.local(u).start()
            self.sibling(u).start()

    def relay(self):
        for chip, near in ((0, 1), (3, 3)):
            @pl.when(self.at.chip == chip)
            def _():
                for u in self.each():
                    self.to(u, near).wait_send()
                    self.to(u, 4 - near).start()
                    self.to(u, 2).start()

        for chip, near, step in ((1, 3, -2), (2, 1, 2)):
            @pl.when(self.at.chip == chip)
            def _():
                for u in self.each():
                    self.to(u, near).wait_recv()
                    self.hop(u, near, step).start()

    def forward(self):
        for i in (1, 3, 2):
            for u in self.each():
                if i == 2:
                    self.to(u, i).wait_recv()
                else:
                    @pl.when(self.at.chip != (2 if i == 1 else 1))
                    def _():
                        self.to(u, i).wait_recv()
                self.side(u, i).start()

    def finish(self):
        for u in self.each():
            self.local(u).wait()
            self.sibling(u).wait()
            for i in (1, 3, 2):
                self.side(u, i).wait()

            @pl.when(self.at.chip != 0)
            def _():
                self.to(u, 1).wait_send()

            @pl.when(self.at.chip != 3)
            def _():
                self.to(u, 3).wait_send()

            @pl.when(self.at.edge)
            def _():
                self.to(u, 2).wait_send()

            @pl.when(~self.at.edge)
            def _():
                self.hop(u, 1, 2).wait_send()

    @staticmethod
    def scratch(z):
        return [DMA((2, 4)), DMA((2, 4)), DMA((2, 4)), DMA((2, 4)), DMA((2,)), DMA((2,))]


def place_rows(flat, piece, offset):
    wide = piece.shape[1] + 128
    base, shift = offset // 128 * 128, offset % 128
    padded = jnp.concatenate([piece, jnp.zeros((8, 128), F32)], axis=1)
    flat[:, base : base + wide] += pltpu.roll(padded, shift, 1) if shift else padded


def take_row(flat, start, width):
    base, shift = start // 128 * 128, start % 128
    wide = -(-(shift + width) // 128) * 128
    v = flat[:, base : base + wide]
    if shift:
        v = pltpu.roll(v, wide - shift, 1)
    return v[0:1, 0:width]


def kernel_first(z, n_g, n_b, qb, order, length, xt, ct, wv, w, pk, upw, dnw,
                 ua, wf, wo2, wol, upa, dna, xao, n1o, qo, ko, vo, p_fo, p_ro, o_fo,
                 prm, live, wo_f, o_r, hid, xh, rs_o, n2a,
                 x, up, wr, pa, xa, n1, q, k, v, p_f, p_r, o_f, vt, vrt, wvm, wo_r, kp, qp, gflat, bflat, n2,
                 mz_s, mz_r, rz_s, rz_r, mx_s, mx_r, us, ur, oz_s, oz_r, ox_s, ox_r, loc, pz_s, pz_r, px_s, px_r, wl, wb, ns, nr, *rest):
    at = Place(z)
    me, s, C, S, FW, RW, SH, D, R, N = at.k, at.s, z.ctx, z.seq, z.full_width, z.rest_width, z.shard, z.width, z.rows, z.slot
    ffg = FarGather(at, (upw, dnw), (upa, dna), rest[:6])
    tok = CtxGather(at, x, xa, rest[6:12])
    bufs = rest[12:]
    others = [lax.rem(me + i, C) for i in range(1, C)]
    greet(others, at.seqs[1:], False)

    x[...] = jnp.transpose(xt[...].astype(F32)).astype(BF16)
    half, lens = z.block_len, length[0]
    row = lax.broadcasted_iota(jnp.int32, (R, 128), 0)
    where = jnp.where(row < half, order[2 * me] * half + row, order[2 * me + 1] * half + row - half)
    live[...] = jnp.where(where < lens, 1.0, 0.0)
    up[...] = (jnp.transpose(ct[...].astype(F32)) * live[:, 0:1]).astype(BF16)
    wr[...] = jnp.zeros_like(wr)
    wr[:, 0:RW] = wv[:, z.main :]
    met(C + S - 2)

    def rows_of(j):
        return pl.ds(pl.multiple_of(j * SH, 8), SH)

    def cols(j):
        return wv.at[:, pl.ds(pl.multiple_of(j * FW, FW), FW)]

    def main(m, j):
        return wf.at[m, rows_of(j), pl.ds(0, FW)]

    def tail(m, j):
        return wf.at[m, rows_of(j), pl.ds(FW, FW)]

    def both(m, j):
        return wf.at[m, rows_of(j)]

    before, after = wo2.at[pl.ds(0, SH)], wo2.at[pl.ds(SH, SH)]
    lastrows = w.at[pl.ds(z.main - (C - 1) * SH, RW)]

    for i in range(1, C):
        rcopy(pk, pa.at[s, me], pz_s.at[i], pz_r.at[i], ctx=others[i - 1]).start()
    pltpu.make_async_copy(pk, pa.at[s, me], loc.at[3]).start()

    @pl.when(s < 3)
    def _():
        for i in range(1, C):
            j = lax.rem(me + i, C)
            rcopy(cols(j), main(s, me), mz_s.at[i], mz_r.at[me], ctx=j).start()
            rcopy(wr, tail(s, me), rz_s.at[i], rz_r.at[me], ctx=j).start()
        pltpu.make_async_copy(cols(me), main(s, me), loc.at[0]).start()
        pltpu.make_async_copy(wr, tail(s, me), loc.at[1]).start()

    @pl.when(s == 3)
    def _():
        @pl.when(me < C - 1)
        def _():
            rcopy(w, before, oz_s.at[0], oz_r.at[0], ctx=lax.rem(me + 1, C)).start()

        @pl.when(me == C - 1)
        def _():
            for i in range(1, C):
                rcopy(lastrows, wol, oz_s.at[i], oz_r.at[1], ctx=lax.rem(me + i, C)).start()
            pltpu.make_async_copy(lastrows, wol, loc.at[1]).start()

        pltpu.make_async_copy(wv, after, loc.at[0]).start()
        for i in range(1, 4):
            rcopy(w, after, ox_s.at[0, i], ox_r.at[0], seq=at.seqs[i]).start()

    for i in range(1, C):
        rcopy(pk, pa.at[s, lax.rem(me + C - i, C)], pz_s.at[i], pz_r.at[i], ctx=me).wait_recv()
    pltpu.make_async_copy(pk, pa.at[s, me], loc.at[3]).wait()
    for i in range(1, S):
        rcopy(pa.at[s], pa.at[s], px_s.at[i], px_r.at[i], seq=at.seqs[i]).start()

    for b in range(N // half):
        p = order[b] * half + lax.broadcasted_iota(jnp.int32, (half, 128), 0)
        kp[b * half : (b + 1) * half] = jnp.where(p < lens, p, 1 << 30)
    lane = lax.broadcasted_iota(jnp.int32, (8, 128), 1)
    for b in range(N // 128):
        qp[:, b * 128 : (b + 1) * 128] = jnp.where(
            lane < half, order[2 * b] * half + lane, order[2 * b + 1] * half + lane - half)

    @pl.when(s < 3)
    def _():
        for n in range(C):
            src = lax.rem(me + C - n, C)
            if n == 0:
                pltpu.make_async_copy(cols(me), main(s, me), loc.at[0]).wait()
                pltpu.make_async_copy(wr, tail(s, me), loc.at[1]).wait()
            else:
                rcopy(cols(me), main(s, src), mz_s.at[0], mz_r.at[src], ctx=me).wait_recv()
                rcopy(wr, tail(s, src), rz_s.at[0], rz_r.at[src], ctx=me).wait_recv()
            for i in range(1, 4):
                rcopy(both(s, src), both(s, src), mx_s.at[n, i], mx_r.at[s, src], seq=at.seqs[i]).start()

    @pl.when(s == 3)
    def _():
        pltpu.make_async_copy(wv, after, loc.at[0]).wait()

        @pl.when(me > 0)
        def _():
            rcopy(w, before, oz_s.at[0], oz_r.at[0], ctx=me).wait_recv()
            for i in range(1, 4):
                rcopy(before, before, ox_s.at[1, i], ox_r.at[1], seq=at.seqs[i]).start()

        @pl.when(me < C - 1)
        def _():
            rcopy(lastrows, wol, oz_s.at[1], oz_r.at[1], ctx=me).wait_recv()

        @pl.when(me == C - 1)
        def _():
            pltpu.make_async_copy(lastrows, wol, loc.at[1]).wait()

        for i in range(1, 4):
            rcopy(wol, wol, ox_s.at[2, i], ox_r.at[2], seq=at.seqs[i]).start()

    tok.send()
    ffg.start()

    for i in range(1, S):
        rcopy(pa.at[s], pa.at[at.seqs_back[i]], px_s.at[i], px_r.at[i], seq=s).wait()
    gflat[...] = jnp.zeros_like(gflat)
    bflat[...] = jnp.zeros_like(bflat)
    for d in range(S * C):
        t = pa[d // C, d % C].astype(F32)
        place_rows(gflat, jnp.broadcast_to(t[0:1], (8, 128)), d * n_g)
        place_rows(bflat, jnp.broadcast_to(jnp.concatenate([t[1:2], t[2:3], t[3:4]], axis=1), (8, 384)), d * n_b)
    for j in range(2):
        prm[j : j + 1] = take_row(gflat, j * D, D)
    for j in range(10):
        prm[2 + j : 3 + j] = take_row(bflat, j * D, D)

    def norm_rows(j, src):
        n1[block(z, j)] = (norm_stats(src.astype(F32))[0] * prm[0:1] + prm[2:3]).astype(BF16)

    tok.send_rest()
    norm_rows(me, x[...])
    for i in (1, 3, 2):
        tok.forward(i)
        norm_rows(at.back[i], xa[at.back[i]])
    tok.finish()

    def norm_other(j, _):
        d = 2 * j + 1 - at.core
        norm_rows(d, xa[d])
        return 0

    lax.fori_loop(0, at.chips, norm_other, 0)
    ffg.relay()

    for m in range(3):
        @pl.when(s != m)
        def _():
            for src in range(C):
                rcopy(both(m, src), both(m, src), mx_s.at[0, 0], mx_r.at[m, src], seq=s).wait_recv()
    wload = [pltpu.make_async_copy(wf.at[m], wvm.at[m], wl.at[m]) for m in range(3)]
    for c in wload:
        c.start()

    @pl.when(s != 3)
    def _():
        rcopy(w, after, ox_s.at[0, 0], ox_r.at[0], seq=s).wait_recv()

        @pl.when(me > 0)
        def _():
            rcopy(w, before, ox_s.at[1, 0], ox_r.at[1], seq=s).wait_recv()

        rcopy(wol, wol, ox_s.at[2, 0], ox_r.at[2], seq=s).wait_recv()

    wload += [
        pltpu.make_async_copy(wo2.at[pl.ds(pl.multiple_of(SH - (SH - FW) * me, 8), FW)], wo_f, wl.at[3]),
        pltpu.make_async_copy(wol, wo_r, wl.at[4]),
    ]
    wload[3].start()
    wload[4].start()

    def bias(j):
        a = prm[j : j + 1]
        own = jnp.zeros((1, FW), F32)
        for c in range(C):
            own = own + jnp.where(me == c, a[:, c * FW : (c + 1) * FW], 0.0)
        return jnp.concatenate([own, a[:, z.main :], jnp.zeros((1, FW - RW), F32)], axis=1)

    wload[0].wait()
    q[...] = (matmul(n1[...], wvm[0]) + bias(3)).astype(BF16)
    wload[1].wait()
    k[...] = matmul(n1[...], wvm[1]).astype(BF16)
    wload[2].wait()
    v[...] = (matmul(n1[...], wvm[2]) + bias(4)).astype(BF16)
    backs = [pltpu.make_async_copy(a, b, wb.at[i]) for i, (a, b) in enumerate(((n1, n1o), (q, qo), (k, ko), (v, vo), (xa, xao)))]
    for c in backs:
        c.start()
    vt[...] = turn(v[:, 0:FW])
    vrt[...] = turn(v[:, FW : 2 * FW])[0:RW]
    mine = block(z, me)

    for i in range(1, S):
        rcopy(up, ua.at[s], us.at[i], ur.at[i], seq=at.seqs[i]).start()
    pltpu.make_async_copy(up, ua.at[s], loc.at[2]).start()

    def steps(j, _):
        r = pl.ds(pl.multiple_of(j * qb, qb), qb)
        mask = jnp.where(jnp.concatenate([kp[...]] * (qb // 128), axis=1) <= qp[0:1, r], 0.0, NEG)
        o_f[r] = attend_block(z.full, k[:, 0:FW], vt[...], q[r, 0:FW], mask, z.head, p_f.at[j])
        return 0

    lax.fori_loop(0, N // qb, steps, 0)
    mask = jnp.where(kp[...] <= qp[0:1, mine], 0.0, NEG)
    o_r[...] = attend_block(z.rest, k[:, FW : 2 * FW], vrt[...], q[mine, FW : 2 * FW], mask, z.head, p_r)
    more = [pltpu.make_async_copy(a, b, wb.at[5 + i]) for i, (a, b) in enumerate(((p_f, p_fo), (p_r, p_ro), (o_f, o_fo)))]
    for c in more:
        c.start()
    wload[3].wait()
    wload[4].wait()
    red = CtxReduce(at, lambda d: matmul(o_f[block(z, d)], wo_f[...]), bufs)
    red.start()
    ffg.forward()
    own = matmul(o_r[...], wo_r[...]) + prm[5:6] + x[...].astype(F32)
    hidden = red.finish() + own
    xhat, rstd = norm_stats(hidden)
    n2[...] = (xhat * prm[1:2] + prm[6:7]).astype(BF16)
    copies = [rcopy(n2, n2a.at[s], ns.at[i], nr.at[i], seq=at.seqs[i]) for i in (2, 1, 3)]
    for c in copies:
        c.start()
    n2a[s] = n2[...]
    hid[...] = hidden
    xh[...] = xhat
    rs_o[...] = jnp.broadcast_to(rstd, rs_o.shape)

    red.close()
    ffg.finish()
    pltpu.make_async_copy(up, ua.at[s], loc.at[2]).wait()
    for i in range(1, S):
        rcopy(up, ua.at[s], us.at[i], ur.at[i], seq=at.seqs[i]).wait()
    for i in range(1, C):
        rcopy(pk, pa.at[s, me], pz_s.at[i], pz_r.at[i], ctx=me).wait_send()

    @pl.when(s < 3)
    def _():
        for i in range(1, C):
            rcopy(cols(me), main(s, me), mz_s.at[i], mz_r.at[me], ctx=me).wait_send()
            rcopy(wr, tail(s, me), rz_s.at[i], rz_r.at[me], ctx=me).wait_send()
        for n in range(C):
            for i in range(1, 4):
                rcopy(both(s, me), both(s, me), mx_s.at[n, i], mx_r.at[s, me], seq=s).wait_send()

    @pl.when(s == 3)
    def _():
        @pl.when(me < C - 1)
        def _():
            rcopy(w, before, oz_s.at[0], oz_r.at[0], ctx=me).wait_send()

        @pl.when(me == C - 1)
        def _():
            for i in range(1, C):
                rcopy(lastrows, wol, oz_s.at[i], oz_r.at[1], ctx=me).wait_send()

        for i in range(1, 4):
            rcopy(w, after, ox_s.at[0, i], ox_r.at[0], seq=s).wait_send()

            @pl.when(me > 0)
            def _():
                rcopy(before, before, ox_s.at[1, i], ox_r.at[1], seq=s).wait_send()

            rcopy(wol, wol, ox_s.at[2, i], ox_r.at[2], seq=s).wait_send()

    for c in backs + more:
        c.wait()
    for c in copies:
        c.wait()


def stage_first_kernel(z, tokens, lengths, block_order, w, up_weights, down_weights, norm_gains, biases, cotangent):
    N, D, FW, RW, R, S, C, SH, qb = z.slot, z.width, z.full_width, z.rest_width, z.rows, z.seq, z.ctx, z.shard, 256
    nq, W2 = N // qb, 2 * FW
    n_g, n_b = norm_gains.shape[0], biases.shape[0]
    pk = jnp.concatenate([jnp.pad(norm_gains, (0, 128 - n_g)), jnp.pad(biases, (0, 896 - n_b))]).reshape(8, 128)
    ins = (block_order, lengths, tokens[0].T, cotangent[0].T, w, w, pk, up_weights.T, down_weights)
    shapes = dict(
        ua=(S, R, D), w3=(3, D, W2), wo2=(2 * SH, D), wo_r=(RW, D), up_t=(C, SH, D), down=(C, SH, D), xa=(C, R, D), n1=(N, D), q=(N, W2),
        k=(N, W2), v=(N, W2), p_f=(nq, z.full, N, qb), p_r=(z.rest, N, R), o_f=(N, FW))
    wide = dict(prm=(12, D), live=(R, 128), wo_f=(FW, D), o_r=(R, RW), hid=(R, D), xh=(R, D), rs=(R, 128), n2a=(S, R, D))
    low = ("wo_f", "o_r", "n2a")
    outs = [sds(a) for a in shapes.values()] + [sds(a, BF16 if n in low else F32) for n, a in wide.items()]
    V = pltpu.VMEM
    scratch = [
        V((R, D), BF16), V((R, D), BF16), V((SH, FW), BF16), V((S, C, 8, 128), BF16), V((C, R, D), BF16), V((N, D), BF16),
        V((N, W2), BF16), V((N, W2), BF16), V((N, W2), BF16), V((nq, z.full, N, qb), BF16), V((z.rest, N, R), BF16), V((N, FW), BF16),
        V((FW, N), BF16), V((RW, N), BF16), V((3, D, W2), BF16), V((RW, D), BF16), V((N, 128), jnp.int32), V((8, N), jnp.int32),
        V((8, -(-2 * D // 128) * 128 + 256), F32), V((8, -(-10 * D // 128) * 128 + 512), F32), V((R, D), BF16),
        DMA((C,)), DMA((C,)), DMA((C,)), DMA((C,)), DMA((C, 4)), DMA((3, C)), DMA((4,)), DMA((4,)), DMA((C,)), DMA((2,)), DMA((3, 4)),
        DMA((3,)), DMA((4,)), DMA((C,)), DMA((C,)), DMA((S,)), DMA((S,)), DMA((5,)), DMA((8,)), DMA((S,)), DMA((S,)),
        *FarGather.scratch(z), *CtxGather.scratch(z), *CtxReduce.scratch(z),
    ]
    spaces = {"v": pltpu.VMEM, "a": pl.ANY, "s": pltpu.SMEM}
    out = pl.pallas_call(
        partial(kernel_first, z, n_g, n_b, qb), name="first_half", out_shape=outs,
        in_specs=[pl.BlockSpec(memory_space=spaces[c]) for c in "ssvvvaavv"],
        out_specs=[pl.BlockSpec(memory_space=spaces[c]) for c in "a" * 14 + "v" * 8],
        scratch_shapes=scratch,
        compiler_params=pltpu.CompilerParams(collective_id=0, has_side_effects=True, vmem_limit_bytes=VMEM_LIMIT),
    )(*ins)
    return dict(zip(tuple(shapes) + tuple(wide), out))


def ff_block(z, j):
    return pl.ds(pl.multiple_of(j * z.shard, 8), z.shard)


def kernel_f(z, n2h, uah, uph, dnh, prm, hid, xh, rs_i, live, out, gh_o, gb_o, sm, bu, gba, ffr,
             n2, ua, up_t, down, act, gpre, gsend, grecv, fsend, frecv, g32, fs, fr, ld, gs, gr, cs, cr, ps, pr, wb, *gsem):
    at = Place(z)
    S, R, D, C = z.seq, z.rows, z.width, z.ctx
    units, step = up_t.shape[0], 256
    b_up = prm[pl.ds(8 + at.s, 1)]
    greet([at.sib] + at.same[1:], at.seqs[1:], False)
    chunks = [slice(c0, min(c0 + step, units)) for c0 in range(0, units, step)]
    loads = [pltpu.make_async_copy(n2h, n2, ld.at[0]), pltpu.make_async_copy(uah, ua, ld.at[1])]
    for i, c in enumerate(chunks):
        loads.append(pltpu.make_async_copy(uph.at[c], up_t.at[c], ld.at[2 + 2 * i]))
        loads.append(pltpu.make_async_copy(dnh.at[c], down.at[c], ld.at[3 + 2 * i]))
    for c in loads:
        c.start()
    loads[0].wait()
    loads[1].wait()
    for i, c in enumerate(chunks):
        loads[2 + 2 * i].wait()
        pre = matmul(n2[...], up_t[c], 1, 1) + b_up[:, c]
        loads[3 + 2 * i].wait()
        gact = matmul(ua[...], down[c], 1, 1)
        cdf = 0.5 * (1.0 + lax.erf(pre * (0.5 ** 0.5)))
        act[:, c] = (pre * cdf).astype(BF16)
        dgelu = cdf + pre * jnp.exp(-0.5 * pre * pre) * (1.0 / math.sqrt(2.0 * math.pi))
        g = (gact * dgelu).astype(BF16)
        gpre[:, c] = g
        bu[:, c] = jnp.sum(g.astype(F32), axis=0, keepdims=True)
    met(at.chips + S - 1)

    def gcopy(i):
        return rcopy(gsend.at[i], grecv.at[i], gs.at[i], gr.at[i], seq=at.seqs[i])

    def fcopy(i):
        return rcopy(fsend.at[i], frecv.at[i], cs.at[i], cr.at[i], seq=at.seqs[i])

    def pair(t, u):
        return rcopy(fs.at[t, u], fr.at[t, u], ps.at[t, u], pr.at[t, u], ctx=at.sib)

    def weight_grad(u, left, right):
        for c in chunks:
            g32[u, c] = matmul(left[:, c], right[...], 0, 0)
        for t in range(4):
            fs[t, u] = g32[u, ff_block(z, 2 * at.ring[t] + 1 - at.core)].astype(BF16)
            pair(t, u).start()

    def both(u):
        for t in range(4):
            pair(t, u).wait_recv()
            fr[t, u] = (g32[u, ff_block(z, at.same[t])] + fr[t, u].astype(F32)).astype(BF16)
            pltpu.make_async_copy(fr.at[t, u], ffr.at[t, u], wb.at[t, u]).start()

    for i in (2, 1, 3):
        gsend[i] = matmul(gpre[block(z, at.seqs[i])], up_t[...]).astype(BF16)
        gcopy(i).start()
    mine = block(z, at.s)
    gn2 = matmul(gpre[mine], up_t[...])
    weight_grad(0, gpre, n2)
    for i in range(1, S):
        gcopy(i).wait_recv()
        gn2 = gn2 + grecv[i].astype(F32)
    xhat = xh[...]
    up_own = ua[mine].astype(F32)
    gh = up_own + norm_back(gn2, xhat, rs_i[:, :1], prm[1:2])
    gb_o[...] = gh.astype(BF16)
    gat = DirectGather(at, gb_o, gba, gsem)
    gat.send()
    gh_o[...] = gh
    sm[0:1] = jnp.sum(gn2 * xhat, axis=0, keepdims=True)
    sm[1:2] = jnp.sum(gn2, axis=0, keepdims=True)
    sm[2:3] = jnp.sum(gb_o[...].astype(F32), axis=0, keepdims=True)
    sm[3:4] = jnp.sum(up_own, axis=0, keepdims=True)
    for i in (2, 1, 3):
        fsend[i] = matmul(act[block(z, at.seqs[i])], down[...]).astype(BF16)
        fcopy(i).start()
    ff = matmul(act[mine], down[...])
    weight_grad(1, act, ua)
    both(0)
    for i in (1, 3):
        gat.forward(i)
    both(1)
    for i in range(1, S):
        fcopy(i).wait_recv()
        ff = ff + frecv[i].astype(F32)
    out[...] = jnp.transpose(live[:, :1] * (hid[...] + ff + prm[7:8])).astype(BF16)
    gat.forward(2)
    gat.finish()
    for t in range(4):
        for u in range(2):
            pair(t, u).wait_send()
            pltpu.make_async_copy(fr.at[t, u], ffr.at[t, u], wb.at[t, u]).wait()
    for i in range(1, S):
        gcopy(i).wait_send()
        fcopy(i).wait_send()


def stage_f_kernel(z, b):
    R, D, S, U, C, SH = z.rows, z.width, z.seq, z.ctx * z.shard, z.ctx, z.shard
    outs = [sds((D, R)), sds((R, D), F32), sds((R, D)), sds((4, D), F32), sds((1, U), F32), sds((C, R, D)), sds((4, 2, SH, D))]
    V = pltpu.VMEM
    scratch = [
        V((S * R, D), BF16), V((S * R, D), BF16), V((U, D), BF16), V((U, D), BF16), V((S * R, U), BF16), V((S * R, U), BF16),
        *[V((S, R, D), BF16) for _ in range(4)], V((2, U, D), F32), V((4, 2, SH, D), BF16), V((4, 2, SH, D), BF16),
        DMA((2 + 2 * -(-U // 256),)), *[DMA((S,)) for _ in range(4)], DMA((4, 2)), DMA((4, 2)), DMA((4, 2)),
        *DirectGather.scratch(z),
    ]
    return call(
        partial(kernel_f, z), "feed_forward", outs,
        (b["n2a"].reshape(S * R, D), b["ua"].reshape(S * R, D), b["up_t"].reshape(U, D), b["down"].reshape(U, D),
         b["prm"], b["hid"], b["xh"], b["rs"], b["live"]), scratch, 2, "aaaa" + "v" * 5, "v" * 5 + "aa",
    )


class SmallSum:
    def __init__(self, at, buf, rsib, rchip, rseq, sems):
        self.at, self.buf, self.rsib, self.rchip, self.rseq = at, buf, rsib, rchip, rseq
        self.s0, self.r0, self.s1, self.r1, self.s2, self.r2 = sems

    def sib(self):
        return rcopy(self.buf.at[0], self.rsib, self.s0, self.r0, ctx=self.at.sib)

    def chip(self, i):
        return rcopy(self.buf.at[1], self.rchip.at[i], self.s1.at[i], self.r1.at[i], ctx=self.at.same[i])

    def line(self, i):
        return rcopy(self.buf.at[2], self.rseq.at[i], self.s2.at[i], self.r2.at[i], seq=self.at.seqs[i])

    def first(self, value):
        self.buf[0] = value
        self.sib().start()

    def second(self):
        self.sib().wait_recv()
        self.buf[1] = self.buf[0] + self.rsib[...]
        for i in range(1, self.at.chips):
            self.chip(i).start()

    def third(self):
        total = self.buf[1]
        for i in range(1, self.at.chips):
            self.chip(i).wait_recv()
            total = total + self.rchip[i]
        self.buf[2] = total
        for i in range(1, len(self.at.seqs)):
            self.line(i).start()

    def last(self):
        total = self.buf[2]
        for i in range(1, len(self.at.seqs)):
            self.line(i).wait_recv()
            total = total + self.rseq[i]
        return total

    def close(self):
        self.sib().wait_send()
        for i in range(1, self.at.chips):
            self.chip(i).wait_send()
        for i in range(1, len(self.at.seqs)):
            self.line(i).wait_send()

    @staticmethod
    def scratch(z, rows):
        n, shape = z.ctx // 2, (rows, z.width)
        return [
            pltpu.VMEM((3,) + shape, F32), pltpu.VMEM(shape, F32), pltpu.VMEM((n,) + shape, F32),
            pltpu.VMEM((z.seq,) + shape, F32), DMA, DMA, DMA((n,)), DMA((n,)), DMA((z.seq,)), DMA((z.seq,)),
        ]


def attend_block_back(heads, k_t, v, q, go, p_ref, head, gk, gv):
    parts = []
    for h in range(heads):
        goh = of_head(go, h, head).astype(BF16)
        p = p_ref[h]
        pf = p.astype(F32)
        gp = matmul(v, goh, 1, 1)
        delta = jnp.sum(gp * pf, axis=0, keepdims=True)
        gs = (pf * (gp - delta)).astype(BF16)
        gk[...] += matmul(gs, of_head(q, h, head).astype(BF16))
        gv[...] += matmul(p, goh)
        parts.append(matmul(k_t[h * head : (h + 1) * head], gs))
    g_t = parts[0] if len(parts) == 1 else jnp.concatenate(parts, axis=0)
    return (jnp.transpose(g_t) * head ** -0.5).astype(BF16)


def kernel_de(z, qb, gbah, kh, oh, vh, qh, pfh, prh, wh, n1h, xah, ffr,
              wo_f, wo_r, o_r, gh, prm, sm4, bu,
              gtok, ga, gup, gdn, tot, bup,
              gba, k, o_f, v, q, p_f, p_r, w, n1, xa, ld,
              go, kt, krt, gk, gv, gkr, gvr, gcat, gw, gwr, gwo, gwor, sums, ffz, ffo, comb, mid, fz_s, fz_r, fo, fm,
              rf, rr, ro, ror, sf_s, sf_r, sr_s, sr_r, so_s, so_r, sor_s, sor_r,
              zs, zr, land, landr, zs_s, zs_r, zr_s, zr_r,
              buf32, obs, obn, orrs, orr, ob_s, ob_r, orr_s, orr_r, *rest):
    at = Place(z)
    s, me, C, S, FW, RW, SH, D = at.s, at.k, z.ctx, z.seq, z.full_width, z.rest_width, z.shard, z.width
    bufs, small = rest[:11], rest[11:]
    scale, top = z.head ** -0.5, TOP(z)
    mine = block(z, me)
    greet([lax.rem(me + i, C) for i in range(1, C)], at.seqs[1:], False)
    pairs = ((gbah, gba), (kh, k), (oh, o_f), (vh, v), (qh, q), (pfh, p_f), (prh, p_r), (wh, w), (n1h, n1), (xah, xa))
    loads = [pltpu.make_async_copy(a, b, ld.at[i]) for i, (a, b) in enumerate(pairs)]
    for c in loads:
        c.start()
    ownff = pltpu.make_async_copy(ffr.at[0], ffo, fo.at[0])
    ownff.start()
    farff = pltpu.make_async_copy(ffr.at[2], comb, fo.at[1])
    farff.start()
    met(C + S - 2)

    def fz(t):
        return rcopy(ffr.at[t], ffz.at[t], fz_s.at[t], fz_r.at[t], ctx=at.same[t])

    def via(t):
        return rcopy(ffr.at[t], mid, fm.at[0], fm.at[1], ctx=at.same[4 - t])

    def across():
        return rcopy(comb, ffz.at[2], fz_s.at[2], fz_r.at[2], ctx=at.same[2])

    @pl.when(at.chip == 0)
    def _():
        via(3).start()

    @pl.when(at.chip == 3)
    def _():
        via(1).start()

    @pl.when(~at.edge)
    def _():
        fz(1).start()
        fz(3).start()

    gk[...] = jnp.zeros_like(gk)
    gv[...] = jnp.zeros_like(gv)
    gkr[...] = jnp.zeros_like(gkr)
    gvr[...] = jnp.zeros_like(gvr)
    gcat[0, :, FW:] = jnp.zeros((z.slot, FW), BF16)
    for c in loads[:3]:
        c.wait()
    go[...] = matmul(gba[...], wo_f[...], 1, 1).astype(BF16)
    kt[...] = turn(k[:, 0:FW])
    krt[...] = turn(k[:, FW : 2 * FW])[0:RW]
    gwo[...] = matmul(o_f[...], gba[...], 0, 0).astype(BF16)
    gwor[...] = matmul(o_r[...], gba[mine], 0, 0).astype(BF16)

    def up(ref, dst, ssem, rsem, i, m=None):
        return rcopy(ref if m is None else ref.at[m], dst.at[i], ssem.at[i], rsem.at[i], seq=at.seqs[i])

    for i in range(1, S):
        @pl.when(at.seqs[i] == 3)
        def _():
            up(gwo, ro, so_s, so_r, i).start()
            up(gwor, ror, sor_s, sor_r, i).start()

    for c in loads[3:6]:
        c.wait()

    def steps(j, _):
        r = pl.ds(pl.multiple_of(j * qb, qb), qb)
        gcat[0, r, 0:FW] = attend_block_back(z.full, kt[...], v[:, 0:FW], q[r, 0:FW], go[r], p_f.at[j], z.head, gk, gv)
        return 0

    lax.fori_loop(0, z.slot // qb, steps, 0)

    farff.wait()

    @pl.when(at.chip == 0)
    def _():
        via(3).wait_send()
        fz(1).start()

    @pl.when(at.chip == 3)
    def _():
        via(1).wait_send()
        fz(3).start()

    @pl.when(~at.edge)
    def _():
        via(1).wait_recv()
        for u in range(2):
            comb[u] = (comb[u].astype(F32) + mid[u].astype(F32)).astype(BF16)

    across().start()
    loads[6].wait()
    gor = matmul(gba[mine], wo_r[...], 1, 1).astype(BF16)
    gor = jnp.concatenate([gor, jnp.zeros((z.rows, FW - RW), BF16)], axis=1)
    gcat[0, mine, FW : FW + RW] = attend_block_back(
        z.rest, krt[...], v[:, FW : 2 * FW], q[mine, FW : 2 * FW], gor, p_r, z.head, gkr, gvr)
    gcat[1, :, 0:FW] = (gk[...] * scale).astype(BF16)
    gcat[1, :, FW:] = (gkr[...] * scale).astype(BF16)
    gcat[2, :, 0:FW] = gv[...].astype(BF16)
    gcat[2, :, FW:] = gvr[...].astype(BF16)
    for c in loads[7:10]:
        c.wait()

    for m in (2, 1, 0):
        g = matmul(n1[...], gcat[m], 0, 0).reshape(C, SH, 2 * FW)
        gw[m] = g[:, :, 0:FW].astype(BF16)
        g = g[:, :, FW : FW + RW]
        low = jnp.concatenate([g[:, top:], jnp.zeros((C, 2 * top - SH, RW), F32)], axis=1)
        gwr[m] = jnp.concatenate([g[:, :top], low], axis=2).astype(BF16)
    for i in (2, 1, 3):
        m = at.seqs[i]

        @pl.when(m < 3)
        def _():
            up(gw, rf, sf_s, sf_r, i, m).start()
            up(gwr, rr, sr_s, sr_r, i, m).start()

    sums[...] = jnp.zeros_like(sums)

    def part(d):
        r = block(z, d)
        total = matmul(gcat[0, r], w[0], 1, 1) + matmul(gcat[1, r], w[1], 1, 1) + matmul(gcat[2, r], w[2], 1, 1)
        sums[8:9] += jnp.sum(total * norm_stats(xa[r].astype(F32))[0], axis=0, keepdims=True)
        sums[9:10] += jnp.sum(total, axis=0, keepdims=True)
        return total

    red = CtxReduce(at, part, bufs)
    red.start()
    own = part(me)

    def cols(m):
        a = jnp.sum(gcat[m].astype(F32), axis=0, keepdims=True)
        return jnp.concatenate([jnp.where(me == c, a[:, 0:FW], 0.0) for c in range(C)] + [a[:, FW : FW + RW]], axis=1)

    sums[0:4] = sm4[...]
    sums[4:5] = cols(0)
    sums[5:6] = cols(2)
    sums[6:7] = bu[...]
    se = SmallSum(at, *small[:4], small[4:])
    se.first(sums[...])

    se.second()

    def zf(i):
        return rcopy(zs.at[lax.rem(me + i, C)], land.at[i], zs_s.at[i], zs_r.at[i], ctx=lax.rem(me + i, C))

    def zrr(i):
        return rcopy(zr.at[lax.rem(me + i, C)], landr.at[i], zr_s.at[i], zr_r.at[i], ctx=lax.rem(me + i, C))

    def shift():
        return rcopy(obs, obn, ob_s, ob_r, ctx=lax.rem(me + C - 1, C))

    def tail(i):
        return rcopy(orrs, orr.at[i], orr_s, orr_r.at[i], ctx=C - 1)

    @pl.when(s < 3)
    def _():
        for i in range(1, S):
            up(gw, rf, sf_s, sf_r, i, 0).wait_recv()
            up(gwr, rr, sr_s, sr_r, i, 0).wait_recv()

        def add(j, _):
            t, u = gw[s, j].astype(F32), gwr[s, j].astype(F32)
            for i in range(1, S):
                t = t + rf[i, j].astype(F32)
                u = u + rr[i, j].astype(F32)
            zs[j] = t.astype(BF16)
            zr[j] = u.astype(BF16)
            return 0

        lax.fori_loop(0, C, add, 0)
        for i in range(1, C):
            zf(i).start()
            zrr(i).start()

    @pl.when(s == 3)
    def _():
        for i in range(1, S):
            up(gwo, ro, so_s, so_r, i).wait_recv()
            up(gwor, ror, sor_s, sor_r, i).wait_recv()
        t, u = gwo[...].astype(F32), gwor[...].astype(F32)
        for i in range(1, S):
            t = t + ro[i].astype(F32)
            u = u + ror[i].astype(F32)
        buf32[pl.ds(0, FW)] = t
        obs[...] = t.astype(BF16)
        orrs[...] = u.astype(BF16)

        @pl.when(me > 0)
        def _():
            shift().start()

        for i in range(C - 1):
            @pl.when(me == i)
            def _():
                tail(i).start()

    se.third()

    ownff.wait()
    across().wait_recv()
    for u, g in enumerate((gup, gdn)):
        g[...] = ffo[u].astype(F32) + ffz[2, u].astype(F32)
    for t in (1, 3):
        @pl.when(at.chip != (0 if t == 1 else 3))
        def _():
            fz(t).wait_recv()
            for u, g in enumerate((gup, gdn)):
                g[...] += ffz[t, u].astype(F32)

    xhat, rstd = norm_stats(xa[mine].astype(F32))
    gn1 = red.finish(own)
    gtok[...] = jnp.transpose(gh[...] + norm_back(gn1, xhat, rstd, prm[0:1]))

    @pl.when(s < 3)
    def _():
        ga[:, pl.ds(pl.multiple_of(me * FW, FW), FW)] = zs[me].astype(F32)
        remain = zr[me].astype(F32)
        for i in range(1, C):
            zf(i).wait_recv()
            zrr(i).wait_recv()
            j = lax.rem(me + C - i, C)
            ga[:, pl.ds(pl.multiple_of(j * FW, FW), FW)] = land[i].astype(F32)
            remain = remain + landr[i].astype(F32)
        ga[0:top, z.main :] = remain[:, 0:RW]
        ga[top:SH, z.main :] = remain[0 : SH - top, RW : 2 * RW]
        for i in range(1, C):
            zf(i).wait_send()
            zrr(i).wait_send()

    @pl.when(s == 3)
    def _():
        @pl.when(me < C - 1)
        def _():
            shift().wait_recv()
            buf32[pl.ds(FW, FW)] = obn[...].astype(F32)

        @pl.when(me == C - 1)
        def _():
            u = orrs[...].astype(F32)
            for i in range(C - 1):
                tail(i).wait_recv()
                u = u + orr[i].astype(F32)
            buf32[pl.ds(FW, RW)] = u

        ga[...] = buf32[pl.ds(pl.multiple_of((SH - FW) * me, 8), SH)]

        @pl.when(me > 0)
        def _():
            shift().wait_send()

        @pl.when(me < C - 1)
        def _():
            tail(0).wait_send()

    tot[...] = se.last()
    bup[s] = se.buf[2, 6:7]
    for i in range(1, S):
        bup[at.seqs_back[i]] = se.rseq[i, 6:7]
    red.close()
    se.close()
    across().wait_send()

    @pl.when(at.chip != 3)
    def _():
        fz(1).wait_send()

    @pl.when(at.chip != 0)
    def _():
        fz(3).wait_send()
    for i in range(1, S):
        m = at.seqs[i]

        @pl.when(m < 3)
        def _():
            up(gw, rf, sf_s, sf_r, i, m).wait_send()
            up(gwr, rr, sr_s, sr_r, i, m).wait_send()

        @pl.when(m == 3)
        def _():
            up(gwo, ro, so_s, so_r, i).wait_send()
            up(gwor, ror, sor_s, sor_r, i).wait_send()


def TOP(z):
    return -(-z.shard // 16) * 8


def stage_de_kernel(z, b, gba, ffr, gh, sm4, bu):
    C, S, D, FW, RW, SH, N, R, qb = z.ctx, z.seq, z.width, z.full_width, z.rest_width, z.shard, z.slot, z.rows, 256
    nq, W2, top = N // qb, 2 * FW, TOP(z)
    outs = [sds((D, R), F32), sds((SH, D), F32), sds((SH, D), F32), sds((SH, D), F32), sds((10, D), F32), sds((S, 1, D), F32)]
    V = pltpu.VMEM
    scratch = [
        V((N, D), BF16), V((N, W2), BF16), V((N, FW), BF16), V((N, W2), BF16), V((N, W2), BF16), V((nq, z.full, N, qb), BF16),
        V((z.rest, N, R), BF16), V((3, D, W2), BF16), V((N, D), BF16), V((N, D), BF16), DMA((10,)),
        V((N, FW), BF16), V((FW, N), BF16), V((RW, N), BF16), *[V((N, FW), F32) for _ in range(4)],
        V((3, N, W2), BF16), V((3, C, SH, FW), BF16), V((3, C, top, 2 * RW), BF16), V((FW, D), BF16), V((RW, D), BF16), V((10, D), F32),
        V((4, 2, SH, D), BF16), V((2, SH, D), BF16), V((2, SH, D), BF16), V((2, SH, D), BF16), DMA((4,)), DMA((4,)), DMA((2,)), DMA((2,)),
        V((S, C, SH, FW), BF16), V((S, C, top, 2 * RW), BF16), V((S, FW, D), BF16), V((S, RW, D), BF16), *[DMA((S,)) for _ in range(8)],
        V((C, SH, FW), BF16), V((C, top, 2 * RW), BF16), V((C, SH, FW), BF16), V((C, top, 2 * RW), BF16),
        *[DMA((C,)) for _ in range(4)],
        V((2 * FW, D), F32), V((FW, D), BF16), V((FW, D), BF16), V((RW, D), BF16), V((C, RW, D), BF16),
        DMA, DMA, DMA, DMA((C,)),
        *CtxReduce.scratch(z), *SmallSum.scratch(z, 10),
    ]
    gtok, ga, gup, gdn, tot, bup = call(
        partial(kernel_de, z, qb), "attention_back", outs,
        (gba.reshape(N, D), b["k"], b["o_f"], b["v"], b["q"], b["p_f"], b["p_r"], b["w3"], b["n1"], b["xa"].reshape(N, D), ffr,
         b["wo_f"], b["wo_r"], b["o_r"], gh, b["prm"], sm4, bu),
        scratch, 4, "a" * 11 + "v" * 7, "v" * 6,
    )
    names = ("gain2", "shift2", "b_o", "b_down", "b_q", "b_v", None, None, "gain1", "shift1")
    return gtok, ga, gup, gdn, {n: tot[j : j + 1] for j, n in enumerate(names) if n}, bup.reshape(-1)


def kernel_leave(n, *refs):
    ins, outs, bufs, sems = refs[:n], refs[n : 2 * n], refs[2 * n : 3 * n], refs[3 * n]
    loads = [pltpu.make_async_copy(ins[i], bufs[i], sems.at[0, i]) for i in range(n)]
    stores = [pltpu.make_async_copy(bufs[i], outs[i], sems.at[1, i]) for i in range(n)]
    for c in loads:
        c.start()
    for a, b in zip(loads, stores):
        a.wait()
        b.start()
    for c in stores:
        c.wait()


def leave(arrays):
    n = len(arrays)
    return pl.pallas_call(
        partial(kernel_leave, n), name="leave", out_shape=[sds(a.shape, a.dtype) for a in arrays],
        in_specs=[pl.BlockSpec(memory_space=pl.ANY)] * n, out_specs=[pl.BlockSpec(memory_space=pl.ANY)] * n,
        scratch_shapes=[pltpu.VMEM(a.shape, a.dtype) for a in arrays] + [DMA((2, n))],
    )(*arrays)


def shards(tokens, lengths, block_order, attention_weights, up_weights, down_weights, norm_gains, biases, cotangent):
    z = Sizes(tokens.shape[1], tokens.shape[2], block_order.shape[0])
    i, s = lax.axis_index("ctx"), lax.axis_index("seq")
    me, D = s * z.ctx + i, z.width
    n_g, n_b = norm_gains.shape[0], biases.shape[0]
    fast = (
        z.ctx == 8 and z.seq == 4 and 0 < D - z.main <= z.shard and z.rest == 1 and z.full_width == 128
        and z.ctx * up_weights.shape[1] == D and z.rows == 2 * z.block_len and n_g <= 128 and n_b <= 384
    )
    if fast:
        b = stage_first_kernel(
            z, tokens, lengths, block_order, attention_weights, up_weights, down_weights, norm_gains, biases, cotangent)
        output, gh, _, sm4, bu, gba, ffr = stage_f_kernel(z, b)
        gtok, gw, g_up_own, g_down_own, tot, b_up_all = stage_de_kernel(z, b, gba, ffr, gh, sm4, bu)
    else:
        x, cot, length = tokens[0], cotangent[0], lengths[0]
        pos = (block_order[:, None] * z.block_len + jnp.arange(z.block_len, dtype=jnp.int32)[None, :]).reshape(z.slot)
        my_pos = lax.dynamic_slice_in_dim(pos, i * z.rows, z.rows)
        live = (my_pos < length).astype(F32)[:, None]
        lanes = -(-(n_g + n_b) // 1024) * 8
        packed = jnp.pad(jnp.concatenate([norm_gains, biases]), (0, lanes * 128 - n_g - n_b)).reshape(lanes, 128)
        upstream = (live * cot.astype(F32)).astype(BF16)
        x_all, wf, wr, wo_f, wo_r = stage_a(z, x, attention_weights)
        ua = lax.all_gather(upstream, "seq", axis=0, tiled=True)
        both = lax.all_gather(packed, ("seq", "ctx"), axis=0).reshape(z.seq * z.ctx, lanes * 128)
        gains = both[:, :n_g].reshape(-1).astype(F32)
        bias = both[:, n_g : n_g + n_b].reshape(-1).astype(F32)
        row = lambda v: v[None, :]
        piece = [row(bias[j * D : (j + 1) * D]) for j in range(6)]
        gain1, gain2 = row(gains[:D]), row(gains[D:])
        units = z.ctx * up_weights.shape[1]
        b_up = row(lax.dynamic_slice_in_dim(bias[6 * D :], s * units, units))
        prm = dict(gain2=gain2, shift2=piece[4], b_o=piece[3], b_down=piece[5], b_up=b_up)
        fslice = lambda v: lax.dynamic_slice(v, (0, i * z.full_width), (1, z.full_width))
        up_t = lax.all_gather(up_weights.T, "ctx", axis=0, tiled=True)
        down = lax.all_gather(down_weights, "ctx", axis=0, tiled=True)
        b = stage_b(z, x_all, wf, wr, gain1, piece[0], fslice(piece[1]), piece[1][:, z.main :],
                    fslice(piece[2]), piece[2][:, z.main :], pos, length)
        output, gh, gb, g_up_t, g_down, small = stage_c(z, b, wo_f, wo_r, x, upstream, ua, live, up_t, down, prm)
        g_up_own = lax.psum_scatter(g_up_t, "ctx", scatter_dimension=0, tiled=True).astype(F32).T
        g_down_own = lax.psum_scatter(g_down, "ctx", scatter_dimension=0, tiled=True).astype(F32)
        gba = lax.all_gather(gb, "ctx", axis=0, tiled=True) if z.full else None
        d = stage_d(z, b, gb, gba, wo_f, wo_r)
        gtok, gw, tot, b_up_all = stage_e(z, d, wf, wr, x, gh, gain1, small)
    if fast:
        output, gtok, gw, g_up_own, g_down_own = leave((output, gtok, gw, g_up_own, g_down_own))
        output, gtok, g_up_own = output.T, gtok.T, g_up_own.T
    g_gain = lax.dynamic_slice_in_dim(jnp.concatenate([tot["gain1"][0], tot["gain2"][0]]), me * n_g, n_g)
    g_bias = lax.dynamic_slice_in_dim(jnp.concatenate([tot[n][0] for n in ("shift1", "b_q", "b_v", "b_o", "shift2", "b_down")] + [b_up_all]), me * n_b, n_b)
    return output[None], gtok[None], gw, g_up_own, g_down_own, g_gain, g_bias


def solution(mesh):
    in_specs = (
        P("seq", "ctx", None), P("seq"), P(), P(("seq", "ctx"), None), P(None, ("seq", "ctx")),
        P(("seq", "ctx"), None), P(("seq", "ctx")), P(("seq", "ctx")), P("seq", "ctx", None),
    )
    out_specs = (
        P("seq", "ctx", None), P("seq", "ctx", None), P(("seq", "ctx"), None), P(None, ("seq", "ctx")),
        P(("seq", "ctx"), None), P(("seq", "ctx")), P(("seq", "ctx")),
    )
    return jax.shard_map(shards, mesh=mesh, in_specs=in_specs, out_specs=out_specs, check_vma=False)
```

```python
import math
from functools import partial

import jax
import jax.numpy as jnp
from jax import lax
from jax.experimental import pallas as pl
from jax.experimental.pallas import tpu as pltpu
from jax.sharding import PartitionSpec as P

HEADS = 17
EPS = 1e-05
F32 = jnp.float32
BF16 = jnp.bfloat16


def norm_stats(values):
    centre = values - jnp.mean(values, axis=-1, keepdims=True)
    rstd = lax.rsqrt(jnp.mean(centre * centre, axis=-1, keepdims=True) + EPS)
    return centre * rstd, rstd


def norm_back(grad, xhat, rstd, gain):
    e = grad * gain
    mean_e = jnp.mean(e, axis=-1, keepdims=True)
    mean_ex = jnp.mean(e * xhat, axis=-1, keepdims=True)
    return (e - mean_e - xhat * mean_ex) * rstd


def dot(a, b, ca, cb):
    return lax.dot_general(a, b, (((ca,), (cb,)), ((), ())), preferred_element_type=F32)


def rows_sum(v):
    return jnp.sum(v.astype(F32), axis=0, keepdims=True)


class Sizes:
    def __init__(self, rows, width, block_count):
        self.rows, self.width = rows, width
        self.ctx, self.seq = lax.axis_size("ctx"), lax.axis_size("seq")
        self.slot = rows * self.ctx
        self.block_len = self.slot // block_count
        self.head = width // HEADS
        self.full = HEADS // self.ctx
        self.full_width = self.full * self.head
        self.main = self.full_width * self.ctx
        self.rest = HEADS - self.full * self.ctx
        self.rest_width = self.rest * self.head
        self.shard = width // self.ctx


def stage_a(z, x, w):
    k = lax.axis_index("ctx")
    x_all = lax.all_gather(x, "ctx", axis=0, tiled=True)
    w_all = lax.all_gather(w, "seq", axis=0)
    wm = w_all[:3, :, : z.main].reshape(3, z.shard, z.ctx, z.full_width)
    wf = lax.all_to_all(wm, "ctx", split_axis=2, concat_axis=1, tiled=True).reshape(
        3, z.width, z.full_width
    )
    wr = lax.all_gather(w_all[:3, :, z.main :], "ctx", axis=1, tiled=True)
    wo = lax.all_gather(w_all[3], "ctx", axis=0, tiled=True)
    wo_f = lax.dynamic_slice_in_dim(wo, k * z.full_width, z.full_width)
    wo_r = wo[z.main :]
    return x_all, wf, wr, wo_f, wo_r


def heads_of(v, h):
    return v.reshape(v.shape[0], -1, h).transpose(1, 0, 2)


def attend(z, q, k, v, qpos, kpos, length):
    s = jnp.einsum("hqd,hkd->hkq", heads_of(q, z.head), heads_of(k, z.head), preferred_element_type=F32)
    s = s * (z.head ** -0.5)
    seen = (kpos[:, None] <= qpos[None, :]) & (kpos[:, None] < length)
    s = jnp.where(seen[None], s, -1e30)
    e = jnp.exp(s - jnp.max(s, axis=1, keepdims=True))
    p = (e / jnp.sum(e, axis=1, keepdims=True)).astype(BF16)
    o = jnp.einsum("hkq,hkd->qhd", p, heads_of(v, z.head), preferred_element_type=F32)
    return p, o.reshape(q.shape).astype(BF16)


def stage_b(z, x_all, wf, wr, gain, shift, bq_f, bq_r, bv_f, bv_r, pos, length):
    i = lax.axis_index("ctx")
    n1 = (norm_stats(x_all.astype(F32))[0] * gain + shift).astype(BF16)
    mine = lax.dynamic_slice_in_dim(n1, i * z.rows, z.rows)
    qpos = lax.dynamic_slice_in_dim(pos, i * z.rows, z.rows)
    out = dict(n1=n1)
    if z.full:
        q = (dot(n1, wf[0], 1, 0) + bq_f).astype(BF16)
        k = dot(n1, wf[1], 1, 0).astype(BF16)
        v = (dot(n1, wf[2], 1, 0) + bv_f).astype(BF16)
        p, o = attend(z, q, k, v, pos, pos, length)
        out.update(q_f=q, k_f=k, v_f=v, p_f=p, o_f=o)
    if z.rest:
        q = (dot(mine, wr[0], 1, 0) + bq_r).astype(BF16)
        k = dot(n1, wr[1], 1, 0).astype(BF16)
        v = (dot(n1, wr[2], 1, 0) + bv_r).astype(BF16)
        p, o = attend(z, q, k, v, qpos, pos, length)
        out.update(q_r=q, k_r=k, v_r=v, p_r=p, o_r=o)
    return out


def stage_c(z, b, wo_f, wo_r, x, upstream, ua, live, up_t, down, prm):
    branch = prm["b_o"]
    if z.full:
        part = dot(b["o_f"], wo_f, 1, 0).astype(BF16)
        branch = branch + lax.psum_scatter(part.astype(F32), "ctx", scatter_dimension=0, tiled=True)
    if z.rest:
        branch = branch + dot(b["o_r"], wo_r, 1, 0)
    hidden = x.astype(F32) + branch
    xhat, rstd = norm_stats(hidden)
    n2 = (xhat * prm["gain2"] + prm["shift2"]).astype(BF16)
    n2a = lax.all_gather(n2, "seq", axis=0, tiled=True)
    pre = dot(n2a, up_t, 1, 1) + prm["b_up"]
    cdf = 0.5 * (1.0 + lax.erf(pre * (0.5 ** 0.5)))
    act = (pre * cdf).astype(BF16)
    dgelu = cdf + pre * jnp.exp(-0.5 * pre * pre) * (1.0 / math.sqrt(2.0 * math.pi))
    gact = dot(ua, down, 1, 1)
    gpre = (gact * dgelu).astype(BF16)
    gn2p = dot(gpre, up_t, 1, 0).astype(BF16)
    gn2 = lax.psum_scatter(gn2p.astype(F32), "seq", scatter_dimension=0, tiled=True)
    ffp = dot(act, down, 1, 0).astype(BF16)
    ff = lax.psum_scatter(ffp.astype(F32), "seq", scatter_dimension=0, tiled=True)
    output = (live * (hidden + ff + prm["b_down"])).astype(BF16)
    g_up_t = dot(gpre, n2a, 0, 0).astype(BF16)
    g_down = dot(act, ua, 0, 0).astype(BF16)
    gh = upstream.astype(F32) + norm_back(gn2, xhat, rstd, prm["gain2"])
    gb = gh.astype(BF16)
    small = dict(gain2=rows_sum(gn2 * xhat), shift2=rows_sum(gn2), b_o=rows_sum(gb),
                 b_down=rows_sum(upstream), b_up=rows_sum(gpre))
    return output, gh, gb, g_up_t, g_down, small


def attend_back(z, q, k, v, p, go):
    gp = jnp.einsum("hqd,hkd->hkq", heads_of(go, z.head), heads_of(v, z.head), preferred_element_type=F32)
    pf = p.astype(F32)
    delta = jnp.sum(gp * pf, axis=1, keepdims=True)
    gs = (pf * (gp - delta)).astype(BF16)
    sc = z.head ** -0.5
    gq = jnp.einsum("hkq,hkd->qhd", gs, heads_of(k, z.head), preferred_element_type=F32) * sc
    gk = jnp.einsum("hkq,hqd->khd", gs, heads_of(q, z.head), preferred_element_type=F32) * sc
    gv = jnp.einsum("hkq,hqd->khd", p, heads_of(go, z.head), preferred_element_type=F32)
    return gq.reshape(q.shape).astype(BF16), gk.reshape(k.shape).astype(BF16), gv.reshape(v.shape).astype(BF16)


def stage_d(z, b, gb, gba, wo_f, wo_r):
    i = lax.axis_index("ctx")
    n1 = b["n1"]
    mine = lax.dynamic_slice_in_dim(n1, i * z.rows, z.rows)
    out = {}
    if z.full:
        go = dot(gba, wo_f, 1, 1).astype(BF16)
        gq, gk, gv = attend_back(z, b["q_f"], b["k_f"], b["v_f"], b["p_f"], go)
        out.update(gq_f=gq, gk_f=gk, gv_f=gv, gwo_f=dot(b["o_f"], gba, 0, 0))
        out["gw_f"] = jnp.stack([dot(n1, g, 0, 0) for g in (gq, gk, gv)])
    if z.rest:
        go = dot(gb, wo_r, 1, 1).astype(BF16)
        gq, gk, gv = attend_back(z, b["q_r"], b["k_r"], b["v_r"], b["p_r"], go)
        out.update(gq_r=gq, gk_r=gk, gv_r=gv, gwo_r=dot(b["o_r"], gb, 0, 0))
        out["gw_r"] = jnp.stack([dot(mine, gq, 0, 0), dot(n1, gk, 0, 0), dot(n1, gv, 0, 0)])
    return out


def stage_e(z, d, wf, wr, x, gh, gain1, small):
    i, s = lax.axis_index("ctx"), lax.axis_index("seq")
    part = 0.0
    own = 0.0
    if z.full:
        part = part + dot(d["gq_f"], wf[0], 1, 1) + dot(d["gk_f"], wf[1], 1, 1) + dot(d["gv_f"], wf[2], 1, 1)
    if z.rest:
        part = part + dot(d["gk_r"], wr[1], 1, 1) + dot(d["gv_r"], wr[2], 1, 1)
        own = own + dot(d["gq_r"], wr[0], 1, 1)
    gn1 = own + lax.psum_scatter(part.astype(BF16).astype(F32), "ctx", scatter_dimension=0, tiled=True)
    xhat, rstd = norm_stats(x.astype(F32))
    gtok = gh + norm_back(gn1, xhat, rstd, gain1)
    small = dict(small, gain1=rows_sum(gn1 * xhat), shift1=rows_sum(gn1))
    row = jnp.zeros((1, z.width), F32)
    for name, key in (("b_q", "gq"), ("b_v", "gv")):
        r = row
        if z.full:
            r = lax.dynamic_update_slice(r, rows_sum(d[key + "_f"]), (0, i * z.full_width))
        if z.rest:
            r = r.at[:, z.main :].add(rows_sum(d[key + "_r"]))
        small[name] = r
    full = jnp.zeros((4, z.width, z.width), F32)
    if z.full:
        full = lax.dynamic_update_slice(full, d["gw_f"], (0, 0, i * z.full_width))
        full = lax.dynamic_update_slice(full, d["gwo_f"][None], (3, i * z.full_width, 0))
    if z.rest:
        full = full.at[:3, :, z.main :].add(d["gw_r"])
        full = full.at[3, z.main :, :].add(d["gwo_r"])
    gw = lax.psum_scatter(full.reshape(4 * z.width, z.width).astype(BF16), ("seq", "ctx"), scatter_dimension=0, tiled=True)
    b_up_all = lax.all_gather(lax.psum(small.pop("b_up"), "ctx")[0], "seq", axis=0, tiled=True)
    names = list(small)
    tot = lax.psum(jnp.concatenate([small[n] for n in names]), ("seq", "ctx"))
    return gtok, gw.astype(F32), {n: tot[j : j + 1] for j, n in enumerate(names)}, b_up_all


MESH = pl.DeviceIdType.MESH
DMA = pltpu.SemaphoreType.DMA
VMEM_LIMIT = 56 << 20


def rcopy(src, dst, ssem, rsem, **dev):
    return pltpu.make_async_remote_copy(
        src_ref=src, dst_ref=dst, send_sem=ssem, recv_sem=rsem, device_id=dev, device_id_type=MESH
    )


def greet(ctx_peers, seq_peers, wait=True):
    sem = pltpu.get_barrier_semaphore()
    for p in ctx_peers:
        pl.semaphore_signal(sem, inc=1, device_id={"ctx": p}, device_id_type=MESH)
    for p in seq_peers:
        pl.semaphore_signal(sem, inc=1, device_id={"seq": p}, device_id_type=MESH)
    if wait:
        met(len(ctx_peers) + len(seq_peers))


def met(count):
    pl.semaphore_wait(pltpu.get_barrier_semaphore(), count)


class Place:
    def __init__(self, z):
        self.k, self.s = lax.axis_index("ctx"), lax.axis_index("seq")
        self.chips, self.ctx = z.ctx // 2, z.ctx
        self.core = lax.rem(self.k, 2)
        self.chip = self.k // 2
        self.sib = self.k + 1 - 2 * self.core
        self.edge = (self.chip == 0) | (self.chip == self.chips - 1)
        self.ring = [lax.rem(self.chip + i, self.chips) for i in range(self.chips)]
        self.same = [2 * q + self.core for q in self.ring]
        self.back = [2 * lax.rem(self.chip + self.chips - i, self.chips) + self.core for i in range(self.chips)]
        self.seqs = [lax.rem(self.s + i, z.seq) for i in range(z.seq)]
        self.seqs_back = [lax.rem(self.s + z.seq - i, z.seq) for i in range(z.seq)]


def call(body, name, outs, ins, scratch, cid, in_spaces, out_spaces, cost=None):
    spaces = {"v": pltpu.VMEM, "a": pl.ANY}
    return pl.pallas_call(
        body,
        name=name,
        out_shape=outs,
        in_specs=[pl.BlockSpec(memory_space=spaces[c]) for c in in_spaces],
        out_specs=[pl.BlockSpec(memory_space=spaces[c]) for c in out_spaces],
        scratch_shapes=scratch,
        compiler_params=pltpu.CompilerParams(
            collective_id=cid, has_side_effects=True, vmem_limit_bytes=VMEM_LIMIT
        ),
        cost_estimate=cost,
    )(*ins)


def sds(shape, dtype=BF16):
    return jax.ShapeDtypeStruct(shape, dtype)


class CtxGather:
    def __init__(self, at, own, dst, sems):
        self.at, self.own, self.dst = at, own, dst
        self.ss, self.rs, self.fs, self.fr, self.lo, self.ho = sems

    def to(self, i):
        return rcopy(self.own, self.dst.at[self.at.k], self.ss.at[i], self.rs.at[i], ctx=self.at.same[i])

    def side(self, i):
        b = self.dst.at[self.at.back[i]]
        return rcopy(b, b, self.fs.at[i], self.fr.at[i], ctx=self.at.sib)

    def hop(self, i, step):
        b = self.dst.at[self.at.back[i]]
        return rcopy(b, b, self.ho, self.rs.at[2], ctx=lax.rem(self.at.k + step + self.at.ctx, self.at.ctx))

    def sibling(self):
        return rcopy(self.own, self.dst.at[self.at.k], self.fs.at[0], self.fr.at[0], ctx=self.at.sib)

    def local(self):
        return pltpu.make_async_copy(self.own, self.dst.at[self.at.k], self.lo)

    def send(self):
        @pl.when(self.at.chip != 3)
        def _():
            self.to(1).start()

        @pl.when(self.at.chip != 0)
        def _():
            self.to(3).start()

        self.sibling().start()
        self.local().start()

    def send_rest(self):
        @pl.when(self.at.chip == 0)
        def _():
            self.to(1).wait_send()
            self.to(3).start()
            self.to(2).start()

        @pl.when(self.at.chip == 3)
        def _():
            self.to(3).wait_send()
            self.to(1).start()
            self.to(2).start()

        @pl.when(self.at.chip == 1)
        def _():
            self.to(3).wait_recv()
            self.hop(3, -2).start()

        @pl.when(self.at.chip == 2)
        def _():
            self.to(1).wait_recv()
            self.hop(1, 2).start()

    def forward(self, i):
        if i == 2:
            self.to(i).wait_recv()
        else:
            @pl.when(self.at.chip != (2 if i == 1 else 1))
            def _():
                self.to(i).wait_recv()
        self.side(i).start()

    def finish(self):
        self.local().wait()
        self.sibling().wait()
        for i in (1, 3, 2):
            self.side(i).wait()

        @pl.when(self.at.chip != 0)
        def _():
            self.to(1).wait_send()

        @pl.when(self.at.chip != 3)
        def _():
            self.to(3).wait_send()

        @pl.when(self.at.edge)
        def _():
            self.to(2).wait_send()

        @pl.when(~self.at.edge)
        def _():
            self.hop(1, 2).wait_send()

    @staticmethod
    def scratch(z):
        return [DMA((4,)), DMA((4,)), DMA((4,)), DMA((4,)), DMA, DMA]


class DirectGather:
    def __init__(self, at, own, dst, sems):
        self.at, self.own, self.dst, self.sems = at, own, dst, sems

    def send(self):
        at, ss, rs = self.at, self.sems[0], self.sems[1]
        for i in range(1, at.chips):
            rcopy(self.own, self.dst.at[at.k], ss.at[i], rs.at[i], ctx=at.same[i]).start()
        rcopy(self.own, self.dst.at[at.k], ss.at[0], rs.at[0], ctx=at.sib).start()
        pltpu.make_async_copy(self.own, self.dst.at[at.k], self.sems[4]).start()

    def forward(self, i):
        at, ss, rs, fs, fr = self.at, *self.sems[:4]
        src = at.back[i]
        rcopy(self.own, self.dst.at[src], ss.at[i], rs.at[i], ctx=at.same[i]).wait_recv()
        rcopy(self.dst.at[src], self.dst.at[src], fs.at[i], fr.at[i], ctx=at.sib).start()

    def finish(self):
        at, ss, rs, fs, fr = self.at, *self.sems[:4]
        pltpu.make_async_copy(self.own, self.dst.at[at.k], self.sems[4]).wait()
        rcopy(self.own, self.dst.at[at.k], ss.at[0], rs.at[0], ctx=at.sib).wait()
        for i in range(1, at.chips):
            rcopy(self.own, self.dst.at[at.k], ss.at[i], rs.at[i], ctx=at.same[i]).wait_send()
            rcopy(self.own, self.dst.at[at.k], fs.at[i], fr.at[i], ctx=at.sib).wait()

    @staticmethod
    def scratch(z):
        n = z.ctx // 2
        return [DMA((n,)), DMA((n,)), DMA((n,)), DMA((n,)), DMA]


def matmul(a, b, ca=1, cb=0):
    return lax.dot_general(a, b, (((ca,), (cb,)), ((), ())), preferred_element_type=F32)


def block(z, d):
    return pl.ds(pl.multiple_of(d * z.rows, z.rows), z.rows)


class CtxReduce:
    def __init__(self, at, part, bufs):
        self.at, self.part = at, part
        self.sb, self.sr, self.zb, self.zr, self.mid, self.ss, self.sn, self.zs, self.zn, self.ms, self.mn = bufs
        self.first = jnp.where(at.chip == 3, 1, 3)
        self.second = 4 - self.first

    def core_at(self, t):
        return 2 * lax.rem(self.at.chip + t, 4) + self.at.core

    def sib(self, t):
        return rcopy(self.sb.at[t], self.sr.at[t], self.ss.at[t], self.sn.at[t], ctx=self.at.sib)

    def far(self, t):
        return rcopy(self.zb.at[t], self.zr.at[t], self.zs.at[t], self.zn.at[t], ctx=self.core_at(t))

    def via(self):
        return rcopy(self.zb.at[self.first], self.mid, self.ms, self.mn, ctx=self.core_at(self.second))

    def start(self):
        at = self.at
        for t in (self.first, self.second, 2, 0):
            self.sb[t] = self.part(self.core_at(t) + 1 - 2 * at.core).astype(BF16)
            self.sib(t).start()
        for n, t in enumerate((self.first, self.second, 2)):
            mine = self.part(self.core_at(t))
            self.sib(t).wait_recv()
            mine = mine + self.sr[t].astype(F32)
            self.zb[t] = mine.astype(BF16)
            if n < 2:
                @pl.when(~at.edge)
                def _():
                    self.far(t).start()
            if n == 0:
                @pl.when(at.edge)
                def _():
                    self.via().start()
            if n == 2:
                @pl.when(at.edge)
                def _():
                    self.via().wait_send()
                    self.far(self.second).start()

                @pl.when(~at.edge)
                def _():
                    self.via().wait_recv()
                    self.zb[2] = (mine + self.mid[...].astype(F32)).astype(BF16)

                self.far(2).start()

    def finish(self, own=None):
        at = self.at
        total = self.part(at.k) if own is None else own
        self.sib(0).wait_recv()
        total = total + self.sr[0].astype(F32)
        for t in (1, 3, 2):
            if t == 2:
                self.far(2).wait_recv()
            else:
                none = at.chip == (0 if t == 1 else 3)

                @pl.when(none)
                def _():
                    self.zr[t] = jnp.zeros(self.zr.shape[1:], BF16)

                @pl.when(~none)
                def _():
                    self.far(t).wait_recv()
            total = total + self.zr[t].astype(F32)
        return total

    def close(self):
        for t in range(4):
            self.sib(t).wait_send()
        self.far(2).wait_send()
        self.far(self.second).wait_send()

        @pl.when(~self.at.edge)
        def _():
            self.far(self.first).wait_send()

    @staticmethod
    def scratch(z):
        return [pltpu.VMEM((4, z.rows, z.width), BF16)] * 4 + [pltpu.VMEM((z.rows, z.width), BF16)] + [DMA((4,))] * 4 + [DMA, DMA]


NEG = -1e30


def turn(v):
    return jnp.transpose(v.astype(F32)).astype(BF16)


def of_head(v, h, head):
    lane = lax.broadcasted_iota(jnp.int32, v.shape, 1) // head
    return jnp.where(lane == h, v.astype(F32), 0.0)


def attend_block(heads, k, v_t, q, mask, head, p_ref):
    parts = []
    for h in range(heads):
        qh = (of_head(q, h, head) * head ** -0.5).astype(BF16)
        s = matmul(k, qh, 1, 1) + mask
        e = jnp.exp(s - jnp.max(s, axis=0, keepdims=True))
        p = (e * (1.0 / jnp.sum(e, axis=0, keepdims=True))).astype(BF16)
        p_ref[h] = p
        parts.append(matmul(v_t[h * head : (h + 1) * head], p))
    o_t = parts[0] if len(parts) == 1 else jnp.concatenate(parts, axis=0)
    return jnp.transpose(o_t).astype(BF16)


class FarGather:
    def __init__(self, at, own, dst, sems):
        self.at, self.own, self.dst = at, own, dst
        self.ss, self.rs, self.fs, self.fr, self.lo, self.ho = sems

    def each(self):
        return range(len(self.own))

    def to(self, u, i):
        return rcopy(self.own[u], self.dst[u].at[self.at.k], self.ss.at[u, i], self.rs.at[u, i], ctx=self.at.same[i])

    def side(self, u, i):
        b = self.dst[u].at[self.at.back[i]]
        return rcopy(b, b, self.fs.at[u, i], self.fr.at[u, i], ctx=self.at.sib)

    def hop(self, u, i, step):
        b = self.dst[u].at[self.at.back[i]]
        return rcopy(b, b, self.ho.at[u], self.rs.at[u, 2], ctx=lax.rem(self.at.k + step + self.at.ctx, self.at.ctx))

    def local(self, u):
        return pltpu.make_async_copy(self.own[u], self.dst[u].at[self.at.k], self.lo.at[u])

    def sibling(self, u):
        return rcopy(self.own[u], self.dst[u].at[self.at.k], self.fs.at[u, 0], self.fr.at[u, 0], ctx=self.at.sib)

    def start(self):
        for u in self.each():
            @pl.when(self.at.chip != 3)
            def _():
                self.to(u, 1).start()

            @pl.when(self.at.chip != 0)
            def _():
                self.to(u, 3).start()

            self.local(u).start()
            self.sibling(u).start()

    def relay(self):
        for chip, near in ((0, 1), (3, 3)):
            @pl.when(self.at.chip == chip)
            def _():
                for u in self.each():
                    self.to(u, near).wait_send()
                    self.to(u, 4 - near).start()
                    self.to(u, 2).start()

        for chip, near, step in ((1, 3, -2), (2, 1, 2)):
            @pl.when(self.at.chip == chip)
            def _():
                for u in self.each():
                    self.to(u, near).wait_recv()
                    self.hop(u, near, step).start()

    def forward(self):
        for i in (1, 3, 2):
            for u in self.each():
                if i == 2:
                    self.to(u, i).wait_recv()
                else:
                    @pl.when(self.at.chip != (2 if i == 1 else 1))
                    def _():
                        self.to(u, i).wait_recv()
                self.side(u, i).start()

    def finish(self):
        for u in self.each():
            self.local(u).wait()
            self.sibling(u).wait()
            for i in (1, 3, 2):
                self.side(u, i).wait()

            @pl.when(self.at.chip != 0)
            def _():
                self.to(u, 1).wait_send()

            @pl.when(self.at.chip != 3)
            def _():
                self.to(u, 3).wait_send()

            @pl.when(self.at.edge)
            def _():
                self.to(u, 2).wait_send()

            @pl.when(~self.at.edge)
            def _():
                self.hop(u, 1, 2).wait_send()

    @staticmethod
    def scratch(z):
        return [DMA((2, 4)), DMA((2, 4)), DMA((2, 4)), DMA((2, 4)), DMA((2,)), DMA((2,))]


def place_rows(flat, piece, offset):
    wide = piece.shape[1] + 128
    base, shift = offset // 128 * 128, offset % 128
    padded = jnp.concatenate([piece, jnp.zeros((8, 128), F32)], axis=1)
    flat[:, base : base + wide] += pltpu.roll(padded, shift, 1) if shift else padded


def take_row(flat, start, width):
    base, shift = start // 128 * 128, start % 128
    wide = -(-(shift + width) // 128) * 128
    v = flat[:, base : base + wide]
    if shift:
        v = pltpu.roll(v, wide - shift, 1)
    return v[0:1, 0:width]


def kernel_first(z, n_g, n_b, qb, order, length, xt, ct, wv, w, pk, upw, dnw,
                 ua, wf, wo2, wol, upa, dna, xao, n1o, qo, ko, vo, p_fo, p_ro, o_fo,
                 prm, live, wo_f, o_r, hid, xh, rs_o, n2a,
                 x, up, wr, pa, xa, n1, q, k, v, p_f, p_r, o_f, vt, vrt, wvm, wo_r, kp, qp, gflat, bflat, n2,
                 mz_s, mz_r, rz_s, rz_r, mx_s, mx_r, us, ur, oz_s, oz_r, ox_s, ox_r, loc, pz_s, pz_r, px_s, px_r, wl, wb, ns, nr, *rest):
    at = Place(z)
    me, s, C, S, FW, RW, SH, D, R, N = at.k, at.s, z.ctx, z.seq, z.full_width, z.rest_width, z.shard, z.width, z.rows, z.slot
    ffg = FarGather(at, (upw, dnw), (upa, dna), rest[:6])
    tok = CtxGather(at, x, xa, rest[6:12])
    bufs = rest[12:]
    others = [lax.rem(me + i, C) for i in range(1, C)]
    greet(others, at.seqs[1:], False)

    x[...] = jnp.transpose(xt[...].astype(F32)).astype(BF16)
    half, lens = z.block_len, length[0]
    row = lax.broadcasted_iota(jnp.int32, (R, 128), 0)
    where = jnp.where(row < half, order[2 * me] * half + row, order[2 * me + 1] * half + row - half)
    live[...] = jnp.where(where < lens, 1.0, 0.0)
    up[...] = (jnp.transpose(ct[...].astype(F32)) * live[:, 0:1]).astype(BF16)
    wr[...] = jnp.zeros_like(wr)
    wr[:, 0:RW] = wv[:, z.main :]
    met(C + S - 2)

    def rows_of(j):
        return pl.ds(pl.multiple_of(j * SH, 8), SH)

    def cols(j):
        return wv.at[:, pl.ds(pl.multiple_of(j * FW, FW), FW)]

    def main(m, j):
        return wf.at[m, rows_of(j), pl.ds(0, FW)]

    def tail(m, j):
        return wf.at[m, rows_of(j), pl.ds(FW, FW)]

    def both(m, j):
        return wf.at[m, rows_of(j)]

    before, after = wo2.at[pl.ds(0, SH)], wo2.at[pl.ds(SH, SH)]
    lastrows = w.at[pl.ds(z.main - (C - 1) * SH, RW)]

    for i in range(1, C):
        rcopy(pk, pa.at[s, me], pz_s.at[i], pz_r.at[i], ctx=others[i - 1]).start()
    pltpu.make_async_copy(pk, pa.at[s, me], loc.at[3]).start()

    @pl.when(s < 3)
    def _():
        for i in range(1, C):
            j = lax.rem(me + i, C)
            rcopy(cols(j), main(s, me), mz_s.at[i], mz_r.at[me], ctx=j).start()
            rcopy(wr, tail(s, me), rz_s.at[i], rz_r.at[me], ctx=j).start()
        pltpu.make_async_copy(cols(me), main(s, me), loc.at[0]).start()
        pltpu.make_async_copy(wr, tail(s, me), loc.at[1]).start()

    @pl.when(s == 3)
    def _():
        @pl.when(me < C - 1)
        def _():
            rcopy(w, before, oz_s.at[0], oz_r.at[0], ctx=lax.rem(me + 1, C)).start()

        @pl.when(me == C - 1)
        def _():
            for i in range(1, C):
                rcopy(lastrows, wol, oz_s.at[i], oz_r.at[1], ctx=lax.rem(me + i, C)).start()
            pltpu.make_async_copy(lastrows, wol, loc.at[1]).start()

        pltpu.make_async_copy(wv, after, loc.at[0]).start()
        for i in range(1, 4):
            rcopy(w, after, ox_s.at[0, i], ox_r.at[0], seq=at.seqs[i]).start()

    for i in range(1, C):
        rcopy(pk, pa.at[s, lax.rem(me + C - i, C)], pz_s.at[i], pz_r.at[i], ctx=me).wait_recv()
    pltpu.make_async_copy(pk, pa.at[s, me], loc.at[3]).wait()
    for i in range(1, S):
        rcopy(pa.at[s], pa.at[s], px_s.at[i], px_r.at[i], seq=at.seqs[i]).start()

    for b in range(N // half):
        p = order[b] * half + lax.broadcasted_iota(jnp.int32, (half, 128), 0)
        kp[b * half : (b + 1) * half] = jnp.where(p < lens, p, 1 << 30)
    lane = lax.broadcasted_iota(jnp.int32, (8, 128), 1)
    for b in range(N // 128):
        qp[:, b * 128 : (b + 1) * 128] = jnp.where(
            lane < half, order[2 * b] * half + lane, order[2 * b + 1] * half + lane - half)

    @pl.when(s < 3)
    def _():
        for n in range(C):
            src = lax.rem(me + C - n, C)
            if n == 0:
                pltpu.make_async_copy(cols(me), main(s, me), loc.at[0]).wait()
                pltpu.make_async_copy(wr, tail(s, me), loc.at[1]).wait()
            else:
                rcopy(cols(me), main(s, src), mz_s.at[0], mz_r.at[src], ctx=me).wait_recv()
                rcopy(wr, tail(s, src), rz_s.at[0], rz_r.at[src], ctx=me).wait_recv()
            for i in range(1, 4):
                rcopy(both(s, src), both(s, src), mx_s.at[n, i], mx_r.at[s, src], seq=at.seqs[i]).start()

    @pl.when(s == 3)
    def _():
        pltpu.make_async_copy(wv, after, loc.at[0]).wait()

        @pl.when(me > 0)
        def _():
            rcopy(w, before, oz_s.at[0], oz_r.at[0], ctx=me).wait_recv()
            for i in range(1, 4):
                rcopy(before, before, ox_s.at[1, i], ox_r.at[1], seq=at.seqs[i]).start()

        @pl.when(me < C - 1)
        def _():
            rcopy(lastrows, wol, oz_s.at[1], oz_r.at[1], ctx=me).wait_recv()

        @pl.when(me == C - 1)
        def _():
            pltpu.make_async_copy(lastrows, wol, loc.at[1]).wait()

        for i in range(1, 4):
            rcopy(wol, wol, ox_s.at[2, i], ox_r.at[2], seq=at.seqs[i]).start()

    tok.send()
    ffg.start()

    for i in range(1, S):
        rcopy(pa.at[s], pa.at[at.seqs_back[i]], px_s.at[i], px_r.at[i], seq=s).wait()
    gflat[...] = jnp.zeros_like(gflat)
    bflat[...] = jnp.zeros_like(bflat)
    for d in range(S * C):
        t = pa[d // C, d % C].astype(F32)
        place_rows(gflat, jnp.broadcast_to(t[0:1], (8, 128)), d * n_g)
        place_rows(bflat, jnp.broadcast_to(jnp.concatenate([t[1:2], t[2:3], t[3:4]], axis=1), (8, 384)), d * n_b)
    for j in range(2):
        prm[j : j + 1] = take_row(gflat, j * D, D)
    for j in range(10):
        prm[2 + j : 3 + j] = take_row(bflat, j * D, D)

    def norm_rows(j, src):
        n1[block(z, j)] = (norm_stats(src.astype(F32))[0] * prm[0:1] + prm[2:3]).astype(BF16)

    tok.send_rest()
    norm_rows(me, x[...])
    for i in (1, 3, 2):
        tok.forward(i)
        norm_rows(at.back[i], xa[at.back[i]])
    tok.finish()

    def norm_other(j, _):
        d = 2 * j + 1 - at.core
        norm_rows(d, xa[d])
        return 0

    lax.fori_loop(0, at.chips, norm_other, 0)
    ffg.relay()

    for m in range(3):
        @pl.when(s != m)
        def _():
            for src in range(C):
                rcopy(both(m, src), both(m, src), mx_s.at[0, 0], mx_r.at[m, src], seq=s).wait_recv()
    wload = [pltpu.make_async_copy(wf.at[m], wvm.at[m], wl.at[m]) for m in range(3)]
    for c in wload:
        c.start()

    @pl.when(s != 3)
    def _():
        rcopy(w, after, ox_s.at[0, 0], ox_r.at[0], seq=s).wait_recv()

        @pl.when(me > 0)
        def _():
            rcopy(w, before, ox_s.at[1, 0], ox_r.at[1], seq=s).wait_recv()

        rcopy(wol, wol, ox_s.at[2, 0], ox_r.at[2], seq=s).wait_recv()

    wload += [
        pltpu.make_async_copy(wo2.at[pl.ds(pl.multiple_of(SH - (SH - FW) * me, 8), FW)], wo_f, wl.at[3]),
        pltpu.make_async_copy(wol, wo_r, wl.at[4]),
    ]
    wload[3].start()
    wload[4].start()

    def bias(j):
        a = prm[j : j + 1]
        own = jnp.zeros((1, FW), F32)
        for c in range(C):
            own = own + jnp.where(me == c, a[:, c * FW : (c + 1) * FW], 0.0)
        return jnp.concatenate([own, a[:, z.main :], jnp.zeros((1, FW - RW), F32)], axis=1)

    wload[0].wait()
    q[...] = (matmul(n1[...], wvm[0]) + bias(3)).astype(BF16)
    wload[1].wait()
    k[...] = matmul(n1[...], wvm[1]).astype(BF16)
    wload[2].wait()
    v[...] = (matmul(n1[...], wvm[2]) + bias(4)).astype(BF16)
    backs = [pltpu.make_async_copy(a, b, wb.at[i]) for i, (a, b) in enumerate(((n1, n1o), (q, qo), (k, ko), (v, vo), (xa, xao)))]
    for c in backs:
        c.start()
    vt[...] = turn(v[:, 0:FW])
    vrt[...] = turn(v[:, FW : 2 * FW])[0:RW]
    mine = block(z, me)

    for i in range(1, S):
        rcopy(up, ua.at[s], us.at[i], ur.at[i], seq=at.seqs[i]).start()
    pltpu.make_async_copy(up, ua.at[s], loc.at[2]).start()

    def steps(j, _):
        r = pl.ds(pl.multiple_of(j * qb, qb), qb)
        mask = jnp.where(jnp.concatenate([kp[...]] * (qb // 128), axis=1) <= qp[0:1, r], 0.0, NEG)
        o_f[r] = attend_block(z.full, k[:, 0:FW], vt[...], q[r, 0:FW], mask, z.head, p_f.at[j])
        return 0

    lax.fori_loop(0, N // qb, steps, 0)
    mask = jnp.where(kp[...] <= qp[0:1, mine], 0.0, NEG)
    o_r[...] = attend_block(z.rest, k[:, FW : 2 * FW], vrt[...], q[mine, FW : 2 * FW], mask, z.head, p_r)
    more = [pltpu.make_async_copy(a, b, wb.at[5 + i]) for i, (a, b) in enumerate(((p_f, p_fo), (p_r, p_ro), (o_f, o_fo)))]
    for c in more:
        c.start()
    wload[3].wait()
    wload[4].wait()
    red = CtxReduce(at, lambda d: matmul(o_f[block(z, d)], wo_f[...]), bufs)
    red.start()
    ffg.forward()
    own = matmul(o_r[...], wo_r[...]) + prm[5:6] + x[...].astype(F32)
    hidden = red.finish() + own
    xhat, rstd = norm_stats(hidden)
    n2[...] = (xhat * prm[1:2] + prm[6:7]).astype(BF16)
    copies = [rcopy(n2, n2a.at[s], ns.at[i], nr.at[i], seq=at.seqs[i]) for i in (2, 1, 3)]
    for c in copies:
        c.start()
    n2a[s] = n2[...]
    hid[...] = hidden
    xh[...] = xhat
    rs_o[...] = jnp.broadcast_to(rstd, rs_o.shape)

    red.close()
    ffg.finish()
    pltpu.make_async_copy(up, ua.at[s], loc.at[2]).wait()
    for i in range(1, S):
        rcopy(up, ua.at[s], us.at[i], ur.at[i], seq=at.seqs[i]).wait()
    for i in range(1, C):
        rcopy(pk, pa.at[s, me], pz_s.at[i], pz_r.at[i], ctx=me).wait_send()

    @pl.when(s < 3)
    def _():
        for i in range(1, C):
            rcopy(cols(me), main(s, me), mz_s.at[i], mz_r.at[me], ctx=me).wait_send()
            rcopy(wr, tail(s, me), rz_s.at[i], rz_r.at[me], ctx=me).wait_send()
        for n in range(C):
            for i in range(1, 4):
                rcopy(both(s, me), both(s, me), mx_s.at[n, i], mx_r.at[s, me], seq=s).wait_send()

    @pl.when(s == 3)
    def _():
        @pl.when(me < C - 1)
        def _():
            rcopy(w, before, oz_s.at[0], oz_r.at[0], ctx=me).wait_send()

        @pl.when(me == C - 1)
        def _():
            for i in range(1, C):
                rcopy(lastrows, wol, oz_s.at[i], oz_r.at[1], ctx=me).wait_send()

        for i in range(1, 4):
            rcopy(w, after, ox_s.at[0, i], ox_r.at[0], seq=s).wait_send()

            @pl.when(me > 0)
            def _():
                rcopy(before, before, ox_s.at[1, i], ox_r.at[1], seq=s).wait_send()

            rcopy(wol, wol, ox_s.at[2, i], ox_r.at[2], seq=s).wait_send()

    for c in backs + more:
        c.wait()
    for c in copies:
        c.wait()


def stage_first_kernel(z, tokens, lengths, block_order, w, up_weights, down_weights, norm_gains, biases, cotangent):
    N, D, FW, RW, R, S, C, SH, qb = z.slot, z.width, z.full_width, z.rest_width, z.rows, z.seq, z.ctx, z.shard, 512
    nq, W2 = N // qb, 2 * FW
    n_g, n_b = norm_gains.shape[0], biases.shape[0]
    pk = jnp.concatenate([jnp.pad(norm_gains, (0, 128 - n_g)), jnp.pad(biases, (0, 896 - n_b))]).reshape(8, 128)
    ins = (block_order, lengths, tokens[0].T, cotangent[0].T, w, w, pk, up_weights.T, down_weights)
    shapes = dict(
        ua=(S, R, D), w3=(3, D, W2), wo2=(2 * SH, D), wo_r=(RW, D), up_t=(C, SH, D), down=(C, SH, D), xa=(C, R, D), n1=(N, D), q=(N, W2),
        k=(N, W2), v=(N, W2), p_f=(nq, z.full, N, qb), p_r=(z.rest, N, R), o_f=(N, FW))
    wide = dict(prm=(12, D), live=(R, 128), wo_f=(FW, D), o_r=(R, RW), hid=(R, D), xh=(R, D), rs=(R, 128), n2a=(S, R, D))
    low = ("wo_f", "o_r", "n2a")
    outs = [sds(a) for a in shapes.values()] + [sds(a, BF16 if n in low else F32) for n, a in wide.items()]
    V = pltpu.VMEM
    scratch = [
        V((R, D), BF16), V((R, D), BF16), V((SH, FW), BF16), V((S, C, 8, 128), BF16), V((C, R, D), BF16), V((N, D), BF16),
        V((N, W2), BF16), V((N, W2), BF16), V((N, W2), BF16), V((nq, z.full, N, qb), BF16), V((z.rest, N, R), BF16), V((N, FW), BF16),
        V((FW, N), BF16), V((RW, N), BF16), V((3, D, W2), BF16), V((RW, D), BF16), V((N, 128), jnp.int32), V((8, N), jnp.int32),
        V((8, -(-2 * D // 128) * 128 + 256), F32), V((8, -(-10 * D // 128) * 128 + 512), F32), V((R, D), BF16),
        DMA((C,)), DMA((C,)), DMA((C,)), DMA((C,)), DMA((C, 4)), DMA((3, C)), DMA((4,)), DMA((4,)), DMA((C,)), DMA((2,)), DMA((3, 4)),
        DMA((3,)), DMA((4,)), DMA((C,)), DMA((C,)), DMA((S,)), DMA((S,)), DMA((5,)), DMA((8,)), DMA((S,)), DMA((S,)),
        *FarGather.scratch(z), *CtxGather.scratch(z), *CtxReduce.scratch(z),
    ]
    spaces = {"v": pltpu.VMEM, "a": pl.ANY, "s": pltpu.SMEM}
    out = pl.pallas_call(
        partial(kernel_first, z, n_g, n_b, qb), name="first_half", out_shape=outs,
        in_specs=[pl.BlockSpec(memory_space=spaces[c]) for c in "ssvvvaavv"],
        out_specs=[pl.BlockSpec(memory_space=spaces[c]) for c in "a" * 14 + "v" * 8],
        scratch_shapes=scratch,
        compiler_params=pltpu.CompilerParams(collective_id=0, has_side_effects=True, vmem_limit_bytes=VMEM_LIMIT),
    )(*ins)
    return dict(zip(tuple(shapes) + tuple(wide), out))


def ff_block(z, j):
    return pl.ds(pl.multiple_of(j * z.shard, 8), z.shard)


def kernel_f(z, n2h, uah, uph, dnh, prm, hid, xh, rs_i, live, out, gh_o, gb_o, sm, bu, gba, ffr,
             n2, ua, up_t, down, act, gpre, gsend, grecv, fsend, frecv, g32, fs, fr, ld, gs, gr, cs, cr, ps, pr, wb, *gsem):
    at = Place(z)
    S, R, D, C = z.seq, z.rows, z.width, z.ctx
    units, step = up_t.shape[0], 256
    b_up = prm[pl.ds(8 + at.s, 1)]
    greet([at.sib] + at.same[1:], at.seqs[1:], False)
    chunks = [slice(c0, min(c0 + step, units)) for c0 in range(0, units, step)]
    loads = [pltpu.make_async_copy(n2h, n2, ld.at[0]), pltpu.make_async_copy(uah, ua, ld.at[1])]
    for i, c in enumerate(chunks):
        loads.append(pltpu.make_async_copy(uph.at[c], up_t.at[c], ld.at[2 + 2 * i]))
        loads.append(pltpu.make_async_copy(dnh.at[c], down.at[c], ld.at[3 + 2 * i]))
    for c in loads:
        c.start()
    loads[0].wait()
    loads[1].wait()
    for i, c in enumerate(chunks):
        loads[2 + 2 * i].wait()
        pre = matmul(n2[...], up_t[c], 1, 1) + b_up[:, c]
        loads[3 + 2 * i].wait()
        gact = matmul(ua[...], down[c], 1, 1)
        cdf = 0.5 * (1.0 + lax.erf(pre * (0.5 ** 0.5)))
        act[:, c] = (pre * cdf).astype(BF16)
        dgelu = cdf + pre * jnp.exp(-0.5 * pre * pre) * (1.0 / math.sqrt(2.0 * math.pi))
        g = (gact * dgelu).astype(BF16)
        gpre[:, c] = g
        bu[:, c] = jnp.sum(g.astype(F32), axis=0, keepdims=True)
    met(at.chips + S - 1)

    def gcopy(i):
        return rcopy(gsend.at[i], grecv.at[i], gs.at[i], gr.at[i], seq=at.seqs[i])

    def fcopy(i):
        return rcopy(fsend.at[i], frecv.at[i], cs.at[i], cr.at[i], seq=at.seqs[i])

    def pair(t, u):
        return rcopy(fs.at[t, u], fr.at[t, u], ps.at[t, u], pr.at[t, u], ctx=at.sib)

    def weight_grad(u, left, right):
        for c in chunks:
            g32[u, c] = matmul(left[:, c], right[...], 0, 0)
        for t in range(4):
            fs[t, u] = g32[u, ff_block(z, 2 * at.ring[t] + 1 - at.core)].astype(BF16)
            pair(t, u).start()

    def both(u):
        for t in range(4):
            pair(t, u).wait_recv()
            fr[t, u] = (g32[u, ff_block(z, at.same[t])] + fr[t, u].astype(F32)).astype(BF16)
            pltpu.make_async_copy(fr.at[t, u], ffr.at[t, u], wb.at[t, u]).start()

    for i in (2, 1, 3):
        gsend[i] = matmul(gpre[block(z, at.seqs[i])], up_t[...]).astype(BF16)
        gcopy(i).start()
    mine = block(z, at.s)
    gn2 = matmul(gpre[mine], up_t[...])
    weight_grad(0, gpre, n2)
    for i in range(1, S):
        gcopy(i).wait_recv()
        gn2 = gn2 + grecv[i].astype(F32)
    xhat = xh[...]
    up_own = ua[mine].astype(F32)
    gh = up_own + norm_back(gn2, xhat, rs_i[:, :1], prm[1:2])
    gb_o[...] = gh.astype(BF16)
    gat = DirectGather(at, gb_o, gba, gsem)
    gat.send()
    gh_o[...] = gh
    sm[0:1] = jnp.sum(gn2 * xhat, axis=0, keepdims=True)
    sm[1:2] = jnp.sum(gn2, axis=0, keepdims=True)
    sm[2:3] = jnp.sum(gb_o[...].astype(F32), axis=0, keepdims=True)
    sm[3:4] = jnp.sum(up_own, axis=0, keepdims=True)
    for i in (2, 1, 3):
        fsend[i] = matmul(act[block(z, at.seqs[i])], down[...]).astype(BF16)
        fcopy(i).start()
    ff = matmul(act[mine], down[...])
    weight_grad(1, act, ua)
    both(0)
    for i in (1, 3):
        gat.forward(i)
    both(1)
    for i in range(1, S):
        fcopy(i).wait_recv()
        ff = ff + frecv[i].astype(F32)
    out[...] = jnp.transpose(live[:, :1] * (hid[...] + ff + prm[7:8])).astype(BF16)
    gat.forward(2)
    gat.finish()
    for t in range(4):
        for u in range(2):
            pair(t, u).wait_send()
            pltpu.make_async_copy(fr.at[t, u], ffr.at[t, u], wb.at[t, u]).wait()
    for i in range(1, S):
        gcopy(i).wait_send()
        fcopy(i).wait_send()


def stage_f_kernel(z, b):
    R, D, S, U, C, SH = z.rows, z.width, z.seq, z.ctx * z.shard, z.ctx, z.shard
    outs = [sds((D, R)), sds((R, D), F32), sds((R, D)), sds((4, D), F32), sds((1, U), F32), sds((C, R, D)), sds((4, 2, SH, D))]
    V = pltpu.VMEM
    scratch = [
        V((S * R, D), BF16), V((S * R, D), BF16), V((U, D), BF16), V((U, D), BF16), V((S * R, U), BF16), V((S * R, U), BF16),
        *[V((S, R, D), BF16) for _ in range(4)], V((2, U, D), F32), V((4, 2, SH, D), BF16), V((4, 2, SH, D), BF16),
        DMA((2 + 2 * -(-U // 256),)), *[DMA((S,)) for _ in range(4)], DMA((4, 2)), DMA((4, 2)), DMA((4, 2)),
        *DirectGather.scratch(z),
    ]
    return call(
        partial(kernel_f, z), "feed_forward", outs,
        (b["n2a"].reshape(S * R, D), b["ua"].reshape(S * R, D), b["up_t"].reshape(U, D), b["down"].reshape(U, D),
         b["prm"], b["hid"], b["xh"], b["rs"], b["live"]), scratch, 2, "aaaa" + "v" * 5, "v" * 5 + "aa",
    )


class SmallSum:
    def __init__(self, at, buf, rsib, rchip, rseq, sems):
        self.at, self.buf, self.rsib, self.rchip, self.rseq = at, buf, rsib, rchip, rseq
        self.s0, self.r0, self.s1, self.r1, self.s2, self.r2 = sems

    def sib(self):
        return rcopy(self.buf.at[0], self.rsib, self.s0, self.r0, ctx=self.at.sib)

    def chip(self, i):
        return rcopy(self.buf.at[1], self.rchip.at[i], self.s1.at[i], self.r1.at[i], ctx=self.at.same[i])

    def line(self, i):
        return rcopy(self.buf.at[2], self.rseq.at[i], self.s2.at[i], self.r2.at[i], seq=self.at.seqs[i])

    def first(self, value):
        self.buf[0] = value
        self.sib().start()

    def second(self):
        self.sib().wait_recv()
        self.buf[1] = self.buf[0] + self.rsib[...]
        for i in range(1, self.at.chips):
            self.chip(i).start()

    def third(self):
        total = self.buf[1]
        for i in range(1, self.at.chips):
            self.chip(i).wait_recv()
            total = total + self.rchip[i]
        self.buf[2] = total
        for i in range(1, len(self.at.seqs)):
            self.line(i).start()

    def last(self):
        total = self.buf[2]
        for i in range(1, len(self.at.seqs)):
            self.line(i).wait_recv()
            total = total + self.rseq[i]
        return total

    def close(self):
        self.sib().wait_send()
        for i in range(1, self.at.chips):
            self.chip(i).wait_send()
        for i in range(1, len(self.at.seqs)):
            self.line(i).wait_send()

    @staticmethod
    def scratch(z, rows):
        n, shape = z.ctx // 2, (rows, z.width)
        return [
            pltpu.VMEM((3,) + shape, F32), pltpu.VMEM(shape, F32), pltpu.VMEM((n,) + shape, F32),
            pltpu.VMEM((z.seq,) + shape, F32), DMA, DMA, DMA((n,)), DMA((n,)), DMA((z.seq,)), DMA((z.seq,)),
        ]


def attend_block_back(heads, k_t, v, q, go, p_ref, head, gk, gv):
    parts = []
    for h in range(heads):
        goh = of_head(go, h, head).astype(BF16)
        p = p_ref[h]
        pf = p.astype(F32)
        gp = matmul(v, goh, 1, 1)
        delta = jnp.sum(gp * pf, axis=0, keepdims=True)
        gs = (pf * (gp - delta)).astype(BF16)
        gk[...] += matmul(gs, of_head(q, h, head).astype(BF16))
        gv[...] += matmul(p, goh)
        parts.append(matmul(k_t[h * head : (h + 1) * head], gs))
    g_t = parts[0] if len(parts) == 1 else jnp.concatenate(parts, axis=0)
    return (jnp.transpose(g_t) * head ** -0.5).astype(BF16)


def kernel_de(z, qb, gbah, kh, oh, vh, qh, pfh, prh, wh, n1h, xah, ffr,
              wo_f, wo_r, o_r, gh, prm, sm4, bu,
              gtok, ga, gup, gdn, tot, bup,
              gba, k, o_f, v, q, p_f, p_r, w, n1, xa, ld,
              go, kt, krt, gk, gv, gkr, gvr, gcat, gw, gwr, gwo, gwor, sums, ffz, ffo, comb, mid, fz_s, fz_r, fo, fm,
              rf, rr, ro, ror, sf_s, sf_r, sr_s, sr_r, so_s, so_r, sor_s, sor_r,
              zs, zr, land, landr, zs_s, zs_r, zr_s, zr_r,
              buf32, obs, obn, orrs, orr, ob_s, ob_r, orr_s, orr_r, *rest):
    at = Place(z)
    s, me, C, S, FW, RW, SH, D = at.s, at.k, z.ctx, z.seq, z.full_width, z.rest_width, z.shard, z.width
    bufs, small = rest[:11], rest[11:]
    scale, top = z.head ** -0.5, TOP(z)
    mine = block(z, me)
    greet([lax.rem(me + i, C) for i in range(1, C)], at.seqs[1:], False)
    pairs = ((gbah, gba), (kh, k), (oh, o_f), (vh, v), (qh, q), (pfh, p_f), (prh, p_r), (wh, w), (n1h, n1), (xah, xa))
    loads = [pltpu.make_async_copy(a, b, ld.at[i]) for i, (a, b) in enumerate(pairs)]
    for c in loads:
        c.start()
    ownff = pltpu.make_async_copy(ffr.at[0], ffo, fo.at[0])
    ownff.start()
    farff = pltpu.make_async_copy(ffr.at[2], comb, fo.at[1])
    farff.start()
    met(C + S - 2)

    def fz(t):
        return rcopy(ffr.at[t], ffz.at[t], fz_s.at[t], fz_r.at[t], ctx=at.same[t])

    def via(t):
        return rcopy(ffr.at[t], mid, fm.at[0], fm.at[1], ctx=at.same[4 - t])

    def across():
        return rcopy(comb, ffz.at[2], fz_s.at[2], fz_r.at[2], ctx=at.same[2])

    @pl.when(at.chip == 0)
    def _():
        via(3).start()

    @pl.when(at.chip == 3)
    def _():
        via(1).start()

    @pl.when(~at.edge)
    def _():
        fz(1).start()
        fz(3).start()

    gk[...] = jnp.zeros_like(gk)
    gv[...] = jnp.zeros_like(gv)
    gkr[...] = jnp.zeros_like(gkr)
    gvr[...] = jnp.zeros_like(gvr)
    gcat[0, :, FW:] = jnp.zeros((z.slot, FW), BF16)
    for c in loads[:3]:
        c.wait()
    go[...] = matmul(gba[...], wo_f[...], 1, 1).astype(BF16)
    kt[...] = turn(k[:, 0:FW])
    krt[...] = turn(k[:, FW : 2 * FW])[0:RW]
    gwo[...] = matmul(o_f[...], gba[...], 0, 0).astype(BF16)
    gwor[...] = matmul(o_r[...], gba[mine], 0, 0).astype(BF16)

    def up(ref, dst, ssem, rsem, i, m=None):
        return rcopy(ref if m is None else ref.at[m], dst.at[i], ssem.at[i], rsem.at[i], seq=at.seqs[i])

    for i in range(1, S):
        @pl.when(at.seqs[i] == 3)
        def _():
            up(gwo, ro, so_s, so_r, i).start()
            up(gwor, ror, sor_s, sor_r, i).start()

    for c in loads[3:6]:
        c.wait()

    def steps(j, _):
        r = pl.ds(pl.multiple_of(j * qb, qb), qb)
        gcat[0, r, 0:FW] = attend_block_back(z.full, kt[...], v[:, 0:FW], q[r, 0:FW], go[r], p_f.at[j], z.head, gk, gv)
        return 0

    lax.fori_loop(0, z.slot // qb, steps, 0)

    farff.wait()

    @pl.when(at.chip == 0)
    def _():
        via(3).wait_send()
        fz(1).start()

    @pl.when(at.chip == 3)
    def _():
        via(1).wait_send()
        fz(3).start()

    @pl.when(~at.edge)
    def _():
        via(1).wait_recv()
        for u in range(2):
            comb[u] = (comb[u].astype(F32) + mid[u].astype(F32)).astype(BF16)

    across().start()
    loads[6].wait()
    gor = matmul(gba[mine], wo_r[...], 1, 1).astype(BF16)
    gor = jnp.concatenate([gor, jnp.zeros((z.rows, FW - RW), BF16)], axis=1)
    gcat[0, mine, FW : FW + RW] = attend_block_back(
        z.rest, krt[...], v[:, FW : 2 * FW], q[mine, FW : 2 * FW], gor, p_r, z.head, gkr, gvr)
    gcat[1, :, 0:FW] = (gk[...] * scale).astype(BF16)
    gcat[1, :, FW:] = (gkr[...] * scale).astype(BF16)
    gcat[2, :, 0:FW] = gv[...].astype(BF16)
    gcat[2, :, FW:] = gvr[...].astype(BF16)
    for c in loads[7:10]:
        c.wait()

    for m in (2, 1, 0):
        g = matmul(n1[...], gcat[m], 0, 0).reshape(C, SH, 2 * FW)
        gw[m] = g[:, :, 0:FW].astype(BF16)
        g = g[:, :, FW : FW + RW]
        low = jnp.concatenate([g[:, top:], jnp.zeros((C, 2 * top - SH, RW), F32)], axis=1)
        gwr[m] = jnp.concatenate([g[:, :top], low], axis=2).astype(BF16)
    for i in (2, 1, 3):
        m = at.seqs[i]

        @pl.when(m < 3)
        def _():
            up(gw, rf, sf_s, sf_r, i, m).start()
            up(gwr, rr, sr_s, sr_r, i, m).start()

    sums[...] = jnp.zeros_like(sums)

    def part(d):
        r = block(z, d)
        total = matmul(gcat[0, r], w[0], 1, 1) + matmul(gcat[1, r], w[1], 1, 1) + matmul(gcat[2, r], w[2], 1, 1)
        sums[8:9] += jnp.sum(total * norm_stats(xa[r].astype(F32))[0], axis=0, keepdims=True)
        sums[9:10] += jnp.sum(total, axis=0, keepdims=True)
        return total

    red = CtxReduce(at, part, bufs)
    red.start()
    own = part(me)

    def cols(m):
        a = jnp.sum(gcat[m].astype(F32), axis=0, keepdims=True)
        return jnp.concatenate([jnp.where(me == c, a[:, 0:FW], 0.0) for c in range(C)] + [a[:, FW : FW + RW]], axis=1)

    sums[0:4] = sm4[...]
    sums[4:5] = cols(0)
    sums[5:6] = cols(2)
    sums[6:7] = bu[...]
    se = SmallSum(at, *small[:4], small[4:])
    se.first(sums[...])

    se.second()

    def zf(i):
        return rcopy(zs.at[lax.rem(me + i, C)], land.at[i], zs_s.at[i], zs_r.at[i], ctx=lax.rem(me + i, C))

    def zrr(i):
        return rcopy(zr.at[lax.rem(me + i, C)], landr.at[i], zr_s.at[i], zr_r.at[i], ctx=lax.rem(me + i, C))

    def shift():
        return rcopy(obs, obn, ob_s, ob_r, ctx=lax.rem(me + C - 1, C))

    def tail(i):
        return rcopy(orrs, orr.at[i], orr_s, orr_r.at[i], ctx=C - 1)

    @pl.when(s < 3)
    def _():
        for i in range(1, S):
            up(gw, rf, sf_s, sf_r, i, 0).wait_recv()
            up(gwr, rr, sr_s, sr_r, i, 0).wait_recv()

        def add(j, _):
            t, u = gw[s, j].astype(F32), gwr[s, j].astype(F32)
            for i in range(1, S):
                t = t + rf[i, j].astype(F32)
                u = u + rr[i, j].astype(F32)
            zs[j] = t.astype(BF16)
            zr[j] = u.astype(BF16)
            return 0

        lax.fori_loop(0, C, add, 0)
        for i in range(1, C):
            zf(i).start()
            zrr(i).start()

    @pl.when(s == 3)
    def _():
        for i in range(1, S):
            up(gwo, ro, so_s, so_r, i).wait_recv()
            up(gwor, ror, sor_s, sor_r, i).wait_recv()
        t, u = gwo[...].astype(F32), gwor[...].astype(F32)
        for i in range(1, S):
            t = t + ro[i].astype(F32)
            u = u + ror[i].astype(F32)
        buf32[pl.ds(0, FW)] = t
        obs[...] = t.astype(BF16)
        orrs[...] = u.astype(BF16)

        @pl.when(me > 0)
        def _():
            shift().start()

        for i in range(C - 1):
            @pl.when(me == i)
            def _():
                tail(i).start()

    se.third()

    ownff.wait()
    across().wait_recv()
    for u, g in enumerate((gup, gdn)):
        g[...] = ffo[u].astype(F32) + ffz[2, u].astype(F32)
    for t in (1, 3):
        @pl.when(at.chip != (0 if t == 1 else 3))
        def _():
            fz(t).wait_recv()
            for u, g in enumerate((gup, gdn)):
                g[...] += ffz[t, u].astype(F32)

    xhat, rstd = norm_stats(xa[mine].astype(F32))
    gn1 = red.finish(own)
    gtok[...] = jnp.transpose(gh[...] + norm_back(gn1, xhat, rstd, prm[0:1]))

    @pl.when(s < 3)
    def _():
        ga[:, pl.ds(pl.multiple_of(me * FW, FW), FW)] = zs[me].astype(F32)
        remain = zr[me].astype(F32)
        for i in range(1, C):
            zf(i).wait_recv()
            zrr(i).wait_recv()
            j = lax.rem(me + C - i, C)
            ga[:, pl.ds(pl.multiple_of(j * FW, FW), FW)] = land[i].astype(F32)
            remain = remain + landr[i].astype(F32)
        ga[0:top, z.main :] = remain[:, 0:RW]
        ga[top:SH, z.main :] = remain[0 : SH - top, RW : 2 * RW]
        for i in range(1, C):
            zf(i).wait_send()
            zrr(i).wait_send()

    @pl.when(s == 3)
    def _():
        @pl.when(me < C - 1)
        def _():
            shift().wait_recv()
            buf32[pl.ds(FW, FW)] = obn[...].astype(F32)

        @pl.when(me == C - 1)
        def _():
            u = orrs[...].astype(F32)
            for i in range(C - 1):
                tail(i).wait_recv()
                u = u + orr[i].astype(F32)
            buf32[pl.ds(FW, RW)] = u

        ga[...] = buf32[pl.ds(pl.multiple_of((SH - FW) * me, 8), SH)]

        @pl.when(me > 0)
        def _():
            shift().wait_send()

        @pl.when(me < C - 1)
        def _():
            tail(0).wait_send()

    tot[...] = se.last()
    bup[s] = se.buf[2, 6:7]
    for i in range(1, S):
        bup[at.seqs_back[i]] = se.rseq[i, 6:7]
    red.close()
    se.close()
    across().wait_send()

    @pl.when(at.chip != 3)
    def _():
        fz(1).wait_send()

    @pl.when(at.chip != 0)
    def _():
        fz(3).wait_send()
    for i in range(1, S):
        m = at.seqs[i]

        @pl.when(m < 3)
        def _():
            up(gw, rf, sf_s, sf_r, i, m).wait_send()
            up(gwr, rr, sr_s, sr_r, i, m).wait_send()

        @pl.when(m == 3)
        def _():
            up(gwo, ro, so_s, so_r, i).wait_send()
            up(gwor, ror, sor_s, sor_r, i).wait_send()


def TOP(z):
    return -(-z.shard // 16) * 8


def stage_de_kernel(z, b, gba, ffr, gh, sm4, bu):
    C, S, D, FW, RW, SH, N, R, qb = z.ctx, z.seq, z.width, z.full_width, z.rest_width, z.shard, z.slot, z.rows, 512
    nq, W2, top = N // qb, 2 * FW, TOP(z)
    outs = [sds((D, R), F32), sds((SH, D), F32), sds((SH, D), F32), sds((SH, D), F32), sds((10, D), F32), sds((S, 1, D), F32)]
    V = pltpu.VMEM
    scratch = [
        V((N, D), BF16), V((N, W2), BF16), V((N, FW), BF16), V((N, W2), BF16), V((N, W2), BF16), V((nq, z.full, N, qb), BF16),
        V((z.rest, N, R), BF16), V((3, D, W2), BF16), V((N, D), BF16), V((N, D), BF16), DMA((10,)),
        V((N, FW), BF16), V((FW, N), BF16), V((RW, N), BF16), *[V((N, FW), F32) for _ in range(4)],
        V((3, N, W2), BF16), V((3, C, SH, FW), BF16), V((3, C, top, 2 * RW), BF16), V((FW, D), BF16), V((RW, D), BF16), V((10, D), F32),
        V((4, 2, SH, D), BF16), V((2, SH, D), BF16), V((2, SH, D), BF16), V((2, SH, D), BF16), DMA((4,)), DMA((4,)), DMA((2,)), DMA((2,)),
        V((S, C, SH, FW), BF16), V((S, C, top, 2 * RW), BF16), V((S, FW, D), BF16), V((S, RW, D), BF16), *[DMA((S,)) for _ in range(8)],
        V((C, SH, FW), BF16), V((C, top, 2 * RW), BF16), V((C, SH, FW), BF16), V((C, top, 2 * RW), BF16),
        *[DMA((C,)) for _ in range(4)],
        V((2 * FW, D), F32), V((FW, D), BF16), V((FW, D), BF16), V((RW, D), BF16), V((C, RW, D), BF16),
        DMA, DMA, DMA, DMA((C,)),
        *CtxReduce.scratch(z), *SmallSum.scratch(z, 10),
    ]
    gtok, ga, gup, gdn, tot, bup = call(
        partial(kernel_de, z, qb), "attention_back", outs,
        (gba.reshape(N, D), b["k"], b["o_f"], b["v"], b["q"], b["p_f"], b["p_r"], b["w3"], b["n1"], b["xa"].reshape(N, D), ffr,
         b["wo_f"], b["wo_r"], b["o_r"], gh, b["prm"], sm4, bu),
        scratch, 4, "a" * 11 + "v" * 7, "v" * 6,
    )
    names = ("gain2", "shift2", "b_o", "b_down", "b_q", "b_v", None, None, "gain1", "shift1")
    return gtok, ga, gup, gdn, {n: tot[j : j + 1] for j, n in enumerate(names) if n}, bup.reshape(-1)


def kernel_leave(n, *refs):
    ins, outs, bufs, sems = refs[:n], refs[n : 2 * n], refs[2 * n : 3 * n], refs[3 * n]
    loads = [pltpu.make_async_copy(ins[i], bufs[i], sems.at[0, i]) for i in range(n)]
    stores = [pltpu.make_async_copy(bufs[i], outs[i], sems.at[1, i]) for i in range(n)]
    for c in loads:
        c.start()
    for a, b in zip(loads, stores):
        a.wait()
        b.start()
    for c in stores:
        c.wait()


def leave(arrays):
    n = len(arrays)
    return pl.pallas_call(
        partial(kernel_leave, n), name="leave", out_shape=[sds(a.shape, a.dtype) for a in arrays],
        in_specs=[pl.BlockSpec(memory_space=pl.ANY)] * n, out_specs=[pl.BlockSpec(memory_space=pl.ANY)] * n,
        scratch_shapes=[pltpu.VMEM(a.shape, a.dtype) for a in arrays] + [DMA((2, n))],
    )(*arrays)


def shards(tokens, lengths, block_order, attention_weights, up_weights, down_weights, norm_gains, biases, cotangent):
    z = Sizes(tokens.shape[1], tokens.shape[2], block_order.shape[0])
    i, s = lax.axis_index("ctx"), lax.axis_index("seq")
    me, D = s * z.ctx + i, z.width
    n_g, n_b = norm_gains.shape[0], biases.shape[0]
    fast = (
        z.ctx == 8 and z.seq == 4 and 0 < D - z.main <= z.shard and z.rest == 1 and z.full_width == 128
        and z.ctx * up_weights.shape[1] == D and z.rows == 2 * z.block_len and n_g <= 128 and n_b <= 384
    )
    if fast:
        b = stage_first_kernel(
            z, tokens, lengths, block_order, attention_weights, up_weights, down_weights, norm_gains, biases, cotangent)
        output, gh, _, sm4, bu, gba, ffr = stage_f_kernel(z, b)
        gtok, gw, g_up_own, g_down_own, tot, b_up_all = stage_de_kernel(z, b, gba, ffr, gh, sm4, bu)
    else:
        x, cot, length = tokens[0], cotangent[0], lengths[0]
        pos = (block_order[:, None] * z.block_len + jnp.arange(z.block_len, dtype=jnp.int32)[None, :]).reshape(z.slot)
        my_pos = lax.dynamic_slice_in_dim(pos, i * z.rows, z.rows)
        live = (my_pos < length).astype(F32)[:, None]
        lanes = -(-(n_g + n_b) // 1024) * 8
        packed = jnp.pad(jnp.concatenate([norm_gains, biases]), (0, lanes * 128 - n_g - n_b)).reshape(lanes, 128)
        upstream = (live * cot.astype(F32)).astype(BF16)
        x_all, wf, wr, wo_f, wo_r = stage_a(z, x, attention_weights)
        ua = lax.all_gather(upstream, "seq", axis=0, tiled=True)
        both = lax.all_gather(packed, ("seq", "ctx"), axis=0).reshape(z.seq * z.ctx, lanes * 128)
        gains = both[:, :n_g].reshape(-1).astype(F32)
        bias = both[:, n_g : n_g + n_b].reshape(-1).astype(F32)
        row = lambda v: v[None, :]
        piece = [row(bias[j * D : (j + 1) * D]) for j in range(6)]
        gain1, gain2 = row(gains[:D]), row(gains[D:])
        units = z.ctx * up_weights.shape[1]
        b_up = row(lax.dynamic_slice_in_dim(bias[6 * D :], s * units, units))
        prm = dict(gain2=gain2, shift2=piece[4], b_o=piece[3], b_down=piece[5], b_up=b_up)
        fslice = lambda v: lax.dynamic_slice(v, (0, i * z.full_width), (1, z.full_width))
        up_t = lax.all_gather(up_weights.T, "ctx", axis=0, tiled=True)
        down = lax.all_gather(down_weights, "ctx", axis=0, tiled=True)
        b = stage_b(z, x_all, wf, wr, gain1, piece[0], fslice(piece[1]), piece[1][:, z.main :],
                    fslice(piece[2]), piece[2][:, z.main :], pos, length)
        output, gh, gb, g_up_t, g_down, small = stage_c(z, b, wo_f, wo_r, x, upstream, ua, live, up_t, down, prm)
        g_up_own = lax.psum_scatter(g_up_t, "ctx", scatter_dimension=0, tiled=True).astype(F32).T
        g_down_own = lax.psum_scatter(g_down, "ctx", scatter_dimension=0, tiled=True).astype(F32)
        gba = lax.all_gather(gb, "ctx", axis=0, tiled=True) if z.full else None
        d = stage_d(z, b, gb, gba, wo_f, wo_r)
        gtok, gw, tot, b_up_all = stage_e(z, d, wf, wr, x, gh, gain1, small)
    if fast:
        output, gtok, gw, g_up_own, g_down_own = leave((output, gtok, gw, g_up_own, g_down_own))
        output, gtok, g_up_own = output.T, gtok.T, g_up_own.T
    g_gain = lax.dynamic_slice_in_dim(jnp.concatenate([tot["gain1"][0], tot["gain2"][0]]), me * n_g, n_g)
    g_bias = lax.dynamic_slice_in_dim(jnp.concatenate([tot[n][0] for n in ("shift1", "b_q", "b_v", "b_o", "shift2", "b_down")] + [b_up_all]), me * n_b, n_b)
    return output[None], gtok[None], gw, g_up_own, g_down_own, g_gain, g_bias


def solution(mesh):
    in_specs = (
        P("seq", "ctx", None), P("seq"), P(), P(("seq", "ctx"), None), P(None, ("seq", "ctx")),
        P(("seq", "ctx"), None), P(("seq", "ctx")), P(("seq", "ctx")), P("seq", "ctx", None),
    )
    out_specs = (
        P("seq", "ctx", None), P("seq", "ctx", None), P(("seq", "ctx"), None), P(None, ("seq", "ctx")),
        P(("seq", "ctx"), None), P(("seq", "ctx")), P(("seq", "ctx")),
    )
    return jax.shard_map(shards, mesh=mesh, in_specs=in_specs, out_specs=out_specs, check_vma=False)
```
